32 devices in a mesh: rep: 4 (over x, core), seq: 8 (over z, y).
Axes of the slice: x: 2, y: 2, z: 4, core: 2. Of those that a mesh axis runs over, the one named last changes fastest.
Arguments:
- tokens: bfloat16 [4, 1536, 768], P('rep', 'seq'), may hold values from -6 to 6
- segment_ids: int32 [4, 1536], P('rep', 'seq'), may hold values from 0 to 3, never falling along the last dimension, each value on 1 to 768 neighbouring positions
- query_key_value_weight: bfloat16 [768, 2304], P('seq'), may hold values from -0.21875 to 0.21875
- output_weight: bfloat16 [768, 768], P('seq'), may hold values from -1.75 to 1.75
- up_weight: bfloat16 [768, 3072], P('seq'), may hold values from -0.21875 to 0.21875
- down_weight: bfloat16 [3072, 768], P('seq'), may hold values from -0.109375 to 0.109375
- ln_gains: bfloat16 [2, 768], P(None, 'seq'), may hold values from 0.5 to 1.5
- ln_biases: bfloat16 [2, 768], P(None, 'seq'), may hold values from -2 to 2
- biases: bfloat16 [4, 768], P(None, 'seq'), may hold values from -3 to 3
- up_projection_bias: bfloat16 [3072], P('seq'), may hold values from -3 to 3
- cotangent: bfloat16 [4, 1536, 768], P('rep', 'seq'), may hold values from -6 to 6
Outputs:
- output: bfloat16 [4, 1536, 768], P('rep', 'seq')
- grad_tokens: float32 [4, 1536, 768], P('rep', 'seq')
- grad_w_qkv: float32 [768, 2304], P('seq')
- grad_w_out: float32 [768, 768], P('seq')
- grad_w_up: float32 [768, 3072], P('seq')
- grad_w_down: float32 [3072, 768], P('seq')
- grad_ln_gains: float32 [2, 768], P(None, 'seq')
- grad_ln_biases: float32 [2, 768], P(None, 'seq')
- grad_biases: float32 [4, 768], P(None, 'seq')
- grad_up_bias: float32 [3072], P('seq')
The draws below stay inside these ranges and needn't reach their ends.
Inputs may be any that keep to these rules, and one draw needn't show every extreme that they name: `segment_ids`: along each sequence the ids never fall; each of the 4 documents of a sequence holds 1 to 768 tokens, and one holds exactly 768.
All inputs are finite; a program needn't handle non-finite values.
Results may differ from the reference program's by a relative error of at most 0.015.
Values may be sent and summed in bfloat16 or wider, within the bound.
No kernel may reach another device: no remote copies, remote signals or barrier semaphores. Data moves between devices by JAX's collectives and lax.ppermute only.
A program may use at most 256 MiB of HBM per device.

```python
import math
import jax
import jax.numpy as jnp
import numpy as np
from jax import lax

D = 768
HEADS = 12
HD = 64
FF = 3072
SEQS = 4
SEQLEN = 1536
SEGS = 4
SEGMOST = 768


def block_levels(own_key, extent, pieces, low, high):
    level = 1.0
    for position, shards_of in pieces:
        steps = jax.random.uniform(jax.random.fold_in(jax.random.fold_in(own_key, 6), position), (shards_of,), jnp.float32, low / len(pieces), high / len(pieces))
        level = level * jnp.repeat(jnp.exp(steps), extent[position] // shards_of).reshape((-1,) + (1,) * (len(extent) - 1 - position))
    return level


def profile(count, total, bound, slope):
    portions = [(1 << 20) // math.isqrt(standing ** slope) + 1 for standing in range(2, count + 1)]
    rest, given = total - bound - (count - 1), [1] * (count - 1)
    while rest > 0:
        movable = [i for i in range(count - 1) if given[i] < bound]
        pool, remaining = sum([portions[i] for i in movable]), rest
        for i in movable:
            more = min(bound - given[i], max(1, remaining * portions[i] // pool), rest)
            given[i] = given[i] + more
            rest = rest - more
    return np.array([bound] + given)


def uneven_parts(key, number_of, total, reach, slope):
    if number_of == 2:
        one = jax.random.randint(key, (), max(1, total - reach), min(reach, total - 1) + 1)
        return jnp.stack([one, total - one])
    tallies = jnp.asarray(profile(number_of, total, reach, slope), jnp.int32)
    couples = (number_of - 1) // 2
    giver, receiver = tallies[1:1 + 2 * couples:2], tallies[2:2 + 2 * couples:2]
    room = jnp.minimum(giver - 1, reach - receiver)
    moved = jax.random.randint(jax.random.fold_in(key, 1), (couples,), 0, 1 << 20) % (room + 1)
    tallies = tallies.at[1:1 + 2 * couples:2].set(giver - moved).at[2:2 + 2 * couples:2].set(receiver + moved)
    return tallies[jax.random.permutation(jax.random.fold_in(key, 2), number_of)]


def scatter_about(stream_key, shape, width, reach, shards=(), held_as=jnp.bfloat16):
    factor_of = block_levels(stream_key, shape, shards, -0.22, 0.18) if shards else 1.0
    values = jax.random.normal(stream_key, shape, jnp.float32) * width * factor_of
    return jnp.minimum(jnp.maximum(values, -reach), reach).astype(held_as)


def setup_inputs(seed: int = 0) -> dict:
    key_list = jax.random.split(jax.random.key(seed), 12)
    return {
        "tokens": scatter_about(key_list[0], (SEQS, SEQLEN, D), 1.0, 6.0, ((0, 4), (1, 8))),
        "segment_ids": jax.vmap(lambda own: jnp.searchsorted(jnp.cumsum(uneven_parts(own, SEGS, SEQLEN, SEGMOST, 2)), jnp.arange(SEQLEN), side="right"))(jax.random.split(key_list[1], SEQS)).reshape((SEQS, SEQLEN)).astype(jnp.int32),
        "query_key_value_weight": scatter_about(key_list[2], (D, 3 * D), D ** -0.5, 0.21875, ((0, 8),)),
        "output_weight": scatter_about(key_list[3], (D, D), (max(1, D // 64)) ** -0.5, 1.75, ((0, 8),)),
        "up_weight": scatter_about(key_list[4], (D, FF), D ** -0.5, 0.21875, ((0, 8),)),
        "down_weight": scatter_about(key_list[5], (FF, D), FF ** -0.5, 0.109375, ((0, 8),)),
        "ln_gains": jnp.clip(1.0 + 0.1 * jax.random.normal(key_list[6], (2, D), jnp.float32), 0.5, 1.5).astype(jnp.bfloat16),
        "ln_biases": scatter_about(key_list[7], (2, D), 0.3, 2.0, ((1, 8),)),
        "biases": scatter_about(key_list[8], (4, D), 0.5, 3.0, ((1, 8),)),
        "up_projection_bias": scatter_about(key_list[9], (FF,), 0.5, 3.0, ((0, 8),)),
        "cotangent": scatter_about(key_list[10], (SEQS, SEQLEN, D), 1.0, 6.0, ((0, 4), (1, 8))),
    }


@jax.custom_vjp
def low(v):
    return lax.optimization_barrier(v.astype(jnp.bfloat16)).astype(jnp.float32)

@jax.custom_vjp
def reduced_backward(v):
    return v

def low_keep(v):
    return (low(v), None)

def low_pass(kept, grad):
    return (grad,)

def back_keep(v):
    return (v, None)

def back_low(kept, grad):
    return (low(grad),)
low.defvjp(low_keep, low_pass)
reduced_backward.defvjp(back_keep, back_low)
norm_eps = 1e-05
highest_precision = lax.Precision.HIGHEST

def layer_norm(values, gain, shift):
    center = values - lax.optimization_barrier(jnp.mean(values, axis=-1, keepdims=True))
    spread = lax.optimization_barrier(jnp.mean(center * center, axis=-1, keepdims=True))
    return center * lax.rsqrt(spread + norm_eps) * gain + shift

def attend_sequence(inputs):
    queries, keys_all, values_all, seg_all = inputs
    length = queries.shape[0]
    block_rows = math.gcd(length, 512)
    blocks = length // block_rows
    head_scale = HD ** (-0.5)
    key_pos = jnp.arange(length, dtype=jnp.int32)

    def one_block(parts):
        query_block, query_seg, offset = parts
        scores = jnp.einsum('qhd,khd->hqk', query_block, keys_all, precision=highest_precision) * head_scale
        scores = reduced_backward(scores)
        query_pos = offset + jnp.arange(block_rows, dtype=jnp.int32)
        allowed = (query_seg[:, None] == seg_all[None, :]) & (key_pos[None, :] <= query_pos[:, None])
        scores = jnp.where(allowed[None], scores, -1e+30)
        top_score = lax.optimization_barrier(jnp.max(scores, axis=-1, keepdims=True))
        log_total = top_score + jnp.log(lax.optimization_barrier(jnp.sum(jnp.exp(scores - top_score), axis=-1, keepdims=True)))
        weights_p = low(jnp.exp(scores - log_total))
        return jnp.einsum('hqk,khd->qhd', weights_p, values_all, precision=highest_precision)
    result = lax.map(jax.checkpoint(one_block), (queries.reshape(blocks, block_rows, HEADS, HD), seg_all.reshape(blocks, block_rows), jnp.arange(blocks, dtype=jnp.int32) * block_rows))
    return result.reshape(length, HEADS * HD)

def layer(tokens_f, query_key_value_weight, output_weight, up_weight, down_weight, ln_gains, ln_biases, biases, up_projection_bias, segment_ids):
    seq_count = tokens_f.shape[0]
    length = tokens_f.shape[1]
    hidden_first = low(layer_norm(tokens_f, ln_gains[0], ln_biases[0]))
    query_key_value_bias = jnp.concatenate([biases[0], jnp.zeros_like(biases[0]), biases[1]])
    projected_rows = jnp.einsum('kqy,yg->kqg', hidden_first, query_key_value_weight, precision=highest_precision) + query_key_value_bias
    projected_rows = low(reduced_backward(projected_rows))
    heads_view = projected_rows.reshape(seq_count, length, 3, HEADS, HD)
    attention_result = lax.map(attend_sequence, (heads_view[:, :, 0], heads_view[:, :, 1], heads_view[:, :, 2], segment_ids))
    attention_result = low(reduced_backward(attention_result))
    mixed_attention = reduced_backward(jnp.einsum('kqy,yg->kqg', attention_result, output_weight, precision=highest_precision)) + biases[2]
    residual_first = tokens_f + mixed_attention
    hidden_second = low(layer_norm(residual_first, ln_gains[1], ln_biases[1]))
    upward_rows = reduced_backward(jnp.einsum('uct,tm->ucm', hidden_second, up_weight, precision=highest_precision) + up_projection_bias)
    activation_values = low(jax.nn.gelu(upward_rows))
    return residual_first + jnp.einsum('yrt,tz->yrz', activation_values, down_weight, precision=highest_precision) + biases[3]

def reference(tokens, segment_ids, query_key_value_weight, output_weight, up_weight, down_weight, ln_gains, ln_biases, biases, up_projection_bias, cotangent):
    floats = tuple((member.astype(jnp.float32) for member in (tokens, query_key_value_weight, output_weight, up_weight, down_weight, ln_gains, ln_biases, biases, up_projection_bias)))

    def forward(tokens_f, qkv_f, out_f, up_f, down_f, gains_f, shifts_f, biases_f, up_shift):
        return layer(tokens_f, qkv_f, out_f, up_f, down_f, gains_f, shifts_f, biases_f, up_shift, segment_ids)
    output, pullback = jax.vjp(forward, *floats)
    gradients = pullback(cotangent.astype(jnp.float32))
    return (output.astype(jnp.bfloat16), gradients[0], gradients[1], gradients[2], gradients[3], gradients[4], gradients[5], gradients[6], gradients[7], gradients[8])
```

```python
import math

import jax
import jax.numpy as jnp
from jax import lax
from jax.experimental import pallas as pl
from jax.experimental.pallas import tpu as pltpu
from jax.sharding import PartitionSpec as P

HEADS = 12
HD = 64


norm_eps = 1e-05
floor_score = -1e30


def layer_norm(values, gain, shift):
    center = values - jnp.mean(values, axis=-1, keepdims=True)
    spread = jnp.mean(center * center, axis=-1, keepdims=True)
    return center * lax.rsqrt(spread + norm_eps) * gain + shift


def head_split(matrix):
    return matrix.reshape(matrix.shape[0], HEADS, HD)


def masked_scores(queries, query_seg, query_pos, key_piece, seg_piece, offset):
    rows = key_piece.shape[0]
    scores = jnp.einsum(
        "qhd,khd->hqk", queries, head_split(key_piece), preferred_element_type=jnp.float32
    ) * HD ** (-0.5)
    key_pos = offset + jnp.arange(rows, dtype=jnp.int32)
    allowed = (query_seg[:, None] == seg_piece[None, :]) & (key_pos[None, :] <= query_pos[:, None])
    return (jnp.where(allowed[None], scores, floor_score), allowed)


def forward_block(running, pieces, offset, queries, query_seg, query_pos):
    top_run, total_run, accum = running
    key_piece, value_piece, seg_piece = pieces
    scores, allowed = masked_scores(queries, query_seg, query_pos, key_piece, seg_piece, offset)
    top_new = jnp.maximum(top_run, jnp.max(scores, axis=-1))
    probs = jnp.where(allowed[None], jnp.exp(scores - top_new[:, :, None]), 0.0)
    factor = jnp.exp(top_run - top_new)
    total_new = total_run * factor + jnp.sum(probs, axis=-1)
    update = jnp.einsum(
        "hqk,khd->qhd",
        probs.astype(jnp.bfloat16),
        head_split(value_piece),
        preferred_element_type=jnp.float32,
    )
    return (top_new, total_new, accum * factor.T[:, :, None] + update)


def in_blocks(block_fn, running, pieces):
    rows = pieces[0].shape[0]
    size = math.gcd(rows, 1024)
    stacked = tuple((member.reshape((rows // size, size) + member.shape[1:]) for member in pieces))
    offsets = jnp.arange(rows // size, dtype=jnp.int32) * size

    def scan_step(state_now, element):
        return (block_fn(state_now, element[0], element[1]), None)

    running, _unused = lax.scan(scan_step, running, (stacked, offsets))
    return running


def backward_block(
    number,
    state_now,
    whole,
    queries,
    query_seg,
    query_pos,
    grad_heads,
    log_total,
    delta,
    block_rows,
):
    grad_query, term = state_now
    offset = number * block_rows
    key_piece = lax.dynamic_slice_in_dim(whole[0], offset, block_rows, 0)
    value_piece = lax.dynamic_slice_in_dim(whole[1], offset, block_rows, 0)
    seg_piece = lax.dynamic_slice_in_dim(whole[2], offset, block_rows, 0)
    scores, allowed = masked_scores(queries, query_seg, query_pos, key_piece, seg_piece, offset)
    probs = jnp.where(allowed[None], jnp.exp(scores - log_total[:, :, None]), 0.0)
    grad_probs = jnp.einsum(
        "qhd,khd->hqk", grad_heads, head_split(value_piece), preferred_element_type=jnp.float32
    )
    grad_scores = (probs * (grad_probs - delta[:, :, None])).astype(jnp.bfloat16)
    grad_query = grad_query + jnp.einsum(
        "hqk,khd->qhd", grad_scores, head_split(key_piece), preferred_element_type=jnp.float32
    )
    grad_key = jnp.einsum(
        "hqk,qhd->khd", grad_scores, queries, preferred_element_type=jnp.float32
    ) * HD ** (-0.5)
    grad_value = jnp.einsum(
        "hqk,qhd->khd", probs.astype(jnp.bfloat16), grad_heads, preferred_element_type=jnp.float32
    )
    joined = jnp.concatenate(
        [grad_key.reshape(block_rows, -1), grad_value.reshape(block_rows, -1)], axis=1
    )
    term = lax.dynamic_update_slice_in_dim(term, joined, offset, 0)
    return (grad_query, term)


def on_device(
    tokens,
    segment_ids,
    query_key_value_weight,
    output_weight,
    up_weight,
    down_weight,
    ln_gains,
    ln_biases,
    biases,
    up_projection_bias,
    cotangent,
):
    gathered = (
        lax.all_gather(query_key_value_weight, "seq", axis=0, tiled=True),
        lax.all_gather(output_weight, "seq", axis=0, tiled=True),
        lax.all_gather(up_weight, "seq", axis=0, tiled=True),
        lax.all_gather(down_weight, "seq", axis=0, tiled=True),
        lax.all_gather(ln_gains, "seq", axis=1, tiled=True),
        lax.all_gather(ln_biases, "seq", axis=1, tiled=True),
        lax.all_gather(biases, "seq", axis=1, tiled=True),
        lax.all_gather(up_projection_bias, "seq", axis=0, tiled=True),
    )
    full_qkv, full_out, full_up, full_down, gains_all, shifts_all, biases_all, up_shift = gathered
    gains_f = gains_all.astype(jnp.float32)
    shifts_f = shifts_all.astype(jnp.float32)
    biases_f = biases_all.astype(jnp.float32)
    up_shift_f = up_shift.astype(jnp.float32)
    tokens_f = tokens[0].astype(jnp.float32)
    seg_local = segment_ids[0]
    tok_rows = tokens_f.shape[0]
    width = tokens_f.shape[1]
    seqlen = tok_rows * lax.axis_size("seq")
    query_pos = lax.axis_index("seq") * tok_rows + jnp.arange(tok_rows, dtype=jnp.int32)
    hidden_first = layer_norm(tokens_f, gains_f[0], shifts_f[0]).astype(jnp.bfloat16)
    query_key_value_bias = jnp.concatenate(
        [biases_f[0], jnp.zeros((width,), jnp.float32), biases_f[1]]
    )
    projected_rows = (
        jnp.dot(hidden_first, full_qkv, preferred_element_type=jnp.float32) + query_key_value_bias
    ).astype(jnp.bfloat16)
    queries = head_split(projected_rows[:, :width])
    key_rows = projected_rows[:, width : 2 * width]
    value_rows = projected_rows[:, 2 * width :]
    initial = (
        jnp.full((HEADS, tok_rows), floor_score, jnp.float32),
        jnp.zeros((HEADS, tok_rows), jnp.float32),
        jnp.zeros((tok_rows, HEADS, HD), jnp.float32),
    )

    def block_fn(running, pieces, offset):
        return forward_block(running, pieces, offset, queries, seg_local, query_pos)

    block_rows = math.gcd(seqlen, 1024)
    key_end = (lax.axis_index("seq") + 1) * tok_rows
    block_count = (key_end + block_rows - 1) // block_rows
    top_run, total_run, accum = in_blocks(
        block_fn,
        initial,
        (
            lax.all_gather(key_rows, "seq", axis=0, tiled=True),
            lax.all_gather(value_rows, "seq", axis=0, tiled=True),
            lax.all_gather(seg_local, "seq", axis=0, tiled=True),
        ),
    )
    log_total = top_run + jnp.log(total_run)
    attended_f = accum / total_run.T[:, :, None]
    attention_result = attended_f.reshape(tok_rows, width).astype(jnp.bfloat16)
    residual_first = (
        tokens_f
        + jnp.dot(attention_result, full_out, preferred_element_type=jnp.float32)
        + biases_f[2]
    )
    hidden_second = layer_norm(residual_first, gains_f[1], shifts_f[1]).astype(jnp.bfloat16)
    upward_rows = jnp.dot(hidden_second, full_up, preferred_element_type=jnp.float32) + up_shift_f
    activated_f, gelu_back = jax.vjp(jax.nn.gelu, upward_rows)
    activation_values = activated_f.astype(jnp.bfloat16)
    result = (
        residual_first
        + jnp.dot(activation_values, full_down, preferred_element_type=jnp.float32)
        + biases_f[3]
    )
    grad_y = cotangent[0]
    grad_y_f = grad_y.astype(jnp.float32)
    grad_down = jnp.einsum(
        "tf,td->fd", activation_values, grad_y, preferred_element_type=jnp.float32
    )
    grad_act = jnp.einsum("td,fd->tf", grad_y, full_down, preferred_element_type=jnp.float32)
    grad_up_pre = gelu_back(grad_act)[0].astype(jnp.bfloat16)
    grad_up = jnp.einsum(
        "td,tf->df", hidden_second, grad_up_pre, preferred_element_type=jnp.float32
    )
    grad_hidden_two = jnp.einsum(
        "tf,df->td", grad_up_pre, full_up, preferred_element_type=jnp.float32
    )
    _unused, norm_two_back = jax.vjp(layer_norm, residual_first, gains_f[1], shifts_f[1])
    grad_sum_part, grad_gain_two, grad_shift_two = norm_two_back(grad_hidden_two)
    grad_first = grad_y_f + grad_sum_part
    grad_first_bf = grad_first.astype(jnp.bfloat16)
    grad_out_w = jnp.einsum(
        "td,te->de", attention_result, grad_first_bf, preferred_element_type=jnp.float32
    )
    grad_attended = jnp.einsum(
        "te,de->td", grad_first_bf, full_out, preferred_element_type=jnp.float32
    ).astype(jnp.bfloat16)
    grad_heads = head_split(grad_attended)
    delta = jnp.einsum("qhd,qhd->hq", grad_heads.astype(jnp.float32), attended_f)
    whole = (
        lax.all_gather(key_rows, "seq", axis=0, tiled=True),
        lax.all_gather(value_rows, "seq", axis=0, tiled=True),
        lax.all_gather(seg_local, "seq", axis=0, tiled=True),
    )

    def backward_step(number, state_now):
        return backward_block(
            number,
            state_now,
            whole,
            queries,
            seg_local,
            query_pos,
            grad_heads,
            log_total,
            delta,
            block_rows,
        )

    start_state = (
        jnp.zeros((tok_rows, HEADS, HD), jnp.float32),
        jnp.zeros((seqlen, 2 * width), jnp.float32),
    )
    grad_query, term = lax.fori_loop(0, block_count, backward_step, start_state)
    grad_kv = lax.psum_scatter(term, "seq", scatter_dimension=0, tiled=True).astype(jnp.bfloat16)
    grad_q = (grad_query * HD ** (-0.5)).reshape(tok_rows, width).astype(jnp.bfloat16)
    grad_proj = jnp.concatenate([grad_q, grad_kv], axis=1)
    grad_qkv_w = jnp.einsum(
        "td,te->de", hidden_first, grad_proj, preferred_element_type=jnp.float32
    )
    grad_hidden_one = jnp.einsum(
        "te,de->td", grad_proj, full_qkv, preferred_element_type=jnp.float32
    )
    _unused_two, norm_one_back = jax.vjp(layer_norm, tokens_f, gains_f[0], shifts_f[0])
    grad_in_part, grad_gain_one, grad_shift_one = norm_one_back(grad_hidden_one)
    grad_tokens = grad_first + grad_in_part
    grad_proj_f = grad_proj.astype(jnp.float32)
    grad_bias_rows = jnp.stack(
        [
            jnp.sum(grad_proj_f[:, :width], axis=0),
            jnp.sum(grad_proj_f[:, 2 * width :], axis=0),
            jnp.sum(grad_first, axis=0),
            jnp.sum(grad_y_f, axis=0),
        ]
    )
    grad_up_shift = jnp.sum(grad_up_pre.astype(jnp.float32), axis=0)
    grad_gains = jnp.stack([grad_gain_one, grad_gain_two])
    grad_shifts = jnp.stack([grad_shift_one, grad_shift_two])
    shares = (
        lax.psum_scatter(grad_qkv_w, "seq", scatter_dimension=0, tiled=True),
        lax.psum_scatter(grad_out_w, "seq", scatter_dimension=0, tiled=True),
        lax.psum_scatter(grad_up, "seq", scatter_dimension=0, tiled=True),
        lax.psum_scatter(grad_down, "seq", scatter_dimension=0, tiled=True),
        lax.psum_scatter(grad_gains, "seq", scatter_dimension=1, tiled=True),
        lax.psum_scatter(grad_shifts, "seq", scatter_dimension=1, tiled=True),
        lax.psum_scatter(grad_bias_rows, "seq", scatter_dimension=1, tiled=True),
        lax.psum_scatter(grad_up_shift, "seq", scatter_dimension=0, tiled=True),
    )
    totals = (
        lax.psum(shares[0].astype(jnp.bfloat16), "rep").astype(jnp.float32),
        lax.psum(shares[1].astype(jnp.bfloat16), "rep").astype(jnp.float32),
        lax.psum(shares[2].astype(jnp.bfloat16), "rep").astype(jnp.float32),
        lax.psum(shares[3].astype(jnp.bfloat16), "rep").astype(jnp.float32),
        lax.psum(shares[4].astype(jnp.bfloat16), "rep").astype(jnp.float32),
        lax.psum(shares[5].astype(jnp.bfloat16), "rep").astype(jnp.float32),
        lax.psum(shares[6].astype(jnp.bfloat16), "rep").astype(jnp.float32),
        lax.psum(shares[7].astype(jnp.bfloat16), "rep").astype(jnp.float32),
    )
    return (
        result.astype(jnp.bfloat16)[None],
        grad_tokens[None],
        totals[0],
        totals[1],
        totals[2],
        totals[3],
        totals[4],
        totals[5],
        totals[6],
        totals[7],
    )


def f32(value):
    return value.astype(jnp.float32)


def b16(value):
    return value.astype(jnp.bfloat16)


def dot_nn(left, right):
    return jnp.dot(left, right, preferred_element_type=jnp.float32)


def dot_nt(left, right):
    return lax.dot_general(
        left, right, (((1,), (1,)), ((), ())), preferred_element_type=jnp.float32
    )


def dot_tn(left, right):
    return lax.dot_general(
        left, right, (((0,), (0,)), ((), ())), preferred_element_type=jnp.float32
    )


def norm_parts(values):
    center = values - jnp.mean(values, axis=-1, keepdims=True)
    rate = lax.rsqrt(jnp.mean(center * center, axis=-1, keepdims=True) + norm_eps)
    return center * rate, rate


def norm_back(grad, hat, rate, gain):
    scaled = grad * gain
    return rate * (
        scaled
        - jnp.mean(scaled, axis=-1, keepdims=True)
        - hat * jnp.mean(scaled * hat, axis=-1, keepdims=True)
    )


def place(coords):
    return coords[0], coords[1], coords[2], coords[3]


def piece_shard(number, y, z):
    if number < 3:
        return 2 * lax.rem(z + 3 - number, 4) + y
    return 2 * lax.rem(z + 7 - number, 4) + 1 - y


class Copies:
    def __init__(self, sems):
        self.sems = sems
        self.held = []

    def add(self, source, target):
        copy = pltpu.make_async_copy(source, target, self.sems.at[len(self.held)])
        copy.start()
        self.held.append(copy)

    def wait(self):
        for copy in self.held:
            copy.wait()
        self.held = []


def fetch_qkv(copies, coords, own, pieces, full):
    x, c, y, z = place(coords)
    rows, cols = own.shape[0], own.shape[1] // 2
    half = rows // 2
    copies.add(own, full.at[pl.ds(pl.multiple_of((2 * z + y) * rows, 16), rows), :])
    for piece, xx, cc in zip(pieces, (x, 1 - x, x, 1 - x), (c, c, 1 - c, 1 - c), strict=True):
        for number in range(7):
            row = piece_shard(number, y, z) * rows + half * cc
            copies.add(
                piece.at[number, pl.ds(0, half), :],
                full.at[
                    pl.ds(pl.multiple_of(row, 16), half),
                    pl.ds(pl.multiple_of(cols * xx, 128), cols),
                ],
            )


def mask_bias(start, me, tok, target):
    keys, lanes = target.shape
    key_pos = (me - 4) * tok + lax.broadcasted_iota(jnp.int32, (keys, lanes), 0)
    lane = lax.broadcasted_iota(jnp.int32, (keys, lanes), 1)
    query_pos = me * tok + jnp.where(lane >= tok, lane - tok, lane)
    target[...] = jnp.where((key_pos >= start) & (key_pos <= query_pos), 0.0, floor_score)


def pair_stack(rows):
    lane = lax.broadcasted_iota(jnp.int32, rows.shape, 1)
    zero = jnp.zeros_like(rows)
    return jnp.concatenate([jnp.where(lane < HD, rows, zero), jnp.where(lane < HD, zero, rows)], axis=0)


def pair_join(transposed):
    both = transposed.T
    tok = both.shape[0] // 2
    lane = lax.broadcasted_iota(jnp.int32, (tok, 2 * HD), 1)
    return jnp.where(lane < HD, both[:tok], both[tok:])


def front_kernel(
    coords, seg, xo, x1, x2, x3, x4, first, own, m7, x7, c7, cx7,
    q_out, kv_out, h_out, a_out, lse_out, start_out, vec_out, upb_out,
    full, small, bias, sems, vsems,
):
    x, c, y, z = place(coords)
    me = 2 * z + y
    tok, width = q_out.shape
    copies, vcopies = Copies(sems), Copies(vsems)
    vcopies.add(first.at[pl.ds(48, 16), pl.ds(0, 512)], small.at[me])
    for number in range(7):
        vcopies.add(m7.at[number, pl.ds(48, 16), pl.ds(0, 512)], small.at[piece_shard(number, y, z)])
    fetch_qkv(copies, coords, own, (m7, x7, c7, cx7), full)
    blocks = (xo, x1, x2, x3, x4)
    lane1 = lax.broadcasted_iota(jnp.int32, (1, tok), 1)
    start = jnp.full(seg.shape, 1 << 30, jnp.int32)
    for number in range(4):
        first_pos = jnp.full((1, 1), 1 << 30, jnp.int32)
        for back in range(5):
            ids = f32(blocks[back][pl.ds(tok, 16), pl.ds(0, tok)])[:1]
            pos = (me - back) * tok + lane1
            hit = (ids == float(number)) & (pos >= 0)
            first_pos = jnp.minimum(
                first_pos, jnp.min(jnp.where(hit, pos, 1 << 30), axis=1, keepdims=True)
            )
        start = jnp.where(seg[...] == number, first_pos, start)
    start_out[...] = start
    mask_bias(start, me, tok, bias)
    vcopies.wait()
    lane = lax.broadcasted_iota(jnp.int32, (8, width), 1)
    part = width // 8
    vec = jnp.zeros((8, width), jnp.float32)
    for shard in range(8):
        block = f32(small[shard])
        spread = jnp.concatenate([block[:8, :128], jnp.zeros((8, width - 128), jnp.float32)], axis=1)
        spread = pltpu.roll(spread, shard * part, 1) if shard else spread
        vec = jnp.where((lane >= shard * part) & (lane < shard * part + part), spread, vec)
        upb_out[:, pl.ds(shard * 384, 384)] = block[:1, 128:512]
    vec_out[...] = vec
    for back in range(5):
        hat, _rate = norm_parts(f32(blocks[back][pl.ds(0, tok), :]))
        h_out[pl.ds((4 - back) * tok, tok), :] = b16(hat * vec[0:1] + vec[2:3])
    copies.wait()
    q_out[...] = b16(dot_nn(h_out[pl.ds(4 * tok, tok), :], full[:, pl.ds(0, width)]) + vec[4:5])

    def project(number, carry):
        col = pl.multiple_of(number * 256, 256)
        shift = jnp.where(number >= width // 256, 1.0, 0.0)
        bias_at = lax.rem(number, width // 256)
        piece = vec_out[pl.ds(5, 1), pl.ds(pl.multiple_of(bias_at * 256, 256), 256)]
        kv_out[:, pl.ds(col, 256)] = b16(
            dot_nn(h_out[...], full[:, pl.ds(pl.multiple_of(width + col, 256), 256)]) + piece * shift
        )
        return carry

    lax.fori_loop(0, 2 * width // 256, project, 0)

    def pair(number, carry):
        col = pl.multiple_of(number * 128, 128)
        queries = pair_stack(q_out[:, pl.ds(col, 128)] * jnp.bfloat16(0.125))
        scores = dot_nt(kv_out[:, pl.ds(col, 128)], queries) + bias[...]
        top = jnp.max(scores, axis=0, keepdims=True)
        probs = jnp.exp(scores - top)
        total = jnp.sum(probs, axis=0, keepdims=True)
        mixed = dot_tn(kv_out[:, pl.ds(pl.multiple_of(width + col, 128), 128)], b16(probs))
        a_out[:, pl.ds(col, 128)] = b16(pair_join(mixed / total))
        lse_out[number] = top + jnp.log(total)
        return carry

    lax.fori_loop(0, width // 128, pair, 0)


def mid_kernel(
    coords, a_in, xo, dy_in, vec_in, upb_in,
    up_own, out_own, um7, ux7, uc7, ucx7, down_own, dm7, dx7, dc7, dcx7,
    y_out, dr_out, da_out, d_other, d_mine, u_other, u_mine, vec_out, upb_out,
    w_up, w_out, w_down, stage_d, stage_u, stage_o, h2_s, dh_s, acc_s, sems, osems,
):
    x, c, y, z = place(coords)
    me = 2 * z + y
    tok, width = a_in.shape
    hidden = w_up.shape[1]
    copies = Copies(sems)
    copies.add(out_own, w_out.at[pl.ds(pl.multiple_of(me * 96, 16), 96), :])
    copies.add(up_own, w_up.at[pl.ds(pl.multiple_of(me * 96, 16), 96), :])
    copies.add(down_own, w_down.at[pl.ds(pl.multiple_of(me * 384, 16), 384), :])
    half_h, half_w = hidden // 2, width // 2
    for piece, xx, cc in zip(
        (um7, ux7, uc7, ucx7), (x, 1 - x, x, 1 - x), (c, c, 1 - c, 1 - c), strict=True
    ):
        for number in range(7):
            row = pl.multiple_of(piece_shard(number, y, z) * 96 + 48 * cc, 16)
            copies.add(
                piece.at[number, :, pl.ds(0, half_h)],
                w_up.at[pl.ds(row, 48), pl.ds(pl.multiple_of(half_h * xx, 128), half_h)],
            )
            copies.add(
                piece.at[number, :, pl.ds(half_h, half_w)],
                w_out.at[pl.ds(row, 48), pl.ds(pl.multiple_of(half_w * xx, 128), half_w)],
            )
    for piece, xx, cc in zip(
        (dm7, dx7, dc7, dcx7), (x, 1 - x, x, 1 - x), (c, c, 1 - c, 1 - c), strict=True
    ):
        for number in range(7):
            row = pl.multiple_of(piece_shard(number, y, z) * 384 + 192 * cc + 96 * xx, 16)
            copies.add(piece.at[number], w_down.at[pl.ds(row, 96), :])
    copies.wait()
    vec = vec_in[...]
    dy = dy_in[...]
    residual = f32(xo[pl.ds(0, tok), :]) + dot_nn(a_in[...], w_out[...]) + vec[6:7]
    hat, _rate = norm_parts(residual)
    acc_s[...] = residual + vec[7:8]
    h2_s[...] = b16(hat * vec[1:2] + vec[3:4])
    dh_s[...] = jnp.zeros_like(dh_s)
    chunk = 512
    root = math.sqrt(2.0 / math.pi)

    def feed(number, carry):
        col = pl.multiple_of(number * chunk, chunk)
        h2 = h2_s[...]
        pre = dot_nn(h2, w_up[:, pl.ds(col, chunk)]) + upb_in[:, pl.ds(col, chunk)]
        square = pre * pre
        bend = jnp.tanh(root * pre * (1.0 + 0.044715 * square))
        act = b16(0.5 * pre * (1.0 + bend))
        acc_s[...] += dot_nn(act, w_down[pl.ds(col, chunk), :])
        slope = 0.5 * (1.0 + bend) + 0.5 * pre * (1.0 - bend * bend) * (
            root * (1.0 + 3.0 * 0.044715 * square)
        )
        grad = dot_nt(dy, w_down[pl.ds(col, chunk), :]) * slope
        low = b16(grad)
        upb_out[:, pl.ds(col, chunk)] = jnp.sum(f32(low), axis=0, keepdims=True)
        dh_s[...] += dot_nt(low, w_up[:, pl.ds(col, chunk)])
        stage_d[pl.ds(col, chunk), :] = b16(dot_tn(act, dy))
        stage_u[:, pl.ds(col, chunk)] = b16(dot_tn(h2, low))
        return carry

    lax.fori_loop(0, hidden // chunk, feed, 0)
    outs = Copies(osems)

    def spread(target_other, target_mine, source_of, where_of):
        for shard in range(8):
            zz = lax.rem(shard // 2 + 4 - z, 4)
            yy = jnp.where(y == shard % 2, 0, 1)
            for xx in range(2):
                far = jnp.where(x == xx, 0, 1)
                outs.add(source_of(shard, 1 - c, xx), where_of(target_other, far, yy, zz))
                outs.add(source_of(shard, c, xx), where_of(target_mine, far, yy, zz))

    spread(
        d_other,
        d_mine,
        lambda s, cc, xx: stage_d.at[pl.ds(pl.multiple_of(s * 384 + 192 * cc + 96 * xx, 16), 96), :],
        lambda ref, far, yy, zz: ref.at[far, yy, zz],
    )
    spread(
        u_other,
        u_mine,
        lambda s, cc, xx: stage_u.at[pl.ds(pl.multiple_of(s * 96 + 48 * cc, 16), 48), pl.ds(half_h * xx, half_h)],
        lambda ref, far, yy, zz: ref.at[yy, far, zz, :, pl.ds(0, half_h)],
    )
    y_out[...] = b16(acc_s[...])
    grad_hidden = dh_s[...]
    residual = f32(xo[pl.ds(0, tok), :]) + dot_nn(a_in[...], w_out[...]) + vec[6:7]
    hat, rate = norm_parts(residual)
    dyf = f32(dy)
    grad_first = dyf + norm_back(grad_hidden, hat, rate, vec[1:2])
    dr_out[...] = grad_first
    low_first = b16(grad_first)
    da_out[...] = b16(dot_nt(low_first, w_out[...]))
    stage_o[...] = b16(dot_tn(a_in[...], low_first))
    zero = jnp.zeros((1, width), jnp.float32)
    vec_out[...] = jnp.concatenate(
        [
            zero,
            jnp.sum(grad_hidden * hat, axis=0, keepdims=True),
            zero,
            jnp.sum(grad_hidden, axis=0, keepdims=True),
            zero,
            zero,
            jnp.sum(grad_first, axis=0, keepdims=True),
            jnp.sum(dyf, axis=0, keepdims=True),
        ],
        axis=0,
    )
    spread(
        u_other,
        u_mine,
        lambda s, cc, xx: stage_o.at[pl.ds(pl.multiple_of(s * 96 + 48 * cc, 16), 48), pl.ds(half_w * xx, half_w)],
        lambda ref, far, yy, zz: ref.at[yy, far, zz, :, pl.ds(half_h, half_w)],
    )
    outs.wait()


def back_kernel(
    coords, start_in, q_in, kv_in, h_in, lse_in, da_in, vec_in, upb_in, xo, x1, x2, x3, x4,
    own, m7, x7, c7, cx7,
    q_other, q_mine, p_own, p_y, p_z,
    full, bias, dq_s, dkv_s, stage, sems, osems,
):
    x, c, y, z = place(coords)
    me = 2 * z + y
    tok, width = q_in.shape
    copies = Copies(sems)
    fetch_qkv(copies, coords, own, (m7, x7, c7, cx7), full)
    mask_bias(start_in[...], me, tok, bias)

    def pair(number, carry):
        col = pl.multiple_of(number * 128, 128)
        vcol = pl.multiple_of(width + col, 128)
        queries = pair_stack(q_in[:, pl.ds(col, 128)] * jnp.bfloat16(0.125))
        grads = pair_stack(da_in[:, pl.ds(col, 128)])
        keys = kv_in[:, pl.ds(col, 128)]
        probs = jnp.exp(dot_nt(keys, queries) + bias[...] - lse_in[number])
        dkv_s[:, pl.ds(vcol, 128)] = b16(dot_nn(b16(probs), grads))
        term = probs * dot_nt(kv_in[:, pl.ds(vcol, 128)], grads)
        low = b16(term - probs * jnp.sum(term, axis=0, keepdims=True))
        dkv_s[:, pl.ds(col, 128)] = b16(dot_nn(low, queries))
        dq_s[:, pl.ds(col, 128)] = b16(pair_join(dot_tn(keys, low)) * 0.125)
        return carry

    lax.fori_loop(0, width // 128, pair, 0)
    copies.wait()
    gain_sum = jnp.zeros((1, width), jnp.float32)
    shift_sum = jnp.zeros((1, width), jnp.float32)
    for back, block in enumerate((xo, x1, x2, x3, x4)):
        rows = pl.ds((4 - back) * tok, tok)
        grad = dot_nt(dkv_s[rows, :], full[:, pl.ds(width, 2 * width)])
        if back == 0:
            grad = grad + dot_nt(dq_s[...], full[:, pl.ds(0, width)])
            p_own[...] = grad
        elif back in (1, 3):
            p_y[back // 2] = b16(grad)
        else:
            p_z[back // 2 - 1] = b16(grad)
        hat, _rate = norm_parts(f32(block[pl.ds(0, tok), :]))
        gain_sum = gain_sum + jnp.sum(grad * hat, axis=0, keepdims=True)
        shift_sum = shift_sum + jnp.sum(grad, axis=0, keepdims=True)
    part = 384

    def weight(number, carry):
        col = pl.multiple_of(number * part, 128)
        half = number // 3
        at = pl.multiple_of((number - 3 * half) * part, 128)

        def put(value):
            value = b16(value)
            for shard in range(8):
                for cc in range(2):
                    row = shard * 96 + cc * 48
                    stage[cc, half, shard, pl.ds(0, 48), pl.ds(at, part)] = value[row : row + 48]

        @pl.when(number < 2)
        def _():
            put(dot_tn(h_in[pl.ds(4 * tok, tok), :], dq_s[:, pl.ds(col, part)]))

        @pl.when(number >= 2)
        def _():
            put(dot_tn(h_in[...], dkv_s[:, pl.ds(pl.multiple_of(col - width, 128), part)]))

        return carry

    lax.fori_loop(0, 3 * width // part, weight, 0)
    vec = vec_in[...]
    bias_q = jnp.sum(f32(dq_s[...]), axis=0, keepdims=True)
    bias_v = jnp.sum(f32(dkv_s[:, pl.ds(width, width)]), axis=0, keepdims=True)
    zero = jnp.zeros((1, width), jnp.float32)
    vec = vec + jnp.concatenate([gain_sum, zero, shift_sum, zero, bias_q, bias_v, zero, zero], axis=0)
    lane = lax.broadcasted_iota(jnp.int32, (8, 128), 1)
    zrow = jnp.zeros((8, 128), jnp.float32)
    for shard in range(8):
        rolled = pltpu.roll(vec, width - shard * 96, 1) if shard else vec
        top = jnp.concatenate([jnp.where(lane < 96, rolled[:, :128], 0.0), zrow], axis=0)
        tail = jnp.broadcast_to(upb_in[:, pl.ds(shard * 384, 384)], (16, 384))
        both = b16(jnp.concatenate([top, tail], axis=1))
        for cc in range(2):
            for xx in range(2):
                stage[cc, xx, shard, pl.ds(48, 16), pl.ds(0, 512)] = both
                stage[cc, xx, shard, pl.ds(48, 16), pl.ds(512, 640)] = jnp.zeros((16, 640), jnp.bfloat16)
    outs = Copies(osems)
    for shard in range(8):
        zz = lax.rem(shard // 2 + 4 - z, 4)
        yy = jnp.where(y == shard % 2, 0, 1)
        for xx in range(2):
            far = jnp.where(x == xx, 0, 1)
            outs.add(stage.at[1 - c, xx, shard], q_other.at[far, yy, zz])
            outs.add(stage.at[c, xx, shard], q_mine.at[far, yy, zz])
    outs.wait()


def finish_d_kernel(coords, f, fx, cf, cfx, out):
    x, c, _y, _z = place(coords)
    for piece, xx, cc in zip((f, fx, cf, cfx), (x, 1 - x, x, 1 - x), (c, c, 1 - c, 1 - c), strict=True):
        out[pl.ds(pl.multiple_of(192 * cc + 96 * xx, 16), 96), :] = f32(piece[...])


def finish_u_kernel(coords, f, fx, cf, cfx, up, out):
    x, c, _y, _z = place(coords)
    half_h, half_w = up.shape[1] // 2, out.shape[1] // 2
    for piece, xx, cc in zip((f, fx, cf, cfx), (x, 1 - x, x, 1 - x), (c, c, 1 - c, 1 - c), strict=True):
        rows = pl.ds(pl.multiple_of(48 * cc, 16), 48)
        up[rows, pl.ds(pl.multiple_of(half_h * xx, 128), half_h)] = f32(piece[:, pl.ds(0, half_h)])
        out[rows, pl.ds(pl.multiple_of(half_w * xx, 128), half_w)] = f32(piece[:, pl.ds(half_h, half_w)])


def finish_q_kernel(coords, f, fx, cf, cfx, qkv):
    x, c, _y, _z = place(coords)
    cols = qkv.shape[1] // 2
    for piece, xx, cc in zip((f, fx, cf, cfx), (x, 1 - x, x, 1 - x), (c, c, 1 - c, 1 - c), strict=True):
        qkv[pl.ds(pl.multiple_of(48 * cc, 16), 48), pl.ds(pl.multiple_of(cols * xx, 128), cols)] = f32(
            piece[pl.ds(0, 48), :]
        )


VM = pl.BlockSpec(memory_space=pltpu.VMEM)
SM = pl.BlockSpec(memory_space=pltpu.SMEM)
AN = pl.BlockSpec(memory_space=pl.ANY)


def shape_of(shape, dtype):
    return jax.ShapeDtypeStruct(shape, dtype)


def call(kernel, ins, outs, out_shape, scratch=(), vmem=40, flops=0, moved=0):
    return pl.pallas_call(
        kernel,
        in_specs=ins,
        out_specs=outs,
        out_shape=out_shape,
        scratch_shapes=list(scratch),
        compiler_params=pltpu.CompilerParams(vmem_limit_bytes=vmem << 20),
        cost_estimate=pl.CostEstimate(flops=flops, bytes_accessed=moved, transcendentals=0),
    )


def swap_rep(value, bit):
    return lax.ppermute(value, "rep", [(k, k ^ bit) for k in range(4)])


def to_core(value):
    return swap_rep(value, 1)


def to_x(value):
    return swap_rep(value, 2)


def to_y(value):
    return lax.ppermute(value, "seq", [(k, k ^ 1) for k in range(8)])


def to_z(value, steps):
    return lax.ppermute(value, "seq", [(k, (k + 2 * steps) % 8) for k in range(8)])


def gather(piece):
    rows, cols = piece.shape
    along = [to_z(piece, k) for k in (1, 2, 3)]
    across = to_y(jnp.concatenate([piece] + along, axis=0))
    seven = jnp.concatenate(along + [across], axis=0)
    other = to_x(seven)
    return [v.reshape(7, rows, cols) for v in (seven, other, to_core(seven), to_core(other))]


def reduce_pieces(other, mine, first, second):
    came = to_core(other)

    def part(index):
        return f32(mine[index]) + f32(came[index])

    came_1 = first(b16(part(1)))

    def part_1(index):
        return part((0,) + index) + f32(came_1[index])

    came_2 = second(b16(part_1((1,))))

    def part_2(index):
        return part_1((0, index)) + f32(came_2[index])

    total = part_2(0)
    for step in (1, 2, 3):
        total = total + f32(to_z(b16(part_2(step)), step))
    total = b16(total)
    over = to_x(total)
    return total, over, to_core(total), to_core(over)


def on_device_fast(
    tokens,
    segment_ids,
    query_key_value_weight,
    output_weight,
    up_weight,
    down_weight,
    ln_gains,
    ln_biases,
    biases,
    up_projection_bias,
    cotangent,
):
    rep, seq = lax.axis_index("rep"), lax.axis_index("seq")
    x, c, z, y = rep // 2, rep % 2, seq // 2, seq % 2
    coords = jnp.stack([x, c, y, z]).astype(jnp.int32)
    tok, width = tokens.shape[1:]
    hidden = up_weight.shape[1]
    keys = 5 * tok
    bf, fl = jnp.bfloat16, jnp.float32
    ids = jnp.pad(segment_ids.astype(bf), ((0, 15), (0, width - tok)))
    own_tokens = jnp.concatenate([tokens[0], ids], axis=0)
    small = jnp.concatenate([ln_gains, ln_biases, biases], axis=0)
    small = jnp.concatenate(
        [
            jnp.pad(small, ((0, 0), (0, 128 - small.shape[1]))),
            jnp.pad(up_projection_bias[None], ((0, 7), (0, 0))),
        ],
        axis=1,
    )
    small = jnp.pad(small, ((0, 8), (0, 3 * width // 2 - small.shape[1])))
    piece_q = jnp.concatenate(
        [
            lax.dynamic_slice(
                query_key_value_weight, (48 * c, 3 * width // 2 * x), (48, 3 * width // 2)
            ),
            small,
        ],
        axis=0,
    )
    piece_u = jnp.concatenate(
        [
            lax.dynamic_slice(up_weight, (48 * c, hidden // 2 * x), (48, hidden // 2)),
            lax.dynamic_slice(output_weight, (48 * c, width // 2 * x), (48, width // 2)),
        ],
        axis=1,
    )
    piece_d = lax.dynamic_slice(down_weight, (192 * c + 96 * x, 0), (96, width))
    x2 = to_z(own_tokens, 1)
    x4 = to_z(own_tokens, 2)
    near = jnp.where(y == 0, own_tokens, x2)
    far = jnp.where(y == 0, x2, x4)
    crossed = to_y(jnp.stack([near, far]))
    x1, x3 = crossed[0], crossed[1]
    got_q = gather(piece_q)
    got_u = gather(piece_u)
    got_d = gather(piece_d)
    seg = jnp.concatenate([segment_ids, segment_ids], axis=1)
    queries, kv, normed, attended, lse, start, vec, upb = call(
        front_kernel,
        [SM] + [VM] * 6 + [AN] * 6,
        [VM] * 8,
        [
            shape_of((tok, width), bf),
            shape_of((keys, 2 * width), bf),
            shape_of((keys, width), bf),
            shape_of((tok, width), bf),
            shape_of((width // 128, 1, 2 * tok), fl),
            shape_of((1, 2 * tok), jnp.int32),
            shape_of((8, width), fl),
            shape_of((1, hidden), fl),
        ],
        [
            pltpu.VMEM((width, 3 * width), bf),
            pltpu.VMEM((8, 16, 512), bf),
            pltpu.VMEM((keys, 2 * tok), fl),
            pltpu.SemaphoreType.DMA((29,)),
            pltpu.SemaphoreType.DMA((8,)),
        ],
        flops=7 * 10**9,
        moved=12 * 10**6,
    )(coords, seg, own_tokens, x1, x2, x3, x4, piece_q, query_key_value_weight, *got_q)
    grad_y = cotangent[0]
    result, grad_first, grad_attended, d_other, d_mine, u_other, u_mine, vec_g, upb_g = call(
        mid_kernel,
        [SM] + [VM] * 5 + [AN] * 11,
        [VM] * 3 + [AN] * 4 + [VM] * 2,
        [
            shape_of((tok, width), bf),
            shape_of((tok, width), fl),
            shape_of((tok, width), bf),
            shape_of((2, 2, 4, 96, width), bf),
            shape_of((2, 2, 4, 96, width), bf),
            shape_of((2, 2, 4, 48, hidden // 2 + width // 2), bf),
            shape_of((2, 2, 4, 48, hidden // 2 + width // 2), bf),
            shape_of((8, width), fl),
            shape_of((1, hidden), fl),
        ],
        [
            pltpu.VMEM((width, hidden), bf),
            pltpu.VMEM((width, width), bf),
            pltpu.VMEM((hidden, width), bf),
            pltpu.VMEM((hidden, width), bf),
            pltpu.VMEM((width, hidden), bf),
            pltpu.VMEM((width, width), bf),
            pltpu.VMEM((tok, width), bf),
            pltpu.VMEM((tok, width), fl),
            pltpu.VMEM((tok, width), fl),
            pltpu.SemaphoreType.DMA((3 + 84,)),
            pltpu.SemaphoreType.DMA((96,)),
        ],
        vmem=48,
        flops=12 * 10**9,
        moved=24 * 10**6,
    )(
        coords, attended, own_tokens, grad_y, vec, upb,
        up_weight, output_weight, *got_u, down_weight, *got_d,
    )
    done_d = reduce_pieces(d_other, d_mine, to_x, to_y)
    done_u = reduce_pieces(u_other, u_mine, to_y, to_x)
    q_other, q_mine, p_own, p_y, p_z = call(
        back_kernel,
        [SM] + [VM] * 13 + [AN] * 5,
        [AN] * 2 + [VM] * 3,
        [
            shape_of((2, 2, 4, 64, 3 * width // 2), bf),
            shape_of((2, 2, 4, 64, 3 * width // 2), bf),
            shape_of((tok, width), fl),
            shape_of((2, tok, width), bf),
            shape_of((2, tok, width), bf),
        ],
        [
            pltpu.VMEM((width, 3 * width), bf),
            pltpu.VMEM((keys, 2 * tok), fl),
            pltpu.VMEM((tok, width), bf),
            pltpu.VMEM((keys, 2 * width), bf),
            pltpu.VMEM((2, 2, 8, 64, 3 * width // 2), bf),
            pltpu.SemaphoreType.DMA((29,)),
            pltpu.SemaphoreType.DMA((32,)),
        ],
        flops=14 * 10**9,
        moved=20 * 10**6,
    )(
        coords, start, queries, kv, normed, lse, grad_attended, vec_g, upb_g,
        own_tokens, x1, x2, x3, x4, query_key_value_weight, *got_q,
    )
    done_q = reduce_pieces(q_other, q_mine, to_x, to_y)
    came = to_y(p_y)
    even = y == 0
    sum_own = p_own + jnp.where(even, f32(came[0]), 0.0)
    sum_2 = b16(f32(p_z[0]) + jnp.where(even, f32(came[1]), f32(came[0])))
    sum_4 = b16(f32(p_z[1]) + jnp.where(even, 0.0, f32(came[1])))
    back_2, back_4 = to_z(sum_2, 3), to_z(sum_4, 2)
    grad_tokens = call(
        tokens_kernel,
        [VM] * 6,
        VM,
        shape_of((tok, width), fl),
        vmem=16,
        flops=10**6,
        moved=3 * 10**6,
    )(sum_own, back_2, back_4, grad_first, own_tokens, vec)
    grad_down = call(
        finish_d_kernel, [SM] + [VM] * 4, VM, shape_of(down_weight.shape, fl), vmem=16, moved=2 * 10**6
    )(coords, *done_d)
    grad_up, grad_out = call(
        finish_u_kernel,
        [SM] + [VM] * 4,
        [VM] * 2,
        [shape_of(up_weight.shape, fl), shape_of(output_weight.shape, fl)],
        vmem=16,
        moved=2 * 10**6,
    )(coords, *done_u)
    grad_qkv = call(
        finish_q_kernel, [SM] + [VM] * 4, VM, shape_of(query_key_value_weight.shape, fl), vmem=16, moved=2 * 10**6
    )(coords, *done_q)
    sums = f32(done_q[0][48:56, :512])
    part = ln_gains.shape[1]
    return (
        result[None],
        grad_tokens[None],
        grad_qkv,
        grad_out,
        grad_up,
        grad_down,
        sums[0:2, :part],
        sums[2:4, :part],
        sums[4:8, :part],
        sums[0, 128:512],
    )


def tokens_kernel(own, near, far, dr, xo, vec_in, grad_out):
    tok = own.shape[0]
    hat, rate = norm_parts(f32(xo[pl.ds(0, tok), :]))
    grad = own[...] + f32(near[...]) + f32(far[...])
    grad_out[...] = dr[...] + norm_back(grad, hat, rate, vec_in[0:1, :])


def solution(mesh):
    placed = (
        P("rep", "seq", None),
        P("rep", "seq"),
        P("seq", None),
        P("seq", None),
        P("seq", None),
        P("seq", None),
        P(None, "seq"),
        P(None, "seq"),
        P(None, "seq"),
        P("seq"),
        P("rep", "seq", None),
    )
    shape = dict(mesh.shape)
    small_slice = shape["rep"] == 4 and shape["seq"] == 8
    return jax.shard_map(
        on_device_fast if small_slice else on_device,
        mesh=mesh,
        in_specs=placed,
        out_specs=(
            P("rep", "seq", None),
            P("rep", "seq", None),
            P("seq", None),
            P("seq", None),
            P("seq", None),
            P("seq", None),
            P(None, "seq"),
            P(None, "seq"),
            P(None, "seq"),
            P("seq"),
        ),
        check_vma=False,
    )
```

```python
import math

import jax
import jax.numpy as jnp
from jax import lax
from jax.experimental import pallas as pl
from jax.experimental.pallas import tpu as pltpu
from jax.sharding import PartitionSpec as P

HEADS = 12
HD = 64


norm_eps = 1e-05
floor_score = -1e30


def layer_norm(values, gain, shift):
    center = values - jnp.mean(values, axis=-1, keepdims=True)
    spread = jnp.mean(center * center, axis=-1, keepdims=True)
    return center * lax.rsqrt(spread + norm_eps) * gain + shift


def head_split(matrix):
    return matrix.reshape(matrix.shape[0], HEADS, HD)


def masked_scores(queries, query_seg, query_pos, key_piece, seg_piece, offset):
    rows = key_piece.shape[0]
    scores = jnp.einsum(
        "qhd,khd->hqk", queries, head_split(key_piece), preferred_element_type=jnp.float32
    ) * HD ** (-0.5)
    key_pos = offset + jnp.arange(rows, dtype=jnp.int32)
    allowed = (query_seg[:, None] == seg_piece[None, :]) & (key_pos[None, :] <= query_pos[:, None])
    return (jnp.where(allowed[None], scores, floor_score), allowed)


def forward_block(running, pieces, offset, queries, query_seg, query_pos):
    top_run, total_run, accum = running
    key_piece, value_piece, seg_piece = pieces
    scores, allowed = masked_scores(queries, query_seg, query_pos, key_piece, seg_piece, offset)
    top_new = jnp.maximum(top_run, jnp.max(scores, axis=-1))
    probs = jnp.where(allowed[None], jnp.exp(scores - top_new[:, :, None]), 0.0)
    factor = jnp.exp(top_run - top_new)
    total_new = total_run * factor + jnp.sum(probs, axis=-1)
    update = jnp.einsum(
        "hqk,khd->qhd",
        probs.astype(jnp.bfloat16),
        head_split(value_piece),
        preferred_element_type=jnp.float32,
    )
    return (top_new, total_new, accum * factor.T[:, :, None] + update)


def in_blocks(block_fn, running, pieces):
    rows = pieces[0].shape[0]
    size = math.gcd(rows, 1024)
    stacked = tuple((member.reshape((rows // size, size) + member.shape[1:]) for member in pieces))
    offsets = jnp.arange(rows // size, dtype=jnp.int32) * size

    def scan_step(state_now, element):
        return (block_fn(state_now, element[0], element[1]), None)

    running, _unused = lax.scan(scan_step, running, (stacked, offsets))
    return running


def backward_block(
    number,
    state_now,
    whole,
    queries,
    query_seg,
    query_pos,
    grad_heads,
    log_total,
    delta,
    block_rows,
):
    grad_query, term = state_now
    offset = number * block_rows
    key_piece = lax.dynamic_slice_in_dim(whole[0], offset, block_rows, 0)
    value_piece = lax.dynamic_slice_in_dim(whole[1], offset, block_rows, 0)
    seg_piece = lax.dynamic_slice_in_dim(whole[2], offset, block_rows, 0)
    scores, allowed = masked_scores(queries, query_seg, query_pos, key_piece, seg_piece, offset)
    probs = jnp.where(allowed[None], jnp.exp(scores - log_total[:, :, None]), 0.0)
    grad_probs = jnp.einsum(
        "qhd,khd->hqk", grad_heads, head_split(value_piece), preferred_element_type=jnp.float32
    )
    grad_scores = (probs * (grad_probs - delta[:, :, None])).astype(jnp.bfloat16)
    grad_query = grad_query + jnp.einsum(
        "hqk,khd->qhd", grad_scores, head_split(key_piece), preferred_element_type=jnp.float32
    )
    grad_key = jnp.einsum(
        "hqk,qhd->khd", grad_scores, queries, preferred_element_type=jnp.float32
    ) * HD ** (-0.5)
    grad_value = jnp.einsum(
        "hqk,qhd->khd", probs.astype(jnp.bfloat16), grad_heads, preferred_element_type=jnp.float32
    )
    joined = jnp.concatenate(
        [grad_key.reshape(block_rows, -1), grad_value.reshape(block_rows, -1)], axis=1
    )
    term = lax.dynamic_update_slice_in_dim(term, joined, offset, 0)
    return (grad_query, term)


def on_device(
    tokens,
    segment_ids,
    query_key_value_weight,
    output_weight,
    up_weight,
    down_weight,
    ln_gains,
    ln_biases,
    biases,
    up_projection_bias,
    cotangent,
):
    gathered = (
        lax.all_gather(query_key_value_weight, "seq", axis=0, tiled=True),
        lax.all_gather(output_weight, "seq", axis=0, tiled=True),
        lax.all_gather(up_weight, "seq", axis=0, tiled=True),
        lax.all_gather(down_weight, "seq", axis=0, tiled=True),
        lax.all_gather(ln_gains, "seq", axis=1, tiled=True),
        lax.all_gather(ln_biases, "seq", axis=1, tiled=True),
        lax.all_gather(biases, "seq", axis=1, tiled=True),
        lax.all_gather(up_projection_bias, "seq", axis=0, tiled=True),
    )
    full_qkv, full_out, full_up, full_down, gains_all, shifts_all, biases_all, up_shift = gathered
    gains_f = gains_all.astype(jnp.float32)
    shifts_f = shifts_all.astype(jnp.float32)
    biases_f = biases_all.astype(jnp.float32)
    up_shift_f = up_shift.astype(jnp.float32)
    tokens_f = tokens[0].astype(jnp.float32)
    seg_local = segment_ids[0]
    tok_rows = tokens_f.shape[0]
    width = tokens_f.shape[1]
    seqlen = tok_rows * lax.axis_size("seq")
    query_pos = lax.axis_index("seq") * tok_rows + jnp.arange(tok_rows, dtype=jnp.int32)
    hidden_first = layer_norm(tokens_f, gains_f[0], shifts_f[0]).astype(jnp.bfloat16)
    query_key_value_bias = jnp.concatenate(
        [biases_f[0], jnp.zeros((width,), jnp.float32), biases_f[1]]
    )
    projected_rows = (
        jnp.dot(hidden_first, full_qkv, preferred_element_type=jnp.float32) + query_key_value_bias
    ).astype(jnp.bfloat16)
    queries = head_split(projected_rows[:, :width])
    key_rows = projected_rows[:, width : 2 * width]
    value_rows = projected_rows[:, 2 * width :]
    initial = (
        jnp.full((HEADS, tok_rows), floor_score, jnp.float32),
        jnp.zeros((HEADS, tok_rows), jnp.float32),
        jnp.zeros((tok_rows, HEADS, HD), jnp.float32),
    )

    def block_fn(running, pieces, offset):
        return forward_block(running, pieces, offset, queries, seg_local, query_pos)

    block_rows = math.gcd(seqlen, 1024)
    key_end = (lax.axis_index("seq") + 1) * tok_rows
    block_count = (key_end + block_rows - 1) // block_rows
    top_run, total_run, accum = in_blocks(
        block_fn,
        initial,
        (
            lax.all_gather(key_rows, "seq", axis=0, tiled=True),
            lax.all_gather(value_rows, "seq", axis=0, tiled=True),
            lax.all_gather(seg_local, "seq", axis=0, tiled=True),
        ),
    )
    log_total = top_run + jnp.log(total_run)
    attended_f = accum / total_run.T[:, :, None]
    attention_result = attended_f.reshape(tok_rows, width).astype(jnp.bfloat16)
    residual_first = (
        tokens_f
        + jnp.dot(attention_result, full_out, preferred_element_type=jnp.float32)
        + biases_f[2]
    )
    hidden_second = layer_norm(residual_first, gains_f[1], shifts_f[1]).astype(jnp.bfloat16)
    upward_rows = jnp.dot(hidden_second, full_up, preferred_element_type=jnp.float32) + up_shift_f
    activated_f, gelu_back = jax.vjp(jax.nn.gelu, upward_rows)
    activation_values = activated_f.astype(jnp.bfloat16)
    result = (
        residual_first
        + jnp.dot(activation_values, full_down, preferred_element_type=jnp.float32)
        + biases_f[3]
    )
    grad_y = cotangent[0]
    grad_y_f = grad_y.astype(jnp.float32)
    grad_down = jnp.einsum(
        "tf,td->fd", activation_values, grad_y, preferred_element_type=jnp.float32
    )
    grad_act = jnp.einsum("td,fd->tf", grad_y, full_down, preferred_element_type=jnp.float32)
    grad_up_pre = gelu_back(grad_act)[0].astype(jnp.bfloat16)
    grad_up = jnp.einsum(
        "td,tf->df", hidden_second, grad_up_pre, preferred_element_type=jnp.float32
    )
    grad_hidden_two = jnp.einsum(
        "tf,df->td", grad_up_pre, full_up, preferred_element_type=jnp.float32
    )
    _unused, norm_two_back = jax.vjp(layer_norm, residual_first, gains_f[1], shifts_f[1])
    grad_sum_part, grad_gain_two, grad_shift_two = norm_two_back(grad_hidden_two)
    grad_first = grad_y_f + grad_sum_part
    grad_first_bf = grad_first.astype(jnp.bfloat16)
    grad_out_w = jnp.einsum(
        "td,te->de", attention_result, grad_first_bf, preferred_element_type=jnp.float32
    )
    grad_attended = jnp.einsum(
        "te,de->td", grad_first_bf, full_out, preferred_element_type=jnp.float32
    ).astype(jnp.bfloat16)
    grad_heads = head_split(grad_attended)
    delta = jnp.einsum("qhd,qhd->hq", grad_heads.astype(jnp.float32), attended_f)
    whole = (
        lax.all_gather(key_rows, "seq", axis=0, tiled=True),
        lax.all_gather(value_rows, "seq", axis=0, tiled=True),
        lax.all_gather(seg_local, "seq", axis=0, tiled=True),
    )

    def backward_step(number, state_now):
        return backward_block(
            number,
            state_now,
            whole,
            queries,
            seg_local,
            query_pos,
            grad_heads,
            log_total,
            delta,
            block_rows,
        )

    start_state = (
        jnp.zeros((tok_rows, HEADS, HD), jnp.float32),
        jnp.zeros((seqlen, 2 * width), jnp.float32),
    )
    grad_query, term = lax.fori_loop(0, block_count, backward_step, start_state)
    grad_kv = lax.psum_scatter(term, "seq", scatter_dimension=0, tiled=True).astype(jnp.bfloat16)
    grad_q = (grad_query * HD ** (-0.5)).reshape(tok_rows, width).astype(jnp.bfloat16)
    grad_proj = jnp.concatenate([grad_q, grad_kv], axis=1)
    grad_qkv_w = jnp.einsum(
        "td,te->de", hidden_first, grad_proj, preferred_element_type=jnp.float32
    )
    grad_hidden_one = jnp.einsum(
        "te,de->td", grad_proj, full_qkv, preferred_element_type=jnp.float32
    )
    _unused_two, norm_one_back = jax.vjp(layer_norm, tokens_f, gains_f[0], shifts_f[0])
    grad_in_part, grad_gain_one, grad_shift_one = norm_one_back(grad_hidden_one)
    grad_tokens = grad_first + grad_in_part
    grad_proj_f = grad_proj.astype(jnp.float32)
    grad_bias_rows = jnp.stack(
        [
            jnp.sum(grad_proj_f[:, :width], axis=0),
            jnp.sum(grad_proj_f[:, 2 * width :], axis=0),
            jnp.sum(grad_first, axis=0),
            jnp.sum(grad_y_f, axis=0),
        ]
    )
    grad_up_shift = jnp.sum(grad_up_pre.astype(jnp.float32), axis=0)
    grad_gains = jnp.stack([grad_gain_one, grad_gain_two])
    grad_shifts = jnp.stack([grad_shift_one, grad_shift_two])
    shares = (
        lax.psum_scatter(grad_qkv_w, "seq", scatter_dimension=0, tiled=True),
        lax.psum_scatter(grad_out_w, "seq", scatter_dimension=0, tiled=True),
        lax.psum_scatter(grad_up, "seq", scatter_dimension=0, tiled=True),
        lax.psum_scatter(grad_down, "seq", scatter_dimension=0, tiled=True),
        lax.psum_scatter(grad_gains, "seq", scatter_dimension=1, tiled=True),
        lax.psum_scatter(grad_shifts, "seq", scatter_dimension=1, tiled=True),
        lax.psum_scatter(grad_bias_rows, "seq", scatter_dimension=1, tiled=True),
        lax.psum_scatter(grad_up_shift, "seq", scatter_dimension=0, tiled=True),
    )
    totals = (
        lax.psum(shares[0].astype(jnp.bfloat16), "rep").astype(jnp.float32),
        lax.psum(shares[1].astype(jnp.bfloat16), "rep").astype(jnp.float32),
        lax.psum(shares[2].astype(jnp.bfloat16), "rep").astype(jnp.float32),
        lax.psum(shares[3].astype(jnp.bfloat16), "rep").astype(jnp.float32),
        lax.psum(shares[4].astype(jnp.bfloat16), "rep").astype(jnp.float32),
        lax.psum(shares[5].astype(jnp.bfloat16), "rep").astype(jnp.float32),
        lax.psum(shares[6].astype(jnp.bfloat16), "rep").astype(jnp.float32),
        lax.psum(shares[7].astype(jnp.bfloat16), "rep").astype(jnp.float32),
    )
    return (
        result.astype(jnp.bfloat16)[None],
        grad_tokens[None],
        totals[0],
        totals[1],
        totals[2],
        totals[3],
        totals[4],
        totals[5],
        totals[6],
        totals[7],
    )


def f32(value):
    return value.astype(jnp.float32)


def b16(value):
    return value.astype(jnp.bfloat16)


def dot_nn(left, right):
    return jnp.dot(left, right, preferred_element_type=jnp.float32)


def dot_nt(left, right):
    return lax.dot_general(
        left, right, (((1,), (1,)), ((), ())), preferred_element_type=jnp.float32
    )


def dot_tn(left, right):
    return lax.dot_general(
        left, right, (((0,), (0,)), ((), ())), preferred_element_type=jnp.float32
    )


def norm_parts(values):
    center = values - jnp.mean(values, axis=-1, keepdims=True)
    rate = lax.rsqrt(jnp.mean(center * center, axis=-1, keepdims=True) + norm_eps)
    return center * rate, rate


def norm_back(grad, hat, rate, gain):
    scaled = grad * gain
    return rate * (
        scaled
        - jnp.mean(scaled, axis=-1, keepdims=True)
        - hat * jnp.mean(scaled * hat, axis=-1, keepdims=True)
    )


def place(coords):
    return coords[0], coords[1], coords[2], coords[3]


def piece_shard(number, y, z):
    if number < 3:
        return 2 * lax.rem(z + 3 - number, 4) + y
    return 2 * lax.rem(z + 7 - number, 4) + 1 - y


def pack96(parts):
    lane = lax.broadcasted_iota(jnp.int32, parts[0].shape, 1)
    one, two, three = (pltpu.roll(parts[k], 128 - 32 * k, 1) for k in (1, 2, 3))
    return jnp.concatenate(
        [
            jnp.where(lane < 96, parts[0], one),
            jnp.where(lane < 64, one, two),
            jnp.where(lane < 32, two, three),
        ],
        axis=1,
    )


def unpack96(block):
    tiles = [block[:, 128 * k : 128 * k + 128] for k in range(3)]
    lane = lax.broadcasted_iota(jnp.int32, tiles[0].shape, 1)
    return [
        tiles[0],
        jnp.where(lane < 32, pltpu.roll(tiles[0], 32, 1), pltpu.roll(tiles[1], 32, 1)),
        jnp.where(lane < 64, pltpu.roll(tiles[1], 64, 1), pltpu.roll(tiles[2], 64, 1)),
        pltpu.roll(tiles[2], 96, 1),
    ]


def choose(parts, index):
    out = parts[0]
    for number in range(1, len(parts)):
        out = jnp.where(index == number, parts[number], out)
    return out


class Copies:
    def __init__(self, sems):
        self.sems = sems
        self.held = []

    def add(self, source, target):
        copy = pltpu.make_async_copy(source, target, self.sems.at[len(self.held)])
        copy.start()
        self.held.append(copy)

    def wait(self):
        for copy in self.held:
            copy.wait()
        self.held = []


def corners(x, c):
    return ((x, c), (1 - x, c), (x, 1 - c), (1 - x, 1 - c))


def fetch_qkv(copies, coords, own, pieces_a, pieces_b, full, full_out=None, own_out=None):
    x, c, y, z = place(coords)
    rows = own.shape[0]
    half, width = rows // 2, own.shape[1] // 3
    row = pl.multiple_of((2 * z + y) * rows, 16)
    copies.add(own, full.at[pl.ds(row, rows), :])
    if full_out is not None:
        copies.add(own_out, full_out.at[pl.ds(row, rows), :])
    for (xx, cc), first, second in zip(corners(x, c), pieces_a, pieces_b, strict=True):
        for number in range(7):
            at = pl.ds(pl.multiple_of(piece_shard(number, y, z) * rows + half * cc, 16), half)
            copies.add(
                first.at[number, pl.ds(0, half), :],
                full.at[at, pl.ds(pl.multiple_of(width * xx, 128), width)],
            )
            side = width // 2
            copies.add(
                second.at[number, :, pl.ds(0, side)],
                full.at[at, pl.ds(pl.multiple_of(2 * width + side * xx, 128), side)],
            )
            if full_out is not None:
                copies.add(
                    second.at[number, :, pl.ds(side, side)],
                    full_out.at[at, pl.ds(pl.multiple_of(side * xx, 128), side)],
                )


def mask_bias(start, me, tok, target):
    keys, lanes = target.shape
    key_pos = (me - 4) * tok + lax.broadcasted_iota(jnp.int32, (keys, lanes), 0)
    lane = lax.broadcasted_iota(jnp.int32, (keys, lanes), 1)
    query_pos = me * tok + jnp.where(lane >= tok, lane - tok, lane)
    target[...] = jnp.where((key_pos >= start) & (key_pos <= query_pos), 0.0, floor_score)


def pair_stack(rows):
    lane = lax.broadcasted_iota(jnp.int32, rows.shape, 1)
    zero = jnp.zeros_like(rows)
    return jnp.concatenate([jnp.where(lane < HD, rows, zero), jnp.where(lane < HD, zero, rows)], axis=0)


def pair_join(transposed):
    both = transposed.T
    tok = both.shape[0] // 2
    lane = lax.broadcasted_iota(jnp.int32, (tok, 2 * HD), 1)
    return jnp.where(lane < HD, both[:tok], both[tok:])


def prep_kernel(
    coords, tokens, segs, qkv, out, up, down, gains, shifts, biases, up_bias,
    t_out, qa_out, qb_out, fu_out, fd_out, scratch,
):
    x, c, _y, _z = place(coords)
    tok, width = tokens.shape
    rows = qkv.shape[0]
    half, side = rows // 2, width // 2
    p = 2 * x + c
    at = pl.ds(pl.multiple_of(half * c, 16), half)
    qa_out[pl.ds(0, half), :] = qkv[at, pl.ds(pl.multiple_of(width * x, 128), width)]
    scratch[...] = jnp.zeros_like(scratch)
    scratch[pl.ds(0, 2), pl.ds(0, rows)] = f32(gains[...])
    scratch[pl.ds(2, 2), pl.ds(0, rows)] = f32(shifts[...])
    scratch[pl.ds(4, 4), pl.ds(0, rows)] = f32(biases[...])
    scratch[pl.ds(0, 1), pl.ds(128, 384)] = f32(up_bias[...])
    qa_out[pl.ds(half, 8), :] = b16(scratch[...])
    qb_out[:, pl.ds(0, side)] = qkv[at, pl.ds(pl.multiple_of(2 * width + side * x, 128), side)]
    qb_out[:, pl.ds(side, side)] = out[at, pl.ds(pl.multiple_of(side * x, 128), side)]
    t_out[pl.ds(0, tok), :] = tokens[...]
    scratch[...] = jnp.zeros_like(scratch)
    scratch[pl.ds(0, 1), pl.ds(0, tok)] = f32(segs[...])
    t_out[pl.ds(tok, 8), :] = b16(scratch[...])
    for group in range(2):
        parts = []
        for shard in range(4 * group, 4 * group + 4):
            parts.append(choose(unpack96(f32(up[:, pl.ds(384 * shard, 384)])), p))
        fu_out[:, pl.ds(384 * group, 384)] = b16(pack96(parts))
    fd_out[...] = down[pl.ds(pl.multiple_of(rows * p, 16), rows), :]


def front_kernel(
    coords, seg, xo, x1, x2, x3, x4, first, own, own_o,
    a7, ax7, ac7, acx7, b7, bx7, bc7, bcx7,
    q_out, kv_out, h_out, a_out, lse_out, start_out, vec_out, upb_out, wo_out, r_out, h2_out,
    full, small, bias, sems, vsems,
):
    x, c, y, z = place(coords)
    me = 2 * z + y
    p = 2 * x + c
    tok, width = q_out.shape
    copies, vcopies = Copies(sems), Copies(vsems)
    vcopies.add(first.at[pl.ds(48, 8), pl.ds(0, 512)], small.at[me])
    for number in range(7):
        vcopies.add(a7.at[number, pl.ds(48, 8), pl.ds(0, 512)], small.at[piece_shard(number, y, z)])
    fetch_qkv(
        copies, coords, own, (a7, ax7, ac7, acx7), (b7, bx7, bc7, bcx7), full, wo_out, own_o
    )
    blocks = (xo, x1, x2, x3, x4)
    lane1 = lax.broadcasted_iota(jnp.int32, (1, tok), 1)
    start = jnp.full(seg.shape, 1 << 30, jnp.int32)
    for number in range(4):
        first_pos = jnp.full((1, 1), 1 << 30, jnp.int32)
        for back in range(5):
            ids = f32(blocks[back][pl.ds(tok, 8), pl.ds(0, tok)])[:1]
            pos = (me - back) * tok + lane1
            hit = (ids == float(number)) & (pos >= 0)
            first_pos = jnp.minimum(
                first_pos, jnp.min(jnp.where(hit, pos, 1 << 30), axis=1, keepdims=True)
            )
        start = jnp.where(seg[...] == number, first_pos, start)
    start_out[...] = start
    mask_bias(start, me, tok, bias)
    vcopies.wait()
    for group in range(2):
        held = [f32(small[4 * group + k]) for k in range(4)]
        vec_out[:, pl.ds(384 * group, 384)] = pack96([block[:, :128] for block in held])
        upb_out[:, pl.ds(384 * group, 384)] = pack96(
            [choose(unpack96(block[:, 128:512]), p) for block in held]
        )
    vec = vec_out[...]
    for back in range(5):
        hat, _rate = norm_parts(f32(blocks[back][pl.ds(0, tok), :]))
        h_out[pl.ds((4 - back) * tok, tok), :] = b16(hat * vec[0:1] + vec[2:3])
    copies.wait()
    q_out[...] = b16(dot_nn(h_out[pl.ds(4 * tok, tok), :], full[:, pl.ds(0, width)]) + vec[4:5])

    def project(number, carry):
        col = pl.multiple_of(number * 256, 256)
        shift = jnp.where(number >= width // 256, 1.0, 0.0)
        bias_at = lax.rem(number, width // 256)
        piece = vec_out[pl.ds(5, 1), pl.ds(pl.multiple_of(bias_at * 256, 256), 256)]
        kv_out[:, pl.ds(col, 256)] = b16(
            dot_nn(h_out[...], full[:, pl.ds(pl.multiple_of(width + col, 256), 256)]) + piece * shift
        )
        return carry

    lax.fori_loop(0, 2 * width // 256, project, 0)

    def pair(number, carry):
        col = pl.multiple_of(number * 128, 128)
        queries = pair_stack(q_out[:, pl.ds(col, 128)] * jnp.bfloat16(0.125))
        scores = dot_nt(kv_out[:, pl.ds(col, 128)], queries) + bias[...]
        top = jnp.max(scores, axis=0, keepdims=True)
        probs = jnp.exp(scores - top)
        total = jnp.sum(probs, axis=0, keepdims=True)
        mixed = dot_tn(kv_out[:, pl.ds(pl.multiple_of(width + col, 128), 128)], b16(probs))
        a_out[:, pl.ds(col, 128)] = b16(pair_join(mixed / total))
        lse_out[number] = top + jnp.log(total)
        return carry

    lax.fori_loop(0, width // 128, pair, 0)
    residual = f32(xo[pl.ds(0, tok), :]) + dot_nn(a_out[...], wo_out[...]) + vec[6:7]
    r_out[...] = residual
    hat, _rate = norm_parts(residual)
    h2_out[...] = b16(hat * vec[1:2] + vec[3:4])


def feed_tokens(h2, dy, w_up, w_down, upb, act_out, du_out, y_acc, dh_acc):
    root = math.sqrt(2.0 / math.pi)
    chunk = 256

    def feed(number, carry):
        col = pl.multiple_of(number * chunk, chunk)
        pre = dot_nn(h2[...], w_up[:, pl.ds(col, chunk)]) + upb[pl.ds(0, 1), pl.ds(col, chunk)]
        square = pre * pre
        bend = jnp.tanh(root * pre * (1.0 + 0.044715 * square))
        act = b16(0.5 * pre * (1.0 + bend))
        slope = 0.5 * (1.0 + bend) + 0.5 * pre * (1.0 - bend * bend) * (
            root * (1.0 + 3.0 * 0.044715 * square)
        )
        low = b16(dot_nt(dy[...], w_down[pl.ds(col, chunk), :]) * slope)
        act_out[:, pl.ds(col, chunk)] = act
        du_out[:, pl.ds(col, chunk)] = low
        return carry

    lax.fori_loop(0, w_up.shape[1] // chunk, feed, 0)
    dh_acc[...] = dot_nt(du_out[...], w_up[...])
    y_acc[...] = dot_nn(act_out[...], w_down[...])


def near_kernel(
    coords, h_own, h_c, dy_own, dy_c, upb, u_own, uz1, uz2, uz3, uy, d_own, dz1, dz2, dz3, dy4,
    act_out, du_out, keep_out, send_out, wu_out, wd_out,
    h2, dy, y_acc, dh_acc, sems,
):
    _x, _c, y, z = place(coords)
    tok = h_own.shape[0]
    copies = Copies(sems)
    for own, ones, four, full in (
        (u_own, (uz1, uz2, uz3), uy, wu_out),
        (d_own, (dz1, dz2, dz3), dy4, wd_out),
    ):
        rows = own.shape[0]
        copies.add(own, full.at[pl.ds(pl.multiple_of((2 * z + y) * rows, 16), rows), :])
        for number in range(7):
            at = pl.ds(pl.multiple_of(piece_shard(number, y, z) * rows, 16), rows)
            copies.add(ones[number] if number < 3 else four.at[pl.ds((number - 3) * rows, rows), :], full.at[at, :])
    h2[pl.ds(0, tok), :] = h_own[...]
    h2[pl.ds(tok, tok), :] = h_c[...]
    dy[pl.ds(0, tok), :] = dy_own[...]
    dy[pl.ds(tok, tok), :] = dy_c[...]
    copies.wait()
    feed_tokens(h2, dy, wu_out, wd_out, upb, act_out, du_out, y_acc, dh_acc)
    keep_out[0] = dh_acc[pl.ds(0, tok), :]
    keep_out[1] = y_acc[pl.ds(0, tok), :]
    send_out[0] = b16(dh_acc[pl.ds(tok, tok), :])
    send_out[1] = b16(y_acc[pl.ds(tok, tok), :])


def far_kernel(
    h_x, h_xc, dy_x, dy_xc, upb, w_up, w_down,
    act_out, du_out, keep_out, send_out,
    h2, dy, y_acc, dh_acc,
):
    tok = h_x.shape[0]
    h2[pl.ds(0, tok), :] = h_x[...]
    h2[pl.ds(tok, tok), :] = h_xc[...]
    dy[pl.ds(0, tok), :] = dy_x[...]
    dy[pl.ds(tok, tok), :] = dy_xc[...]
    feed_tokens(h2, dy, w_up, w_down, upb, act_out, du_out, y_acc, dh_acc)
    keep_out[0] = dh_acc[pl.ds(0, tok), :]
    keep_out[1] = y_acc[pl.ds(0, tok), :]
    send_out[0] = b16(dh_acc[pl.ds(tok, tok), :])
    send_out[1] = b16(y_acc[pl.ds(tok, tok), :])


def weights_kernel(
    coords, h0, h1, h2, h3, d0, d1, d2, d3, act_a, act_b, du_a, du_b,
    u_out, d_out, upb_out,
    hs, dys, acts, dus, stage, sems,
):
    _x, _c, y, z = place(coords)
    tok, width = h0.shape
    for number, (h, d) in enumerate(((h0, d0), (h1, d1), (h2, d2), (h3, d3))):
        hs[pl.ds(number * tok, tok), :] = h[...]
        dys[pl.ds(number * tok, tok), :] = d[...]
    for number, (act, du) in enumerate(((act_a, du_a), (act_b, du_b))):
        acts[pl.ds(2 * number * tok, 2 * tok), :] = act[...]
        dus[pl.ds(2 * number * tok, 2 * tok), :] = du[...]
    upb_out[...] = jnp.sum(f32(dus[...]), axis=0, keepdims=True)

    def weight(number, carry):
        col = pl.multiple_of(number * 256, 256)
        stage[0, pl.ds(col, 256), :] = b16(dot_tn(hs[:, pl.ds(col, 256)], dus[...]))
        stage[1, pl.ds(col, 256), :] = b16(dot_tn(acts[:, pl.ds(col, 256)], dys[...]))
        return carry

    lax.fori_loop(0, width // 256, weight, 0)
    outs = Copies(sems)
    for shard in range(8):
        zz = lax.rem(shard // 2 + 4 - z, 4)
        yy = jnp.where(y == shard % 2, 0, 1)
        rows = pl.ds(shard * (width // 8), width // 8)
        outs.add(stage.at[0, rows, :], u_out.at[yy, zz])
        outs.add(stage.at[1, rows, :], d_out.at[yy, zz])
    outs.wait()


def post_kernel(residual, own, near, across, dy_in, vec_in, w_out, a_in, dr_out, da_out, dw_out, vec_out):
    vec = vec_in[...]
    grad_hidden = own[0] + f32(near[0]) + f32(across[...])
    hat, rate = norm_parts(residual[...])
    dy = f32(dy_in[...])
    grad_first = dy + norm_back(grad_hidden, hat, rate, vec[1:2])
    dr_out[...] = grad_first
    low = b16(grad_first)
    da_out[...] = b16(dot_nt(low, w_out[...]))
    dw_out[...] = b16(dot_tn(a_in[...], low))
    zero = jnp.zeros((1, dy.shape[1]), jnp.float32)
    vec_out[...] = jnp.concatenate(
        [
            zero,
            jnp.sum(grad_hidden * hat, axis=0, keepdims=True),
            zero,
            jnp.sum(grad_hidden, axis=0, keepdims=True),
            zero,
            zero,
            jnp.sum(grad_first, axis=0, keepdims=True),
            jnp.sum(dy, axis=0, keepdims=True),
        ],
        axis=0,
    )


def back_pairs(first, q_in, kv_in, lse_in, da_in, bias, dq, dkv):
    width = q_in.shape[1]

    def pair(number, carry):
        col = pl.multiple_of((first + number) * 128, 128)
        vcol = pl.multiple_of(width + col, 128)
        to = pl.multiple_of(number * 128, 128)
        queries = pair_stack(q_in[:, pl.ds(col, 128)] * jnp.bfloat16(0.125))
        grads = pair_stack(da_in[:, pl.ds(col, 128)])
        keys = kv_in[:, pl.ds(col, 128)]
        probs = jnp.exp(dot_nt(keys, queries) + bias[...] - lse_in[first + number])
        dkv[:, pl.ds(pl.multiple_of(width // 2 + to, 128), 128)] = b16(dot_nn(b16(probs), grads))
        term = probs * dot_nt(kv_in[:, pl.ds(vcol, 128)], grads)
        low = b16(term - probs * jnp.sum(term, axis=0, keepdims=True))
        dkv[:, pl.ds(to, 128)] = b16(dot_nn(low, queries))
        dq[:, pl.ds(to, 128)] = b16(pair_join(dot_tn(keys, low)) * 0.125)
        return carry

    lax.fori_loop(0, 3, pair, 0)


def qkv_weight(h_in, dq, dkv, stage):
    tok, part = dq.shape
    keys = h_in.shape[0]

    def weight(number, carry):
        col = pl.multiple_of(number * 384, 384)
        key = dot_tn(h_in[:, pl.ds(col, 384)], dkv[...])
        query = dot_tn(h_in[pl.ds(keys - tok, tok), pl.ds(col, 384)], dq[...])
        for shard in range(4):
            for cc in range(2):
                for xx in range(2):
                    row = 96 * shard + 48 * cc + 24 * xx
                    stage[cc, xx, 4 * number + shard, pl.ds(0, 24), pl.ds(0, part)] = b16(query[row : row + 24])
                    stage[cc, xx, 4 * number + shard, pl.ds(0, 24), pl.ds(part, 2 * part)] = b16(key[row : row + 24])
        return carry

    lax.fori_loop(0, 2, weight, 0)


def back_a_kernel(
    coords, start_in, q_in, kv_in, h_in, lse_in, da_in, dw_in,
    other, mine, dq_out, dkv_out,
    bias, stage, sems,
):
    x, c, y, z = place(coords)
    tok, width = q_in.shape
    mask_bias(start_in[...], 2 * z + y, tok, bias)
    for shard in range(8):
        for cc in range(2):
            block = f32(dw_in[pl.ds(96 * shard + 48 * cc, 48), :])
            for xx in range(2):
                stage[cc, xx, shard, :, pl.ds(3 * width // 2, width)] = b16(block[24 * xx : 24 * xx + 24])
    back_pairs(0, q_in, kv_in, lse_in, da_in, bias, dq_out, dkv_out)
    qkv_weight(h_in, dq_out, dkv_out, stage)
    outs = Copies(sems)
    for shard in range(8):
        zz = lax.rem(shard // 2 + 4 - z, 4)
        yy = jnp.where(y == shard % 2, 0, 1)
        for xx in range(2):
            far = jnp.where(x == xx, 0, 1)
            outs.add(stage.at[1 - c, xx, shard], other.at[far, yy, zz])
            outs.add(stage.at[c, xx, shard], mine.at[far, yy, zz])
    outs.wait()


def back_b_kernel(
    coords, start_in, q_in, kv_in, h_in, lse_in, da_in, vec_in, upb_in, dq_a, dkv_a, xo, x1, x2, x3, x4,
    own, a7, ax7, ac7, acx7, b7, bx7, bc7, bcx7,
    other, mine, p_own, p_y, p_z,
    full, bias, dq_s, dkv_s, stage, sems, osems,
):
    x, c, y, z = place(coords)
    p = 2 * x + c
    tok, width = q_in.shape
    side = width // 2
    copies = Copies(sems)
    fetch_qkv(copies, coords, own, (a7, ax7, ac7, acx7), (b7, bx7, bc7, bcx7), full)
    mask_bias(start_in[...], 2 * z + y, tok, bias)
    back_pairs(3, q_in, kv_in, lse_in, da_in, bias, dq_s, dkv_s)
    copies.wait()
    gain_sum = jnp.zeros((1, width), jnp.float32)
    shift_sum = jnp.zeros((1, width), jnp.float32)
    for back, block in enumerate((xo, x1, x2, x3, x4)):
        rows = pl.ds((4 - back) * tok, tok)
        grad = jnp.zeros((tok, width), jnp.float32)
        for number, (dq, dkv) in enumerate(((dq_a, dkv_a), (dq_s, dkv_s))):
            at = number * side
            grad = grad + dot_nt(dkv[rows, pl.ds(0, side)], full[:, pl.ds(width + at, side)])
            grad = grad + dot_nt(dkv[rows, pl.ds(side, side)], full[:, pl.ds(2 * width + at, side)])
            if back == 0:
                grad = grad + dot_nt(dq[...], full[:, pl.ds(at, side)])
        if back == 0:
            p_own[...] = grad
        elif back in (1, 3):
            p_y[back // 2] = b16(grad)
        else:
            p_z[back // 2 - 1] = b16(grad)
        hat, _rate = norm_parts(f32(block[pl.ds(0, tok), :]))
        gain_sum = gain_sum + jnp.sum(grad * hat, axis=0, keepdims=True)
        shift_sum = shift_sum + jnp.sum(grad, axis=0, keepdims=True)
    qkv_weight(h_in, dq_s, dkv_s, stage)
    zero = jnp.zeros((1, width), jnp.float32)
    bias_q = jnp.concatenate([jnp.sum(f32(d[...]), axis=0, keepdims=True) for d in (dq_a, dq_s)], axis=1)
    bias_v = jnp.concatenate(
        [jnp.sum(f32(d[:, pl.ds(side, side)]), axis=0, keepdims=True) for d in (dkv_a, dkv_s)], axis=1
    )
    vec = vec_in[...] + jnp.concatenate(
        [gain_sum, zero, shift_sum, zero, bias_q, bias_v, zero, zero], axis=0
    )
    lane = lax.broadcasted_iota(jnp.int32, (8, 128), 1)
    line = lax.broadcasted_iota(jnp.int32, (8, 128), 0)
    for group in range(2):
        cols = pl.ds(384 * group, 384)
        vec_parts = unpack96(vec[:, 384 * group : 384 * group + 384])
        upb_parts = unpack96(jnp.broadcast_to(upb_in[:, cols], (8, 384)))
        for k in range(4):
            both = jnp.concatenate(
                [
                    jnp.where(lane < 96, vec_parts[k], 0.0),
                    jnp.where((lane < 96) & (line == p), upb_parts[k], 0.0),
                    jnp.zeros((8, 3 * side - 256), jnp.float32),
                ],
                axis=1,
            )
            for cc in range(2):
                for xx in range(2):
                    stage[cc, xx, 4 * group + k, pl.ds(24, 8), :] = b16(both)
    outs = Copies(osems)
    for shard in range(8):
        zz = lax.rem(shard // 2 + 4 - z, 4)
        yy = jnp.where(y == shard % 2, 0, 1)
        for xx in range(2):
            far = jnp.where(x == xx, 0, 1)
            outs.add(stage.at[1 - c, xx, shard], other.at[far, yy, zz])
            outs.add(stage.at[c, xx, shard], mine.at[far, yy, zz])
    outs.wait()


def tokens_kernel(own, near, far, dr, xo, vec_in, grad_out):
    tok = own.shape[0]
    hat, rate = norm_parts(f32(xo[pl.ds(0, tok), :]))
    grad = own[...] + f32(near[...]) + f32(far[...])
    grad_out[...] = dr[...] + norm_back(grad, hat, rate, vec_in[0:1, :])


def finish_f_kernel(coords, u0, ux, uc, ucx, d0, dx, dc, dcx, up, down, held):
    x, c, _y, _z = place(coords)
    rows = u0.shape[0]
    for (xx, cc), u, d in zip(corners(x, c), (u0, ux, uc, ucx), (d0, dx, dc, dcx), strict=True):
        p = 2 * xx + cc
        held[p] = u[...]
        down[pl.ds(pl.multiple_of(rows * p, 16), rows), :] = f32(d[...])
    for group in range(2):
        parts = [unpack96(f32(held[k, :, pl.ds(384 * group, 384)])) for k in range(4)]
        for shard in range(4):
            up[:, pl.ds(384 * (4 * group + shard), 384)] = pack96([part[shard] for part in parts])


def finish_q_kernel(coords, a0, ax, ac, acx, b0, bx, bc, bcx, qkv, out):
    x, c, _y, _z = place(coords)
    side = out.shape[1] // 2
    for (xx, cc), a, b in zip(corners(x, c), (a0, ax, ac, acx), (b0, bx, bc, bcx), strict=True):
        rows = pl.ds(pl.multiple_of(48 * cc + 24 * xx, 8), 24)
        first, second = f32(a[...]), f32(b[...])[:24]
        for number in range(3):
            qkv[rows, pl.ds(2 * side * number, side)] = first[:, side * number : side * (number + 1)]
            qkv[rows, pl.ds(2 * side * number + side, side)] = second[:, side * number : side * (number + 1)]
        out[rows, :] = first[:, 3 * side :]


VM = pl.BlockSpec(memory_space=pltpu.VMEM)
SM = pl.BlockSpec(memory_space=pltpu.SMEM)
AN = pl.BlockSpec(memory_space=pl.ANY)


def shape_of(shape, dtype):
    return jax.ShapeDtypeStruct(shape, dtype)


def call(kernel, ins, outs, out_shape, scratch=(), vmem=40, flops=0, moved=0):
    return pl.pallas_call(
        kernel,
        in_specs=ins,
        out_specs=outs,
        out_shape=out_shape,
        scratch_shapes=list(scratch),
        compiler_params=pltpu.CompilerParams(vmem_limit_bytes=vmem << 20),
        cost_estimate=pl.CostEstimate(flops=flops, bytes_accessed=moved, transcendentals=0),
    )


def after(value, *done):
    return lax.optimization_barrier((value,) + done)[0]


def swap_rep(value, bit):
    return lax.ppermute(value, "rep", [(k, k ^ bit) for k in range(4)])


def to_core(value):
    return swap_rep(value, 1)


def to_x(value):
    return swap_rep(value, 2)


def to_y(value):
    return lax.ppermute(value, "seq", [(k, k ^ 1) for k in range(8)])


def to_z(value, steps):
    return lax.ppermute(value, "seq", [(k, (k + 2 * steps) % 8) for k in range(8)])


def join(*parts):
    return jnp.concatenate(parts, axis=0)


def on_device_fast(
    tokens,
    segment_ids,
    query_key_value_weight,
    output_weight,
    up_weight,
    down_weight,
    ln_gains,
    ln_biases,
    biases,
    up_projection_bias,
    cotangent,
):
    rep, seq = lax.axis_index("rep"), lax.axis_index("seq")
    x, c, z, y = rep // 2, rep % 2, seq // 2, seq % 2
    coords = jnp.stack([x, c, y, z]).astype(jnp.int32)
    tok, width = tokens.shape[1:]
    hidden = up_weight.shape[1]
    keys = 5 * tok
    bf, fl = jnp.bfloat16, jnp.float32
    dma = pltpu.SemaphoreType.DMA
    grad_y = cotangent[0]
    dy_x = to_x(grad_y)
    own_tokens, piece_a, piece_b, piece_u, piece_d = call(
        prep_kernel,
        [SM] + [VM] * 10,
        [VM] * 5,
        [
            shape_of((tok + 8, width), bf),
            shape_of((56, width), bf),
            shape_of((48, width), bf),
            shape_of((96, width), bf),
            shape_of((96, width), bf),
        ],
        [pltpu.VMEM((8, width), fl)],
        vmem=16,
        moved=4 * 10**6,
    )(
        coords, tokens[0], segment_ids, query_key_value_weight, output_weight, up_weight, down_weight,
        ln_gains, ln_biases, biases, up_projection_bias[None],
    )

    az = [to_z(piece_a, k) for k in (1, 2, 3)]
    bz = [to_z(after(piece_b, az[k - 1]), k) for k in (1, 2, 3)]
    ay = to_y(join(piece_a, *az))
    x2 = to_z(after(own_tokens, az[2]), 1)
    by = to_y(after(join(piece_b, *bz), ay))
    a7 = join(*az, ay)
    ax7 = to_x(after(a7, dy_x))
    x4 = to_z(x2, 1)
    near = jnp.where(y == 0, own_tokens, x2)
    far = jnp.where(y == 0, x2, x4)
    crossed = to_y(after(jnp.stack([near, far]), by))
    x1, x3 = crossed[0], crossed[1]
    b7 = join(*bz, by)
    bx7 = to_x(after(b7, ax7))
    ac7, bc7 = to_core(a7), to_core(b7)
    acx7, bcx7 = to_core(ax7), to_core(bx7)
    uz = [to_z(after(piece_u, x4), k) for k in (1, 2, 3)]
    dz = [to_z(after(piece_d, uz[k - 1]), k) for k in (1, 2, 3)]
    uy = to_y(after(join(piece_u, *uz), crossed))
    down_y = to_y(after(join(piece_d, *dz), uy))
    dy_c, dy_xc = to_core(grad_y), to_core(dy_x)

    def seven(value):
        return value.reshape(7, value.shape[0] // 7, value.shape[1])

    got_a = [seven(v) for v in (a7, ax7, ac7, acx7)]
    got_b = [seven(v) for v in (b7, bx7, bc7, bcx7)]
    seg = jnp.concatenate([segment_ids, segment_ids], axis=1)
    queries, kv, normed, attended, lse, start, vec, upb, w_out, residual, hidden_2 = call(
        front_kernel,
        [SM] + [VM] * 6 + [AN] * 11,
        [VM] * 11,
        [
            shape_of((tok, width), bf),
            shape_of((keys, 2 * width), bf),
            shape_of((keys, width), bf),
            shape_of((tok, width), bf),
            shape_of((width // 128, 1, 2 * tok), fl),
            shape_of((1, 2 * tok), jnp.int32),
            shape_of((8, width), fl),
            shape_of((8, width), fl),
            shape_of((width, width), bf),
            shape_of((tok, width), fl),
            shape_of((tok, width), bf),
        ],
        [
            pltpu.VMEM((width, 3 * width), bf),
            pltpu.VMEM((8, 8, 512), bf),
            pltpu.VMEM((keys, 2 * tok), fl),
            dma((2 + 84,)),
            dma((8,)),
        ],
        flops=7 * 10**9,
        moved=12 * 10**6,
    )(
        coords, seg, own_tokens, x1, x2, x3, x4, piece_a, query_key_value_weight, output_weight,
        *got_a, *got_b,
    )
    h_x = to_x(hidden_2)
    h_c = to_core(hidden_2)
    feed_shapes = [
        shape_of((2 * tok, width), bf),
        shape_of((2 * tok, width), bf),
        shape_of((2, tok, width), fl),
        shape_of((2, tok, width), bf),
    ]
    feed_scratch = [
        pltpu.VMEM((2 * tok, width), bf),
        pltpu.VMEM((2 * tok, width), bf),
        pltpu.VMEM((2 * tok, width), fl),
        pltpu.VMEM((2 * tok, width), fl),
    ]
    act_a, du_a, keep_a, send_a, w_up, w_down = call(
        near_kernel,
        [SM] + [VM] * 5 + [AN] * 10,
        [VM] * 6,
        feed_shapes + [shape_of((width, width), bf)] * 2,
        feed_scratch + [dma((16,))],
        flops=3 * 10**9,
        moved=6 * 10**6,
    )(coords, hidden_2, h_c, grad_y, dy_c, upb, piece_u, *uz, uy, piece_d, *dz, down_y)
    came_a = to_core(send_a)
    h_xc = to_core(h_x)
    act_b, du_b, keep_b, send_b = call(
        far_kernel,
        [VM] * 7,
        [VM] * 4,
        feed_shapes,
        feed_scratch,
        flops=3 * 10**9,
        moved=6 * 10**6,
    )(h_x, h_xc, dy_x, dy_xc, upb, w_up, w_down)
    came_b = to_core(send_b)
    back_x = to_x(b16(keep_b[0] + f32(came_b[0])))
    u_terms, d_terms, upb_g = call(
        weights_kernel,
        [SM] + [VM] * 12,
        [AN] * 2 + [VM],
        [shape_of((2, 4, 96, width), bf), shape_of((2, 4, 96, width), bf), shape_of((1, width), fl)],
        [pltpu.VMEM((4 * tok, width), bf)] * 4 + [pltpu.VMEM((2, width, width), bf), dma((16,))],
        flops=3 * 10**9,
        moved=6 * 10**6,
    )(coords, hidden_2, h_c, h_x, h_xc, grad_y, dy_c, dy_x, dy_xc, act_a, act_b, du_a, du_b)
    u_came = to_y(u_terms[1])
    d_came = to_y(after(d_terms[1], u_came))
    back_y = to_x(after(b16(keep_b[1] + f32(came_b[1])), back_x))
    grad_first, grad_attended, dw_out, vec_g = call(
        post_kernel,
        [VM] * 8,
        [VM] * 4,
        [
            shape_of((tok, width), fl),
            shape_of((tok, width), bf),
            shape_of((width, width), bf),
            shape_of((8, width), fl),
        ],
        vmem=24,
        flops=10**9,
        moved=4 * 10**6,
    )(residual, keep_a, came_a, back_x, grad_y, vec, w_out, attended)
    back_scratch = [
        pltpu.VMEM((keys, 2 * tok), fl),
    ]
    qa_other, qa_mine, dq_a, dkv_a = call(
        back_a_kernel,
        [SM] + [VM] * 7,
        [AN] * 2 + [VM] * 2,
        [
            shape_of((2, 2, 4, 24, 5 * width // 2), bf),
            shape_of((2, 2, 4, 24, 5 * width // 2), bf),
            shape_of((tok, width // 2), bf),
            shape_of((keys, width), bf),
        ],
        back_scratch + [pltpu.VMEM((2, 2, 8, 24, 5 * width // 2), bf), dma((32,))],
        flops=5 * 10**9,
        moved=10 * 10**6,
    )(coords, start, queries, kv, normed, lse, grad_attended, dw_out)
    qb_other, qb_mine, p_own, p_y, p_z = call(
        back_b_kernel,
        [SM] + [VM] * 15 + [AN] * 9,
        [AN] * 2 + [VM] * 3,
        [
            shape_of((2, 2, 4, 32, 3 * width // 2), bf),
            shape_of((2, 2, 4, 32, 3 * width // 2), bf),
            shape_of((tok, width), fl),
            shape_of((2, tok, width), bf),
            shape_of((2, tok, width), bf),
        ],
        [pltpu.VMEM((width, 3 * width), bf)]
        + back_scratch
        + [
            pltpu.VMEM((tok, width // 2), bf),
            pltpu.VMEM((keys, width), bf),
            pltpu.VMEM((2, 2, 8, 32, 3 * width // 2), bf),
            dma((1 + 56,)),
            dma((32,)),
        ],
        flops=9 * 10**9,
        moved=14 * 10**6,
    )(
        coords, start, queries, kv, normed, lse, grad_attended, vec_g, upb_g, dq_a, dkv_a,
        own_tokens, x1, x2, x3, x4, query_key_value_weight, *got_a, *got_b,
    )
    result = b16(
        residual + vec[7:8] + keep_a[1] + f32(came_a[1]) + f32(back_y)
    )

    def across_core(other, mine):
        came = to_core(other)
        return lambda *index: f32(mine[index]) + f32(came[index])

    def along_z(part, *done):
        total = part(0)
        for step in (1, 2, 3):
            total = total + f32(to_z(after(b16(part(step)), *done), step))
        return b16(total)

    def u_part(*index):
        return f32(u_terms[(0,) + index]) + f32(u_came[index])

    def d_part(*index):
        return f32(d_terms[(0,) + index]) + f32(d_came[index])

    u_sum = along_z(u_part)
    d_sum = along_z(d_part, u_sum)
    qa_1 = across_core(qa_other, qa_mine)
    qa_x = to_x(b16(qa_1(1)))
    p_came = to_y(after(p_y, d_came))
    qb_1 = across_core(qb_other, qb_mine)
    qb_x = to_x(after(b16(qb_1(1)), qa_x))
    even = y == 0
    sum_own = p_own + jnp.where(even, f32(p_came[0]), 0.0)
    sum_4 = b16(f32(p_z[1]) + jnp.where(even, 0.0, f32(p_came[1])))
    hop = to_z(after(sum_4, d_sum), 3)
    sum_2 = b16(f32(p_z[0]) + jnp.where(even, f32(p_came[1]), f32(p_came[0])) + f32(hop))
    back_2 = to_z(sum_2, 3)

    def qa_2(*index):
        return qa_1(0, *index) + f32(qa_x[index])

    def qb_2(*index):
        return qb_1(0, *index) + f32(qb_x[index])

    qa_y = to_y(after(b16(qa_2(1)), p_came))
    qb_y = to_y(after(b16(qb_2(1)), qa_y))

    def qa_3(*index):
        return qa_2(0, *index) + f32(qa_y[index])

    def qb_3(*index):
        return qb_2(0, *index) + f32(qb_y[index])

    qa_sum = along_z(qa_3, back_2)
    qb_sum = along_z(qb_3, qa_sum)

    def spread(total, *done):
        over = to_x(after(total, *done))
        return total, over, to_core(total), to_core(over)

    done_u = spread(u_sum)
    done_d = spread(d_sum)
    done_a = spread(qa_sum)
    done_b = spread(qb_sum)
    grad_tokens = call(
        tokens_kernel, [VM] * 6, VM, shape_of((tok, width), fl), vmem=16, moved=3 * 10**6
    )(sum_own, back_2, jnp.zeros_like(back_2), grad_first, own_tokens, vec)
    grad_up, grad_down = call(
        finish_f_kernel,
        [SM] + [VM] * 8,
        [VM] * 2,
        [shape_of(up_weight.shape, fl), shape_of(down_weight.shape, fl)],
        [pltpu.VMEM((4, 96, width), bf)],
        vmem=16,
        moved=4 * 10**6,
    )(coords, *done_u, *done_d)
    grad_qkv, grad_out = call(
        finish_q_kernel,
        [SM] + [VM] * 8,
        [VM] * 2,
        [shape_of(query_key_value_weight.shape, fl), shape_of(output_weight.shape, fl)],
        vmem=16,
        moved=3 * 10**6,
    )(coords, *done_a, *done_b)
    sums = f32(qb_sum[24:32, :256])
    part = ln_gains.shape[1]
    return (
        result[None],
        grad_tokens[None],
        grad_qkv,
        grad_out,
        grad_up,
        grad_down,
        sums[0:2, :part],
        sums[2:4, :part],
        sums[4:8, :part],
        sums[0:4, 128 : 128 + part].reshape(4 * part),
    )


def solution(mesh):
    placed = (
        P("rep", "seq", None),
        P("rep", "seq"),
        P("seq", None),
        P("seq", None),
        P("seq", None),
        P("seq", None),
        P(None, "seq"),
        P(None, "seq"),
        P(None, "seq"),
        P("seq"),
        P("rep", "seq", None),
    )
    shape = dict(mesh.shape)
    small_slice = shape["rep"] == 4 and shape["seq"] == 8
    return jax.shard_map(
        on_device_fast if small_slice else on_device,
        mesh=mesh,
        in_specs=placed,
        out_specs=(
            P("rep", "seq", None),
            P("rep", "seq", None),
            P("seq", None),
            P("seq", None),
            P("seq", None),
            P("seq", None),
            P(None, "seq"),
            P(None, "seq"),
            P(None, "seq"),
            P("seq"),
        ),
        check_vma=False,
    )
```

```python
import math

import jax
import jax.numpy as jnp
from jax import lax
from jax.experimental import pallas as pl
from jax.experimental.pallas import tpu as pltpu
from jax.sharding import PartitionSpec as P

HEADS = 12
HD = 64


norm_eps = 1e-05
floor_score = -1e30


def layer_norm(values, gain, shift):
    center = values - jnp.mean(values, axis=-1, keepdims=True)
    spread = jnp.mean(center * center, axis=-1, keepdims=True)
    return center * lax.rsqrt(spread + norm_eps) * gain + shift


def head_split(matrix):
    return matrix.reshape(matrix.shape[0], HEADS, HD)


def masked_scores(queries, query_seg, query_pos, key_piece, seg_piece, offset):
    rows = key_piece.shape[0]
    scores = jnp.einsum(
        "qhd,khd->hqk", queries, head_split(key_piece), preferred_element_type=jnp.float32
    ) * HD ** (-0.5)
    key_pos = offset + jnp.arange(rows, dtype=jnp.int32)
    allowed = (query_seg[:, None] == seg_piece[None, :]) & (key_pos[None, :] <= query_pos[:, None])
    return (jnp.where(allowed[None], scores, floor_score), allowed)


def forward_block(running, pieces, offset, queries, query_seg, query_pos):
    top_run, total_run, accum = running
    key_piece, value_piece, seg_piece = pieces
    scores, allowed = masked_scores(queries, query_seg, query_pos, key_piece, seg_piece, offset)
    top_new = jnp.maximum(top_run, jnp.max(scores, axis=-1))
    probs = jnp.where(allowed[None], jnp.exp(scores - top_new[:, :, None]), 0.0)
    factor = jnp.exp(top_run - top_new)
    total_new = total_run * factor + jnp.sum(probs, axis=-1)
    update = jnp.einsum(
        "hqk,khd->qhd",
        probs.astype(jnp.bfloat16),
        head_split(value_piece),
        preferred_element_type=jnp.float32,
    )
    return (top_new, total_new, accum * factor.T[:, :, None] + update)


def in_blocks(block_fn, running, pieces):
    rows = pieces[0].shape[0]
    size = math.gcd(rows, 1024)
    stacked = tuple((member.reshape((rows // size, size) + member.shape[1:]) for member in pieces))
    offsets = jnp.arange(rows // size, dtype=jnp.int32) * size

    def scan_step(state_now, element):
        return (block_fn(state_now, element[0], element[1]), None)

    running, _unused = lax.scan(scan_step, running, (stacked, offsets))
    return running


def backward_block(
    number,
    state_now,
    whole,
    queries,
    query_seg,
    query_pos,
    grad_heads,
    log_total,
    delta,
    block_rows,
):
    grad_query, term = state_now
    offset = number * block_rows
    key_piece = lax.dynamic_slice_in_dim(whole[0], offset, block_rows, 0)
    value_piece = lax.dynamic_slice_in_dim(whole[1], offset, block_rows, 0)
    seg_piece = lax.dynamic_slice_in_dim(whole[2], offset, block_rows, 0)
    scores, allowed = masked_scores(queries, query_seg, query_pos, key_piece, seg_piece, offset)
    probs = jnp.where(allowed[None], jnp.exp(scores - log_total[:, :, None]), 0.0)
    grad_probs = jnp.einsum(
        "qhd,khd->hqk", grad_heads, head_split(value_piece), preferred_element_type=jnp.float32
    )
    grad_scores = (probs * (grad_probs - delta[:, :, None])).astype(jnp.bfloat16)
    grad_query = grad_query + jnp.einsum(
        "hqk,khd->qhd", grad_scores, head_split(key_piece), preferred_element_type=jnp.float32
    )
    grad_key = jnp.einsum(
        "hqk,qhd->khd", grad_scores, queries, preferred_element_type=jnp.float32
    ) * HD ** (-0.5)
    grad_value = jnp.einsum(
        "hqk,qhd->khd", probs.astype(jnp.bfloat16), grad_heads, preferred_element_type=jnp.float32
    )
    joined = jnp.concatenate(
        [grad_key.reshape(block_rows, -1), grad_value.reshape(block_rows, -1)], axis=1
    )
    term = lax.dynamic_update_slice_in_dim(term, joined, offset, 0)
    return (grad_query, term)


def on_device(
    tokens,
    segment_ids,
    query_key_value_weight,
    output_weight,
    up_weight,
    down_weight,
    ln_gains,
    ln_biases,
    biases,
    up_projection_bias,
    cotangent,
):
    gathered = (
        lax.all_gather(query_key_value_weight, "seq", axis=0, tiled=True),
        lax.all_gather(output_weight, "seq", axis=0, tiled=True),
        lax.all_gather(up_weight, "seq", axis=0, tiled=True),
        lax.all_gather(down_weight, "seq", axis=0, tiled=True),
        lax.all_gather(ln_gains, "seq", axis=1, tiled=True),
        lax.all_gather(ln_biases, "seq", axis=1, tiled=True),
        lax.all_gather(biases, "seq", axis=1, tiled=True),
        lax.all_gather(up_projection_bias, "seq", axis=0, tiled=True),
    )
    full_qkv, full_out, full_up, full_down, gains_all, shifts_all, biases_all, up_shift = gathered
    gains_f = gains_all.astype(jnp.float32)
    shifts_f = shifts_all.astype(jnp.float32)
    biases_f = biases_all.astype(jnp.float32)
    up_shift_f = up_shift.astype(jnp.float32)
    tokens_f = tokens[0].astype(jnp.float32)
    seg_local = segment_ids[0]
    tok_rows = tokens_f.shape[0]
    width = tokens_f.shape[1]
    seqlen = tok_rows * lax.axis_size("seq")
    query_pos = lax.axis_index("seq") * tok_rows + jnp.arange(tok_rows, dtype=jnp.int32)
    hidden_first = layer_norm(tokens_f, gains_f[0], shifts_f[0]).astype(jnp.bfloat16)
    query_key_value_bias = jnp.concatenate(
        [biases_f[0], jnp.zeros((width,), jnp.float32), biases_f[1]]
    )
    projected_rows = (
        jnp.dot(hidden_first, full_qkv, preferred_element_type=jnp.float32) + query_key_value_bias
    ).astype(jnp.bfloat16)
    queries = head_split(projected_rows[:, :width])
    key_rows = projected_rows[:, width : 2 * width]
    value_rows = projected_rows[:, 2 * width :]
    initial = (
        jnp.full((HEADS, tok_rows), floor_score, jnp.float32),
        jnp.zeros((HEADS, tok_rows), jnp.float32),
        jnp.zeros((tok_rows, HEADS, HD), jnp.float32),
    )

    def block_fn(running, pieces, offset):
        return forward_block(running, pieces, offset, queries, seg_local, query_pos)

    block_rows = math.gcd(seqlen, 1024)
    key_end = (lax.axis_index("seq") + 1) * tok_rows
    block_count = (key_end + block_rows - 1) // block_rows
    top_run, total_run, accum = in_blocks(
        block_fn,
        initial,
        (
            lax.all_gather(key_rows, "seq", axis=0, tiled=True),
            lax.all_gather(value_rows, "seq", axis=0, tiled=True),
            lax.all_gather(seg_local, "seq", axis=0, tiled=True),
        ),
    )
    log_total = top_run + jnp.log(total_run)
    attended_f = accum / total_run.T[:, :, None]
    attention_result = attended_f.reshape(tok_rows, width).astype(jnp.bfloat16)
    residual_first = (
        tokens_f
        + jnp.dot(attention_result, full_out, preferred_element_type=jnp.float32)
        + biases_f[2]
    )
    hidden_second = layer_norm(residual_first, gains_f[1], shifts_f[1]).astype(jnp.bfloat16)
    upward_rows = jnp.dot(hidden_second, full_up, preferred_element_type=jnp.float32) + up_shift_f
    activated_f, gelu_back = jax.vjp(jax.nn.gelu, upward_rows)
    activation_values = activated_f.astype(jnp.bfloat16)
    result = (
        residual_first
        + jnp.dot(activation_values, full_down, preferred_element_type=jnp.float32)
        + biases_f[3]
    )
    grad_y = cotangent[0]
    grad_y_f = grad_y.astype(jnp.float32)
    grad_down = jnp.einsum(
        "tf,td->fd", activation_values, grad_y, preferred_element_type=jnp.float32
    )
    grad_act = jnp.einsum("td,fd->tf", grad_y, full_down, preferred_element_type=jnp.float32)
    grad_up_pre = gelu_back(grad_act)[0].astype(jnp.bfloat16)
    grad_up = jnp.einsum(
        "td,tf->df", hidden_second, grad_up_pre, preferred_element_type=jnp.float32
    )
    grad_hidden_two = jnp.einsum(
        "tf,df->td", grad_up_pre, full_up, preferred_element_type=jnp.float32
    )
    _unused, norm_two_back = jax.vjp(layer_norm, residual_first, gains_f[1], shifts_f[1])
    grad_sum_part, grad_gain_two, grad_shift_two = norm_two_back(grad_hidden_two)
    grad_first = grad_y_f + grad_sum_part
    grad_first_bf = grad_first.astype(jnp.bfloat16)
    grad_out_w = jnp.einsum(
        "td,te->de", attention_result, grad_first_bf, preferred_element_type=jnp.float32
    )
    grad_attended = jnp.einsum(
        "te,de->td", grad_first_bf, full_out, preferred_element_type=jnp.float32
    ).astype(jnp.bfloat16)
    grad_heads = head_split(grad_attended)
    delta = jnp.einsum("qhd,qhd->hq", grad_heads.astype(jnp.float32), attended_f)
    whole = (
        lax.all_gather(key_rows, "seq", axis=0, tiled=True),
        lax.all_gather(value_rows, "seq", axis=0, tiled=True),
        lax.all_gather(seg_local, "seq", axis=0, tiled=True),
    )

    def backward_step(number, state_now):
        return backward_block(
            number,
            state_now,
            whole,
            queries,
            seg_local,
            query_pos,
            grad_heads,
            log_total,
            delta,
            block_rows,
        )

    start_state = (
        jnp.zeros((tok_rows, HEADS, HD), jnp.float32),
        jnp.zeros((seqlen, 2 * width), jnp.float32),
    )
    grad_query, term = lax.fori_loop(0, block_count, backward_step, start_state)
    grad_kv = lax.psum_scatter(term, "seq", scatter_dimension=0, tiled=True).astype(jnp.bfloat16)
    grad_q = (grad_query * HD ** (-0.5)).reshape(tok_rows, width).astype(jnp.bfloat16)
    grad_proj = jnp.concatenate([grad_q, grad_kv], axis=1)
    grad_qkv_w = jnp.einsum(
        "td,te->de", hidden_first, grad_proj, preferred_element_type=jnp.float32
    )
    grad_hidden_one = jnp.einsum(
        "te,de->td", grad_proj, full_qkv, preferred_element_type=jnp.float32
    )
    _unused_two, norm_one_back = jax.vjp(layer_norm, tokens_f, gains_f[0], shifts_f[0])
    grad_in_part, grad_gain_one, grad_shift_one = norm_one_back(grad_hidden_one)
    grad_tokens = grad_first + grad_in_part
    grad_proj_f = grad_proj.astype(jnp.float32)
    grad_bias_rows = jnp.stack(
        [
            jnp.sum(grad_proj_f[:, :width], axis=0),
            jnp.sum(grad_proj_f[:, 2 * width :], axis=0),
            jnp.sum(grad_first, axis=0),
            jnp.sum(grad_y_f, axis=0),
        ]
    )
    grad_up_shift = jnp.sum(grad_up_pre.astype(jnp.float32), axis=0)
    grad_gains = jnp.stack([grad_gain_one, grad_gain_two])
    grad_shifts = jnp.stack([grad_shift_one, grad_shift_two])
    shares = (
        lax.psum_scatter(grad_qkv_w, "seq", scatter_dimension=0, tiled=True),
        lax.psum_scatter(grad_out_w, "seq", scatter_dimension=0, tiled=True),
        lax.psum_scatter(grad_up, "seq", scatter_dimension=0, tiled=True),
        lax.psum_scatter(grad_down, "seq", scatter_dimension=0, tiled=True),
        lax.psum_scatter(grad_gains, "seq", scatter_dimension=1, tiled=True),
        lax.psum_scatter(grad_shifts, "seq", scatter_dimension=1, tiled=True),
        lax.psum_scatter(grad_bias_rows, "seq", scatter_dimension=1, tiled=True),
        lax.psum_scatter(grad_up_shift, "seq", scatter_dimension=0, tiled=True),
    )
    totals = (
        lax.psum(shares[0].astype(jnp.bfloat16), "rep").astype(jnp.float32),
        lax.psum(shares[1].astype(jnp.bfloat16), "rep").astype(jnp.float32),
        lax.psum(shares[2].astype(jnp.bfloat16), "rep").astype(jnp.float32),
        lax.psum(shares[3].astype(jnp.bfloat16), "rep").astype(jnp.float32),
        lax.psum(shares[4].astype(jnp.bfloat16), "rep").astype(jnp.float32),
        lax.psum(shares[5].astype(jnp.bfloat16), "rep").astype(jnp.float32),
        lax.psum(shares[6].astype(jnp.bfloat16), "rep").astype(jnp.float32),
        lax.psum(shares[7].astype(jnp.bfloat16), "rep").astype(jnp.float32),
    )
    return (
        result.astype(jnp.bfloat16)[None],
        grad_tokens[None],
        totals[0],
        totals[1],
        totals[2],
        totals[3],
        totals[4],
        totals[5],
        totals[6],
        totals[7],
    )


def f32(value):
    return value.astype(jnp.float32)


def b16(value):
    return value.astype(jnp.bfloat16)


def dot_nn(left, right):
    return jnp.dot(left, right, preferred_element_type=jnp.float32)


def dot_nt(left, right):
    return lax.dot_general(
        left, right, (((1,), (1,)), ((), ())), preferred_element_type=jnp.float32
    )


def dot_tn(left, right):
    return lax.dot_general(
        left, right, (((0,), (0,)), ((), ())), preferred_element_type=jnp.float32
    )


def norm_parts(values):
    center = values - jnp.mean(values, axis=-1, keepdims=True)
    rate = lax.rsqrt(jnp.mean(center * center, axis=-1, keepdims=True) + norm_eps)
    return center * rate, rate


def norm_back(grad, hat, rate, gain):
    scaled = grad * gain
    return rate * (
        scaled
        - jnp.mean(scaled, axis=-1, keepdims=True)
        - hat * jnp.mean(scaled * hat, axis=-1, keepdims=True)
    )


def place(coords):
    return coords[0], coords[1], coords[2], coords[3]


def piece_shard(number, y, z):
    if number < 3:
        return 2 * lax.rem(z + 3 - number, 4) + y
    return 2 * lax.rem(z + 7 - number, 4) + 1 - y


def pack96(parts):
    lane = lax.broadcasted_iota(jnp.int32, parts[0].shape, 1)
    one, two, three = (pltpu.roll(parts[k], 128 - 32 * k, 1) for k in (1, 2, 3))
    return jnp.concatenate(
        [
            jnp.where(lane < 96, parts[0], one),
            jnp.where(lane < 64, one, two),
            jnp.where(lane < 32, two, three),
        ],
        axis=1,
    )


def unpack96(block):
    tiles = [block[:, 128 * k : 128 * k + 128] for k in range(3)]
    lane = lax.broadcasted_iota(jnp.int32, tiles[0].shape, 1)
    return [
        tiles[0],
        jnp.where(lane < 32, pltpu.roll(tiles[0], 32, 1), pltpu.roll(tiles[1], 32, 1)),
        jnp.where(lane < 64, pltpu.roll(tiles[1], 64, 1), pltpu.roll(tiles[2], 64, 1)),
        pltpu.roll(tiles[2], 96, 1),
    ]


def choose(parts, index):
    out = parts[0]
    for number in range(1, len(parts)):
        out = jnp.where(index == number, parts[number], out)
    return out


class Copies:
    def __init__(self, sems, first=0):
        self.sems = sems
        self.first = first
        self.held = []

    def add(self, source, target):
        copy = pltpu.make_async_copy(source, target, self.sems.at[self.first + len(self.held)])
        copy.start()
        self.held.append(copy)

    def wait(self):
        for copy in self.held:
            copy.wait()
        self.held = []


def corners(x, c):
    return ((x, c), (1 - x, c), (x, 1 - c), (1 - x, 1 - c))


def fetch_qkv(copies, coords, own, groups, full, full_out=None, own_out=None):
    x, c, y, z = place(coords)
    rows = own.shape[0]
    half, width = rows // 2, own.shape[1] // 3
    row = pl.multiple_of((2 * z + y) * rows, 16)
    copies.add(own, full.at[pl.ds(row, rows), :])
    if full_out is not None:
        copies.add(own_out, full_out.at[pl.ds(row, rows), :])
    wide, side = 3 * width // 2, width // 2
    for number in range(7):
        for (xx, cc), group in zip(corners(x, c), groups, strict=True):
            piece = piece_of(group, number)
            at = pl.ds(pl.multiple_of(piece_shard(number, y, z) * rows + half * cc, 16), half)
            copies.add(
                piece.at[pl.ds(0, half), pl.ds(0, wide)],
                full.at[at, pl.ds(pl.multiple_of(wide * xx, 128), wide)],
            )
            if full_out is not None:
                copies.add(
                    piece.at[pl.ds(0, half), pl.ds(wide, side)],
                    full_out.at[at, pl.ds(pl.multiple_of(side * xx, 128), side)],
                )


def piece_of(group, number):
    behind, across, behind_across = group
    if number < 3:
        return behind.at[number]
    return across.at[0] if number == 3 else behind_across.at[number - 4]


def mask_bias(start, me, tok, target):
    keys, lanes = target.shape
    key_pos = (me - 4) * tok + lax.broadcasted_iota(jnp.int32, (keys, lanes), 0)
    lane = lax.broadcasted_iota(jnp.int32, (keys, lanes), 1)
    query_pos = me * tok + jnp.where(lane >= tok, lane - tok, lane)
    target[...] = jnp.where((key_pos >= start) & (key_pos <= query_pos), 0.0, floor_score)


def pair_stack(rows):
    lane = lax.broadcasted_iota(jnp.int32, rows.shape, 1)
    zero = jnp.zeros_like(rows)
    return jnp.concatenate([jnp.where(lane < HD, rows, zero), jnp.where(lane < HD, zero, rows)], axis=0)


def pair_join(transposed):
    both = transposed.T
    tok = both.shape[0] // 2
    lane = lax.broadcasted_iota(jnp.int32, (tok, 2 * HD), 1)
    return jnp.where(lane < HD, both[:tok], both[tok:])


def prep_kernel(
    coords, tokens, segs, qkv, out, up, down, gains, shifts, biases, up_bias,
    t_out, q_out, f_out,
    scratch, wide, held_g, held_s, held_b, ids, line, sems,
):
    x, c, _y, _z = place(coords)
    tok, width = tokens.shape[1:]
    rows = qkv.shape[0]
    half, side = rows // 2, width // 2
    p = 2 * x + c
    at = pl.ds(pl.multiple_of(half * c, 16), half)
    copies, others = Copies(sems), Copies(sems, 5)
    for source, target in ((gains, held_g), (shifts, held_s), (biases, held_b)):
        copies.add(source, target)
    copies.add(segs, ids)
    copies.add(up_bias, line)
    others.add(up, wide)
    wide_cols = 3 * side
    others.add(
        qkv.at[at, pl.ds(pl.multiple_of(wide_cols * x, 128), wide_cols)],
        q_out.at[pl.ds(0, half), pl.ds(0, wide_cols)],
    )
    others.add(
        out.at[at, pl.ds(pl.multiple_of(side * x, 128), side)],
        q_out.at[pl.ds(0, half), pl.ds(wide_cols, side)],
    )
    others.add(tokens.at[0], t_out.at[pl.ds(0, tok), :])
    others.add(down.at[pl.ds(pl.multiple_of(rows * p, 16), rows), :], f_out.at[pl.ds(rows, rows), :])
    copies.wait()
    scratch[...] = jnp.zeros_like(scratch)
    for first, held in ((0, held_g), (2, held_s), (4, held_b)):
        scratch[pl.ds(first, held.shape[0]), pl.ds(0, rows)] = f32(held[...])
    scratch[pl.ds(0, 1), pl.ds(128, 384)] = f32(line[...])
    q_out[pl.ds(half, 8), pl.ds(0, width)] = b16(scratch[...])
    q_out[pl.ds(half, 8), pl.ds(width, width)] = jnp.zeros((8, width), jnp.bfloat16)
    scratch[...] = jnp.zeros_like(scratch)
    scratch[pl.ds(0, 1), pl.ds(0, tok)] = f32(ids[...])
    t_out[pl.ds(tok, 8), :] = b16(scratch[...])
    others.wait()
    for group in range(2):
        parts = []
        for shard in range(4 * group, 4 * group + 4):
            parts.append(choose(unpack96(f32(wide[:, pl.ds(384 * shard, 384)])), p))
        f_out[pl.ds(0, rows), pl.ds(384 * group, 384)] = b16(pack96(parts))


def front_kernel(
    coords, seg, xo, x1, x2, x3, x4, first, own, own_o,
    g0, g1, g2, g3, g4, g5, g6, g7, g8, g9, g10, g11,
    q_out, kv_out, h_out, a_out, lse_out, start_out, vec_out, upb_out, wo_out, r_out, h2_out,
    full, small, bias, sems, vsems,
):
    x, c, y, z = place(coords)
    me = 2 * z + y
    p = 2 * x + c
    tok, width = q_out.shape
    copies, vcopies = Copies(sems), Copies(vsems)
    vcopies.add(first.at[pl.ds(48, 8), pl.ds(0, 512)], small.at[me])
    for number in range(7):
        source = piece_of((g0, g1, g2), number)
        vcopies.add(source.at[pl.ds(48, 8), pl.ds(0, 512)], small.at[piece_shard(number, y, z)])
    groups = ((g0, g1, g2), (g3, g4, g5), (g6, g7, g8), (g9, g10, g11))
    fetch_qkv(copies, coords, own, groups, full, wo_out, own_o)
    blocks = (xo, x1, x2, x3, x4)
    lane1 = lax.broadcasted_iota(jnp.int32, (1, tok), 1)
    start = jnp.full(seg.shape, 1 << 30, jnp.int32)
    for number in range(4):
        first_pos = jnp.full((1, 1), 1 << 30, jnp.int32)
        for back in range(5):
            ids = f32(blocks[back][pl.ds(tok, 8), pl.ds(0, tok)])[:1]
            pos = (me - back) * tok + lane1
            hit = (ids == float(number)) & (pos >= 0)
            first_pos = jnp.minimum(
                first_pos, jnp.min(jnp.where(hit, pos, 1 << 30), axis=1, keepdims=True)
            )
        start = jnp.where(seg[...] == number, first_pos, start)
    start_out[...] = start
    mask_bias(start, me, tok, bias)
    vcopies.wait()
    for group in range(2):
        held = [f32(small[4 * group + k]) for k in range(4)]
        vec_out[:, pl.ds(384 * group, 384)] = pack96([block[:, :128] for block in held])
        upb_out[:, pl.ds(384 * group, 384)] = pack96(
            [choose(unpack96(block[:, 128:512]), p) for block in held]
        )
    vec = vec_out[...]
    for back in range(5):
        hat, _rate = norm_parts(f32(blocks[back][pl.ds(0, tok), :]))
        h_out[pl.ds((4 - back) * tok, tok), :] = b16(hat * vec[0:1] + vec[2:3])
    copies.wait()
    q_out[...] = b16(dot_nn(h_out[pl.ds(4 * tok, tok), :], full[:, pl.ds(0, width)]) + vec[4:5])

    def project(number, carry):
        col = pl.multiple_of(number * 256, 256)
        shift = jnp.where(number >= width // 256, 1.0, 0.0)
        bias_at = lax.rem(number, width // 256)
        piece = vec_out[pl.ds(5, 1), pl.ds(pl.multiple_of(bias_at * 256, 256), 256)]
        kv_out[:, pl.ds(col, 256)] = b16(
            dot_nn(h_out[...], full[:, pl.ds(pl.multiple_of(width + col, 256), 256)]) + piece * shift
        )
        return carry

    lax.fori_loop(0, 2 * width // 256, project, 0)

    def pair(number, carry):
        col = pl.multiple_of(number * 128, 128)
        queries = pair_stack(q_out[:, pl.ds(col, 128)] * jnp.bfloat16(0.125))
        scores = dot_nt(kv_out[:, pl.ds(col, 128)], queries) + bias[...]
        top = jnp.max(scores, axis=0, keepdims=True)
        probs = jnp.exp(scores - top)
        total = jnp.sum(probs, axis=0, keepdims=True)
        mixed = dot_tn(kv_out[:, pl.ds(pl.multiple_of(width + col, 128), 128)], b16(probs))
        a_out[:, pl.ds(col, 128)] = b16(pair_join(mixed / total))
        lse_out[number] = top + jnp.log(total)
        return carry

    lax.fori_loop(0, width // 128, pair, 0)
    residual = f32(xo[pl.ds(0, tok), :]) + dot_nn(a_out[...], wo_out[...]) + vec[6:7]
    r_out[...] = residual
    hat, _rate = norm_parts(residual)
    h2_out[...] = b16(hat * vec[1:2] + vec[3:4])


def feed_tokens(h2, dy, w_up, w_down, upb, act_out, du_out, y_acc, dh_acc):
    root = math.sqrt(2.0 / math.pi)
    chunk = 256

    def feed(number, carry):
        col = pl.multiple_of(number * chunk, chunk)
        pre = dot_nn(h2[...], w_up[:, pl.ds(col, chunk)]) + upb[pl.ds(0, 1), pl.ds(col, chunk)]
        square = pre * pre
        bend = jnp.tanh(root * pre * (1.0 + 0.044715 * square))
        act = b16(0.5 * pre * (1.0 + bend))
        slope = 0.5 * (1.0 + bend) + 0.5 * pre * (1.0 - bend * bend) * (
            root * (1.0 + 3.0 * 0.044715 * square)
        )
        low = b16(dot_nt(dy[...], w_down[pl.ds(col, chunk), :]) * slope)
        act_out[:, pl.ds(col, chunk)] = act
        du_out[:, pl.ds(col, chunk)] = low
        return carry

    lax.fori_loop(0, w_up.shape[1] // chunk, feed, 0)
    dh_acc[...] = dot_nt(du_out[...], w_up[...])
    y_acc[...] = dot_nn(act_out[...], w_down[...])


def near_kernel(
    coords, h_own, h_c, dy_own, dy_c, upb, own, z1, z2, z3, y0, y13, y2,
    h2, dy, act_out, du_out, keep_out, send_out, wu_out, wd_out,
    y_acc, dh_acc, sems,
):
    _x, _c, y, z = place(coords)
    tok, width = h_own.shape
    rows = width // 8
    copies = Copies(sems)
    across = (y0, y13.at[pl.ds(0, 2 * rows), :], y2, y13.at[pl.ds(2 * rows, 2 * rows), :])
    shards = [(own, 2 * z + y)] + [
        (ref, piece_shard(number, y, z)) for number, ref in enumerate((z1, z2, z3) + across)
    ]
    for ref, shard in shards:
        at = pl.ds(pl.multiple_of(shard * rows, 16), rows)
        copies.add(ref.at[pl.ds(0, rows), :], wu_out.at[at, :])
        copies.add(ref.at[pl.ds(rows, rows), :], wd_out.at[at, :])
    h2[pl.ds(0, tok), :] = h_own[...]
    h2[pl.ds(tok, tok), :] = h_c[...]
    dy[pl.ds(0, tok), :] = dy_own[...]
    dy[pl.ds(tok, tok), :] = dy_c[...]
    copies.wait()
    feed_tokens(h2, dy, wu_out, wd_out, upb, act_out, du_out, y_acc, dh_acc)
    keep_out[0] = dh_acc[pl.ds(0, tok), :]
    keep_out[1] = y_acc[pl.ds(0, tok), :]
    send_out[0] = b16(dh_acc[pl.ds(tok, tok), :])
    send_out[1] = b16(y_acc[pl.ds(tok, tok), :])


def far_kernel(
    h_x, h_xc, dy_x, dy_xc, upb, w_up, w_down, h_near, dy_near, act_near, du_near,
    hs, dys, acts, dus, keep_out, send_out,
    y_acc, dh_acc, sems,
):
    tok = h_x.shape[0]
    copies = Copies(sems)
    for source, target in ((h_near, hs), (dy_near, dys), (act_near, acts), (du_near, dus)):
        copies.add(source, target.at[pl.ds(0, 2 * tok), :])
    later = pl.ds(2 * tok, 2 * tok)
    hs[pl.ds(2 * tok, tok), :] = h_x[...]
    hs[pl.ds(3 * tok, tok), :] = h_xc[...]
    dys[pl.ds(2 * tok, tok), :] = dy_x[...]
    dys[pl.ds(3 * tok, tok), :] = dy_xc[...]
    feed_tokens(
        hs.at[later, :], dys.at[later, :], w_up, w_down, upb, acts.at[later, :], dus.at[later, :], y_acc, dh_acc
    )
    keep_out[0] = dh_acc[pl.ds(0, tok), :]
    keep_out[1] = y_acc[pl.ds(0, tok), :]
    send_out[0] = b16(dh_acc[pl.ds(tok, tok), :])
    send_out[1] = b16(y_acc[pl.ds(tok, tok), :])
    copies.wait()


def weights_kernel(coords, hs, dys, acts, dus, u_out, d_out, upb_out, stage, sems):
    _x, _c, y, z = place(coords)
    width = hs.shape[1]
    rows = width // 8
    upb_out[...] = jnp.sum(f32(dus[...]), axis=0, keepdims=True)

    def weight(number, carry):
        col = pl.multiple_of(number * 256, 256)
        stage[0, pl.ds(col, 256), :] = b16(dot_tn(hs[:, pl.ds(col, 256)], dus[...]))
        stage[1, pl.ds(col, 256), :] = b16(dot_tn(acts[:, pl.ds(col, 256)], dys[...]))
        return carry

    lax.fori_loop(0, width // 256, weight, 0)
    outs = Copies(sems)
    for shard in range(8):
        zz = lax.rem(shard // 2 + 4 - z, 4)
        yy = jnp.where(y == shard % 2, 0, 1)
        outs.add(stage.at[0, pl.ds(shard * rows, rows), :], u_out.at[yy, zz])
        outs.add(stage.at[1, pl.ds(shard * rows, rows), :], d_out.at[yy, zz])
    outs.wait()


def post_kernel(residual, own, near, across, dy_in, vec_in, w_out, a_in, dr_out, da_out, dw_out, vec_out):
    vec = vec_in[...]
    grad_hidden = own[0] + f32(near[0]) + f32(across[...])
    hat, rate = norm_parts(residual[...])
    dy = f32(dy_in[...])
    grad_first = dy + norm_back(grad_hidden, hat, rate, vec[1:2])
    dr_out[...] = grad_first
    low = b16(grad_first)
    da_out[...] = b16(dot_nt(low, w_out[...]))
    dw_out[...] = b16(dot_tn(a_in[...], low))
    zero = jnp.zeros((1, dy.shape[1]), jnp.float32)
    vec_out[...] = jnp.concatenate(
        [
            zero,
            jnp.sum(grad_hidden * hat, axis=0, keepdims=True),
            zero,
            jnp.sum(grad_hidden, axis=0, keepdims=True),
            zero,
            zero,
            jnp.sum(grad_first, axis=0, keepdims=True),
            jnp.sum(dy, axis=0, keepdims=True),
        ],
        axis=0,
    )


def back_pairs(first, q_in, kv_in, lse_in, da_in, bias, dq, dkv):
    width = q_in.shape[1]

    def pair(number, carry):
        col = pl.multiple_of((first + number) * 128, 128)
        vcol = pl.multiple_of(width + col, 128)
        to = pl.multiple_of(number * 128, 128)
        queries = pair_stack(q_in[:, pl.ds(col, 128)] * jnp.bfloat16(0.125))
        grads = pair_stack(da_in[:, pl.ds(col, 128)])
        keys = kv_in[:, pl.ds(col, 128)]
        probs = jnp.exp(dot_nt(keys, queries) + bias[...] - lse_in[first + number])
        dkv[:, pl.ds(pl.multiple_of(width // 2 + to, 128), 128)] = b16(dot_nn(b16(probs), grads))
        term = probs * dot_nt(kv_in[:, pl.ds(vcol, 128)], grads)
        low = b16(term - probs * jnp.sum(term, axis=0, keepdims=True))
        dkv[:, pl.ds(to, 128)] = b16(dot_nn(low, queries))
        dq[:, pl.ds(to, 128)] = b16(pair_join(dot_tn(keys, low)) * 0.125)
        return carry

    lax.fori_loop(0, 3, pair, 0)


def qkv_weight(h_in, dq, dkv, stage):
    tok, part = dq.shape
    keys = h_in.shape[0]

    def weight(number, carry):
        col = pl.multiple_of(number * 384, 384)
        key = dot_tn(h_in[:, pl.ds(col, 384)], dkv[...])
        query = dot_tn(h_in[pl.ds(keys - tok, tok), pl.ds(col, 384)], dq[...])
        for shard in range(4):
            for cc in range(2):
                for xx in range(2):
                    row = 96 * shard + 48 * cc + 24 * xx
                    stage[cc, xx, 4 * number + shard, pl.ds(0, 24), pl.ds(0, part)] = b16(query[row : row + 24])
                    stage[cc, xx, 4 * number + shard, pl.ds(0, 24), pl.ds(part, 2 * part)] = b16(key[row : row + 24])
        return carry

    lax.fori_loop(0, 2, weight, 0)


def back_a_kernel(
    coords, start_in, q_in, kv_in, h_in, lse_in, da_in, dw_in,
    other, mine, dq_out, dkv_out,
    bias, stage, sems,
):
    x, c, y, z = place(coords)
    tok, width = q_in.shape
    mask_bias(start_in[...], 2 * z + y, tok, bias)
    for shard in range(8):
        for cc in range(2):
            block = f32(dw_in[pl.ds(96 * shard + 48 * cc, 48), :])
            for xx in range(2):
                stage[cc, xx, shard, :, pl.ds(3 * width // 2, width)] = b16(block[24 * xx : 24 * xx + 24])
    back_pairs(0, q_in, kv_in, lse_in, da_in, bias, dq_out, dkv_out)
    qkv_weight(h_in, dq_out, dkv_out, stage)
    outs = Copies(sems)
    for shard in range(8):
        zz = lax.rem(shard // 2 + 4 - z, 4)
        yy = jnp.where(y == shard % 2, 0, 1)
        for xx in range(2):
            far = jnp.where(x == xx, 0, 1)
            outs.add(stage.at[1 - c, xx, shard], other.at[far, yy, zz])
            outs.add(stage.at[c, xx, shard], mine.at[far, yy, zz])
    outs.wait()


def back_b_kernel(
    coords, start_in, q_in, kv_in, lse_in, da_in, vec_in, upb_in, dq_a, dkv_a, xo, x1, x2, x3, x4,
    own, g0, g1, g2, g3, g4, g5, g6, g7, g8, g9, g10, g11,
    dq_out, dkv_out, p_own, p_y, p_z, sums_out,
    full, bias, sems,
):
    x, c, y, z = place(coords)
    p = 2 * x + c
    tok, width = q_in.shape
    side = width // 2
    copies = Copies(sems)
    groups = ((g0, g1, g2), (g3, g4, g5), (g6, g7, g8), (g9, g10, g11))
    fetch_qkv(copies, coords, own, groups, full)
    mask_bias(start_in[...], 2 * z + y, tok, bias)
    back_pairs(3, q_in, kv_in, lse_in, da_in, bias, dq_out, dkv_out)
    copies.wait()
    gain_sum = jnp.zeros((1, width), jnp.float32)
    shift_sum = jnp.zeros((1, width), jnp.float32)
    for back, block in enumerate((xo, x1, x2, x3, x4)):
        rows = pl.ds((4 - back) * tok, tok)
        grad = jnp.zeros((tok, width), jnp.float32)
        for number, (dq, dkv) in enumerate(((dq_a, dkv_a), (dq_out, dkv_out))):
            at = number * side
            grad = grad + dot_nt(dkv[rows, pl.ds(0, side)], full[:, pl.ds(width + at, side)])
            grad = grad + dot_nt(dkv[rows, pl.ds(side, side)], full[:, pl.ds(2 * width + at, side)])
            if back == 0:
                grad = grad + dot_nt(dq[...], full[:, pl.ds(at, side)])
        if back == 0:
            p_own[...] = grad
        elif back in (1, 3):
            p_y[back // 2] = b16(grad)
        else:
            p_z[back // 2 - 1] = b16(grad)
        hat, _rate = norm_parts(f32(block[pl.ds(0, tok), :]))
        gain_sum = gain_sum + jnp.sum(grad * hat, axis=0, keepdims=True)
        shift_sum = shift_sum + jnp.sum(grad, axis=0, keepdims=True)
    zero = jnp.zeros((1, width), jnp.float32)
    bias_q = jnp.concatenate([jnp.sum(f32(d[...]), axis=0, keepdims=True) for d in (dq_a, dq_out)], axis=1)
    bias_v = jnp.concatenate(
        [jnp.sum(f32(d[:, pl.ds(side, side)]), axis=0, keepdims=True) for d in (dkv_a, dkv_out)], axis=1
    )
    vec = vec_in[...] + jnp.concatenate(
        [gain_sum, zero, shift_sum, zero, bias_q, bias_v, zero, zero], axis=0
    )
    lane = lax.broadcasted_iota(jnp.int32, (8, 128), 1)
    line = lax.broadcasted_iota(jnp.int32, (8, 128), 0)
    for group in range(2):
        cols = pl.ds(384 * group, 384)
        vec_parts = unpack96(vec[:, 384 * group : 384 * group + 384])
        upb_parts = unpack96(jnp.broadcast_to(upb_in[:, cols], (8, 384)))
        for k in range(4):
            sums_out[4 * group + k] = jnp.concatenate(
                [
                    jnp.where(lane < 96, vec_parts[k], 0.0),
                    jnp.where((lane < 96) & (line == p), upb_parts[k], 0.0),
                ],
                axis=1,
            )


def back_c_kernel(coords, h_in, dq, dkv, sums_in, other, mine, stage, sems):
    x, c, y, z = place(coords)
    qkv_weight(h_in, dq, dkv, stage)
    for shard in range(8):
        row = b16(
            jnp.concatenate([sums_in[shard], jnp.zeros((8, stage.shape[4] - 256), jnp.float32)], axis=1)
        )
        for cc in range(2):
            for xx in range(2):
                stage[cc, xx, shard, pl.ds(24, 8), :] = row
    outs = Copies(sems)
    for shard in range(8):
        zz = lax.rem(shard // 2 + 4 - z, 4)
        yy = jnp.where(y == shard % 2, 0, 1)
        for xx in range(2):
            far = jnp.where(x == xx, 0, 1)
            outs.add(stage.at[1 - c, xx, shard], other.at[far, yy, zz])
            outs.add(stage.at[c, xx, shard], mine.at[far, yy, zz])
    outs.wait()


def tokens_kernel(own, near, dr, xo, vec_in, grad_out):
    tok = own.shape[0]
    hat, rate = norm_parts(f32(xo[pl.ds(0, tok), :]))
    grad = own[...] + f32(near[...])
    grad_out[...] = dr[...] + norm_back(grad, hat, rate, vec_in[0:1, :])


def finish_f_kernel(coords, u0, ux, uc, ucx, d0, dx, dc, dcx, up, down, held):
    x, c, _y, _z = place(coords)
    rows = u0.shape[0]
    for (xx, cc), u, d in zip(corners(x, c), (u0, ux, uc, ucx), (d0, dx, dc, dcx), strict=True):
        p = 2 * xx + cc
        held[p] = u[...]
        down[pl.ds(pl.multiple_of(rows * p, 16), rows), :] = f32(d[...])
    for group in range(2):
        parts = [unpack96(f32(held[k, :, pl.ds(384 * group, 384)])) for k in range(4)]
        for shard in range(4):
            up[:, pl.ds(384 * (4 * group + shard), 384)] = pack96([part[shard] for part in parts])


def finish_q_kernel(coords, a0, ax, ac, acx, b0, bx, bc, bcx, qkv, out):
    x, c, _y, _z = place(coords)
    side = out.shape[1] // 2
    for (xx, cc), a, b in zip(corners(x, c), (a0, ax, ac, acx), (b0, bx, bc, bcx), strict=True):
        rows = pl.ds(pl.multiple_of(48 * cc + 24 * xx, 8), 24)
        first, second = f32(a[...]), f32(b[...])[:24]
        for number in range(3):
            qkv[rows, pl.ds(2 * side * number, side)] = first[:, side * number : side * (number + 1)]
            qkv[rows, pl.ds(2 * side * number + side, side)] = second[:, side * number : side * (number + 1)]
        out[rows, :] = first[:, 3 * side :]


HB = pl.BlockSpec(memory_space=pltpu.HBM)
VM = pl.BlockSpec(memory_space=pltpu.VMEM)
SM = pl.BlockSpec(memory_space=pltpu.SMEM)
AN = pl.BlockSpec(memory_space=pl.ANY)


def shape_of(shape, dtype):
    return jax.ShapeDtypeStruct(shape, dtype)


def call(kernel, ins, outs, out_shape, scratch=(), vmem=40, flops=0, moved=0):
    return pl.pallas_call(
        kernel,
        in_specs=ins,
        out_specs=outs,
        out_shape=out_shape,
        scratch_shapes=list(scratch),
        compiler_params=pltpu.CompilerParams(vmem_limit_bytes=vmem << 20),
        cost_estimate=pl.CostEstimate(flops=flops // 20, bytes_accessed=moved // 20, transcendentals=0),
    )


def after(value, *done):
    return lax.optimization_barrier((value,) + done)[0]


def swap_rep(value, bit):
    return lax.ppermute(value, "rep", [(k, k ^ bit) for k in range(4)])


def to_core(value):
    return swap_rep(value, 1)


def to_x(value):
    return swap_rep(value, 2)


def to_y(value):
    return lax.ppermute(value, "seq", [(k, k ^ 1) for k in range(8)])


def to_z(value, steps):
    return lax.ppermute(value, "seq", [(k, (k + 2 * steps) % 8) for k in range(8)])


def join(*parts):
    return jnp.concatenate(parts, axis=0)


def on_device_fast(
    tokens,
    segment_ids,
    query_key_value_weight,
    output_weight,
    up_weight,
    down_weight,
    ln_gains,
    ln_biases,
    biases,
    up_projection_bias,
    cotangent,
):
    rep, seq = lax.axis_index("rep"), lax.axis_index("seq")
    x, c, z, y = rep // 2, rep % 2, seq // 2, seq % 2
    coords = jnp.stack([x, c, y, z]).astype(jnp.int32)
    tok, width = tokens.shape[1:]
    hidden = up_weight.shape[1]
    keys = 5 * tok
    bf, fl = jnp.bfloat16, jnp.float32
    dma = pltpu.SemaphoreType.DMA
    grad_y = cotangent[0]
    own_tokens, piece_q, piece_f = call(
        prep_kernel,
        [SM] + [HB] * 10,
        [VM] * 3,
        [
            shape_of((tok + 8, width), bf),
            shape_of((56, 2 * width), bf),
            shape_of((192, width), bf),
        ],
        [
            pltpu.VMEM((8, width), fl),
            pltpu.VMEM((96, hidden), bf),
            pltpu.VMEM((2, 96), bf),
            pltpu.VMEM((2, 96), bf),
            pltpu.VMEM((4, 96), bf),
            pltpu.VMEM((1, tok), jnp.int32),
            pltpu.VMEM((1, 384), bf),
            dma((10,)),
        ],
        vmem=60, moved=4 * 10**6,
    )(
        coords, tokens, segment_ids, query_key_value_weight, output_weight, up_weight, down_weight,
        ln_gains, ln_biases, biases, up_projection_bias[None],
    )

    q1, q3 = to_z(piece_q, 1), to_z(piece_q, 3)
    q_y0 = to_y(piece_q)
    dy_x = to_x(grad_y)
    f_y0 = to_y(after(piece_f, q_y0))
    q2 = to_z(after(q1, q3), 1)
    q_xy0 = to_x(after(q_y0, dy_x))
    x2 = to_z(after(own_tokens, q2), 1)
    q_z = join(q1, q2, q3)
    q_y = to_y(after(q_z, f_y0))
    q_xz = to_x(after(q_z, q_xy0))
    f1 = to_z(after(piece_f, q2), 1)
    x4 = to_z(after(x2, f1), 1)
    near = jnp.where(y == 0, own_tokens, x2)
    far = jnp.where(y == 0, x2, x4)
    crossed = to_y(after(jnp.stack([near, far]), q_y))
    x1, x3 = crossed[0], crossed[1]
    q_xy = to_x(after(q_y, q_xz))
    f3 = to_z(after(piece_f, x4), 3)
    f2 = to_z(after(f1, f3), 1)
    q_cy0, q_cxy0 = to_core(after(q_y0, q_xz)), to_core(after(q_xy0, q_xz))
    q_cz, q_cxz = to_core(after(q_z, q_cy0)), to_core(after(q_xz, q_cxy0))
    q_cy = to_core(after(q_y, q_cz))
    f_y13 = to_y(after(join(f1, f3), crossed))
    q_cxy = to_core(after(q_xy, q_cy, q_cxz))
    f_y2 = to_y(after(f2, f_y13))
    dy_c, dy_xc = to_core(grad_y), to_core(dy_x)

    def pieces(value):
        return value.reshape(value.shape[0] // 56, 56, value.shape[1])

    got_q = [
        pieces(v)
        for v in (q_z, q_y0, q_y, q_xz, q_xy0, q_xy, q_cz, q_cy0, q_cy, q_cxz, q_cxy0, q_cxy)
    ]
    seg = jnp.concatenate([segment_ids, segment_ids], axis=1)
    queries, kv, normed, attended, lse, start, vec, upb, w_out, residual, hidden_2 = call(
        front_kernel,
        [SM] + [VM] * 6 + [AN] * 15,
        [VM] * 11,
        [
            shape_of((tok, width), bf),
            shape_of((keys, 2 * width), bf),
            shape_of((keys, width), bf),
            shape_of((tok, width), bf),
            shape_of((width // 128, 1, 2 * tok), fl),
            shape_of((1, 2 * tok), jnp.int32),
            shape_of((8, width), fl),
            shape_of((8, width), fl),
            shape_of((width, width), bf),
            shape_of((tok, width), fl),
            shape_of((tok, width), bf),
        ],
        [
            pltpu.VMEM((width, 3 * width), bf),
            pltpu.VMEM((8, 8, 512), bf),
            pltpu.VMEM((keys, 2 * tok), fl),
            dma((2 + 56,)),
            dma((8,)),
        ],
        flops=7 * 10**9,
        vmem=16, moved=12 * 10**6,
    )(
        coords, seg, own_tokens, x1, x2, x3, x4, piece_q, query_key_value_weight, output_weight, *got_q,
    )
    h_x = to_x(hidden_2)
    h_c = to_core(hidden_2)
    act = shape_of((2 * tok, width), bf)
    acts = shape_of((4 * tok, width), bf)
    feed_shapes = [shape_of((2, tok, width), fl), shape_of((2, tok, width), bf)]
    feed_scratch = [pltpu.VMEM((2 * tok, width), fl), pltpu.VMEM((2 * tok, width), fl)]
    *near_acts, keep_a, send_a, w_up, w_down = call(
        near_kernel,
        [SM] + [VM] * 5 + [AN] * 7,
        [VM] * 8,
        [act] * 4 + feed_shapes + [shape_of((width, width), bf)] * 2,
        feed_scratch + [dma((16,))],
        flops=3 * 10**9,
        vmem=8, moved=6 * 10**6,
    )(coords, hidden_2, h_c, grad_y, dy_c, upb, piece_f, f1, f2, f3, f_y0, f_y13, f_y2)
    came_a = to_core(send_a)
    h_xc = to_core(h_x)
    *all_acts, keep_b, send_b = call(
        far_kernel,
        [VM] * 7 + [AN] * 4,
        [VM] * 6,
        [acts] * 4 + feed_shapes,
        feed_scratch + [dma((4,))],
        flops=3 * 10**9,
        vmem=8, moved=6 * 10**6,
    )(h_x, h_xc, dy_x, dy_xc, upb, w_up, w_down, *near_acts)
    came_b = to_core(send_b)
    back_x = to_x(b16(keep_b[0] + f32(came_b[0])))
    u_terms, d_terms, upb_g = call(
        weights_kernel,
        [SM] + [VM] * 4,
        [AN, AN, VM],
        [shape_of((2, 4, 96, width), bf), shape_of((2, 4, 96, width), bf), shape_of((1, width), fl)],
        [pltpu.VMEM((2, width, width), bf), dma((16,))],
        flops=3 * 10**9,
        vmem=12, moved=6 * 10**6,
    )(coords, *all_acts)
    u_came = to_y(u_terms[1])
    d_came = to_y(after(d_terms[1], u_came))
    back_y = to_x(after(b16(keep_b[1] + f32(came_b[1])), back_x))
    grad_first, grad_attended, dw_out, vec_g = call(
        post_kernel,
        [VM] * 8,
        [VM] * 4,
        [
            shape_of((tok, width), fl),
            shape_of((tok, width), bf),
            shape_of((width, width), bf),
            shape_of((8, width), fl),
        ],
        flops=10**9,
        vmem=10, moved=4 * 10**6,
    )(residual, keep_a, came_a, back_x, grad_y, vec, w_out, attended)
    back_scratch = [
        pltpu.VMEM((keys, 2 * tok), fl),
    ]
    qa_other, qa_mine, dq_a, dkv_a = call(
        back_a_kernel,
        [SM] + [VM] * 7,
        [AN] * 2 + [VM] * 2,
        [
            shape_of((2, 2, 4, 24, 5 * width // 2), bf),
            shape_of((2, 2, 4, 24, 5 * width // 2), bf),
            shape_of((tok, width // 2), bf),
            shape_of((keys, width), bf),
        ],
        back_scratch + [pltpu.VMEM((2, 2, 8, 24, 5 * width // 2), bf), dma((32,))],
        flops=5 * 10**9,
        vmem=16, moved=10 * 10**6,
    )(coords, start, queries, kv, normed, lse, grad_attended, dw_out)
    def across_core(other, mine):
        came = to_core(other)
        return came, lambda *index: f32(mine[index]) + f32(came[index])

    def along_z(part, *done):
        came = [to_z(b16(part(step)), step) for step in (1, 2, 3)]
        came = lax.optimization_barrier((*came, *done))[:3]
        return b16(part(0) + f32(came[0]) + f32(came[1]) + f32(came[2]))

    def u_part(*index):
        return f32(u_terms[(0,) + index]) + f32(u_came[index])

    def d_part(*index):
        return f32(d_terms[(0,) + index]) + f32(d_came[index])

    qa_came, qa_1 = across_core(qa_other, qa_mine)
    dq_b, dkv_b, p_own, p_y, p_z, sums = call(
        back_b_kernel,
        [SM] + [VM] * 14 + [AN] * 13,
        [VM] * 6,
        [
            shape_of((tok, width // 2), bf),
            shape_of((keys, width), bf),
            shape_of((tok, width), fl),
            shape_of((2, tok, width), bf),
            shape_of((2, tok, width), bf),
            shape_of((8, 8, 256), fl),
        ],
        [pltpu.VMEM((width, 3 * width), bf)] + back_scratch + [dma((1 + 28,))],
        flops=6 * 10**9,
        vmem=20, moved=10 * 10**6,
    )(
        coords, start, queries, kv, lse, grad_attended, vec_g, upb_g, dq_a, dkv_a,
        own_tokens, x1, x2, x3, x4, query_key_value_weight, *got_q,
    )
    u_sum = along_z(u_part, dkv_b)
    d_sum = along_z(d_part)
    qa_x = to_x(b16(qa_1(1)))
    p_came = to_y(after(p_y, d_came))
    qb_other, qb_mine = call(
        back_c_kernel,
        [SM] + [VM] * 4,
        [AN] * 2,
        [
            shape_of((2, 2, 4, 32, 3 * width // 2), bf),
            shape_of((2, 2, 4, 32, 3 * width // 2), bf),
        ],
        [pltpu.VMEM((2, 2, 8, 32, 3 * width // 2), bf), dma((32,))],
        flops=3 * 10**9,
        vmem=12, moved=6 * 10**6,
    )(coords, normed, after(dq_b, qa_came), dkv_b, sums)
    result = b16(residual + vec[7:8] + keep_a[1] + f32(came_a[1]) + f32(back_y))
    _qb_came, qb_1 = across_core(qb_other, qb_mine)
    qb_x = to_x(after(b16(qb_1(1)), qa_x))
    even = y == 0
    sum_own = p_own + jnp.where(even, f32(p_came[0]), 0.0)
    sum_4 = b16(f32(p_z[1]) + jnp.where(even, 0.0, f32(p_came[1])))
    hop = to_z(sum_4, 3)
    sum_2 = b16(f32(p_z[0]) + jnp.where(even, f32(p_came[1]), f32(p_came[0])) + f32(hop))
    back_2 = to_z(sum_2, 3)

    def qa_2(*index):
        return qa_1(0, *index) + f32(qa_x[index])

    def qb_2(*index):
        return qb_1(0, *index) + f32(qb_x[index])

    qa_y = to_y(after(b16(qa_2(1)), p_came))
    qb_y = to_y(after(b16(qb_2(1)), qa_y))

    def qa_3(*index):
        return qa_2(0, *index) + f32(qa_y[index])

    def qb_3(*index):
        return qb_2(0, *index) + f32(qb_y[index])

    qa_sum = along_z(qa_3)
    qb_sum = along_z(qb_3)

    def spread(total, *done):
        over = to_x(after(total, *done))
        return total, over, to_core(total), to_core(over)

    done_u = spread(u_sum)
    done_d = spread(d_sum, qa_x)
    done_a = spread(qa_sum)
    done_b = spread(qb_sum)
    grad_tokens = call(
        tokens_kernel, [VM] * 5, VM, shape_of((tok, width), fl), vmem=4, moved=3 * 10**6
    )(sum_own, back_2, grad_first, own_tokens, vec)
    grad_up, grad_down = call(
        finish_f_kernel,
        [SM] + [VM] * 8,
        [VM] * 2,
        [shape_of(up_weight.shape, fl), shape_of(down_weight.shape, fl)],
        [pltpu.VMEM((4, 96, width), bf)],
        vmem=8, moved=4 * 10**6,
    )(coords, *done_u, *done_d)
    grad_qkv, grad_out = call(
        finish_q_kernel,
        [SM] + [VM] * 8,
        [VM] * 2,
        [shape_of(query_key_value_weight.shape, fl), shape_of(output_weight.shape, fl)],
        vmem=8, moved=3 * 10**6,
    )(coords, *done_a, *done_b)
    sums = f32(qb_sum[24:32, :256])
    part = ln_gains.shape[1]
    return (
        result[None],
        grad_tokens[None],
        grad_qkv,
        grad_out,
        grad_up,
        grad_down,
        sums[0:2, :part],
        sums[2:4, :part],
        sums[4:8, :part],
        sums[0:4, 128 : 128 + part].reshape(4 * part),
    )


def solution(mesh):
    placed = (
        P("rep", "seq", None),
        P("rep", "seq"),
        P("seq", None),
        P("seq", None),
        P("seq", None),
        P("seq", None),
        P(None, "seq"),
        P(None, "seq"),
        P(None, "seq"),
        P("seq"),
        P("rep", "seq", None),
    )
    shape = dict(mesh.shape)
    small_slice = shape["rep"] == 4 and shape["seq"] == 8
    return jax.shard_map(
        on_device_fast if small_slice else on_device,
        mesh=mesh,
        in_specs=placed,
        out_specs=(
            P("rep", "seq", None),
            P("rep", "seq", None),
            P("seq", None),
            P("seq", None),
            P("seq", None),
            P("seq", None),
            P(None, "seq"),
            P(None, "seq"),
            P(None, "seq"),
            P("seq"),
        ),
        check_vma=False,
    )
```

```python
import math

import jax
import jax.numpy as jnp
from jax import lax
from jax.experimental import pallas as pl
from jax.experimental.pallas import tpu as pltpu
from jax.sharding import PartitionSpec as P

HEADS = 12
HD = 64


norm_eps = 1e-05
floor_score = -1e30


def layer_norm(values, gain, shift):
    center = values - jnp.mean(values, axis=-1, keepdims=True)
    spread = jnp.mean(center * center, axis=-1, keepdims=True)
    return center * lax.rsqrt(spread + norm_eps) * gain + shift


def head_split(matrix):
    return matrix.reshape(matrix.shape[0], HEADS, HD)


def masked_scores(queries, query_seg, query_pos, key_piece, seg_piece, offset):
    rows = key_piece.shape[0]
    scores = jnp.einsum(
        "qhd,khd->hqk", queries, head_split(key_piece), preferred_element_type=jnp.float32
    ) * HD ** (-0.5)
    key_pos = offset + jnp.arange(rows, dtype=jnp.int32)
    allowed = (query_seg[:, None] == seg_piece[None, :]) & (key_pos[None, :] <= query_pos[:, None])
    return (jnp.where(allowed[None], scores, floor_score), allowed)


def forward_block(running, pieces, offset, queries, query_seg, query_pos):
    top_run, total_run, accum = running
    key_piece, value_piece, seg_piece = pieces
    scores, allowed = masked_scores(queries, query_seg, query_pos, key_piece, seg_piece, offset)
    top_new = jnp.maximum(top_run, jnp.max(scores, axis=-1))
    probs = jnp.where(allowed[None], jnp.exp(scores - top_new[:, :, None]), 0.0)
    factor = jnp.exp(top_run - top_new)
    total_new = total_run * factor + jnp.sum(probs, axis=-1)
    update = jnp.einsum(
        "hqk,khd->qhd",
        probs.astype(jnp.bfloat16),
        head_split(value_piece),
        preferred_element_type=jnp.float32,
    )
    return (top_new, total_new, accum * factor.T[:, :, None] + update)


def in_blocks(block_fn, running, pieces):
    rows = pieces[0].shape[0]
    size = math.gcd(rows, 1024)
    stacked = tuple((member.reshape((rows // size, size) + member.shape[1:]) for member in pieces))
    offsets = jnp.arange(rows // size, dtype=jnp.int32) * size

    def scan_step(state_now, element):
        return (block_fn(state_now, element[0], element[1]), None)

    running, _unused = lax.scan(scan_step, running, (stacked, offsets))
    return running


def backward_block(
    number,
    state_now,
    whole,
    queries,
    query_seg,
    query_pos,
    grad_heads,
    log_total,
    delta,
    block_rows,
):
    grad_query, term = state_now
    offset = number * block_rows
    key_piece = lax.dynamic_slice_in_dim(whole[0], offset, block_rows, 0)
    value_piece = lax.dynamic_slice_in_dim(whole[1], offset, block_rows, 0)
    seg_piece = lax.dynamic_slice_in_dim(whole[2], offset, block_rows, 0)
    scores, allowed = masked_scores(queries, query_seg, query_pos, key_piece, seg_piece, offset)
    probs = jnp.where(allowed[None], jnp.exp(scores - log_total[:, :, None]), 0.0)
    grad_probs = jnp.einsum(
        "qhd,khd->hqk", grad_heads, head_split(value_piece), preferred_element_type=jnp.float32
    )
    grad_scores = (probs * (grad_probs - delta[:, :, None])).astype(jnp.bfloat16)
    grad_query = grad_query + jnp.einsum(
        "hqk,khd->qhd", grad_scores, head_split(key_piece), preferred_element_type=jnp.float32
    )
    grad_key = jnp.einsum(
        "hqk,qhd->khd", grad_scores, queries, preferred_element_type=jnp.float32
    ) * HD ** (-0.5)
    grad_value = jnp.einsum(
        "hqk,qhd->khd", probs.astype(jnp.bfloat16), grad_heads, preferred_element_type=jnp.float32
    )
    joined = jnp.concatenate(
        [grad_key.reshape(block_rows, -1), grad_value.reshape(block_rows, -1)], axis=1
    )
    term = lax.dynamic_update_slice_in_dim(term, joined, offset, 0)
    return (grad_query, term)


def on_device(
    tokens,
    segment_ids,
    query_key_value_weight,
    output_weight,
    up_weight,
    down_weight,
    ln_gains,
    ln_biases,
    biases,
    up_projection_bias,
    cotangent,
):
    gathered = (
        lax.all_gather(query_key_value_weight, "seq", axis=0, tiled=True),
        lax.all_gather(output_weight, "seq", axis=0, tiled=True),
        lax.all_gather(up_weight, "seq", axis=0, tiled=True),
        lax.all_gather(down_weight, "seq", axis=0, tiled=True),
        lax.all_gather(ln_gains, "seq", axis=1, tiled=True),
        lax.all_gather(ln_biases, "seq", axis=1, tiled=True),
        lax.all_gather(biases, "seq", axis=1, tiled=True),
        lax.all_gather(up_projection_bias, "seq", axis=0, tiled=True),
    )
    full_qkv, full_out, full_up, full_down, gains_all, shifts_all, biases_all, up_shift = gathered
    gains_f = gains_all.astype(jnp.float32)
    shifts_f = shifts_all.astype(jnp.float32)
    biases_f = biases_all.astype(jnp.float32)
    up_shift_f = up_shift.astype(jnp.float32)
    tokens_f = tokens[0].astype(jnp.float32)
    seg_local = segment_ids[0]
    tok_rows = tokens_f.shape[0]
    width = tokens_f.shape[1]
    seqlen = tok_rows * lax.axis_size("seq")
    query_pos = lax.axis_index("seq") * tok_rows + jnp.arange(tok_rows, dtype=jnp.int32)
    hidden_first = layer_norm(tokens_f, gains_f[0], shifts_f[0]).astype(jnp.bfloat16)
    query_key_value_bias = jnp.concatenate(
        [biases_f[0], jnp.zeros((width,), jnp.float32), biases_f[1]]
    )
    projected_rows = (
        jnp.dot(hidden_first, full_qkv, preferred_element_type=jnp.float32) + query_key_value_bias
    ).astype(jnp.bfloat16)
    queries = head_split(projected_rows[:, :width])
    key_rows = projected_rows[:, width : 2 * width]
    value_rows = projected_rows[:, 2 * width :]
    initial = (
        jnp.full((HEADS, tok_rows), floor_score, jnp.float32),
        jnp.zeros((HEADS, tok_rows), jnp.float32),
        jnp.zeros((tok_rows, HEADS, HD), jnp.float32),
    )

    def block_fn(running, pieces, offset):
        return forward_block(running, pieces, offset, queries, seg_local, query_pos)

    block_rows = math.gcd(seqlen, 1024)
    key_end = (lax.axis_index("seq") + 1) * tok_rows
    block_count = (key_end + block_rows - 1) // block_rows
    top_run, total_run, accum = in_blocks(
        block_fn,
        initial,
        (
            lax.all_gather(key_rows, "seq", axis=0, tiled=True),
            lax.all_gather(value_rows, "seq", axis=0, tiled=True),
            lax.all_gather(seg_local, "seq", axis=0, tiled=True),
        ),
    )
    log_total = top_run + jnp.log(total_run)
    attended_f = accum / total_run.T[:, :, None]
    attention_result = attended_f.reshape(tok_rows, width).astype(jnp.bfloat16)
    residual_first = (
        tokens_f
        + jnp.dot(attention_result, full_out, preferred_element_type=jnp.float32)
        + biases_f[2]
    )
    hidden_second = layer_norm(residual_first, gains_f[1], shifts_f[1]).astype(jnp.bfloat16)
    upward_rows = jnp.dot(hidden_second, full_up, preferred_element_type=jnp.float32) + up_shift_f
    activated_f, gelu_back = jax.vjp(jax.nn.gelu, upward_rows)
    activation_values = activated_f.astype(jnp.bfloat16)
    result = (
        residual_first
        + jnp.dot(activation_values, full_down, preferred_element_type=jnp.float32)
        + biases_f[3]
    )
    grad_y = cotangent[0]
    grad_y_f = grad_y.astype(jnp.float32)
    grad_down = jnp.einsum(
        "tf,td->fd", activation_values, grad_y, preferred_element_type=jnp.float32
    )
    grad_act = jnp.einsum("td,fd->tf", grad_y, full_down, preferred_element_type=jnp.float32)
    grad_up_pre = gelu_back(grad_act)[0].astype(jnp.bfloat16)
    grad_up = jnp.einsum(
        "td,tf->df", hidden_second, grad_up_pre, preferred_element_type=jnp.float32
    )
    grad_hidden_two = jnp.einsum(
        "tf,df->td", grad_up_pre, full_up, preferred_element_type=jnp.float32
    )
    _unused, norm_two_back = jax.vjp(layer_norm, residual_first, gains_f[1], shifts_f[1])
    grad_sum_part, grad_gain_two, grad_shift_two = norm_two_back(grad_hidden_two)
    grad_first = grad_y_f + grad_sum_part
    grad_first_bf = grad_first.astype(jnp.bfloat16)
    grad_out_w = jnp.einsum(
        "td,te->de", attention_result, grad_first_bf, preferred_element_type=jnp.float32
    )
    grad_attended = jnp.einsum(
        "te,de->td", grad_first_bf, full_out, preferred_element_type=jnp.float32
    ).astype(jnp.bfloat16)
    grad_heads = head_split(grad_attended)
    delta = jnp.einsum("qhd,qhd->hq", grad_heads.astype(jnp.float32), attended_f)
    whole = (
        lax.all_gather(key_rows, "seq", axis=0, tiled=True),
        lax.all_gather(value_rows, "seq", axis=0, tiled=True),
        lax.all_gather(seg_local, "seq", axis=0, tiled=True),
    )

    def backward_step(number, state_now):
        return backward_block(
            number,
            state_now,
            whole,
            queries,
            seg_local,
            query_pos,
            grad_heads,
            log_total,
            delta,
            block_rows,
        )

    start_state = (
        jnp.zeros((tok_rows, HEADS, HD), jnp.float32),
        jnp.zeros((seqlen, 2 * width), jnp.float32),
    )
    grad_query, term = lax.fori_loop(0, block_count, backward_step, start_state)
    grad_kv = lax.psum_scatter(term, "seq", scatter_dimension=0, tiled=True).astype(jnp.bfloat16)
    grad_q = (grad_query * HD ** (-0.5)).reshape(tok_rows, width).astype(jnp.bfloat16)
    grad_proj = jnp.concatenate([grad_q, grad_kv], axis=1)
    grad_qkv_w = jnp.einsum(
        "td,te->de", hidden_first, grad_proj, preferred_element_type=jnp.float32
    )
    grad_hidden_one = jnp.einsum(
        "te,de->td", grad_proj, full_qkv, preferred_element_type=jnp.float32
    )
    _unused_two, norm_one_back = jax.vjp(layer_norm, tokens_f, gains_f[0], shifts_f[0])
    grad_in_part, grad_gain_one, grad_shift_one = norm_one_back(grad_hidden_one)
    grad_tokens = grad_first + grad_in_part
    grad_proj_f = grad_proj.astype(jnp.float32)
    grad_bias_rows = jnp.stack(
        [
            jnp.sum(grad_proj_f[:, :width], axis=0),
            jnp.sum(grad_proj_f[:, 2 * width :], axis=0),
            jnp.sum(grad_first, axis=0),
            jnp.sum(grad_y_f, axis=0),
        ]
    )
    grad_up_shift = jnp.sum(grad_up_pre.astype(jnp.float32), axis=0)
    grad_gains = jnp.stack([grad_gain_one, grad_gain_two])
    grad_shifts = jnp.stack([grad_shift_one, grad_shift_two])
    shares = (
        lax.psum_scatter(grad_qkv_w, "seq", scatter_dimension=0, tiled=True),
        lax.psum_scatter(grad_out_w, "seq", scatter_dimension=0, tiled=True),
        lax.psum_scatter(grad_up, "seq", scatter_dimension=0, tiled=True),
        lax.psum_scatter(grad_down, "seq", scatter_dimension=0, tiled=True),
        lax.psum_scatter(grad_gains, "seq", scatter_dimension=1, tiled=True),
        lax.psum_scatter(grad_shifts, "seq", scatter_dimension=1, tiled=True),
        lax.psum_scatter(grad_bias_rows, "seq", scatter_dimension=1, tiled=True),
        lax.psum_scatter(grad_up_shift, "seq", scatter_dimension=0, tiled=True),
    )
    totals = (
        lax.psum(shares[0].astype(jnp.bfloat16), "rep").astype(jnp.float32),
        lax.psum(shares[1].astype(jnp.bfloat16), "rep").astype(jnp.float32),
        lax.psum(shares[2].astype(jnp.bfloat16), "rep").astype(jnp.float32),
        lax.psum(shares[3].astype(jnp.bfloat16), "rep").astype(jnp.float32),
        lax.psum(shares[4].astype(jnp.bfloat16), "rep").astype(jnp.float32),
        lax.psum(shares[5].astype(jnp.bfloat16), "rep").astype(jnp.float32),
        lax.psum(shares[6].astype(jnp.bfloat16), "rep").astype(jnp.float32),
        lax.psum(shares[7].astype(jnp.bfloat16), "rep").astype(jnp.float32),
    )
    return (
        result.astype(jnp.bfloat16)[None],
        grad_tokens[None],
        totals[0],
        totals[1],
        totals[2],
        totals[3],
        totals[4],
        totals[5],
        totals[6],
        totals[7],
    )


def f32(value):
    return value.astype(jnp.float32)


def b16(value):
    return value.astype(jnp.bfloat16)


def dot_nn(left, right):
    return jnp.dot(left, right, preferred_element_type=jnp.float32)


def dot_nt(left, right):
    return lax.dot_general(
        left, right, (((1,), (1,)), ((), ())), preferred_element_type=jnp.float32
    )


def dot_tn(left, right):
    return lax.dot_general(
        left, right, (((0,), (0,)), ((), ())), preferred_element_type=jnp.float32
    )


def norm_parts(values):
    center = values - jnp.mean(values, axis=-1, keepdims=True)
    rate = lax.rsqrt(jnp.mean(center * center, axis=-1, keepdims=True) + norm_eps)
    return center * rate, rate


def norm_back(grad, hat, rate, gain):
    scaled = grad * gain
    return rate * (
        scaled
        - jnp.mean(scaled, axis=-1, keepdims=True)
        - hat * jnp.mean(scaled * hat, axis=-1, keepdims=True)
    )


def place(coords):
    return coords[0], coords[1], coords[2], coords[3]


def piece_shard(number, y, z):
    if number < 3:
        return 2 * lax.rem(z + 3 - number, 4) + y
    return 2 * lax.rem(z + 7 - number, 4) + 1 - y


def pack96(parts):
    lane = lax.broadcasted_iota(jnp.int32, parts[0].shape, 1)
    one, two, three = (pltpu.roll(parts[k], 128 - 32 * k, 1) for k in (1, 2, 3))
    return jnp.concatenate(
        [
            jnp.where(lane < 96, parts[0], one),
            jnp.where(lane < 64, one, two),
            jnp.where(lane < 32, two, three),
        ],
        axis=1,
    )


def unpack96(block):
    tiles = [block[:, 128 * k : 128 * k + 128] for k in range(3)]
    lane = lax.broadcasted_iota(jnp.int32, tiles[0].shape, 1)
    return [
        tiles[0],
        jnp.where(lane < 32, pltpu.roll(tiles[0], 32, 1), pltpu.roll(tiles[1], 32, 1)),
        jnp.where(lane < 64, pltpu.roll(tiles[1], 64, 1), pltpu.roll(tiles[2], 64, 1)),
        pltpu.roll(tiles[2], 96, 1),
    ]


def choose(parts, index):
    out = parts[0]
    for number in range(1, len(parts)):
        out = jnp.where(index == number, parts[number], out)
    return out


class Copies:
    def __init__(self, sems, first=0):
        self.sems = sems
        self.first = first
        self.held = []

    def add(self, source, target):
        copy = pltpu.make_async_copy(source, target, self.sems.at[self.first + len(self.held)])
        copy.start()
        self.held.append(copy)

    def wait(self):
        for copy in self.held:
            copy.wait()
        self.held = []


def corners(x, c):
    return ((x, c), (1 - x, c), (x, 1 - c), (1 - x, 1 - c))


def fetch_qkv(copies, coords, own, groups, full, full_out=None, own_out=None):
    x, c, y, z = place(coords)
    rows = own.shape[0]
    half, width = rows // 2, own.shape[1] // 3
    row = pl.multiple_of((2 * z + y) * rows, 16)
    copies.add(own, full.at[pl.ds(row, rows), :])
    if full_out is not None:
        copies.add(own_out, full_out.at[pl.ds(row, rows), :])
    wide, side = 3 * width // 2, width // 2
    for number in range(7):
        for (xx, cc), group in zip(corners(x, c), groups, strict=True):
            piece = piece_of(group, number)
            at = pl.ds(pl.multiple_of(piece_shard(number, y, z) * rows + half * cc, 16), half)
            copies.add(
                piece.at[pl.ds(0, half), pl.ds(0, wide)],
                full.at[at, pl.ds(pl.multiple_of(wide * xx, 128), wide)],
            )
            if full_out is not None:
                copies.add(
                    piece.at[pl.ds(0, half), pl.ds(wide, side)],
                    full_out.at[at, pl.ds(pl.multiple_of(side * xx, 128), side)],
                )


def piece_of(group, number):
    behind, across, behind_across = group
    if number < 3:
        return behind.at[number]
    return across.at[0] if number == 3 else behind_across.at[number - 4]


def mask_bias(start, me, tok, target):
    keys, lanes = target.shape
    key_pos = (me - 4) * tok + lax.broadcasted_iota(jnp.int32, (keys, lanes), 0)
    lane = lax.broadcasted_iota(jnp.int32, (keys, lanes), 1)
    query_pos = me * tok + jnp.where(lane >= tok, lane - tok, lane)
    target[...] = jnp.where((key_pos >= start) & (key_pos <= query_pos), 0.0, floor_score)


def pair_stack(rows):
    lane = lax.broadcasted_iota(jnp.int32, rows.shape, 1)
    zero = jnp.zeros_like(rows)
    return jnp.concatenate([jnp.where(lane < HD, rows, zero), jnp.where(lane < HD, zero, rows)], axis=0)


def pair_join(transposed):
    both = transposed.T
    tok = both.shape[0] // 2
    lane = lax.broadcasted_iota(jnp.int32, (tok, 2 * HD), 1)
    return jnp.where(lane < HD, both[:tok], both[tok:])


def prep_kernel(
    coords, tokens, segs, qkv, out, up, down, gains, shifts, biases, up_bias,
    t_out, q_out, f_out,
    scratch, wide, held_g, held_s, held_b, ids, line, sems,
):
    x, c, _y, _z = place(coords)
    tok, width = tokens.shape[1:]
    rows = qkv.shape[0]
    half, side = rows // 2, width // 2
    p = 2 * x + c
    at = pl.ds(pl.multiple_of(half * c, 16), half)
    copies, others = Copies(sems), Copies(sems, 5)
    for source, target in ((gains, held_g), (shifts, held_s), (biases, held_b)):
        copies.add(source, target)
    copies.add(segs, ids)
    copies.add(up_bias, line)
    others.add(up, wide)
    wide_cols = 3 * side
    others.add(
        qkv.at[at, pl.ds(pl.multiple_of(wide_cols * x, 128), wide_cols)],
        q_out.at[pl.ds(0, half), pl.ds(0, wide_cols)],
    )
    others.add(
        out.at[at, pl.ds(pl.multiple_of(side * x, 128), side)],
        q_out.at[pl.ds(0, half), pl.ds(wide_cols, side)],
    )
    others.add(tokens.at[0], t_out.at[pl.ds(0, tok), :])
    others.add(down.at[pl.ds(pl.multiple_of(rows * p, 16), rows), :], f_out.at[pl.ds(rows, rows), :])
    copies.wait()
    scratch[...] = jnp.zeros_like(scratch)
    for first, held in ((0, held_g), (2, held_s), (4, held_b)):
        scratch[pl.ds(first, held.shape[0]), pl.ds(0, rows)] = f32(held[...])
    scratch[pl.ds(0, 1), pl.ds(128, 384)] = f32(line[...])
    q_out[pl.ds(half, 8), pl.ds(0, width)] = b16(scratch[...])
    q_out[pl.ds(half, 8), pl.ds(width, width)] = jnp.zeros((8, width), jnp.bfloat16)
    scratch[...] = jnp.zeros_like(scratch)
    scratch[pl.ds(0, 1), pl.ds(0, tok)] = f32(ids[...])
    t_out[pl.ds(tok, 8), :] = b16(scratch[...])
    others.wait()
    for group in range(2):
        parts = []
        for shard in range(4 * group, 4 * group + 4):
            parts.append(choose(unpack96(f32(wide[:, pl.ds(384 * shard, 384)])), p))
        f_out[pl.ds(0, rows), pl.ds(384 * group, 384)] = b16(pack96(parts))


def front_kernel(
    coords, seg, xo, x1, x2, x3, x4, first, own, own_o,
    g0, g1, g2, g3, g4, g5, g6, g7, g8, g9, g10, g11,
    q_out, kv_out, h_out, a_out, lse_out, start_out, vec_out, upb_out, wo_out, r_out, h2_out,
    full, small, bias, sems, vsems,
):
    x, c, y, z = place(coords)
    me = 2 * z + y
    p = 2 * x + c
    tok, width = q_out.shape
    copies, vcopies = Copies(sems), Copies(vsems)
    vcopies.add(first.at[pl.ds(48, 8), pl.ds(0, 512)], small.at[me])
    for number in range(7):
        source = piece_of((g0, g1, g2), number)
        vcopies.add(source.at[pl.ds(48, 8), pl.ds(0, 512)], small.at[piece_shard(number, y, z)])
    groups = ((g0, g1, g2), (g3, g4, g5), (g6, g7, g8), (g9, g10, g11))
    fetch_qkv(copies, coords, own, groups, full, wo_out, own_o)
    blocks = (xo, x1, x2, x3, x4)
    lane1 = lax.broadcasted_iota(jnp.int32, (1, tok), 1)
    start = jnp.full(seg.shape, 1 << 30, jnp.int32)
    for number in range(4):
        first_pos = jnp.full((1, 1), 1 << 30, jnp.int32)
        for back in range(5):
            ids = f32(blocks[back][pl.ds(tok, 8), pl.ds(0, tok)])[:1]
            pos = (me - back) * tok + lane1
            hit = (ids == float(number)) & (pos >= 0)
            first_pos = jnp.minimum(
                first_pos, jnp.min(jnp.where(hit, pos, 1 << 30), axis=1, keepdims=True)
            )
        start = jnp.where(seg[...] == number, first_pos, start)
    start_out[...] = start
    mask_bias(start, me, tok, bias)
    vcopies.wait()
    for group in range(2):
        held = [f32(small[4 * group + k]) for k in range(4)]
        vec_out[:, pl.ds(384 * group, 384)] = pack96([block[:, :128] for block in held])
        upb_out[:, pl.ds(384 * group, 384)] = pack96(
            [choose(unpack96(block[:, 128:512]), p) for block in held]
        )
    vec = vec_out[...]
    for back in range(5):
        hat, _rate = norm_parts(f32(blocks[back][pl.ds(0, tok), :]))
        h_out[pl.ds((4 - back) * tok, tok), :] = b16(hat * vec[0:1] + vec[2:3])
    copies.wait()
    q_out[...] = b16(dot_nn(h_out[pl.ds(4 * tok, tok), :], full[:, pl.ds(0, width)]) + vec[4:5])

    def project(number, carry):
        col = pl.multiple_of(number * 256, 256)
        shift = jnp.where(number >= width // 256, 1.0, 0.0)
        bias_at = lax.rem(number, width // 256)
        piece = vec_out[pl.ds(5, 1), pl.ds(pl.multiple_of(bias_at * 256, 256), 256)]
        kv_out[:, pl.ds(col, 256)] = b16(
            dot_nn(h_out[...], full[:, pl.ds(pl.multiple_of(width + col, 256), 256)]) + piece * shift
        )
        return carry

    lax.fori_loop(0, 2 * width // 256, project, 0)

    def pair(number, carry):
        col = pl.multiple_of(number * 128, 128)
        queries = pair_stack(q_out[:, pl.ds(col, 128)] * jnp.bfloat16(0.125))
        scores = dot_nt(kv_out[:, pl.ds(col, 128)], queries) + bias[...]
        top = jnp.max(scores, axis=0, keepdims=True)
        probs = jnp.exp(scores - top)
        total = jnp.sum(probs, axis=0, keepdims=True)
        mixed = dot_tn(kv_out[:, pl.ds(pl.multiple_of(width + col, 128), 128)], b16(probs))
        a_out[:, pl.ds(col, 128)] = b16(pair_join(mixed / total))
        lse_out[number] = top + jnp.log(total)
        return carry

    lax.fori_loop(0, width // 128, pair, 0)
    residual = f32(xo[pl.ds(0, tok), :]) + dot_nn(a_out[...], wo_out[...]) + vec[6:7]
    r_out[...] = residual
    hat, _rate = norm_parts(residual)
    h2_out[...] = b16(hat * vec[1:2] + vec[3:4])


def feed_tokens(h2, dy, w_up, w_down, upb, act_out, du_out, y_acc, dh_acc):
    root = math.sqrt(2.0 / math.pi)
    chunk = 256

    def feed(number, carry):
        col = pl.multiple_of(number * chunk, chunk)
        pre = dot_nn(h2[...], w_up[:, pl.ds(col, chunk)]) + upb[pl.ds(0, 1), pl.ds(col, chunk)]
        square = pre * pre
        bend = jnp.tanh(root * pre * (1.0 + 0.044715 * square))
        act = b16(0.5 * pre * (1.0 + bend))
        slope = 0.5 * (1.0 + bend) + 0.5 * pre * (1.0 - bend * bend) * (
            root * (1.0 + 3.0 * 0.044715 * square)
        )
        low = b16(dot_nt(dy[...], w_down[pl.ds(col, chunk), :]) * slope)
        act_out[:, pl.ds(col, chunk)] = act
        du_out[:, pl.ds(col, chunk)] = low
        return carry

    lax.fori_loop(0, w_up.shape[1] // chunk, feed, 0)
    dh_acc[...] = dot_nt(du_out[...], w_up[...])
    y_acc[...] = dot_nn(act_out[...], w_down[...])


def near_kernel(
    coords, h_own, h_c, dy_own, dy_c, upb, own, z1, z2, z3, y0, y13, y2,
    h2, dy, act_out, du_out, keep_out, send_out, wu_out, wd_out,
    y_acc, dh_acc, sems,
):
    _x, _c, y, z = place(coords)
    tok, width = h_own.shape
    rows = width // 8
    copies = Copies(sems)
    across = (y0, y13.at[pl.ds(0, 2 * rows), :], y2, y13.at[pl.ds(2 * rows, 2 * rows), :])
    shards = [(own, 2 * z + y)] + [
        (ref, piece_shard(number, y, z)) for number, ref in enumerate((z1, z2, z3) + across)
    ]
    for ref, shard in shards:
        at = pl.ds(pl.multiple_of(shard * rows, 16), rows)
        copies.add(ref.at[pl.ds(0, rows), :], wu_out.at[at, :])
        copies.add(ref.at[pl.ds(rows, rows), :], wd_out.at[at, :])
    h2[pl.ds(0, tok), :] = h_own[...]
    h2[pl.ds(tok, tok), :] = h_c[...]
    dy[pl.ds(0, tok), :] = dy_own[...]
    dy[pl.ds(tok, tok), :] = dy_c[...]
    copies.wait()
    feed_tokens(h2, dy, wu_out, wd_out, upb, act_out, du_out, y_acc, dh_acc)
    keep_out[0] = dh_acc[pl.ds(0, tok), :]
    keep_out[1] = y_acc[pl.ds(0, tok), :]
    send_out[0] = b16(dh_acc[pl.ds(tok, tok), :])
    send_out[1] = b16(y_acc[pl.ds(tok, tok), :])


def far_kernel(
    h_x, h_xc, dy_x, dy_xc, upb, w_up, w_down, h_near, dy_near, act_near, du_near,
    hs, dys, acts, dus, keep_out, send_out,
    y_acc, dh_acc, sems,
):
    tok = h_x.shape[0]
    copies = Copies(sems)
    for source, target in ((h_near, hs), (dy_near, dys), (act_near, acts), (du_near, dus)):
        copies.add(source, target.at[pl.ds(0, 2 * tok), :])
    later = pl.ds(2 * tok, 2 * tok)
    hs[pl.ds(2 * tok, tok), :] = h_x[...]
    hs[pl.ds(3 * tok, tok), :] = h_xc[...]
    dys[pl.ds(2 * tok, tok), :] = dy_x[...]
    dys[pl.ds(3 * tok, tok), :] = dy_xc[...]
    feed_tokens(
        hs.at[later, :], dys.at[later, :], w_up, w_down, upb, acts.at[later, :], dus.at[later, :], y_acc, dh_acc
    )
    keep_out[0] = dh_acc[pl.ds(0, tok), :]
    keep_out[1] = y_acc[pl.ds(0, tok), :]
    send_out[0] = b16(dh_acc[pl.ds(tok, tok), :])
    send_out[1] = b16(y_acc[pl.ds(tok, tok), :])
    copies.wait()


def weights_kernel(coords, hs, dys, acts, dus, u_out, d_out, upb_out, stage, sems):
    _x, _c, y, z = place(coords)
    width = hs.shape[1]
    rows = width // 8
    upb_out[...] = jnp.sum(f32(dus[...]), axis=0, keepdims=True)

    def weight(number, carry):
        col = pl.multiple_of(number * 256, 256)
        stage[0, pl.ds(col, 256), :] = b16(dot_tn(hs[:, pl.ds(col, 256)], dus[...]))
        stage[1, pl.ds(col, 256), :] = b16(dot_tn(acts[:, pl.ds(col, 256)], dys[...]))
        return carry

    lax.fori_loop(0, width // 256, weight, 0)
    outs = Copies(sems)
    for shard in range(8):
        zz = lax.rem(shard // 2 + 4 - z, 4)
        yy = jnp.where(y == shard % 2, 0, 1)
        outs.add(stage.at[0, pl.ds(shard * rows, rows), :], u_out.at[yy, zz])
        outs.add(stage.at[1, pl.ds(shard * rows, rows), :], d_out.at[yy, zz])
    outs.wait()


def post_kernel(residual, own, near, across, dy_in, vec_in, w_out, a_in, dr_out, da_out, dw_out, vec_out):
    vec = vec_in[...]
    grad_hidden = own[0] + f32(near[0]) + f32(across[...])
    hat, rate = norm_parts(residual[...])
    dy = f32(dy_in[...])
    grad_first = dy + norm_back(grad_hidden, hat, rate, vec[1:2])
    dr_out[...] = grad_first
    low = b16(grad_first)
    da_out[...] = b16(dot_nt(low, w_out[...]))
    dw_out[...] = b16(dot_tn(a_in[...], low))
    zero = jnp.zeros((1, dy.shape[1]), jnp.float32)
    vec_out[...] = jnp.concatenate(
        [
            zero,
            jnp.sum(grad_hidden * hat, axis=0, keepdims=True),
            zero,
            jnp.sum(grad_hidden, axis=0, keepdims=True),
            zero,
            zero,
            jnp.sum(grad_first, axis=0, keepdims=True),
            jnp.sum(dy, axis=0, keepdims=True),
        ],
        axis=0,
    )


def back_pairs(first, q_in, kv_in, lse_in, da_in, bias, dq, dkv):
    width = q_in.shape[1]

    def pair(number, carry):
        col = pl.multiple_of((first + number) * 128, 128)
        vcol = pl.multiple_of(width + col, 128)
        to = pl.multiple_of(number * 128, 128)
        queries = pair_stack(q_in[:, pl.ds(col, 128)] * jnp.bfloat16(0.125))
        grads = pair_stack(da_in[:, pl.ds(col, 128)])
        keys = kv_in[:, pl.ds(col, 128)]
        probs = jnp.exp(dot_nt(keys, queries) + bias[...] - lse_in[first + number])
        dkv[:, pl.ds(pl.multiple_of(width // 2 + to, 128), 128)] = b16(dot_nn(b16(probs), grads))
        term = probs * dot_nt(kv_in[:, pl.ds(vcol, 128)], grads)
        low = b16(term - probs * jnp.sum(term, axis=0, keepdims=True))
        dkv[:, pl.ds(to, 128)] = b16(dot_nn(low, queries))
        dq[:, pl.ds(to, 128)] = b16(pair_join(dot_tn(keys, low)) * 0.125)
        return carry

    lax.fori_loop(0, 3, pair, 0)


def qkv_weight(h_in, dq, dkv, stage):
    tok, part = dq.shape
    keys = h_in.shape[0]

    def weight(number, carry):
        col = pl.multiple_of(number * 384, 384)
        key = dot_tn(h_in[:, pl.ds(col, 384)], dkv[...])
        query = dot_tn(h_in[pl.ds(keys - tok, tok), pl.ds(col, 384)], dq[...])
        for shard in range(4):
            for cc in range(2):
                for xx in range(2):
                    row = 96 * shard + 48 * cc + 24 * xx
                    stage[cc, xx, 4 * number + shard, pl.ds(0, 24), pl.ds(0, part)] = b16(query[row : row + 24])
                    stage[cc, xx, 4 * number + shard, pl.ds(0, 24), pl.ds(part, 2 * part)] = b16(key[row : row + 24])
        return carry

    lax.fori_loop(0, 2, weight, 0)


def back_a_kernel(
    coords, start_in, q_in, kv_in, h_in, lse_in, da_in, dw_in,
    other, mine, dq_out, dkv_out,
    bias, stage, sems,
):
    x, c, y, z = place(coords)
    tok, width = q_in.shape
    mask_bias(start_in[...], 2 * z + y, tok, bias)
    for shard in range(8):
        for cc in range(2):
            block = f32(dw_in[pl.ds(96 * shard + 48 * cc, 48), :])
            for xx in range(2):
                stage[cc, xx, shard, :, pl.ds(3 * width // 2, width)] = b16(block[24 * xx : 24 * xx + 24])
    back_pairs(0, q_in, kv_in, lse_in, da_in, bias, dq_out, dkv_out)
    qkv_weight(h_in, dq_out, dkv_out, stage)
    outs = Copies(sems)
    for shard in range(8):
        zz = lax.rem(shard // 2 + 4 - z, 4)
        yy = jnp.where(y == shard % 2, 0, 1)
        for xx in range(2):
            far = jnp.where(x == xx, 0, 1)
            outs.add(stage.at[1 - c, xx, shard], other.at[far, yy, zz])
            outs.add(stage.at[c, xx, shard], mine.at[far, yy, zz])
    outs.wait()


def back_b_kernel(
    coords, start_in, q_in, kv_in, lse_in, da_in, vec_in, upb_in, dq_a, dkv_a, xo, x1, x2, x3, x4,
    own, g0, g1, g2, g3, g4, g5, g6, g7, g8, g9, g10, g11,
    dq_out, dkv_out, p_own, p_y, p_z, sums_out,
    full, bias, sems,
):
    x, c, y, z = place(coords)
    p = 2 * x + c
    tok, width = q_in.shape
    side = width // 2
    copies = Copies(sems)
    groups = ((g0, g1, g2), (g3, g4, g5), (g6, g7, g8), (g9, g10, g11))
    fetch_qkv(copies, coords, own, groups, full)
    mask_bias(start_in[...], 2 * z + y, tok, bias)
    back_pairs(3, q_in, kv_in, lse_in, da_in, bias, dq_out, dkv_out)
    copies.wait()
    gain_sum = jnp.zeros((1, width), jnp.float32)
    shift_sum = jnp.zeros((1, width), jnp.float32)
    for back, block in enumerate((xo, x1, x2, x3, x4)):
        rows = pl.ds((4 - back) * tok, tok)
        grad = jnp.zeros((tok, width), jnp.float32)
        for number, (dq, dkv) in enumerate(((dq_a, dkv_a), (dq_out, dkv_out))):
            at = number * side
            grad = grad + dot_nt(dkv[rows, pl.ds(0, side)], full[:, pl.ds(width + at, side)])
            grad = grad + dot_nt(dkv[rows, pl.ds(side, side)], full[:, pl.ds(2 * width + at, side)])
            if back == 0:
                grad = grad + dot_nt(dq[...], full[:, pl.ds(at, side)])
        if back == 0:
            p_own[...] = grad
        elif back in (1, 3):
            p_y[back // 2] = b16(grad)
        else:
            p_z[back // 2 - 1] = b16(grad)
        hat, _rate = norm_parts(f32(block[pl.ds(0, tok), :]))
        gain_sum = gain_sum + jnp.sum(grad * hat, axis=0, keepdims=True)
        shift_sum = shift_sum + jnp.sum(grad, axis=0, keepdims=True)
    zero = jnp.zeros((1, width), jnp.float32)
    bias_q = jnp.concatenate([jnp.sum(f32(d[...]), axis=0, keepdims=True) for d in (dq_a, dq_out)], axis=1)
    bias_v = jnp.concatenate(
        [jnp.sum(f32(d[:, pl.ds(side, side)]), axis=0, keepdims=True) for d in (dkv_a, dkv_out)], axis=1
    )
    vec = vec_in[...] + jnp.concatenate(
        [gain_sum, zero, shift_sum, zero, bias_q, bias_v, zero, zero], axis=0
    )
    lane = lax.broadcasted_iota(jnp.int32, (8, 128), 1)
    line = lax.broadcasted_iota(jnp.int32, (8, 128), 0)
    for group in range(2):
        cols = pl.ds(384 * group, 384)
        vec_parts = unpack96(vec[:, 384 * group : 384 * group + 384])
        upb_parts = unpack96(jnp.broadcast_to(upb_in[:, cols], (8, 384)))
        for k in range(4):
            sums_out[4 * group + k] = jnp.concatenate(
                [
                    jnp.where(lane < 96, vec_parts[k], 0.0),
                    jnp.where((lane < 96) & (line == p), upb_parts[k], 0.0),
                ],
                axis=1,
            )


def back_c_kernel(coords, h_in, dq, dkv, sums_in, other, mine, stage, sems):
    x, c, y, z = place(coords)
    qkv_weight(h_in, dq, dkv, stage)
    for shard in range(8):
        row = b16(
            jnp.concatenate([sums_in[shard], jnp.zeros((8, stage.shape[4] - 256), jnp.float32)], axis=1)
        )
        for cc in range(2):
            for xx in range(2):
                stage[cc, xx, shard, pl.ds(24, 8), :] = row
    outs = Copies(sems)
    for shard in range(8):
        zz = lax.rem(shard // 2 + 4 - z, 4)
        yy = jnp.where(y == shard % 2, 0, 1)
        for xx in range(2):
            far = jnp.where(x == xx, 0, 1)
            outs.add(stage.at[1 - c, xx, shard], other.at[far, yy, zz])
            outs.add(stage.at[c, xx, shard], mine.at[far, yy, zz])
    outs.wait()


def tokens_kernel(own, near, dr, xo, vec_in, grad_out):
    tok = own.shape[0]
    hat, rate = norm_parts(f32(xo[pl.ds(0, tok), :]))
    grad = own[...] + f32(near[...])
    grad_out[...] = dr[...] + norm_back(grad, hat, rate, vec_in[0:1, :])


def finish_f_kernel(coords, f0, fx, fc, fcx, up, down, held):
    x, c, _y, _z = place(coords)
    rows = f0.shape[0] // 2
    for (xx, cc), f in zip(corners(x, c), (f0, fx, fc, fcx), strict=True):
        p = 2 * xx + cc
        held[p] = f[pl.ds(0, rows), :]
        down[pl.ds(pl.multiple_of(rows * p, 16), rows), :] = f32(f[pl.ds(rows, rows), :])
    for group in range(2):
        parts = [unpack96(f32(held[k, :, pl.ds(384 * group, 384)])) for k in range(4)]
        for shard in range(4):
            up[:, pl.ds(384 * (4 * group + shard), 384)] = pack96([part[shard] for part in parts])


def finish_q_kernel(coords, a0, ax, ac, acx, b0, bx, bc, bcx, qkv, out):
    x, c, _y, _z = place(coords)
    side = out.shape[1] // 2
    for (xx, cc), a, b in zip(corners(x, c), (a0, ax, ac, acx), (b0, bx, bc, bcx), strict=True):
        rows = pl.ds(pl.multiple_of(48 * cc + 24 * xx, 8), 24)
        first, second = f32(a[...]), f32(b[...])[:24]
        for number in range(3):
            qkv[rows, pl.ds(2 * side * number, side)] = first[:, side * number : side * (number + 1)]
            qkv[rows, pl.ds(2 * side * number + side, side)] = second[:, side * number : side * (number + 1)]
        out[rows, :] = first[:, 3 * side :]


HB = pl.BlockSpec(memory_space=pltpu.HBM)
VM = pl.BlockSpec(memory_space=pltpu.VMEM)
SM = pl.BlockSpec(memory_space=pltpu.SMEM)
AN = pl.BlockSpec(memory_space=pl.ANY)


def shape_of(shape, dtype):
    return jax.ShapeDtypeStruct(shape, dtype)


def call(kernel, ins, outs, out_shape, scratch=(), vmem=40, flops=0, moved=0):
    return pl.pallas_call(
        kernel,
        in_specs=ins,
        out_specs=outs,
        out_shape=out_shape,
        scratch_shapes=list(scratch),
        compiler_params=pltpu.CompilerParams(vmem_limit_bytes=vmem << 20),
        cost_estimate=pl.CostEstimate(flops=flops, bytes_accessed=moved, transcendentals=0),
    )


def fence(*values):
    return lax.optimization_barrier(values)


def swap_rep(value, bit):
    return lax.ppermute(value, "rep", [(k, k ^ bit) for k in range(4)])


def to_core(value):
    return swap_rep(value, 1)


def to_x(value):
    return swap_rep(value, 2)


def to_y(value):
    return lax.ppermute(value, "seq", [(k, k ^ 1) for k in range(8)])


def to_z(value, steps):
    return lax.ppermute(value, "seq", [(k, (k + 2 * steps) % 8) for k in range(8)])


def join(*parts):
    return jnp.concatenate(parts, axis=0)


def on_device_fast(
    tokens,
    segment_ids,
    query_key_value_weight,
    output_weight,
    up_weight,
    down_weight,
    ln_gains,
    ln_biases,
    biases,
    up_projection_bias,
    cotangent,
):
    rep, seq = lax.axis_index("rep"), lax.axis_index("seq")
    x, c, z, y = rep // 2, rep % 2, seq // 2, seq % 2
    coords = jnp.stack([x, c, y, z]).astype(jnp.int32)
    tok, width = tokens.shape[1:]
    hidden = up_weight.shape[1]
    keys = 5 * tok
    bf, fl = jnp.bfloat16, jnp.float32
    dma = pltpu.SemaphoreType.DMA
    grad_y = cotangent[0]
    own_tokens, piece_q, piece_f = call(
        prep_kernel,
        [SM] + [HB] * 10,
        [VM] * 3,
        [
            shape_of((tok + 8, width), bf),
            shape_of((56, 2 * width), bf),
            shape_of((192, width), bf),
        ],
        [
            pltpu.VMEM((8, width), fl),
            pltpu.VMEM((96, hidden), bf),
            pltpu.VMEM((2, 96), bf),
            pltpu.VMEM((2, 96), bf),
            pltpu.VMEM((4, 96), bf),
            pltpu.VMEM((1, tok), jnp.int32),
            pltpu.VMEM((1, 384), bf),
            dma((10,)),
        ],
        vmem=60, moved=4 * 10**6,
    )(
        coords, tokens, segment_ids, query_key_value_weight, output_weight, up_weight, down_weight,
        ln_gains, ln_biases, biases, up_projection_bias[None],
    )

    q1, q3, q_y0, dy_x = fence(to_z(piece_q, 1), to_z(piece_q, 3), to_y(piece_q), to_x(grad_y))
    own_tokens, piece_f, q1, q_y0 = fence(own_tokens, piece_f, q1, q_y0, q3, dy_x)[:4]
    q2, x2, q_xy0, f_y0 = fence(to_z(q1, 1), to_z(own_tokens, 1), to_x(q_y0), to_y(piece_f))
    q_z = join(q1, q2, q3)
    q_z, x2 = fence(q_z, x2, q_xy0, f_y0)[:2]
    q_y, q_xz, x4 = fence(to_y(q_z), to_x(q_z), to_z(x2, 1))
    near = jnp.where(y == 0, own_tokens, x2)
    far = jnp.where(y == 0, x2, x4)
    near_far, q_y, piece_f = fence(jnp.stack([near, far]), q_y, piece_f, q_xz)[:3]
    crossed, q_xy, f1, f3 = fence(to_y(near_far), to_x(q_y), to_z(piece_f, 1), to_z(piece_f, 3))
    x1, x3 = crossed[0], crossed[1]
    q_z, q_y0, q_y, q_xz, q_xy0, q_xy = fence(q_z, q_y0, q_y, q_xz, q_xy0, q_xy, f1, f3, crossed)[:6]
    q_cz, q_cy0, q_cy, q_cxz, q_cxy0, q_cxy = fence(
        *(to_core(v) for v in (q_z, q_y0, q_y, q_xz, q_xy0, q_xy))
    )
    f_13, f_1, q_cz = fence(join(f1, f3), f1, q_cz, q_cy0, q_cy, q_cxz, q_cxy0, q_cxy)[:3]
    f_y13, f2 = to_y(f_13), to_z(f_1, 1)
    dy_c, dy_xc = to_core(grad_y), to_core(dy_x)

    def pieces(value):
        return value.reshape(value.shape[0] // 56, 56, value.shape[1])

    got_q = [
        pieces(v)
        for v in (q_z, q_y0, q_y, q_xz, q_xy0, q_xy, q_cz, q_cy0, q_cy, q_cxz, q_cxy0, q_cxy)
    ]
    seg = jnp.concatenate([segment_ids, segment_ids], axis=1)
    front = call(
        front_kernel,
        [SM] + [VM] * 6 + [AN] * 15,
        [VM] * 11,
        [
            shape_of((tok, width), bf),
            shape_of((keys, 2 * width), bf),
            shape_of((keys, width), bf),
            shape_of((tok, width), bf),
            shape_of((width // 128, 1, 2 * tok), fl),
            shape_of((1, 2 * tok), jnp.int32),
            shape_of((8, width), fl),
            shape_of((8, width), fl),
            shape_of((width, width), bf),
            shape_of((tok, width), fl),
            shape_of((tok, width), bf),
        ],
        [
            pltpu.VMEM((width, 3 * width), bf),
            pltpu.VMEM((8, 8, 512), bf),
            pltpu.VMEM((keys, 2 * tok), fl),
            dma((2 + 56,)),
            dma((8,)),
        ],
        flops=7 * 10**9,
        vmem=16, moved=12 * 10**6,
    )(
        coords, seg, own_tokens, x1, x2, x3, x4, piece_q, query_key_value_weight, output_weight, *got_q,
    )
    *front, f_y13, f2, dy_c, dy_xc = fence(*front, f_y13, f2, dy_c, dy_xc)
    queries, kv, normed, attended, lse, start, vec, upb, w_out, residual, hidden_2 = front
    h_x, h_c, f_y2 = fence(to_x(hidden_2), to_core(hidden_2), to_y(f2))
    act = shape_of((2 * tok, width), bf)
    acts = shape_of((4 * tok, width), bf)
    feed_shapes = [shape_of((2, tok, width), fl), shape_of((2, tok, width), bf)]
    feed_scratch = [pltpu.VMEM((2 * tok, width), fl), pltpu.VMEM((2 * tok, width), fl)]
    *near_acts, keep_a, send_a, w_up, w_down = call(
        near_kernel,
        [SM] + [VM] * 5 + [AN] * 7,
        [VM] * 8,
        [act] * 4 + feed_shapes + [shape_of((width, width), bf)] * 2,
        feed_scratch + [dma((16,))],
        flops=3 * 10**9,
        vmem=8, moved=6 * 10**6,
    )(coords, hidden_2, h_c, grad_y, dy_c, upb, piece_f, f1, f2, f3, f_y0, f_y13, f_y2)
    h_xc = to_core(h_x)
    keep_a, send_a, h_xc, w_up = fence(keep_a, send_a, h_xc, w_up)
    came_a = to_core(send_a)
    *all_acts, keep_b, send_b = call(
        far_kernel,
        [VM] * 7 + [AN] * 4,
        [VM] * 6,
        [acts] * 4 + feed_shapes,
        feed_scratch + [dma((4,))],
        flops=3 * 10**9,
        vmem=8, moved=6 * 10**6,
    )(h_x, h_xc, dy_x, dy_xc, upb, w_up, w_down, *near_acts)
    keep_b, send_b, came_a = fence(keep_b, send_b, came_a)
    keep_b, came_b, *all_acts = fence(keep_b, to_core(send_b), *all_acts)
    back_x = to_x(b16(keep_b[0] + f32(came_b[0])))
    u_terms, d_terms, upb_g = call(
        weights_kernel,
        [SM] + [VM] * 4,
        [AN, AN, VM],
        [shape_of((2, 4, 96, width), bf), shape_of((2, 4, 96, width), bf), shape_of((1, width), fl)],
        [pltpu.VMEM((2, width, width), bf), dma((16,))],
        flops=3 * 10**9,
        vmem=12, moved=6 * 10**6,
    )(coords, *all_acts)
    back_x, u_terms, d_terms = fence(back_x, u_terms, d_terms)
    u_came = to_y(u_terms[1])
    back_y = to_x(b16(keep_b[1] + f32(came_b[1])))
    grad_first, grad_attended, dw_out, vec_g = call(
        post_kernel,
        [VM] * 8,
        [VM] * 4,
        [
            shape_of((tok, width), fl),
            shape_of((tok, width), bf),
            shape_of((width, width), bf),
            shape_of((8, width), fl),
        ],
        flops=10**9,
        vmem=10, moved=4 * 10**6,
    )(residual, keep_a, came_a, back_x, grad_y, vec, w_out, attended)
    back_scratch = [
        pltpu.VMEM((keys, 2 * tok), fl),
    ]
    qa_other, qa_mine, dq_a, dkv_a = call(
        back_a_kernel,
        [SM] + [VM] * 7,
        [AN] * 2 + [VM] * 2,
        [
            shape_of((2, 2, 4, 24, 5 * width // 2), bf),
            shape_of((2, 2, 4, 24, 5 * width // 2), bf),
            shape_of((tok, width // 2), bf),
            shape_of((keys, width), bf),
        ],
        back_scratch + [pltpu.VMEM((2, 2, 8, 24, 5 * width // 2), bf), dma((32,))],
        flops=5 * 10**9,
        vmem=16, moved=10 * 10**6,
    )(coords, start, queries, kv, normed, lse, grad_attended, dw_out)
    def both(mine, came):
        return lambda *index: f32(mine[index]) + f32(came[index])

    def along_z(part):
        return [to_z(b16(part(step)), step) for step in (1, 2, 3)]

    def z_sum(part, came):
        return b16(part(0) + f32(came[0]) + f32(came[1]) + f32(came[2]))

    dq_a, qa_other, u_came, back_y, d_send = fence(dq_a, qa_other, u_came, back_y, d_terms[1])
    qa_came, d_came = to_core(qa_other), to_y(d_send)
    u_part = both(u_terms[0], u_came)
    u_z = along_z(u_part)
    dq_b, dkv_b, p_own, p_y, p_z, sums = call(
        back_b_kernel,
        [SM] + [VM] * 14 + [AN] * 13,
        [VM] * 6,
        [
            shape_of((tok, width // 2), bf),
            shape_of((keys, width), bf),
            shape_of((tok, width), fl),
            shape_of((2, tok, width), bf),
            shape_of((2, tok, width), bf),
            shape_of((8, 8, 256), fl),
        ],
        [pltpu.VMEM((width, 3 * width), bf)] + back_scratch + [dma((1 + 28,))],
        flops=6 * 10**9,
        vmem=20, moved=10 * 10**6,
    )(
        coords, start, queries, kv, lse, grad_attended, vec_g, upb_g, dq_a, dkv_a,
        own_tokens, x1, x2, x3, x4, query_key_value_weight, *got_q,
    )
    dq_b, qa_came, d_came, p_y, *u_z = fence(dq_b, qa_came, d_came, p_y, *u_z)
    qa_1 = both(qa_mine, qa_came)
    d_part = both(d_terms[0], d_came)
    qa_x, p_came = to_x(b16(qa_1(1))), to_y(p_y)
    d_z = along_z(d_part)
    qb_other, qb_mine = call(
        back_c_kernel,
        [SM] + [VM] * 4,
        [AN] * 2,
        [
            shape_of((2, 2, 4, 32, 3 * width // 2), bf),
            shape_of((2, 2, 4, 32, 3 * width // 2), bf),
        ],
        [pltpu.VMEM((2, 2, 8, 32, 3 * width // 2), bf), dma((32,))],
        flops=3 * 10**9,
        vmem=12, moved=6 * 10**6,
    )(coords, normed, dq_b, dkv_b, sums)
    qb_other, qa_x, p_came, *d_z = fence(qb_other, qa_x, p_came, *d_z)
    even = y == 0
    sum_own = p_own + jnp.where(even, f32(p_came[0]), 0.0)
    sum_4 = b16(f32(p_z[1]) + jnp.where(even, 0.0, f32(p_came[1])))

    def qa_2(*index):
        return qa_1(0, *index) + f32(qa_x[index])

    f_tot = join(z_sum(u_part, u_z), z_sum(d_part, d_z))
    qb_came, qa_y, hop, f_x = fence(
        to_core(qb_other), to_y(b16(qa_2(1))), to_z(sum_4, 3), to_x(f_tot)
    )
    qb_1 = both(qb_mine, qb_came)

    def qa_3(*index):
        return qa_2(0, *index) + f32(qa_y[index])

    qb_x, *qa_z = fence(to_x(b16(qb_1(1))), *along_z(qa_3))
    qa_sum = z_sum(qa_3, qa_z)

    def qb_2(*index):
        return qb_1(0, *index) + f32(qb_x[index])

    sum_2 = b16(f32(p_z[0]) + jnp.where(even, f32(p_came[1]), f32(p_came[0])) + f32(hop))
    qb_y, back_2, a_x, a_c, a_xc = fence(
        to_y(b16(qb_2(1))), to_z(sum_2, 3), to_x(qa_sum), to_core(qa_sum), swap_rep(qa_sum, 3)
    )

    def qb_3(*index):
        return qb_2(0, *index) + f32(qb_y[index])

    f_tot, f_x = fence(f_tot, f_x, back_2, qb_y)[:2]
    *qb_z, f_c, f_xc = fence(*along_z(qb_3), to_core(f_tot), to_core(f_x))
    qb_sum = z_sum(qb_3, qb_z)
    b_x, b_c, b_xc = to_x(qb_sum), to_core(qb_sum), swap_rep(qb_sum, 3)
    result = b16(residual + vec[7:8] + keep_a[1] + f32(came_a[1]) + f32(back_y))
    grad_tokens = call(
        tokens_kernel, [VM] * 5, VM, shape_of((tok, width), fl), vmem=4, moved=3 * 10**6
    )(sum_own, back_2, grad_first, own_tokens, vec)
    grad_up, grad_down = call(
        finish_f_kernel,
        [SM] + [VM] * 4,
        [VM] * 2,
        [shape_of(up_weight.shape, fl), shape_of(down_weight.shape, fl)],
        [pltpu.VMEM((4, 96, width), bf)],
        vmem=8, moved=4 * 10**6,
    )(coords, f_tot, f_x, f_c, f_xc)
    grad_qkv, grad_out = call(
        finish_q_kernel,
        [SM] + [VM] * 8,
        [VM] * 2,
        [shape_of(query_key_value_weight.shape, fl), shape_of(output_weight.shape, fl)],
        vmem=8, moved=3 * 10**6,
    )(coords, qa_sum, a_x, a_c, a_xc, qb_sum, b_x, b_c, b_xc)
    sums = f32(qb_sum[24:32, :256])
    part = ln_gains.shape[1]
    return (
        result[None],
        grad_tokens[None],
        grad_qkv,
        grad_out,
        grad_up,
        grad_down,
        sums[0:2, :part],
        sums[2:4, :part],
        sums[4:8, :part],
        sums[0:4, 128 : 128 + part].reshape(4 * part),
    )


def solution(mesh):
    placed = (
        P("rep", "seq", None),
        P("rep", "seq"),
        P("seq", None),
        P("seq", None),
        P("seq", None),
        P("seq", None),
        P(None, "seq"),
        P(None, "seq"),
        P(None, "seq"),
        P("seq"),
        P("rep", "seq", None),
    )
    shape = dict(mesh.shape)
    small_slice = shape["rep"] == 4 and shape["seq"] == 8
    return jax.shard_map(
        on_device_fast if small_slice else on_device,
        mesh=mesh,
        in_specs=placed,
        out_specs=(
            P("rep", "seq", None),
            P("rep", "seq", None),
            P("seq", None),
            P("seq", None),
            P("seq", None),
            P("seq", None),
            P(None, "seq"),
            P(None, "seq"),
            P(None, "seq"),
            P("seq"),
        ),
        check_vma=False,
    )
```

```python
import math

import jax
import jax.numpy as jnp
from jax import lax
from jax.experimental import pallas as pl
from jax.experimental.pallas import tpu as pltpu
from jax.sharding import PartitionSpec as P

HEADS = 12
HD = 64


norm_eps = 1e-05
floor_score = -1e30


def layer_norm(values, gain, shift):
    center = values - jnp.mean(values, axis=-1, keepdims=True)
    spread = jnp.mean(center * center, axis=-1, keepdims=True)
    return center * lax.rsqrt(spread + norm_eps) * gain + shift


def head_split(matrix):
    return matrix.reshape(matrix.shape[0], HEADS, HD)


def masked_scores(queries, query_seg, query_pos, key_piece, seg_piece, offset):
    rows = key_piece.shape[0]
    scores = jnp.einsum(
        "qhd,khd->hqk", queries, head_split(key_piece), preferred_element_type=jnp.float32
    ) * HD ** (-0.5)
    key_pos = offset + jnp.arange(rows, dtype=jnp.int32)
    allowed = (query_seg[:, None] == seg_piece[None, :]) & (key_pos[None, :] <= query_pos[:, None])
    return (jnp.where(allowed[None], scores, floor_score), allowed)


def forward_block(running, pieces, offset, queries, query_seg, query_pos):
    top_run, total_run, accum = running
    key_piece, value_piece, seg_piece = pieces
    scores, allowed = masked_scores(queries, query_seg, query_pos, key_piece, seg_piece, offset)
    top_new = jnp.maximum(top_run, jnp.max(scores, axis=-1))
    probs = jnp.where(allowed[None], jnp.exp(scores - top_new[:, :, None]), 0.0)
    factor = jnp.exp(top_run - top_new)
    total_new = total_run * factor + jnp.sum(probs, axis=-1)
    update = jnp.einsum(
        "hqk,khd->qhd",
        probs.astype(jnp.bfloat16),
        head_split(value_piece),
        preferred_element_type=jnp.float32,
    )
    return (top_new, total_new, accum * factor.T[:, :, None] + update)


def in_blocks(block_fn, running, pieces):
    rows = pieces[0].shape[0]
    size = math.gcd(rows, 1024)
    stacked = tuple((member.reshape((rows // size, size) + member.shape[1:]) for member in pieces))
    offsets = jnp.arange(rows // size, dtype=jnp.int32) * size

    def scan_step(state_now, element):
        return (block_fn(state_now, element[0], element[1]), None)

    running, _unused = lax.scan(scan_step, running, (stacked, offsets))
    return running


def backward_block(
    number,
    state_now,
    whole,
    queries,
    query_seg,
    query_pos,
    grad_heads,
    log_total,
    delta,
    block_rows,
):
    grad_query, term = state_now
    offset = number * block_rows
    key_piece = lax.dynamic_slice_in_dim(whole[0], offset, block_rows, 0)
    value_piece = lax.dynamic_slice_in_dim(whole[1], offset, block_rows, 0)
    seg_piece = lax.dynamic_slice_in_dim(whole[2], offset, block_rows, 0)
    scores, allowed = masked_scores(queries, query_seg, query_pos, key_piece, seg_piece, offset)
    probs = jnp.where(allowed[None], jnp.exp(scores - log_total[:, :, None]), 0.0)
    grad_probs = jnp.einsum(
        "qhd,khd->hqk", grad_heads, head_split(value_piece), preferred_element_type=jnp.float32
    )
    grad_scores = (probs * (grad_probs - delta[:, :, None])).astype(jnp.bfloat16)
    grad_query = grad_query + jnp.einsum(
        "hqk,khd->qhd", grad_scores, head_split(key_piece), preferred_element_type=jnp.float32
    )
    grad_key = jnp.einsum(
        "hqk,qhd->khd", grad_scores, queries, preferred_element_type=jnp.float32
    ) * HD ** (-0.5)
    grad_value = jnp.einsum(
        "hqk,qhd->khd", probs.astype(jnp.bfloat16), grad_heads, preferred_element_type=jnp.float32
    )
    joined = jnp.concatenate(
        [grad_key.reshape(block_rows, -1), grad_value.reshape(block_rows, -1)], axis=1
    )
    term = lax.dynamic_update_slice_in_dim(term, joined, offset, 0)
    return (grad_query, term)


def on_device(
    tokens,
    segment_ids,
    query_key_value_weight,
    output_weight,
    up_weight,
    down_weight,
    ln_gains,
    ln_biases,
    biases,
    up_projection_bias,
    cotangent,
):
    gathered = (
        lax.all_gather(query_key_value_weight, "seq", axis=0, tiled=True),
        lax.all_gather(output_weight, "seq", axis=0, tiled=True),
        lax.all_gather(up_weight, "seq", axis=0, tiled=True),
        lax.all_gather(down_weight, "seq", axis=0, tiled=True),
        lax.all_gather(ln_gains, "seq", axis=1, tiled=True),
        lax.all_gather(ln_biases, "seq", axis=1, tiled=True),
        lax.all_gather(biases, "seq", axis=1, tiled=True),
        lax.all_gather(up_projection_bias, "seq", axis=0, tiled=True),
    )
    full_qkv, full_out, full_up, full_down, gains_all, shifts_all, biases_all, up_shift = gathered
    gains_f = gains_all.astype(jnp.float32)
    shifts_f = shifts_all.astype(jnp.float32)
    biases_f = biases_all.astype(jnp.float32)
    up_shift_f = up_shift.astype(jnp.float32)
    tokens_f = tokens[0].astype(jnp.float32)
    seg_local = segment_ids[0]
    tok_rows = tokens_f.shape[0]
    width = tokens_f.shape[1]
    seqlen = tok_rows * lax.axis_size("seq")
    query_pos = lax.axis_index("seq") * tok_rows + jnp.arange(tok_rows, dtype=jnp.int32)
    hidden_first = layer_norm(tokens_f, gains_f[0], shifts_f[0]).astype(jnp.bfloat16)
    query_key_value_bias = jnp.concatenate(
        [biases_f[0], jnp.zeros((width,), jnp.float32), biases_f[1]]
    )
    projected_rows = (
        jnp.dot(hidden_first, full_qkv, preferred_element_type=jnp.float32) + query_key_value_bias
    ).astype(jnp.bfloat16)
    queries = head_split(projected_rows[:, :width])
    key_rows = projected_rows[:, width : 2 * width]
    value_rows = projected_rows[:, 2 * width :]
    initial = (
        jnp.full((HEADS, tok_rows), floor_score, jnp.float32),
        jnp.zeros((HEADS, tok_rows), jnp.float32),
        jnp.zeros((tok_rows, HEADS, HD), jnp.float32),
    )

    def block_fn(running, pieces, offset):
        return forward_block(running, pieces, offset, queries, seg_local, query_pos)

    block_rows = math.gcd(seqlen, 1024)
    key_end = (lax.axis_index("seq") + 1) * tok_rows
    block_count = (key_end + block_rows - 1) // block_rows
    top_run, total_run, accum = in_blocks(
        block_fn,
        initial,
        (
            lax.all_gather(key_rows, "seq", axis=0, tiled=True),
            lax.all_gather(value_rows, "seq", axis=0, tiled=True),
            lax.all_gather(seg_local, "seq", axis=0, tiled=True),
        ),
    )
    log_total = top_run + jnp.log(total_run)
    attended_f = accum / total_run.T[:, :, None]
    attention_result = attended_f.reshape(tok_rows, width).astype(jnp.bfloat16)
    residual_first = (
        tokens_f
        + jnp.dot(attention_result, full_out, preferred_element_type=jnp.float32)
        + biases_f[2]
    )
    hidden_second = layer_norm(residual_first, gains_f[1], shifts_f[1]).astype(jnp.bfloat16)
    upward_rows = jnp.dot(hidden_second, full_up, preferred_element_type=jnp.float32) + up_shift_f
    activated_f, gelu_back = jax.vjp(jax.nn.gelu, upward_rows)
    activation_values = activated_f.astype(jnp.bfloat16)
    result = (
        residual_first
        + jnp.dot(activation_values, full_down, preferred_element_type=jnp.float32)
        + biases_f[3]
    )
    grad_y = cotangent[0]
    grad_y_f = grad_y.astype(jnp.float32)
    grad_down = jnp.einsum(
        "tf,td->fd", activation_values, grad_y, preferred_element_type=jnp.float32
    )
    grad_act = jnp.einsum("td,fd->tf", grad_y, full_down, preferred_element_type=jnp.float32)
    grad_up_pre = gelu_back(grad_act)[0].astype(jnp.bfloat16)
    grad_up = jnp.einsum(
        "td,tf->df", hidden_second, grad_up_pre, preferred_element_type=jnp.float32
    )
    grad_hidden_two = jnp.einsum(
        "tf,df->td", grad_up_pre, full_up, preferred_element_type=jnp.float32
    )
    _unused, norm_two_back = jax.vjp(layer_norm, residual_first, gains_f[1], shifts_f[1])
    grad_sum_part, grad_gain_two, grad_shift_two = norm_two_back(grad_hidden_two)
    grad_first = grad_y_f + grad_sum_part
    grad_first_bf = grad_first.astype(jnp.bfloat16)
    grad_out_w = jnp.einsum(
        "td,te->de", attention_result, grad_first_bf, preferred_element_type=jnp.float32
    )
    grad_attended = jnp.einsum(
        "te,de->td", grad_first_bf, full_out, preferred_element_type=jnp.float32
    ).astype(jnp.bfloat16)
    grad_heads = head_split(grad_attended)
    delta = jnp.einsum("qhd,qhd->hq", grad_heads.astype(jnp.float32), attended_f)
    whole = (
        lax.all_gather(key_rows, "seq", axis=0, tiled=True),
        lax.all_gather(value_rows, "seq", axis=0, tiled=True),
        lax.all_gather(seg_local, "seq", axis=0, tiled=True),
    )

    def backward_step(number, state_now):
        return backward_block(
            number,
            state_now,
            whole,
            queries,
            seg_local,
            query_pos,
            grad_heads,
            log_total,
            delta,
            block_rows,
        )

    start_state = (
        jnp.zeros((tok_rows, HEADS, HD), jnp.float32),
        jnp.zeros((seqlen, 2 * width), jnp.float32),
    )
    grad_query, term = lax.fori_loop(0, block_count, backward_step, start_state)
    grad_kv = lax.psum_scatter(term, "seq", scatter_dimension=0, tiled=True).astype(jnp.bfloat16)
    grad_q = (grad_query * HD ** (-0.5)).reshape(tok_rows, width).astype(jnp.bfloat16)
    grad_proj = jnp.concatenate([grad_q, grad_kv], axis=1)
    grad_qkv_w = jnp.einsum(
        "td,te->de", hidden_first, grad_proj, preferred_element_type=jnp.float32
    )
    grad_hidden_one = jnp.einsum(
        "te,de->td", grad_proj, full_qkv, preferred_element_type=jnp.float32
    )
    _unused_two, norm_one_back = jax.vjp(layer_norm, tokens_f, gains_f[0], shifts_f[0])
    grad_in_part, grad_gain_one, grad_shift_one = norm_one_back(grad_hidden_one)
    grad_tokens = grad_first + grad_in_part
    grad_proj_f = grad_proj.astype(jnp.float32)
    grad_bias_rows = jnp.stack(
        [
            jnp.sum(grad_proj_f[:, :width], axis=0),
            jnp.sum(grad_proj_f[:, 2 * width :], axis=0),
            jnp.sum(grad_first, axis=0),
            jnp.sum(grad_y_f, axis=0),
        ]
    )
    grad_up_shift = jnp.sum(grad_up_pre.astype(jnp.float32), axis=0)
    grad_gains = jnp.stack([grad_gain_one, grad_gain_two])
    grad_shifts = jnp.stack([grad_shift_one, grad_shift_two])
    shares = (
        lax.psum_scatter(grad_qkv_w, "seq", scatter_dimension=0, tiled=True),
        lax.psum_scatter(grad_out_w, "seq", scatter_dimension=0, tiled=True),
        lax.psum_scatter(grad_up, "seq", scatter_dimension=0, tiled=True),
        lax.psum_scatter(grad_down, "seq", scatter_dimension=0, tiled=True),
        lax.psum_scatter(grad_gains, "seq", scatter_dimension=1, tiled=True),
        lax.psum_scatter(grad_shifts, "seq", scatter_dimension=1, tiled=True),
        lax.psum_scatter(grad_bias_rows, "seq", scatter_dimension=1, tiled=True),
        lax.psum_scatter(grad_up_shift, "seq", scatter_dimension=0, tiled=True),
    )
    totals = (
        lax.psum(shares[0].astype(jnp.bfloat16), "rep").astype(jnp.float32),
        lax.psum(shares[1].astype(jnp.bfloat16), "rep").astype(jnp.float32),
        lax.psum(shares[2].astype(jnp.bfloat16), "rep").astype(jnp.float32),
        lax.psum(shares[3].astype(jnp.bfloat16), "rep").astype(jnp.float32),
        lax.psum(shares[4].astype(jnp.bfloat16), "rep").astype(jnp.float32),
        lax.psum(shares[5].astype(jnp.bfloat16), "rep").astype(jnp.float32),
        lax.psum(shares[6].astype(jnp.bfloat16), "rep").astype(jnp.float32),
        lax.psum(shares[7].astype(jnp.bfloat16), "rep").astype(jnp.float32),
    )
    return (
        result.astype(jnp.bfloat16)[None],
        grad_tokens[None],
        totals[0],
        totals[1],
        totals[2],
        totals[3],
        totals[4],
        totals[5],
        totals[6],
        totals[7],
    )


def f32(value):
    return value.astype(jnp.float32)


def b16(value):
    return value.astype(jnp.bfloat16)


def dot_nn(left, right):
    return jnp.dot(left, right, preferred_element_type=jnp.float32)


def dot_nt(left, right):
    return lax.dot_general(
        left, right, (((1,), (1,)), ((), ())), preferred_element_type=jnp.float32
    )


def dot_tn(left, right):
    return lax.dot_general(
        left, right, (((0,), (0,)), ((), ())), preferred_element_type=jnp.float32
    )


def norm_parts(values):
    center = values - jnp.mean(values, axis=-1, keepdims=True)
    rate = lax.rsqrt(jnp.mean(center * center, axis=-1, keepdims=True) + norm_eps)
    return center * rate, rate


def norm_back(grad, hat, rate, gain):
    scaled = grad * gain
    return rate * (
        scaled
        - jnp.mean(scaled, axis=-1, keepdims=True)
        - hat * jnp.mean(scaled * hat, axis=-1, keepdims=True)
    )


def place():
    rep, seq = lax.axis_index("rep"), lax.axis_index("seq")
    return lax.div(rep, 2), lax.rem(rep, 2), lax.rem(seq, 2), lax.div(seq, 2)


def piece_shard(number, y, z):
    if number < 3:
        return 2 * lax.rem(z + 3 - number, 4) + y
    return 2 * lax.rem(z + 7 - number, 4) + 1 - y


def pack96(parts):
    lane = lax.broadcasted_iota(jnp.int32, parts[0].shape, 1)
    one, two, three = (pltpu.roll(parts[k], 128 - 32 * k, 1) for k in (1, 2, 3))
    return jnp.concatenate(
        [
            jnp.where(lane < 96, parts[0], one),
            jnp.where(lane < 64, one, two),
            jnp.where(lane < 32, two, three),
        ],
        axis=1,
    )


def unpack96(block):
    tiles = [block[:, 128 * k : 128 * k + 128] for k in range(3)]
    lane = lax.broadcasted_iota(jnp.int32, tiles[0].shape, 1)
    return [
        tiles[0],
        jnp.where(lane < 32, pltpu.roll(tiles[0], 32, 1), pltpu.roll(tiles[1], 32, 1)),
        jnp.where(lane < 64, pltpu.roll(tiles[1], 64, 1), pltpu.roll(tiles[2], 64, 1)),
        pltpu.roll(tiles[2], 96, 1),
    ]


def choose(parts, index):
    out = parts[0]
    for number in range(1, len(parts)):
        out = jnp.where(index == number, parts[number], out)
    return out


class Copies:
    def __init__(self, sems, first=0):
        self.sems = sems
        self.first = first
        self.held = []

    def add(self, source, target):
        copy = pltpu.make_async_copy(source, target, self.sems.at[self.first + len(self.held)])
        copy.start()
        self.held.append(copy)

    def wait(self):
        for copy in self.held:
            copy.wait()
        self.held = []


def corners(x, c):
    return ((x, c), (1 - x, c), (x, 1 - c), (1 - x, 1 - c))


def fetch_qkv(copies, own, groups, full, full_out=None, own_out=None):
    x, c, y, z = place()
    rows = own.shape[0]
    half, width = rows // 2, own.shape[1] // 3
    row = pl.multiple_of((2 * z + y) * rows, 16)
    copies.add(own, full.at[pl.ds(row, rows), :])
    if full_out is not None:
        copies.add(own_out, full_out.at[pl.ds(row, rows), :])
    wide, side = 3 * width // 2, width // 2
    for number in range(7):
        for (xx, cc), group in zip(corners(x, c), groups, strict=True):
            piece = piece_of(group, number)
            at = pl.ds(pl.multiple_of(piece_shard(number, y, z) * rows + half * cc, 16), half)
            copies.add(
                piece.at[pl.ds(0, half), pl.ds(0, wide)],
                full.at[at, pl.ds(pl.multiple_of(wide * xx, 128), wide)],
            )
            if full_out is not None:
                copies.add(
                    piece.at[pl.ds(0, half), pl.ds(wide, side)],
                    full_out.at[at, pl.ds(pl.multiple_of(side * xx, 128), side)],
                )


def piece_of(group, number):
    behind, across, behind_across = group
    if number < 3:
        return behind.at[number]
    return across.at[0] if number == 3 else behind_across.at[number - 4]


def mask_bias(start, me, tok, target):
    keys, lanes = target.shape
    key_pos = (me - 4) * tok + lax.broadcasted_iota(jnp.int32, (keys, lanes), 0)
    lane = lax.broadcasted_iota(jnp.int32, (keys, lanes), 1)
    query_pos = me * tok + jnp.where(lane >= tok, lane - tok, lane)
    target[...] = jnp.where((key_pos >= start) & (key_pos <= query_pos), 0.0, floor_score)


def pair_stack(rows):
    lane = lax.broadcasted_iota(jnp.int32, rows.shape, 1)
    zero = jnp.zeros_like(rows)
    return jnp.concatenate([jnp.where(lane < HD, rows, zero), jnp.where(lane < HD, zero, rows)], axis=0)


def pair_join(transposed):
    both = transposed.T
    tok = both.shape[0] // 2
    lane = lax.broadcasted_iota(jnp.int32, (tok, 2 * HD), 1)
    return jnp.where(lane < HD, both[:tok], both[tok:])


def prep_kernel(
    tokens, segs, qkv, out, up, down, gains, shifts, biases, up_bias,
    t_out, q_out, f_out,
    scratch, wide, held_g, held_s, held_b, ids, line, sems,
):
    x, c, _y, _z = place()
    tok, width = tokens.shape[1:]
    rows = qkv.shape[0]
    half, side = rows // 2, width // 2
    p = 2 * x + c
    at = pl.ds(pl.multiple_of(half * c, 16), half)
    copies, others = Copies(sems), Copies(sems, 5)
    for source, target in ((gains, held_g), (shifts, held_s), (biases, held_b)):
        copies.add(source, target)
    copies.add(segs, ids)
    copies.add(up_bias, line)
    others.add(up, wide)
    wide_cols = 3 * side
    others.add(
        qkv.at[at, pl.ds(pl.multiple_of(wide_cols * x, 128), wide_cols)],
        q_out.at[pl.ds(0, half), pl.ds(0, wide_cols)],
    )
    others.add(
        out.at[at, pl.ds(pl.multiple_of(side * x, 128), side)],
        q_out.at[pl.ds(0, half), pl.ds(wide_cols, side)],
    )
    others.add(tokens.at[0], t_out.at[pl.ds(0, tok), :])
    others.add(down.at[pl.ds(pl.multiple_of(rows * p, 16), rows), :], f_out.at[pl.ds(rows, rows), :])
    copies.wait()
    scratch[...] = jnp.zeros_like(scratch)
    for first, held in ((0, held_g), (2, held_s), (4, held_b)):
        scratch[pl.ds(first, held.shape[0]), pl.ds(0, rows)] = f32(held[...])
    parts = unpack96(jnp.broadcast_to(f32(line[...]).reshape(1, line.shape[0]), (8, line.shape[0])))
    lane = lax.broadcasted_iota(jnp.int32, (8, 128), 1)
    row = lax.broadcasted_iota(jnp.int32, (8, 128), 0)
    ups = jnp.zeros((8, 128), jnp.float32)
    for number in range(4):
        ups = jnp.where((row == number) & (lane < rows), parts[number], ups)
    smalls = b16(jnp.concatenate([scratch[:, pl.ds(0, 128)], ups], axis=0))
    q_out[pl.ds(0, 16), pl.ds(2 * width, 128)] = smalls
    q_out[pl.ds(16, half - 16), pl.ds(2 * width, 128)] = jnp.zeros((half - 16, 128), jnp.bfloat16)
    scratch[...] = jnp.zeros_like(scratch)
    scratch[pl.ds(0, 1), pl.ds(0, tok)] = f32(ids[...])
    t_out[pl.ds(tok, 8), :] = b16(scratch[...])
    others.wait()
    for group in range(2):
        parts = []
        for shard in range(4 * group, 4 * group + 4):
            parts.append(choose(unpack96(f32(wide[:, pl.ds(384 * shard, 384)])), p))
        f_out[pl.ds(0, rows), pl.ds(384 * group, 384)] = b16(pack96(parts))


def front_kernel(
    seg, xo, x1, x2, x3, x4, first, own, own_o,
    g0, g1, g2, g3, g4, g5, g6, g7, g8, g9, g10, g11,
    q_out, kv_out, h_out, a_out, lse_out, start_out, vec_out, upb_out, wo_out, r_out, h2_out,
    full, small, bias, sems, vsems,
):
    x, c, y, z = place()
    me = 2 * z + y
    p = 2 * x + c
    tok, width = q_out.shape
    copies, vcopies = Copies(sems), Copies(vsems)
    vcopies.add(first.at[pl.ds(0, 16), pl.ds(2 * width, 128)], small.at[me])
    for number in range(7):
        source = piece_of((g0, g1, g2), number)
        vcopies.add(source.at[pl.ds(0, 16), pl.ds(2 * width, 128)], small.at[piece_shard(number, y, z)])
    groups = ((g0, g1, g2), (g3, g4, g5), (g6, g7, g8), (g9, g10, g11))
    fetch_qkv(copies, own, groups, full, wo_out, own_o)
    blocks = (xo, x1, x2, x3, x4)
    lane1 = lax.broadcasted_iota(jnp.int32, (1, tok), 1)
    start = jnp.full(seg.shape, 1 << 30, jnp.int32)
    for number in range(4):
        first_pos = jnp.full((1, 1), 1 << 30, jnp.int32)
        for back in range(5):
            ids = f32(blocks[back][pl.ds(tok, 8), pl.ds(0, tok)])[:1]
            pos = (me - back) * tok + lane1
            hit = (ids == float(number)) & (pos >= 0)
            first_pos = jnp.minimum(
                first_pos, jnp.min(jnp.where(hit, pos, 1 << 30), axis=1, keepdims=True)
            )
        start = jnp.where(seg[...] == number, first_pos, start)
    start_out[...] = start
    mask_bias(start, me, tok, bias)
    vcopies.wait()
    for group in range(2):
        held = [f32(small[4 * group + k]) for k in range(4)]
        vec_out[:, pl.ds(384 * group, 384)] = pack96([block[:8] for block in held])
        upb_out[:, pl.ds(384 * group, 384)] = pack96(
            [choose([jnp.broadcast_to(block[k : k + 1], (8, 128)) for k in range(8, 12)], p) for block in held]
        )
    vec = vec_out[...]
    for back in range(5):
        hat, _rate = norm_parts(f32(blocks[back][pl.ds(0, tok), :]))
        h_out[pl.ds((4 - back) * tok, tok), :] = b16(hat * vec[0:1] + vec[2:3])
    copies.wait()
    q_out[...] = b16(dot_nn(h_out[pl.ds(4 * tok, tok), :], full[:, pl.ds(0, width)]) + vec[4:5])

    def project(number, carry):
        col = pl.multiple_of(number * 256, 256)
        shift = jnp.where(number >= width // 256, 1.0, 0.0)
        bias_at = lax.rem(number, width // 256)
        piece = vec_out[pl.ds(5, 1), pl.ds(pl.multiple_of(bias_at * 256, 256), 256)]
        kv_out[:, pl.ds(col, 256)] = b16(
            dot_nn(h_out[...], full[:, pl.ds(pl.multiple_of(width + col, 256), 256)]) + piece * shift
        )
        return carry

    lax.fori_loop(0, 2 * width // 256, project, 0)

    def pair(number, carry):
        col = pl.multiple_of(number * 128, 128)
        queries = pair_stack(q_out[:, pl.ds(col, 128)] * jnp.bfloat16(0.125))
        scores = dot_nt(kv_out[:, pl.ds(col, 128)], queries) + bias[...]
        top = jnp.max(scores, axis=0, keepdims=True)
        probs = jnp.exp(scores - top)
        total = jnp.sum(probs, axis=0, keepdims=True)
        mixed = dot_tn(kv_out[:, pl.ds(pl.multiple_of(width + col, 128), 128)], b16(probs))
        a_out[:, pl.ds(col, 128)] = b16(pair_join(mixed / total))
        lse_out[number] = top + jnp.log(total)
        return carry

    lax.fori_loop(0, width // 128, pair, 0)
    residual = f32(xo[pl.ds(0, tok), :]) + dot_nn(a_out[...], wo_out[...]) + vec[6:7]
    r_out[...] = residual
    hat, _rate = norm_parts(residual)
    h2_out[...] = b16(hat * vec[1:2] + vec[3:4])


def feed_tokens(h2, dy, w_up, w_down, upb, act_out, du_out, y_acc, dh_acc):
    root = math.sqrt(2.0 / math.pi)
    chunk = 256

    def feed(number, carry):
        col = pl.multiple_of(number * chunk, chunk)
        pre = dot_nn(h2[...], w_up[:, pl.ds(col, chunk)]) + upb[pl.ds(0, 1), pl.ds(col, chunk)]
        square = pre * pre
        bend = jnp.tanh(root * pre * (1.0 + 0.044715 * square))
        act = b16(0.5 * pre * (1.0 + bend))
        slope = 0.5 * (1.0 + bend) + 0.5 * pre * (1.0 - bend * bend) * (
            root * (1.0 + 3.0 * 0.044715 * square)
        )
        low = b16(dot_nt(dy[...], w_down[pl.ds(col, chunk), :]) * slope)
        act_out[:, pl.ds(col, chunk)] = act
        du_out[:, pl.ds(col, chunk)] = low
        return carry

    lax.fori_loop(0, w_up.shape[1] // chunk, feed, 0)
    dh_acc[...] = dot_nt(du_out[...], w_up[...])
    y_acc[...] = dot_nn(act_out[...], w_down[...])


def assemble_kernel(own, z1, z2, z3, y0, y13, wu_out, wd_out, sems):
    _x, _c, y, z = place()
    rows = own.shape[0] // 2
    copies = Copies(sems)
    pieces = [(own, 2 * z + y)]
    for number, ref in ((0, z1), (1, z2), (2, z3), (3, y0)):
        pieces.append((ref, piece_shard(number, y, z)))
    for number, first in ((4, 0), (6, 2 * rows)):
        pieces.append((y13.at[pl.ds(first, 2 * rows), :], piece_shard(number, y, z)))
    for ref, shard in pieces:
        at = pl.ds(pl.multiple_of(shard * rows, 16), rows)
        copies.add(ref.at[pl.ds(0, rows), :], wu_out.at[at, :])
        copies.add(ref.at[pl.ds(rows, rows), :], wd_out.at[at, :])
    copies.wait()


def near_kernel(
    h_own, h_c, dy_own, dy_c, upb, y2, _wu, _wd,
    h2, dy, act_out, du_out, keep_out, send_out, wu_out, wd_out,
    y_acc, dh_acc, sems,
):
    _x, _c, y, z = place()
    tok, width = h_own.shape
    rows = width // 8
    copies = Copies(sems)
    at = pl.ds(pl.multiple_of(piece_shard(5, y, z) * rows, 16), rows)
    copies.add(y2.at[pl.ds(0, rows), :], wu_out.at[at, :])
    copies.add(y2.at[pl.ds(rows, rows), :], wd_out.at[at, :])
    h2[pl.ds(0, tok), :] = h_own[...]
    h2[pl.ds(tok, tok), :] = h_c[...]
    dy[pl.ds(0, tok), :] = dy_own[...]
    dy[pl.ds(tok, tok), :] = dy_c[...]
    copies.wait()
    feed_tokens(h2, dy, wu_out, wd_out, upb, act_out, du_out, y_acc, dh_acc)
    keep_out[0] = dh_acc[pl.ds(0, tok), :]
    keep_out[1] = y_acc[pl.ds(0, tok), :]
    send_out[0] = b16(dh_acc[pl.ds(tok, tok), :])
    send_out[1] = b16(y_acc[pl.ds(tok, tok), :])


def far_kernel(
    h_x, h_xc, dy_x, dy_xc, upb, w_up, w_down, h_near, dy_near, act_near, du_near,
    hs, dys, acts, dus, keep_out, send_out,
    y_acc, dh_acc, sems,
):
    tok = h_x.shape[0]
    copies = Copies(sems)
    for source, target in ((h_near, hs), (dy_near, dys), (act_near, acts), (du_near, dus)):
        copies.add(source, target.at[pl.ds(0, 2 * tok), :])
    later = pl.ds(2 * tok, 2 * tok)
    hs[pl.ds(2 * tok, tok), :] = h_x[...]
    hs[pl.ds(3 * tok, tok), :] = h_xc[...]
    dys[pl.ds(2 * tok, tok), :] = dy_x[...]
    dys[pl.ds(3 * tok, tok), :] = dy_xc[...]
    feed_tokens(
        hs.at[later, :], dys.at[later, :], w_up, w_down, upb, acts.at[later, :], dus.at[later, :], y_acc, dh_acc
    )
    keep_out[0] = dh_acc[pl.ds(0, tok), :]
    keep_out[1] = y_acc[pl.ds(0, tok), :]
    send_out[0] = b16(dh_acc[pl.ds(tok, tok), :])
    send_out[1] = b16(y_acc[pl.ds(tok, tok), :])
    copies.wait()


def weights_kernel(hs, dys, acts, dus, u_out, d_out, upb_out, stage, sems):
    _x, _c, y, z = place()
    width = hs.shape[1]
    rows = width // 8
    upb_out[...] = jnp.sum(f32(dus[...]), axis=0, keepdims=True)

    def weight(number, carry):
        col = pl.multiple_of(number * 256, 256)
        stage[0, pl.ds(col, 256), :] = b16(dot_tn(hs[:, pl.ds(col, 256)], dus[...]))
        stage[1, pl.ds(col, 256), :] = b16(dot_tn(acts[:, pl.ds(col, 256)], dys[...]))
        return carry

    lax.fori_loop(0, width // 256, weight, 0)
    outs = Copies(sems)
    for shard in range(8):
        zz = lax.rem(shard // 2 + 4 - z, 4)
        yy = jnp.where(y == shard % 2, 0, 1)
        outs.add(stage.at[0, pl.ds(shard * rows, rows), :], u_out.at[yy, zz])
        outs.add(stage.at[1, pl.ds(shard * rows, rows), :], d_out.at[yy, zz])
    outs.wait()


def scatter(stage, other, mine, sems):
    x, c, y, z = place()
    outs = Copies(sems)
    for shard in range(8):
        zz = lax.rem(shard // 2 + 4 - z, 4)
        yy = jnp.where(y == shard % 2, 0, 1)
        for xx in range(2):
            far = jnp.where(x == xx, 0, 1)
            outs.add(stage.at[1 - c, xx, shard], other.at[far, yy, zz])
            outs.add(stage.at[c, xx, shard], mine.at[far, yy, zz])
    outs.wait()


def post_kernel(
    residual, own, near, across, dy_in, vec_in, w_out, a_in,
    dr_out, da_out, dw_out, vec_out,
):
    vec = vec_in[...]
    grad_hidden = own[0] + f32(near[0]) + f32(across[...])
    hat, rate = norm_parts(residual[...])
    dy = f32(dy_in[...])
    grad_first = dy + norm_back(grad_hidden, hat, rate, vec[1:2])
    dr_out[...] = grad_first
    low = b16(grad_first)
    da_out[...] = b16(dot_nt(low, w_out[...]))
    dw_out[...] = dot_tn(a_in[...], low)
    zero = jnp.zeros((1, dy.shape[1]), jnp.float32)
    vec_out[...] = jnp.concatenate(
        [
            zero,
            jnp.sum(grad_hidden * hat, axis=0, keepdims=True),
            zero,
            jnp.sum(grad_hidden, axis=0, keepdims=True),
            zero,
            zero,
            jnp.sum(grad_first, axis=0, keepdims=True),
            jnp.sum(dy, axis=0, keepdims=True),
        ],
        axis=0,
    )


def back_pairs(first, q_in, kv_in, lse_in, da_in, bias, dq, dkv):
    width = q_in.shape[1]

    def pair(number, carry):
        col = pl.multiple_of((first + number) * 128, 128)
        vcol = pl.multiple_of(width + col, 128)
        to = pl.multiple_of(number * 128, 128)
        queries = pair_stack(q_in[:, pl.ds(col, 128)] * jnp.bfloat16(0.125))
        grads = pair_stack(da_in[:, pl.ds(col, 128)])
        keys = kv_in[:, pl.ds(col, 128)]
        probs = jnp.exp(dot_nt(keys, queries) + bias[...] - lse_in[first + number])
        dkv[:, pl.ds(pl.multiple_of(width // 2 + to, 128), 128)] = b16(dot_nn(b16(probs), grads))
        term = probs * dot_nt(kv_in[:, pl.ds(vcol, 128)], grads)
        low = b16(term - probs * jnp.sum(term, axis=0, keepdims=True))
        dkv[:, pl.ds(to, 128)] = b16(dot_nn(low, queries))
        dq[:, pl.ds(to, 128)] = b16(pair_join(dot_tn(keys, low)) * 0.125)
        return carry

    lax.fori_loop(0, 3, pair, 0)


def qkv_weight(h_in, dq, dkv, stage, tail):
    tok, part = dq.shape
    keys = h_in.shape[0]

    def weight(number, carry):
        col = pl.multiple_of(number * 384, 384)
        key = dot_tn(h_in[:, pl.ds(col, 384)], dkv[...])
        query = dot_tn(h_in[pl.ds(keys - tok, tok), pl.ds(col, 384)], dq[...])
        for shard in range(4):
            for cc in range(2):
                for xx in range(2):
                    rows = slice(96 * shard + 48 * cc + 24 * xx, 96 * shard + 48 * cc + 24 * xx + 24)
                    blocks = [query[rows], key[rows, :part], key[rows, part:]] + tail(4 * number + shard, 48 * cc + 24 * xx)
                    stage[cc, xx, 4 * number + shard] = b16(jnp.concatenate(blocks, axis=0))
        return carry

    lax.fori_loop(0, 2, weight, 0)


def back_a_kernel(
    start_in, q_in, kv_in, h_in, lse_in, da_in, dw_in,
    other, mine, dq_out, dkv_out,
    bias, stage, sems,
):
    _x, _c, y, z = place()
    mask_bias(start_in[...], 2 * z + y, q_in.shape[0], bias)
    back_pairs(0, q_in, kv_in, lse_in, da_in, bias, dq_out, dkv_out)
    side = q_in.shape[1] // 2

    def out_rows(shard, row):
        rows = dw_in[pl.ds(pl.multiple_of(96 * shard + row, 8), 24), :]
        return [rows[:, :side], rows[:, side:]]

    qkv_weight(h_in, dq_out, dkv_out, stage, out_rows)
    scatter(stage, other, mine, sems)


def back_b_kernel(
    start_in, q_in, kv_in, lse_in, da_in, vec_in, upb_in, dq_a, dkv_a, xo, x1, x2, x3, x4,
    own, g0, g1, g2, g3, g4, g5, g6, g7, g8, g9, g10, g11,
    dq_out, dkv_out, p_own, p_y, p_z, sums_out,
    full, bias, sems,
):
    x, c, y, z = place()
    p = 2 * x + c
    tok, width = q_in.shape
    side = width // 2
    copies = Copies(sems)
    groups = ((g0, g1, g2), (g3, g4, g5), (g6, g7, g8), (g9, g10, g11))
    fetch_qkv(copies, own, groups, full)
    mask_bias(start_in[...], 2 * z + y, tok, bias)
    back_pairs(3, q_in, kv_in, lse_in, da_in, bias, dq_out, dkv_out)
    copies.wait()
    gain_sum = jnp.zeros((1, width), jnp.float32)
    shift_sum = jnp.zeros((1, width), jnp.float32)
    for back, block in enumerate((xo, x1, x2, x3, x4)):
        rows = pl.ds((4 - back) * tok, tok)
        grad = jnp.zeros((tok, width), jnp.float32)
        for number, (dq, dkv) in enumerate(((dq_a, dkv_a), (dq_out, dkv_out))):
            at = number * side
            grad = grad + dot_nt(dkv[rows, pl.ds(0, side)], full[:, pl.ds(width + at, side)])
            grad = grad + dot_nt(dkv[rows, pl.ds(side, side)], full[:, pl.ds(2 * width + at, side)])
            if back == 0:
                grad = grad + dot_nt(dq[...], full[:, pl.ds(at, side)])
        if back == 0:
            p_own[...] = grad
        elif back in (1, 3):
            p_y[back // 2] = b16(grad)
        else:
            p_z[back // 2 - 1] = b16(grad)
        hat, _rate = norm_parts(f32(block[pl.ds(0, tok), :]))
        gain_sum = gain_sum + jnp.sum(grad * hat, axis=0, keepdims=True)
        shift_sum = shift_sum + jnp.sum(grad, axis=0, keepdims=True)
    zero = jnp.zeros((1, width), jnp.float32)
    bias_q = jnp.concatenate([jnp.sum(f32(d[...]), axis=0, keepdims=True) for d in (dq_a, dq_out)], axis=1)
    bias_v = jnp.concatenate(
        [jnp.sum(f32(d[:, pl.ds(side, side)]), axis=0, keepdims=True) for d in (dkv_a, dkv_out)], axis=1
    )
    vec = vec_in[...] + jnp.concatenate(
        [gain_sum, zero, shift_sum, zero, bias_q, bias_v, zero, zero], axis=0
    )
    lane = lax.broadcasted_iota(jnp.int32, (8, 128), 1)
    line = lax.broadcasted_iota(jnp.int32, (8, 128), 0)
    for group in range(2):
        cols = pl.ds(384 * group, 384)
        vec_parts = unpack96(vec[:, 384 * group : 384 * group + 384])
        upb_parts = unpack96(jnp.broadcast_to(upb_in[:, cols], (8, 384)))
        for k in range(4):
            sums_out[4 * group + k] = jnp.concatenate(
                [
                    jnp.where(lane < 96, vec_parts[k], 0.0),
                    jnp.where((lane < 96) & (line == p), upb_parts[k], 0.0),
                ],
                axis=1,
            )


def back_c_kernel(h_in, dq, dkv, sums_in, other, mine, stage, sems):
    blank = jnp.zeros((8, 128), jnp.float32)
    qkv_weight(
        h_in, dq, dkv, stage, lambda shard, _row: [jnp.concatenate([sums_in[shard], blank], axis=1)]
    )
    scatter(stage, other, mine, sems)


def tokens_kernel(own, near, dr, xo, vec_in, grad_out):
    tok = own.shape[0]
    hat, rate = norm_parts(f32(xo[pl.ds(0, tok), :]))
    grad = own[...] + f32(near[...])
    grad_out[...] = dr[...] + norm_back(grad, hat, rate, vec_in[0:1, :])


def finish_f_kernel(f0, fx, fc, fcx, up, down, held):
    x, c, _y, _z = place()
    rows = f0.shape[0] // 2
    for (xx, cc), f in zip(corners(x, c), (f0, fx, fc, fcx), strict=True):
        p = 2 * xx + cc
        held[p] = f[pl.ds(0, rows), :]
        down[pl.ds(pl.multiple_of(rows * p, 16), rows), :] = f32(f[pl.ds(rows, rows), :])
    for group in range(2):
        parts = [unpack96(f32(held[k, :, pl.ds(384 * group, 384)])) for k in range(4)]
        for shard in range(4):
            up[:, pl.ds(384 * (4 * group + shard), 384)] = pack96([part[shard] for part in parts])


def finish_q_kernel(f0, fx, fc, fcx, qkv, out):
    x, c, _y, _z = place()
    side = out.shape[1] // 2
    for (xx, cc), piece in zip(corners(x, c), (f0, fx, fc, fcx), strict=True):
        rows = pl.ds(pl.multiple_of(48 * cc + 24 * xx, 8), 24)
        blocks = f32(piece[...])
        for number in range(3):
            first, second = 24 * number, 24 * (number + 5)
            qkv[rows, pl.ds(2 * side * number, side)] = blocks[first : first + 24]
            qkv[rows, pl.ds(2 * side * number + side, side)] = blocks[second : second + 24]
        out[rows, pl.ds(0, side)] = blocks[72:96]
        out[rows, pl.ds(side, side)] = blocks[96:120]


HB = pl.BlockSpec(memory_space=pltpu.HBM)
VM = pl.BlockSpec(memory_space=pltpu.VMEM)
AN = pl.BlockSpec(memory_space=pl.ANY)


def shape_of(shape, dtype):
    return jax.ShapeDtypeStruct(shape, dtype)


def call(kernel, ins, outs, out_shape, scratch=(), vmem=40, flops=0, moved=0, aliases=None):
    return pl.pallas_call(
        kernel,
        in_specs=ins,
        out_specs=outs,
        out_shape=out_shape,
        scratch_shapes=list(scratch),
        input_output_aliases=aliases or {},
        compiler_params=pltpu.CompilerParams(vmem_limit_bytes=vmem << 20),
        cost_estimate=pl.CostEstimate(flops=flops, bytes_accessed=moved, transcendentals=0),
    )


def fence(*values):
    return lax.optimization_barrier(values)


def swap_rep(value, bit):
    return lax.ppermute(value, "rep", [(k, k ^ bit) for k in range(4)])


def to_core(value):
    return swap_rep(value, 1)


def to_x(value):
    return swap_rep(value, 2)


def to_y(value):
    return lax.ppermute(value, "seq", [(k, k ^ 1) for k in range(8)])


def to_z(value, steps):
    return lax.ppermute(value, "seq", [(k, (k + 2 * steps) % 8) for k in range(8)])


def join(*parts):
    return jnp.concatenate(parts, axis=0)


def on_device_fast(
    tokens,
    segment_ids,
    query_key_value_weight,
    output_weight,
    up_weight,
    down_weight,
    ln_gains,
    ln_biases,
    biases,
    up_projection_bias,
    cotangent,
):
    seq = lax.axis_index("seq")
    y = seq % 2
    tok, width = tokens.shape[1:]
    hidden = up_weight.shape[1]
    keys = 5 * tok
    bf, fl = jnp.bfloat16, jnp.float32
    dma = pltpu.SemaphoreType.DMA
    grad_y = cotangent[0]
    own_tokens, piece_q, piece_f = call(
        prep_kernel,
        [HB] * 10,
        [VM] * 3,
        [
            shape_of((tok + 8, width), bf),
            shape_of((48, 2 * width + 128), bf),
            shape_of((192, width), bf),
        ],
        [
            pltpu.VMEM((8, width), fl),
            pltpu.VMEM((96, hidden), bf),
            pltpu.VMEM((2, 96), bf),
            pltpu.VMEM((2, 96), bf),
            pltpu.VMEM((4, 96), bf),
            pltpu.VMEM((1, tok), jnp.int32),
            pltpu.VMEM((384,), bf),
            dma((10,)),
        ],
        vmem=60, moved=4 * 10**6,
    )(
        tokens, segment_ids, query_key_value_weight, output_weight, up_weight, down_weight,
        ln_gains, ln_biases, biases, up_projection_bias,
    )

    q1, q3, q_y0, dy_x = fence(to_z(piece_q, 1), to_z(piece_q, 3), to_y(piece_q), to_x(grad_y))
    own_tokens, piece_f, q1, q_y0 = fence(own_tokens, piece_f, q1, q_y0, q3, dy_x)[:4]
    q2, x2, q_xy0, f_y0 = fence(to_z(q1, 1), to_z(own_tokens, 1), to_x(q_y0), to_y(piece_f))
    q_z = join(q1, q2, q3)
    q_z, x2 = fence(q_z, x2, q_xy0, f_y0)[:2]
    q_y, q_xz, x4 = fence(to_y(q_z), to_x(q_z), to_z(x2, 1))
    near = jnp.where(y == 0, own_tokens, x2)
    far = jnp.where(y == 0, x2, x4)
    near_far, q_y, piece_f = fence(jnp.stack([near, far]), q_y, piece_f, q_xz)[:3]
    crossed, q_xy, f1, f3 = fence(to_y(near_far), to_x(q_y), to_z(piece_f, 1), to_z(piece_f, 3))
    x1, x3 = crossed[0], crossed[1]
    q_z, q_y0, q_y, q_xz, q_xy0, q_xy = fence(q_z, q_y0, q_y, q_xz, q_xy0, q_xy, f1, f3, crossed)[:6]
    q_cz, q_cy0, q_cy, q_cxz, q_cxy0, q_cxy = fence(
        *(to_core(v) for v in (q_z, q_y0, q_y, q_xz, q_xy0, q_xy))
    )
    f_13, f_1, q_cz = fence(join(f1, f3), f1, q_cz, q_cy0, q_cy, q_cxz, q_cxy0, q_cxy)[:3]
    f_y13, f2 = to_y(f_13), to_z(f_1, 1)
    dy_c, dy_xc = to_core(grad_y), to_core(dy_x)

    def pieces(value):
        return value.reshape(value.shape[0] // 48, 48, value.shape[1])

    got_q = [
        pieces(v)
        for v in (q_z, q_y0, q_y, q_xz, q_xy0, q_xy, q_cz, q_cy0, q_cy, q_cxz, q_cxy0, q_cxy)
    ]
    seg = jnp.concatenate([segment_ids, segment_ids], axis=1)
    front = call(
        front_kernel,
        [VM] * 6 + [AN] * 15,
        [VM] * 11,
        [
            shape_of((tok, width), bf),
            shape_of((keys, 2 * width), bf),
            shape_of((keys, width), bf),
            shape_of((tok, width), bf),
            shape_of((width // 128, 1, 2 * tok), fl),
            shape_of((1, 2 * tok), jnp.int32),
            shape_of((8, width), fl),
            shape_of((8, width), fl),
            shape_of((width, width), bf),
            shape_of((tok, width), fl),
            shape_of((tok, width), bf),
        ],
        [
            pltpu.VMEM((width, 3 * width), bf),
            pltpu.VMEM((8, 16, 128), bf),
            pltpu.VMEM((keys, 2 * tok), fl),
            dma((2 + 56,)),
            dma((8,)),
        ],
        flops=7 * 10**9,
        vmem=16, moved=12 * 10**6,
    )(
        seg, own_tokens, x1, x2, x3, x4, piece_q, query_key_value_weight, output_weight, *got_q,
    )
    *front, f_y13, f2, dy_c, dy_xc = fence(*front, f_y13, f2, dy_c, dy_xc)
    queries, kv, normed, attended, lse, start, vec, upb, w_out, residual, hidden_2 = front
    w_half = call(
        assemble_kernel,
        [AN] * 6,
        [VM] * 2,
        [shape_of((width, width), bf)] * 2,
        [dma((14,))],
        vmem=4,
        moved=5 * 10**6,
    )(piece_f, f1, f2, f3, f_y0, f_y13)
    h_x, h_c, f_y2, *w_half = fence(to_x(hidden_2), to_core(hidden_2), to_y(f2), *w_half)
    act = shape_of((2 * tok, width), bf)
    acts = shape_of((4 * tok, width), bf)
    feed_shapes = [shape_of((2, tok, width), fl), shape_of((2, tok, width), bf)]
    feed_scratch = [pltpu.VMEM((2 * tok, width), fl), pltpu.VMEM((2 * tok, width), fl)]
    *near_acts, keep_a, send_a, w_up, w_down = call(
        near_kernel,
        [VM] * 5 + [AN] + [VM] * 2,
        [VM] * 8,
        [act] * 4 + feed_shapes + [shape_of((width, width), bf)] * 2,
        feed_scratch + [dma((2,))],
        flops=3 * 10**9,
        vmem=8,
        moved=6 * 10**6,
        aliases={6: 6, 7: 7},
    )(hidden_2, h_c, grad_y, dy_c, upb, f_y2, *w_half)
    h_xc = to_core(h_x)
    keep_a, send_a, h_xc, w_up = fence(keep_a, send_a, h_xc, w_up)
    came_a = to_core(send_a)
    *all_acts, keep_b, send_b = call(
        far_kernel,
        [VM] * 7 + [AN] * 4,
        [VM] * 6,
        [acts] * 4 + feed_shapes,
        feed_scratch + [dma((4,))],
        flops=3 * 10**9,
        vmem=8, moved=6 * 10**6,
    )(h_x, h_xc, dy_x, dy_xc, upb, w_up, w_down, *near_acts)
    keep_b, send_b, came_a = fence(keep_b, send_b, came_a)
    keep_b, came_b, *all_acts = fence(keep_b, to_core(send_b), *all_acts)
    back_x = to_x(b16(keep_b[0] + f32(came_b[0])))
    u_terms, d_terms, upb_g = call(
        weights_kernel,
        [VM] * 4,
        [AN, AN, VM],
        [shape_of((2, 4, 96, width), bf), shape_of((2, 4, 96, width), bf), shape_of((1, width), fl)],
        [pltpu.VMEM((2, width, width), bf), dma((16,))],
        flops=3 * 10**9,
        vmem=12, moved=6 * 10**6,
    )(*all_acts)
    back_x, u_terms, d_terms, keep_b = fence(back_x, u_terms, d_terms, keep_b)
    u_came = to_y(u_terms[1])
    back_y = to_x(b16(keep_b[1] + f32(came_b[1])))
    grad_first, grad_attended, dw_out, vec_g = call(
        post_kernel,
        [VM] * 8,
        [VM] * 4,
        [
            shape_of((tok, width), fl),
            shape_of((tok, width), bf),
            shape_of((width, width), fl),
            shape_of((8, width), fl),
        ],
        vmem=12,
        flops=10**9,
        moved=4 * 10**6,
    )(residual, keep_a, came_a, back_x, grad_y, vec, w_out, attended)
    back_scratch = [
        pltpu.VMEM((keys, 2 * tok), fl),
    ]
    qa_other, qa_mine, dq_a, dkv_a = call(
        back_a_kernel,
        [VM] * 7,
        [AN] * 2 + [VM] * 2,
        [
            shape_of((2, 2, 4, 120, width // 2), bf),
            shape_of((2, 2, 4, 120, width // 2), bf),
            shape_of((tok, width // 2), bf),
            shape_of((keys, width), bf),
        ],
        back_scratch + [pltpu.VMEM((2, 2, 8, 120, width // 2), bf), dma((32,))],
        flops=5 * 10**9,
        vmem=16, moved=10 * 10**6,
    )(start, queries, kv, normed, lse, grad_attended, dw_out)

    def both(mine, came):
        return lambda *index: f32(mine[index]) + f32(came[index])

    def z_far(part):
        return to_z(b16(part(2)), 1), to_z(b16(part(3)), 3)

    def z_sum(part, *came):
        return b16(part(0) + sum(f32(v) for v in came))

    dq_a, qa_other, u_came, back_y, d_send = fence(
        dq_a, qa_other, u_came, back_y, d_terms[1]
    )
    d_came, qa_came = to_y(d_send), to_core(qa_other)
    u_part = both(u_terms[0], u_came)
    u_z2, u_z3 = z_far(u_part)
    dq_b, dkv_b, p_own, p_y, p_z, sums = call(
        back_b_kernel,
        [VM] * 14 + [AN] * 13,
        [VM] * 6,
        [
            shape_of((tok, width // 2), bf),
            shape_of((keys, width), bf),
            shape_of((tok, width), fl),
            shape_of((2, tok, width), bf),
            shape_of((2, tok, width), bf),
            shape_of((8, 8, 256), fl),
        ],
        [pltpu.VMEM((width, 3 * width), bf)] + back_scratch + [dma((1 + 28,))],
        flops=6 * 10**9,
        vmem=20, moved=10 * 10**6,
    )(
        start, queries, kv, lse, grad_attended, vec_g, upb_g, dq_a, dkv_a,
        own_tokens, x1, x2, x3, x4, query_key_value_weight, *got_q,
    )
    dq_b, qa_came, d_came, p_y, u_z2, u_z3 = fence(
        dq_b, qa_came, d_came, p_y, u_z2, u_z3
    )
    p_came = to_y(p_y)
    qa_1 = both(qa_mine, qa_came)
    qa_send = b16(qa_1(1))
    qa_x = to_x(qa_send[:, :, :96])
    d_part = both(d_terms[0], d_came)
    d_z2, d_z3 = z_far(d_part)
    u_z1 = to_z(b16(u_part(1) + f32(u_z2)), 1)
    qb_other, qb_mine = call(
        back_c_kernel,
        [VM] * 4,
        [AN] * 2,
        [
            shape_of((2, 2, 4, 80, width // 2), bf),
            shape_of((2, 2, 4, 80, width // 2), bf),
        ],
        [pltpu.VMEM((2, 2, 8, 80, width // 2), bf), dma((32,))],
        flops=3 * 10**9,
        vmem=12, moved=6 * 10**6,
    )(normed, dq_b, dkv_b, sums)
    qb_other, qa_x, p_came, d_z2, d_z3, u_z1, qa_rest = fence(
        qb_other, qa_x, p_came, d_z2, d_z3, u_z1, qa_send[:, :, 96:]
    )
    qb_came, qa_x2 = to_core(qb_other), to_x(qa_rest)
    even = y == 0
    sum_own = p_own + jnp.where(even, f32(p_came[0]), 0.0)
    sum_4 = b16(f32(p_z[1]) + jnp.where(even, 0.0, f32(p_came[1])))
    sum_2 = f32(p_z[0]) + jnp.where(even, f32(p_came[1]), f32(p_came[0]))
    qb_came, qa_x, qa_x2, sum_4, d_z2 = fence(qb_came, qa_x, qa_x2, sum_4, d_z2)

    def qa_2(*index):
        return qa_1(0, *index) + jnp.concatenate([f32(qa_x[index]), f32(qa_x2[index])], axis=-2)

    qb_1 = both(qb_mine, qb_came)
    qb_x, qa_y, hop, d_z1 = fence(
        to_x(b16(qb_1(1))), to_y(b16(qa_2(1))), to_z(sum_4, 3), to_z(b16(d_part(1) + f32(d_z2)), 1)
    )

    def qb_2(*index):
        return qb_1(0, *index) + f32(qb_x[index])

    f_tot = join(z_sum(u_part, u_z1, u_z3), z_sum(d_part, d_z1, d_z3))
    f_tot, hop = fence(f_tot, hop)
    qb_y, back_2, f_x = fence(to_y(b16(qb_2(1))), to_z(b16(sum_2 + f32(hop)), 3), to_x(f_tot))

    def q_3(*index):
        first = qa_2(0, *index) + f32(qa_y[index])
        return jnp.concatenate([first, qb_2(0, *index) + f32(qb_y[index])], axis=-2)

    f_tot, f_x, back_2, qb_y = fence(f_tot, f_x, back_2, qb_y)
    *q_z, f_tot, f_x = fence(*(to_z(b16(q_3(step)), step) for step in (1, 2, 3)), f_tot, f_x)
    f_c, f_xc = to_core(f_tot), to_core(f_x)
    q_sum = z_sum(q_3, *q_z)
    q_fx, q_fc, q_fxc = to_x(q_sum), to_core(q_sum), swap_rep(q_sum, 3)
    result = b16(residual + vec[7:8] + keep_a[1] + f32(came_a[1]) + f32(back_y))
    grad_tokens = call(
        tokens_kernel, [VM] * 5, VM, shape_of((tok, width), fl), vmem=4, moved=3 * 10**6
    )(sum_own, back_2, grad_first, own_tokens, vec)
    grad_up, grad_down = call(
        finish_f_kernel,
        [VM] * 4,
        [VM] * 2,
        [shape_of(up_weight.shape, fl), shape_of(down_weight.shape, fl)],
        [pltpu.VMEM((4, 96, width), bf)],
        vmem=8, moved=4 * 10**6,
    )(f_tot, f_x, f_c, f_xc)
    grad_qkv, grad_out = call(
        finish_q_kernel,
        [VM] * 4,
        [VM] * 2,
        [shape_of(query_key_value_weight.shape, fl), shape_of(output_weight.shape, fl)],
        vmem=8, moved=3 * 10**6,
    )(q_sum, q_fx, q_fc, q_fxc)
    sums = f32(q_sum[192:200, :256])
    part = ln_gains.shape[1]
    return (
        result[None],
        grad_tokens[None],
        grad_qkv,
        grad_out,
        grad_up,
        grad_down,
        sums[0:2, :part],
        sums[2:4, :part],
        sums[4:8, :part],
        sums[0:4, 128 : 128 + part].reshape(4 * part),
    )


def solution(mesh):
    placed = (
        P("rep", "seq", None),
        P("rep", "seq"),
        P("seq", None),
        P("seq", None),
        P("seq", None),
        P("seq", None),
        P(None, "seq"),
        P(None, "seq"),
        P(None, "seq"),
        P("seq"),
        P("rep", "seq", None),
    )
    shape = dict(mesh.shape)
    small_slice = shape["rep"] == 4 and shape["seq"] == 8
    return jax.shard_map(
        on_device_fast if small_slice else on_device,
        mesh=mesh,
        in_specs=placed,
        out_specs=(
            P("rep", "seq", None),
            P("rep", "seq", None),
            P("seq", None),
            P("seq", None),
            P("seq", None),
            P("seq", None),
            P(None, "seq"),
            P(None, "seq"),
            P(None, "seq"),
            P("seq"),
        ),
        check_vma=False,
    )
```

```python
import math

import jax
import jax.numpy as jnp
from jax import lax
from jax.experimental import pallas as pl
from jax.experimental.pallas import tpu as pltpu
from jax.sharding import PartitionSpec as P

HEADS = 12
HD = 64


norm_eps = 1e-05
floor_score = -1e30


def layer_norm(values, gain, shift):
    center = values - jnp.mean(values, axis=-1, keepdims=True)
    spread = jnp.mean(center * center, axis=-1, keepdims=True)
    return center * lax.rsqrt(spread + norm_eps) * gain + shift


def head_split(matrix):
    return matrix.reshape(matrix.shape[0], HEADS, HD)


def masked_scores(queries, query_seg, query_pos, key_piece, seg_piece, offset):
    rows = key_piece.shape[0]
    scores = jnp.einsum(
        "qhd,khd->hqk", queries, head_split(key_piece), preferred_element_type=jnp.float32
    ) * HD ** (-0.5)
    key_pos = offset + jnp.arange(rows, dtype=jnp.int32)
    allowed = (query_seg[:, None] == seg_piece[None, :]) & (key_pos[None, :] <= query_pos[:, None])
    return (jnp.where(allowed[None], scores, floor_score), allowed)


def forward_block(running, pieces, offset, queries, query_seg, query_pos):
    top_run, total_run, accum = running
    key_piece, value_piece, seg_piece = pieces
    scores, allowed = masked_scores(queries, query_seg, query_pos, key_piece, seg_piece, offset)
    top_new = jnp.maximum(top_run, jnp.max(scores, axis=-1))
    probs = jnp.where(allowed[None], jnp.exp(scores - top_new[:, :, None]), 0.0)
    factor = jnp.exp(top_run - top_new)
    total_new = total_run * factor + jnp.sum(probs, axis=-1)
    update = jnp.einsum(
        "hqk,khd->qhd",
        probs.astype(jnp.bfloat16),
        head_split(value_piece),
        preferred_element_type=jnp.float32,
    )
    return (top_new, total_new, accum * factor.T[:, :, None] + update)


def in_blocks(block_fn, running, pieces):
    rows = pieces[0].shape[0]
    size = math.gcd(rows, 1024)
    stacked = tuple((member.reshape((rows // size, size) + member.shape[1:]) for member in pieces))
    offsets = jnp.arange(rows // size, dtype=jnp.int32) * size

    def scan_step(state_now, element):
        return (block_fn(state_now, element[0], element[1]), None)

    running, _unused = lax.scan(scan_step, running, (stacked, offsets))
    return running


def backward_block(
    number,
    state_now,
    whole,
    queries,
    query_seg,
    query_pos,
    grad_heads,
    log_total,
    delta,
    block_rows,
):
    grad_query, term = state_now
    offset = number * block_rows
    key_piece = lax.dynamic_slice_in_dim(whole[0], offset, block_rows, 0)
    value_piece = lax.dynamic_slice_in_dim(whole[1], offset, block_rows, 0)
    seg_piece = lax.dynamic_slice_in_dim(whole[2], offset, block_rows, 0)
    scores, allowed = masked_scores(queries, query_seg, query_pos, key_piece, seg_piece, offset)
    probs = jnp.where(allowed[None], jnp.exp(scores - log_total[:, :, None]), 0.0)
    grad_probs = jnp.einsum(
        "qhd,khd->hqk", grad_heads, head_split(value_piece), preferred_element_type=jnp.float32
    )
    grad_scores = (probs * (grad_probs - delta[:, :, None])).astype(jnp.bfloat16)
    grad_query = grad_query + jnp.einsum(
        "hqk,khd->qhd", grad_scores, head_split(key_piece), preferred_element_type=jnp.float32
    )
    grad_key = jnp.einsum(
        "hqk,qhd->khd", grad_scores, queries, preferred_element_type=jnp.float32
    ) * HD ** (-0.5)
    grad_value = jnp.einsum(
        "hqk,qhd->khd", probs.astype(jnp.bfloat16), grad_heads, preferred_element_type=jnp.float32
    )
    joined = jnp.concatenate(
        [grad_key.reshape(block_rows, -1), grad_value.reshape(block_rows, -1)], axis=1
    )
    term = lax.dynamic_update_slice_in_dim(term, joined, offset, 0)
    return (grad_query, term)


def on_device(
    tokens,
    segment_ids,
    query_key_value_weight,
    output_weight,
    up_weight,
    down_weight,
    ln_gains,
    ln_biases,
    biases,
    up_projection_bias,
    cotangent,
):
    gathered = (
        lax.all_gather(query_key_value_weight, "seq", axis=0, tiled=True),
        lax.all_gather(output_weight, "seq", axis=0, tiled=True),
        lax.all_gather(up_weight, "seq", axis=0, tiled=True),
        lax.all_gather(down_weight, "seq", axis=0, tiled=True),
        lax.all_gather(ln_gains, "seq", axis=1, tiled=True),
        lax.all_gather(ln_biases, "seq", axis=1, tiled=True),
        lax.all_gather(biases, "seq", axis=1, tiled=True),
        lax.all_gather(up_projection_bias, "seq", axis=0, tiled=True),
    )
    full_qkv, full_out, full_up, full_down, gains_all, shifts_all, biases_all, up_shift = gathered
    gains_f = gains_all.astype(jnp.float32)
    shifts_f = shifts_all.astype(jnp.float32)
    biases_f = biases_all.astype(jnp.float32)
    up_shift_f = up_shift.astype(jnp.float32)
    tokens_f = tokens[0].astype(jnp.float32)
    seg_local = segment_ids[0]
    tok_rows = tokens_f.shape[0]
    width = tokens_f.shape[1]
    seqlen = tok_rows * lax.axis_size("seq")
    query_pos = lax.axis_index("seq") * tok_rows + jnp.arange(tok_rows, dtype=jnp.int32)
    hidden_first = layer_norm(tokens_f, gains_f[0], shifts_f[0]).astype(jnp.bfloat16)
    query_key_value_bias = jnp.concatenate(
        [biases_f[0], jnp.zeros((width,), jnp.float32), biases_f[1]]
    )
    projected_rows = (
        jnp.dot(hidden_first, full_qkv, preferred_element_type=jnp.float32) + query_key_value_bias
    ).astype(jnp.bfloat16)
    queries = head_split(projected_rows[:, :width])
    key_rows = projected_rows[:, width : 2 * width]
    value_rows = projected_rows[:, 2 * width :]
    initial = (
        jnp.full((HEADS, tok_rows), floor_score, jnp.float32),
        jnp.zeros((HEADS, tok_rows), jnp.float32),
        jnp.zeros((tok_rows, HEADS, HD), jnp.float32),
    )

    def block_fn(running, pieces, offset):
        return forward_block(running, pieces, offset, queries, seg_local, query_pos)

    block_rows = math.gcd(seqlen, 1024)
    key_end = (lax.axis_index("seq") + 1) * tok_rows
    block_count = (key_end + block_rows - 1) // block_rows
    top_run, total_run, accum = in_blocks(
        block_fn,
        initial,
        (
            lax.all_gather(key_rows, "seq", axis=0, tiled=True),
            lax.all_gather(value_rows, "seq", axis=0, tiled=True),
            lax.all_gather(seg_local, "seq", axis=0, tiled=True),
        ),
    )
    log_total = top_run + jnp.log(total_run)
    attended_f = accum / total_run.T[:, :, None]
    attention_result = attended_f.reshape(tok_rows, width).astype(jnp.bfloat16)
    residual_first = (
        tokens_f
        + jnp.dot(attention_result, full_out, preferred_element_type=jnp.float32)
        + biases_f[2]
    )
    hidden_second = layer_norm(residual_first, gains_f[1], shifts_f[1]).astype(jnp.bfloat16)
    upward_rows = jnp.dot(hidden_second, full_up, preferred_element_type=jnp.float32) + up_shift_f
    activated_f, gelu_back = jax.vjp(jax.nn.gelu, upward_rows)
    activation_values = activated_f.astype(jnp.bfloat16)
    result = (
        residual_first
        + jnp.dot(activation_values, full_down, preferred_element_type=jnp.float32)
        + biases_f[3]
    )
    grad_y = cotangent[0]
    grad_y_f = grad_y.astype(jnp.float32)
    grad_down = jnp.einsum(
        "tf,td->fd", activation_values, grad_y, preferred_element_type=jnp.float32
    )
    grad_act = jnp.einsum("td,fd->tf", grad_y, full_down, preferred_element_type=jnp.float32)
    grad_up_pre = gelu_back(grad_act)[0].astype(jnp.bfloat16)
    grad_up = jnp.einsum(
        "td,tf->df", hidden_second, grad_up_pre, preferred_element_type=jnp.float32
    )
    grad_hidden_two = jnp.einsum(
        "tf,df->td", grad_up_pre, full_up, preferred_element_type=jnp.float32
    )
    _unused, norm_two_back = jax.vjp(layer_norm, residual_first, gains_f[1], shifts_f[1])
    grad_sum_part, grad_gain_two, grad_shift_two = norm_two_back(grad_hidden_two)
    grad_first = grad_y_f + grad_sum_part
    grad_first_bf = grad_first.astype(jnp.bfloat16)
    grad_out_w = jnp.einsum(
        "td,te->de", attention_result, grad_first_bf, preferred_element_type=jnp.float32
    )
    grad_attended = jnp.einsum(
        "te,de->td", grad_first_bf, full_out, preferred_element_type=jnp.float32
    ).astype(jnp.bfloat16)
    grad_heads = head_split(grad_attended)
    delta = jnp.einsum("qhd,qhd->hq", grad_heads.astype(jnp.float32), attended_f)
    whole = (
        lax.all_gather(key_rows, "seq", axis=0, tiled=True),
        lax.all_gather(value_rows, "seq", axis=0, tiled=True),
        lax.all_gather(seg_local, "seq", axis=0, tiled=True),
    )

    def backward_step(number, state_now):
        return backward_block(
            number,
            state_now,
            whole,
            queries,
            seg_local,
            query_pos,
            grad_heads,
            log_total,
            delta,
            block_rows,
        )

    start_state = (
        jnp.zeros((tok_rows, HEADS, HD), jnp.float32),
        jnp.zeros((seqlen, 2 * width), jnp.float32),
    )
    grad_query, term = lax.fori_loop(0, block_count, backward_step, start_state)
    grad_kv = lax.psum_scatter(term, "seq", scatter_dimension=0, tiled=True).astype(jnp.bfloat16)
    grad_q = (grad_query * HD ** (-0.5)).reshape(tok_rows, width).astype(jnp.bfloat16)
    grad_proj = jnp.concatenate([grad_q, grad_kv], axis=1)
    grad_qkv_w = jnp.einsum(
        "td,te->de", hidden_first, grad_proj, preferred_element_type=jnp.float32
    )
    grad_hidden_one = jnp.einsum(
        "te,de->td", grad_proj, full_qkv, preferred_element_type=jnp.float32
    )
    _unused_two, norm_one_back = jax.vjp(layer_norm, tokens_f, gains_f[0], shifts_f[0])
    grad_in_part, grad_gain_one, grad_shift_one = norm_one_back(grad_hidden_one)
    grad_tokens = grad_first + grad_in_part
    grad_proj_f = grad_proj.astype(jnp.float32)
    grad_bias_rows = jnp.stack(
        [
            jnp.sum(grad_proj_f[:, :width], axis=0),
            jnp.sum(grad_proj_f[:, 2 * width :], axis=0),
            jnp.sum(grad_first, axis=0),
            jnp.sum(grad_y_f, axis=0),
        ]
    )
    grad_up_shift = jnp.sum(grad_up_pre.astype(jnp.float32), axis=0)
    grad_gains = jnp.stack([grad_gain_one, grad_gain_two])
    grad_shifts = jnp.stack([grad_shift_one, grad_shift_two])
    shares = (
        lax.psum_scatter(grad_qkv_w, "seq", scatter_dimension=0, tiled=True),
        lax.psum_scatter(grad_out_w, "seq", scatter_dimension=0, tiled=True),
        lax.psum_scatter(grad_up, "seq", scatter_dimension=0, tiled=True),
        lax.psum_scatter(grad_down, "seq", scatter_dimension=0, tiled=True),
        lax.psum_scatter(grad_gains, "seq", scatter_dimension=1, tiled=True),
        lax.psum_scatter(grad_shifts, "seq", scatter_dimension=1, tiled=True),
        lax.psum_scatter(grad_bias_rows, "seq", scatter_dimension=1, tiled=True),
        lax.psum_scatter(grad_up_shift, "seq", scatter_dimension=0, tiled=True),
    )
    totals = (
        lax.psum(shares[0].astype(jnp.bfloat16), "rep").astype(jnp.float32),
        lax.psum(shares[1].astype(jnp.bfloat16), "rep").astype(jnp.float32),
        lax.psum(shares[2].astype(jnp.bfloat16), "rep").astype(jnp.float32),
        lax.psum(shares[3].astype(jnp.bfloat16), "rep").astype(jnp.float32),
        lax.psum(shares[4].astype(jnp.bfloat16), "rep").astype(jnp.float32),
        lax.psum(shares[5].astype(jnp.bfloat16), "rep").astype(jnp.float32),
        lax.psum(shares[6].astype(jnp.bfloat16), "rep").astype(jnp.float32),
        lax.psum(shares[7].astype(jnp.bfloat16), "rep").astype(jnp.float32),
    )
    return (
        result.astype(jnp.bfloat16)[None],
        grad_tokens[None],
        totals[0],
        totals[1],
        totals[2],
        totals[3],
        totals[4],
        totals[5],
        totals[6],
        totals[7],
    )


def f32(value):
    return value.astype(jnp.float32)


def b16(value):
    return value.astype(jnp.bfloat16)


def dot_nn(left, right):
    return jnp.dot(left, right, preferred_element_type=jnp.float32)


def dot_nt(left, right):
    return lax.dot_general(
        left, right, (((1,), (1,)), ((), ())), preferred_element_type=jnp.float32
    )


def dot_tn(left, right):
    return lax.dot_general(
        left, right, (((0,), (0,)), ((), ())), preferred_element_type=jnp.float32
    )


def norm_parts(values):
    center = values - jnp.mean(values, axis=-1, keepdims=True)
    rate = lax.rsqrt(jnp.mean(center * center, axis=-1, keepdims=True) + norm_eps)
    return center * rate, rate


def norm_back(grad, hat, rate, gain):
    scaled = grad * gain
    return rate * (
        scaled
        - jnp.mean(scaled, axis=-1, keepdims=True)
        - hat * jnp.mean(scaled * hat, axis=-1, keepdims=True)
    )


def place():
    rep, seq = lax.axis_index("rep"), lax.axis_index("seq")
    return lax.div(rep, 2), lax.rem(rep, 2), lax.rem(seq, 2), lax.div(seq, 2)


def piece_shard(number, y, z):
    if number < 3:
        return 2 * lax.rem(z + 3 - number, 4) + y
    return 2 * lax.rem(z + 7 - number, 4) + 1 - y


def pack96(parts):
    lane = lax.broadcasted_iota(jnp.int32, parts[0].shape, 1)
    one, two, three = (pltpu.roll(parts[k], 128 - 32 * k, 1) for k in (1, 2, 3))
    return jnp.concatenate(
        [
            jnp.where(lane < 96, parts[0], one),
            jnp.where(lane < 64, one, two),
            jnp.where(lane < 32, two, three),
        ],
        axis=1,
    )


def unpack96(block):
    tiles = [block[:, 128 * k : 128 * k + 128] for k in range(3)]
    lane = lax.broadcasted_iota(jnp.int32, tiles[0].shape, 1)
    return [
        tiles[0],
        jnp.where(lane < 32, pltpu.roll(tiles[0], 32, 1), pltpu.roll(tiles[1], 32, 1)),
        jnp.where(lane < 64, pltpu.roll(tiles[1], 64, 1), pltpu.roll(tiles[2], 64, 1)),
        pltpu.roll(tiles[2], 96, 1),
    ]


def choose(parts, index):
    out = parts[0]
    for number in range(1, len(parts)):
        out = jnp.where(index == number, parts[number], out)
    return out


class Copies:
    def __init__(self, sems, first=0):
        self.sems = sems
        self.first = first
        self.held = []

    def add(self, source, target):
        copy = pltpu.make_async_copy(source, target, self.sems.at[self.first + len(self.held)])
        copy.start()
        self.held.append(copy)

    def wait(self):
        for copy in self.held:
            copy.wait()
        self.held = []


def corners(x, c):
    return ((x, c), (1 - x, c), (x, 1 - c), (1 - x, 1 - c))


def fetch_qkv(copies, own, groups, full, full_out=None, own_out=None):
    x, c, y, z = place()
    rows = own.shape[0]
    half, width = rows // 2, own.shape[1] // 3
    row = pl.multiple_of((2 * z + y) * rows, 16)
    copies.add(own, full.at[pl.ds(row, rows), :])
    if full_out is not None:
        copies.add(own_out, full_out.at[pl.ds(row, rows), :])
    wide, side = 3 * width // 2, width // 2
    for number in range(7):
        for (xx, cc), group in zip(corners(x, c), groups, strict=True):
            piece = piece_of(group, number)
            at = pl.ds(pl.multiple_of(piece_shard(number, y, z) * rows + half * cc, 16), half)
            copies.add(
                piece.at[pl.ds(0, half), pl.ds(0, wide)],
                full.at[at, pl.ds(pl.multiple_of(wide * xx, 128), wide)],
            )
            if full_out is not None:
                copies.add(
                    piece.at[pl.ds(0, half), pl.ds(wide, side)],
                    full_out.at[at, pl.ds(pl.multiple_of(side * xx, 128), side)],
                )


def piece_of(group, number):
    behind, across, behind_across = group
    if number < 3:
        return behind.at[number]
    return across.at[0] if number == 3 else behind_across.at[number - 4]


def mask_bias(start, me, tok, target):
    keys, lanes = target.shape
    key_pos = (me - 4) * tok + lax.broadcasted_iota(jnp.int32, (keys, lanes), 0)
    lane = lax.broadcasted_iota(jnp.int32, (keys, lanes), 1)
    query_pos = me * tok + jnp.where(lane >= tok, lane - tok, lane)
    target[...] = jnp.where((key_pos >= start) & (key_pos <= query_pos), 0.0, floor_score)


def pair_stack(rows):
    lane = lax.broadcasted_iota(jnp.int32, rows.shape, 1)
    zero = jnp.zeros_like(rows)
    return jnp.concatenate([jnp.where(lane < HD, rows, zero), jnp.where(lane < HD, zero, rows)], axis=0)


def pair_join(transposed):
    both = transposed.T
    tok = both.shape[0] // 2
    lane = lax.broadcasted_iota(jnp.int32, (tok, 2 * HD), 1)
    return jnp.where(lane < HD, both[:tok], both[tok:])


def prep_kernel(
    tokens, segs, qkv, out, up, down, gains, shifts, biases, up_bias,
    t_out, q_out, f_out,
    scratch, wide, held_g, held_s, held_b, ids, line, sems,
):
    x, c, _y, _z = place()
    tok, width = tokens.shape[1:]
    rows = qkv.shape[0]
    half, side = rows // 2, width // 2
    p = 2 * x + c
    at = pl.ds(pl.multiple_of(half * c, 16), half)
    copies, others = Copies(sems), Copies(sems, 5)
    for source, target in ((gains, held_g), (shifts, held_s), (biases, held_b)):
        copies.add(source, target)
    copies.add(segs, ids)
    copies.add(up_bias, line)
    others.add(up, wide)
    wide_cols = 3 * side
    others.add(
        qkv.at[at, pl.ds(pl.multiple_of(wide_cols * x, 128), wide_cols)],
        q_out.at[pl.ds(0, half), pl.ds(0, wide_cols)],
    )
    others.add(
        out.at[at, pl.ds(pl.multiple_of(side * x, 128), side)],
        q_out.at[pl.ds(0, half), pl.ds(wide_cols, side)],
    )
    others.add(tokens.at[0], t_out.at[pl.ds(0, tok), :])
    others.add(down.at[pl.ds(pl.multiple_of(rows * p, 16), rows), :], f_out.at[pl.ds(rows, rows), :])
    copies.wait()
    scratch[...] = jnp.zeros_like(scratch)
    for first, held in ((0, held_g), (2, held_s), (4, held_b)):
        scratch[pl.ds(first, held.shape[0]), pl.ds(0, rows)] = f32(held[...])
    parts = unpack96(jnp.broadcast_to(f32(line[...]).reshape(1, line.shape[0]), (8, line.shape[0])))
    lane = lax.broadcasted_iota(jnp.int32, (8, 128), 1)
    row = lax.broadcasted_iota(jnp.int32, (8, 128), 0)
    ups = jnp.zeros((8, 128), jnp.float32)
    for number in range(4):
        ups = jnp.where((row == number) & (lane < rows), parts[number], ups)
    smalls = b16(jnp.concatenate([scratch[:, pl.ds(0, 128)], ups], axis=0))
    q_out[pl.ds(0, 16), pl.ds(2 * width, 128)] = smalls
    q_out[pl.ds(16, half - 16), pl.ds(2 * width, 128)] = jnp.zeros((half - 16, 128), jnp.bfloat16)
    scratch[...] = jnp.zeros_like(scratch)
    scratch[pl.ds(0, 1), pl.ds(0, tok)] = f32(ids[...])
    t_out[pl.ds(tok, 8), :] = b16(scratch[...])
    others.wait()
    for group in range(2):
        parts = []
        for shard in range(4 * group, 4 * group + 4):
            parts.append(choose(unpack96(f32(wide[:, pl.ds(384 * shard, 384)])), p))
        f_out[pl.ds(0, rows), pl.ds(384 * group, 384)] = b16(pack96(parts))


def front_kernel(
    seg, xo, x1, x2, x3, x4, first, own, own_o,
    g0, g1, g2, g3, g4, g5, g6, g7, g8, g9, g10, g11,
    q_out, kv_out, h_out, a_out, lse_out, start_out, vec_out, upb_out, wo_out, r_out, h2_out,
    full, small, bias, sems, vsems,
):
    x, c, y, z = place()
    me = 2 * z + y
    p = 2 * x + c
    tok, width = q_out.shape
    copies, vcopies = Copies(sems), Copies(vsems)
    vcopies.add(first.at[pl.ds(0, 16), pl.ds(2 * width, 128)], small.at[me])
    for number in range(7):
        source = piece_of((g0, g1, g2), number)
        vcopies.add(source.at[pl.ds(0, 16), pl.ds(2 * width, 128)], small.at[piece_shard(number, y, z)])
    groups = ((g0, g1, g2), (g3, g4, g5), (g6, g7, g8), (g9, g10, g11))
    fetch_qkv(copies, own, groups, full, wo_out, own_o)
    blocks = (xo, x1, x2, x3, x4)
    lane1 = lax.broadcasted_iota(jnp.int32, (1, tok), 1)
    start = jnp.full(seg.shape, 1 << 30, jnp.int32)
    for number in range(4):
        first_pos = jnp.full((1, 1), 1 << 30, jnp.int32)
        for back in range(5):
            ids = f32(blocks[back][pl.ds(tok, 8), pl.ds(0, tok)])[:1]
            pos = (me - back) * tok + lane1
            hit = (ids == float(number)) & (pos >= 0)
            first_pos = jnp.minimum(
                first_pos, jnp.min(jnp.where(hit, pos, 1 << 30), axis=1, keepdims=True)
            )
        start = jnp.where(seg[...] == number, first_pos, start)
    start_out[...] = start
    mask_bias(start, me, tok, bias)
    vcopies.wait()
    for group in range(2):
        held = [f32(small[4 * group + k]) for k in range(4)]
        vec_out[:, pl.ds(384 * group, 384)] = pack96([block[:8] for block in held])
        upb_out[:, pl.ds(384 * group, 384)] = pack96(
            [choose([jnp.broadcast_to(block[k : k + 1], (8, 128)) for k in range(8, 12)], p) for block in held]
        )
    vec = vec_out[...]
    for back in range(5):
        hat, _rate = norm_parts(f32(blocks[back][pl.ds(0, tok), :]))
        h_out[pl.ds((4 - back) * tok, tok), :] = b16(hat * vec[0:1] + vec[2:3])
    copies.wait()
    q_out[...] = b16(dot_nn(h_out[pl.ds(4 * tok, tok), :], full[:, pl.ds(0, width)]) + vec[4:5])

    def project(number, carry):
        col = pl.multiple_of(number * 256, 256)
        shift = jnp.where(number >= width // 256, 1.0, 0.0)
        bias_at = lax.rem(number, width // 256)
        piece = vec_out[pl.ds(5, 1), pl.ds(pl.multiple_of(bias_at * 256, 256), 256)]
        kv_out[:, pl.ds(col, 256)] = b16(
            dot_nn(h_out[...], full[:, pl.ds(pl.multiple_of(width + col, 256), 256)]) + piece * shift
        )
        return carry

    lax.fori_loop(0, 2 * width // 256, project, 0)

    def pair(number, carry):
        col = pl.multiple_of(number * 128, 128)
        queries = pair_stack(q_out[:, pl.ds(col, 128)] * jnp.bfloat16(0.125))
        scores = dot_nt(kv_out[:, pl.ds(col, 128)], queries) + bias[...]
        top = jnp.max(scores, axis=0, keepdims=True)
        probs = jnp.exp(scores - top)
        total = jnp.sum(probs, axis=0, keepdims=True)
        mixed = dot_tn(kv_out[:, pl.ds(pl.multiple_of(width + col, 128), 128)], b16(probs))
        a_out[:, pl.ds(col, 128)] = b16(pair_join(mixed / total))
        lse_out[number] = top + jnp.log(total)
        return carry

    lax.fori_loop(0, width // 128, pair, 0)
    residual = f32(xo[pl.ds(0, tok), :]) + dot_nn(a_out[...], wo_out[...]) + vec[6:7]
    r_out[...] = residual
    hat, _rate = norm_parts(residual)
    h2_out[...] = b16(hat * vec[1:2] + vec[3:4])


def feed_tokens(h2, dy, w_up, w_down, upb, act_out, du_out, y_acc, dh_acc):
    root = math.sqrt(2.0 / math.pi)
    chunk = 256

    def feed(number, carry):
        col = pl.multiple_of(number * chunk, chunk)
        pre = dot_nn(h2[...], w_up[:, pl.ds(col, chunk)]) + upb[pl.ds(0, 1), pl.ds(col, chunk)]
        square = pre * pre
        bend = jnp.tanh(root * pre * (1.0 + 0.044715 * square))
        act = b16(0.5 * pre * (1.0 + bend))
        slope = 0.5 * (1.0 + bend) + 0.5 * pre * (1.0 - bend * bend) * (
            root * (1.0 + 3.0 * 0.044715 * square)
        )
        low = b16(dot_nt(dy[...], w_down[pl.ds(col, chunk), :]) * slope)
        act_out[:, pl.ds(col, chunk)] = act
        du_out[:, pl.ds(col, chunk)] = low
        return carry

    lax.fori_loop(0, w_up.shape[1] // chunk, feed, 0)
    dh_acc[...] = dot_nt(du_out[...], w_up[...])
    y_acc[...] = dot_nn(act_out[...], w_down[...])


def assemble_kernel(own, z1, z2, z3, y0, y13, wu_out, wd_out, sems):
    _x, _c, y, z = place()
    rows = own.shape[0] // 2
    copies = Copies(sems)
    pieces = [(own, 2 * z + y)]
    for number, ref in ((0, z1), (1, z2), (2, z3), (3, y0)):
        pieces.append((ref, piece_shard(number, y, z)))
    for number, first in ((4, 0), (6, 2 * rows)):
        pieces.append((y13.at[pl.ds(first, 2 * rows), :], piece_shard(number, y, z)))
    for ref, shard in pieces:
        at = pl.ds(pl.multiple_of(shard * rows, 16), rows)
        copies.add(ref.at[pl.ds(0, rows), :], wu_out.at[at, :])
        copies.add(ref.at[pl.ds(rows, rows), :], wd_out.at[at, :])
    copies.wait()


def near_kernel(
    h_own, h_c, dy_own, dy_c, upb, y2, _wu, _wd,
    h2, dy, act_out, du_out, keep_out, send_out, wu_out, wd_out,
    y_acc, dh_acc, sems,
):
    _x, _c, y, z = place()
    tok, width = h_own.shape
    rows = width // 8
    copies = Copies(sems)
    at = pl.ds(pl.multiple_of(piece_shard(5, y, z) * rows, 16), rows)
    copies.add(y2.at[pl.ds(0, rows), :], wu_out.at[at, :])
    copies.add(y2.at[pl.ds(rows, rows), :], wd_out.at[at, :])
    h2[pl.ds(0, tok), :] = h_own[...]
    h2[pl.ds(tok, tok), :] = h_c[...]
    dy[pl.ds(0, tok), :] = dy_own[...]
    dy[pl.ds(tok, tok), :] = dy_c[...]
    copies.wait()
    feed_tokens(h2, dy, wu_out, wd_out, upb, act_out, du_out, y_acc, dh_acc)
    keep_out[0] = dh_acc[pl.ds(0, tok), :]
    keep_out[1] = y_acc[pl.ds(0, tok), :]
    send_out[0] = b16(dh_acc[pl.ds(tok, tok), :])
    send_out[1] = b16(y_acc[pl.ds(tok, tok), :])


def far_kernel(
    h_x, h_xc, dy_x, dy_xc, upb, w_up, w_down, h_near, dy_near, act_near, du_near,
    hs, dys, acts, dus, keep_out, send_out,
    y_acc, dh_acc, sems,
):
    tok = h_x.shape[0]
    copies = Copies(sems)
    for source, target in ((h_near, hs), (dy_near, dys), (act_near, acts), (du_near, dus)):
        copies.add(source, target.at[pl.ds(0, 2 * tok), :])
    later = pl.ds(2 * tok, 2 * tok)
    hs[pl.ds(2 * tok, tok), :] = h_x[...]
    hs[pl.ds(3 * tok, tok), :] = h_xc[...]
    dys[pl.ds(2 * tok, tok), :] = dy_x[...]
    dys[pl.ds(3 * tok, tok), :] = dy_xc[...]
    feed_tokens(
        hs.at[later, :], dys.at[later, :], w_up, w_down, upb, acts.at[later, :], dus.at[later, :], y_acc, dh_acc
    )
    keep_out[0] = dh_acc[pl.ds(0, tok), :]
    keep_out[1] = y_acc[pl.ds(0, tok), :]
    send_out[0] = b16(dh_acc[pl.ds(tok, tok), :])
    send_out[1] = b16(y_acc[pl.ds(tok, tok), :])
    copies.wait()


def weights_kernel(hs, dys, acts, dus, u_out, d_out, upb_out, stage, sems):
    _x, _c, y, z = place()
    width = hs.shape[1]
    rows = width // 8
    upb_out[...] = jnp.sum(f32(dus[...]), axis=0, keepdims=True)

    def weight(number, carry):
        col = pl.multiple_of(number * 256, 256)
        stage[0, pl.ds(col, 256), :] = b16(dot_tn(hs[:, pl.ds(col, 256)], dus[...]))
        stage[1, pl.ds(col, 256), :] = b16(dot_tn(acts[:, pl.ds(col, 256)], dys[...]))
        return carry

    lax.fori_loop(0, width // 256, weight, 0)
    outs = Copies(sems)
    for shard in range(8):
        zz = lax.rem(shard // 2 + 4 - z, 4)
        yy = jnp.where(y == shard % 2, 0, 1)
        outs.add(stage.at[0, pl.ds(shard * rows, rows), :], u_out.at[yy, zz])
        outs.add(stage.at[1, pl.ds(shard * rows, rows), :], d_out.at[yy, zz])
    outs.wait()


def scatter(stage, other, mine, sems):
    x, c, y, z = place()
    outs = Copies(sems)
    for shard in range(8):
        zz = lax.rem(shard // 2 + 4 - z, 4)
        yy = jnp.where(y == shard % 2, 0, 1)
        for xx in range(2):
            far = jnp.where(x == xx, 0, 1)
            outs.add(stage.at[1 - c, xx, shard], other.at[far, yy, zz])
            outs.add(stage.at[c, xx, shard], mine.at[far, yy, zz])
    outs.wait()


def post_kernel(
    residual, own, near, across, dy_in, vec_in, w_out, a_in,
    dr_out, da_out, dw_out, vec_out,
):
    vec = vec_in[...]
    grad_hidden = own[0] + f32(near[0]) + f32(across[...])
    hat, rate = norm_parts(residual[...])
    dy = f32(dy_in[...])
    grad_first = dy + norm_back(grad_hidden, hat, rate, vec[1:2])
    dr_out[...] = grad_first
    low = b16(grad_first)
    da_out[...] = b16(dot_nt(low, w_out[...]))
    dw_out[...] = dot_tn(a_in[...], low)
    zero = jnp.zeros((1, dy.shape[1]), jnp.float32)
    vec_out[...] = jnp.concatenate(
        [
            zero,
            jnp.sum(grad_hidden * hat, axis=0, keepdims=True),
            zero,
            jnp.sum(grad_hidden, axis=0, keepdims=True),
            zero,
            zero,
            jnp.sum(grad_first, axis=0, keepdims=True),
            jnp.sum(dy, axis=0, keepdims=True),
        ],
        axis=0,
    )


def back_pairs(first, q_in, kv_in, lse_in, da_in, bias, dq, dkv):
    width = q_in.shape[1]

    def pair(number, carry):
        col = pl.multiple_of((first + number) * 128, 128)
        vcol = pl.multiple_of(width + col, 128)
        to = pl.multiple_of(number * 128, 128)
        queries = pair_stack(q_in[:, pl.ds(col, 128)] * jnp.bfloat16(0.125))
        grads = pair_stack(da_in[:, pl.ds(col, 128)])
        keys = kv_in[:, pl.ds(col, 128)]
        probs = jnp.exp(dot_nt(keys, queries) + bias[...] - lse_in[first + number])
        dkv[:, pl.ds(pl.multiple_of(width // 2 + to, 128), 128)] = b16(dot_nn(b16(probs), grads))
        term = probs * dot_nt(kv_in[:, pl.ds(vcol, 128)], grads)
        low = b16(term - probs * jnp.sum(term, axis=0, keepdims=True))
        dkv[:, pl.ds(to, 128)] = b16(dot_nn(low, queries))
        dq[:, pl.ds(to, 128)] = b16(pair_join(dot_tn(keys, low)) * 0.125)
        return carry

    lax.fori_loop(0, 3, pair, 0)


def qkv_weight(h_in, dq, dkv, stage, tail):
    tok, part = dq.shape
    keys = h_in.shape[0]

    def weight(number, carry):
        col = pl.multiple_of(number * 384, 384)
        key = dot_tn(h_in[:, pl.ds(col, 384)], dkv[...])
        query = dot_tn(h_in[pl.ds(keys - tok, tok), pl.ds(col, 384)], dq[...])
        for shard in range(4):
            for cc in range(2):
                for xx in range(2):
                    rows = slice(96 * shard + 48 * cc + 24 * xx, 96 * shard + 48 * cc + 24 * xx + 24)
                    blocks = [query[rows], key[rows, :part], key[rows, part:]] + tail(4 * number + shard, 48 * cc + 24 * xx)
                    stage[cc, xx, 4 * number + shard] = b16(jnp.concatenate(blocks, axis=0))
        return carry

    lax.fori_loop(0, 2, weight, 0)


def back_a_kernel(
    start_in, q_in, kv_in, h_in, lse_in, da_in, dw_in,
    other, mine, dq_out, dkv_out,
    bias, stage, sems,
):
    _x, _c, y, z = place()
    mask_bias(start_in[...], 2 * z + y, q_in.shape[0], bias)
    back_pairs(0, q_in, kv_in, lse_in, da_in, bias, dq_out, dkv_out)
    side = q_in.shape[1] // 2

    def out_rows(shard, row):
        rows = dw_in[pl.ds(pl.multiple_of(96 * shard + row, 8), 24), :]
        return [rows[:, :side], rows[:, side:]]

    qkv_weight(h_in, dq_out, dkv_out, stage, out_rows)
    scatter(stage, other, mine, sems)


def back_b_kernel(
    start_in, q_in, kv_in, lse_in, da_in, vec_in, upb_in, dq_a, dkv_a, xo, x1, x2, x3, x4,
    own, g0, g1, g2, g3, g4, g5, g6, g7, g8, g9, g10, g11,
    dq_out, dkv_out, p_own, p_y, p_z, sums_out,
    full, bias, sems,
):
    x, c, y, z = place()
    p = 2 * x + c
    tok, width = q_in.shape
    side = width // 2
    copies = Copies(sems)
    groups = ((g0, g1, g2), (g3, g4, g5), (g6, g7, g8), (g9, g10, g11))
    fetch_qkv(copies, own, groups, full)
    mask_bias(start_in[...], 2 * z + y, tok, bias)
    back_pairs(3, q_in, kv_in, lse_in, da_in, bias, dq_out, dkv_out)
    copies.wait()
    gain_sum = jnp.zeros((1, width), jnp.float32)
    shift_sum = jnp.zeros((1, width), jnp.float32)
    for back, block in enumerate((xo, x1, x2, x3, x4)):
        rows = pl.ds((4 - back) * tok, tok)
        grad = jnp.zeros((tok, width), jnp.float32)
        for number, (dq, dkv) in enumerate(((dq_a, dkv_a), (dq_out, dkv_out))):
            at = number * side
            grad = grad + dot_nt(dkv[rows, pl.ds(0, side)], full[:, pl.ds(width + at, side)])
            grad = grad + dot_nt(dkv[rows, pl.ds(side, side)], full[:, pl.ds(2 * width + at, side)])
            if back == 0:
                grad = grad + dot_nt(dq[...], full[:, pl.ds(at, side)])
        if back == 0:
            p_own[...] = grad
        elif back in (1, 3):
            p_y[back // 2] = b16(grad)
        else:
            p_z[back // 2 - 1] = b16(grad)
        hat, _rate = norm_parts(f32(block[pl.ds(0, tok), :]))
        gain_sum = gain_sum + jnp.sum(grad * hat, axis=0, keepdims=True)
        shift_sum = shift_sum + jnp.sum(grad, axis=0, keepdims=True)
    zero = jnp.zeros((1, width), jnp.float32)
    bias_q = jnp.concatenate([jnp.sum(f32(d[...]), axis=0, keepdims=True) for d in (dq_a, dq_out)], axis=1)
    bias_v = jnp.concatenate(
        [jnp.sum(f32(d[:, pl.ds(side, side)]), axis=0, keepdims=True) for d in (dkv_a, dkv_out)], axis=1
    )
    vec = vec_in[...] + jnp.concatenate(
        [gain_sum, zero, shift_sum, zero, bias_q, bias_v, zero, zero], axis=0
    )
    lane = lax.broadcasted_iota(jnp.int32, (8, 128), 1)
    line = lax.broadcasted_iota(jnp.int32, (8, 128), 0)
    for group in range(2):
        cols = pl.ds(384 * group, 384)
        vec_parts = unpack96(vec[:, 384 * group : 384 * group + 384])
        upb_parts = unpack96(jnp.broadcast_to(upb_in[:, cols], (8, 384)))
        for k in range(4):
            sums_out[4 * group + k] = jnp.concatenate(
                [
                    jnp.where(lane < 96, vec_parts[k], 0.0),
                    jnp.where((lane < 96) & (line == p), upb_parts[k], 0.0),
                ],
                axis=1,
            )


def back_c_kernel(h_in, dq, dkv, sums_in, other, mine, stage, sems):
    blank = jnp.zeros((8, 128), jnp.float32)
    qkv_weight(
        h_in, dq, dkv, stage, lambda shard, _row: [jnp.concatenate([sums_in[shard], blank], axis=1)]
    )
    scatter(stage, other, mine, sems)


def tokens_kernel(own, near, dr, xo, vec_in, grad_out):
    tok = own.shape[0]
    hat, rate = norm_parts(f32(xo[pl.ds(0, tok), :]))
    grad = own[...] + f32(near[...])
    grad_out[...] = dr[...] + norm_back(grad, hat, rate, vec_in[0:1, :])


def finish_f_kernel(f0, fx, fc, fcx, up, down, held):
    x, c, _y, _z = place()
    rows = f0.shape[0] // 2
    for (xx, cc), f in zip(corners(x, c), (f0, fx, fc, fcx), strict=True):
        p = 2 * xx + cc
        held[p] = f[pl.ds(0, rows), :]
        down[pl.ds(pl.multiple_of(rows * p, 16), rows), :] = f32(f[pl.ds(rows, rows), :])
    for group in range(2):
        parts = [unpack96(f32(held[k, :, pl.ds(384 * group, 384)])) for k in range(4)]
        for shard in range(4):
            up[:, pl.ds(384 * (4 * group + shard), 384)] = pack96([part[shard] for part in parts])


def finish_q_kernel(f0, fx, fc, fcx, qkv, out):
    x, c, _y, _z = place()
    side = out.shape[1] // 2
    for (xx, cc), piece in zip(corners(x, c), (f0, fx, fc, fcx), strict=True):
        rows = pl.ds(pl.multiple_of(48 * cc + 24 * xx, 8), 24)
        blocks = f32(piece[...])
        for number in range(3):
            first, second = 24 * number, 24 * (number + 5)
            qkv[rows, pl.ds(2 * side * number, side)] = blocks[first : first + 24]
            qkv[rows, pl.ds(2 * side * number + side, side)] = blocks[second : second + 24]
        out[rows, pl.ds(0, side)] = blocks[72:96]
        out[rows, pl.ds(side, side)] = blocks[96:120]


HB = pl.BlockSpec(memory_space=pltpu.HBM)
VM = pl.BlockSpec(memory_space=pltpu.VMEM)
AN = pl.BlockSpec(memory_space=pl.ANY)


def shape_of(shape, dtype):
    return jax.ShapeDtypeStruct(shape, dtype)


def call(kernel, ins, outs, out_shape, scratch=(), vmem=40, flops=0, moved=0, aliases=None):
    return pl.pallas_call(
        kernel,
        in_specs=ins,
        out_specs=outs,
        out_shape=out_shape,
        scratch_shapes=list(scratch),
        input_output_aliases=aliases or {},
        compiler_params=pltpu.CompilerParams(vmem_limit_bytes=vmem << 20),
        cost_estimate=pl.CostEstimate(flops=flops, bytes_accessed=moved, transcendentals=0),
    )


def fence(*values):
    return lax.optimization_barrier(values)


def swap_rep(value, bit):
    return lax.ppermute(value, "rep", [(k, k ^ bit) for k in range(4)])


def to_core(value):
    return swap_rep(value, 1)


def to_x(value):
    return swap_rep(value, 2)


def to_y(value):
    return lax.ppermute(value, "seq", [(k, k ^ 1) for k in range(8)])


def to_z(value, steps):
    return lax.ppermute(value, "seq", [(k, (k + 2 * steps) % 8) for k in range(8)])


def join(*parts):
    return jnp.concatenate(parts, axis=0)


def on_device_fast(
    tokens,
    segment_ids,
    query_key_value_weight,
    output_weight,
    up_weight,
    down_weight,
    ln_gains,
    ln_biases,
    biases,
    up_projection_bias,
    cotangent,
):
    seq = lax.axis_index("seq")
    y = seq % 2
    tok, width = tokens.shape[1:]
    hidden = up_weight.shape[1]
    keys = 5 * tok
    bf, fl = jnp.bfloat16, jnp.float32
    dma = pltpu.SemaphoreType.DMA
    grad_y = cotangent[0]
    own_tokens, piece_q, piece_f = call(
        prep_kernel,
        [HB] * 10,
        [VM] * 3,
        [
            shape_of((tok + 8, width), bf),
            shape_of((48, 2 * width + 128), bf),
            shape_of((192, width), bf),
        ],
        [
            pltpu.VMEM((8, width), fl),
            pltpu.VMEM((96, hidden), bf),
            pltpu.VMEM((2, 96), bf),
            pltpu.VMEM((2, 96), bf),
            pltpu.VMEM((4, 96), bf),
            pltpu.VMEM((1, tok), jnp.int32),
            pltpu.VMEM((384,), bf),
            dma((10,)),
        ],
        vmem=60, moved=4 * 10**6,
    )(
        tokens, segment_ids, query_key_value_weight, output_weight, up_weight, down_weight,
        ln_gains, ln_biases, biases, up_projection_bias,
    )

    q1, q3, q_y0, dy_x = fence(to_z(piece_q, 1), to_z(piece_q, 3), to_y(piece_q), to_x(grad_y))
    own_tokens, piece_f, q1, q_y0 = fence(own_tokens, piece_f, q1, q_y0, q3, dy_x)[:4]
    q2, x2, q_xy0, f_y0 = fence(to_z(q1, 1), to_z(own_tokens, 1), to_x(q_y0), to_y(piece_f))
    q_z = join(q1, q2, q3)
    q_z, x2 = fence(q_z, x2, q_xy0, f_y0)[:2]
    q_y, q_xz, x4 = fence(to_y(q_z), to_x(q_z), to_z(x2, 1))
    near = jnp.where(y == 0, own_tokens, x2)
    far = jnp.where(y == 0, x2, x4)
    near_far, q_y, piece_f = fence(jnp.stack([near, far]), q_y, piece_f, q_xz)[:3]
    crossed, q_xy, f1, f3 = fence(to_y(near_far), to_x(q_y), to_z(piece_f, 1), to_z(piece_f, 3))
    x1, x3 = crossed[0], crossed[1]
    q_z, q_y0, q_y, q_xz, q_xy0, q_xy = fence(q_z, q_y0, q_y, q_xz, q_xy0, q_xy, f1, f3, crossed)[:6]
    q_cz, q_cy0, q_cy, q_cxz, q_cxy0, q_cxy = fence(
        *(to_core(v) for v in (q_z, q_y0, q_y, q_xz, q_xy0, q_xy))
    )
    f_13, f_1, q_cz = fence(join(f1, f3), f1, q_cz, q_cy0, q_cy, q_cxz, q_cxy0, q_cxy)[:3]
    f_y13, f2 = to_y(f_13), to_z(f_1, 1)
    dy_c, dy_xc = to_core(grad_y), to_core(dy_x)

    def pieces(value):
        return value.reshape(value.shape[0] // 48, 48, value.shape[1])

    got_q = [
        pieces(v)
        for v in (q_z, q_y0, q_y, q_xz, q_xy0, q_xy, q_cz, q_cy0, q_cy, q_cxz, q_cxy0, q_cxy)
    ]
    seg = jnp.concatenate([segment_ids, segment_ids], axis=1)
    front = call(
        front_kernel,
        [VM] * 6 + [AN] * 15,
        [VM] * 11,
        [
            shape_of((tok, width), bf),
            shape_of((keys, 2 * width), bf),
            shape_of((keys, width), bf),
            shape_of((tok, width), bf),
            shape_of((width // 128, 1, 2 * tok), fl),
            shape_of((1, 2 * tok), jnp.int32),
            shape_of((8, width), fl),
            shape_of((8, width), fl),
            shape_of((width, width), bf),
            shape_of((tok, width), fl),
            shape_of((tok, width), bf),
        ],
        [
            pltpu.VMEM((width, 3 * width), bf),
            pltpu.VMEM((8, 16, 128), bf),
            pltpu.VMEM((keys, 2 * tok), fl),
            dma((2 + 56,)),
            dma((8,)),
        ],
        flops=7 * 10**9,
        vmem=16, moved=12 * 10**6,
    )(
        seg, own_tokens, x1, x2, x3, x4, piece_q, query_key_value_weight, output_weight, *got_q,
    )
    *front, f_y13, f2, dy_c, dy_xc = fence(*front, f_y13, f2, dy_c, dy_xc)
    queries, kv, normed, attended, lse, start, vec, upb, w_out, residual, hidden_2 = front
    w_half = call(
        assemble_kernel,
        [AN] * 6,
        [VM] * 2,
        [shape_of((width, width), bf)] * 2,
        [dma((14,))],
        vmem=4,
        moved=5 * 10**6,
    )(piece_f, f1, f2, f3, f_y0, f_y13)
    h_x, h_c, f_y2, *w_half = fence(to_x(hidden_2), to_core(hidden_2), to_y(f2), *w_half)
    act = shape_of((2 * tok, width), bf)
    acts = shape_of((4 * tok, width), bf)
    feed_shapes = [shape_of((2, tok, width), fl), shape_of((2, tok, width), bf)]
    feed_scratch = [pltpu.VMEM((2 * tok, width), fl), pltpu.VMEM((2 * tok, width), fl)]
    *near_acts, keep_a, send_a, w_up, w_down = call(
        near_kernel,
        [VM] * 5 + [AN] + [VM] * 2,
        [VM] * 8,
        [act] * 4 + feed_shapes + [shape_of((width, width), bf)] * 2,
        feed_scratch + [dma((2,))],
        flops=3 * 10**9,
        vmem=8,
        moved=6 * 10**6,
        aliases={6: 6, 7: 7},
    )(hidden_2, h_c, grad_y, dy_c, upb, f_y2, *w_half)
    h_xc = to_core(h_x)
    keep_a, send_a, h_xc, w_up = fence(keep_a, send_a, h_xc, w_up)
    came_a = to_core(send_a)
    *all_acts, keep_b, send_b = call(
        far_kernel,
        [VM] * 7 + [AN] * 4,
        [VM] * 6,
        [acts] * 4 + feed_shapes,
        feed_scratch + [dma((4,))],
        flops=3 * 10**9,
        vmem=8, moved=6 * 10**6,
    )(h_x, h_xc, dy_x, dy_xc, upb, w_up, w_down, *near_acts)
    keep_b, send_b, came_a = fence(keep_b, send_b, came_a)
    keep_b, came_b, *all_acts = fence(keep_b, to_core(send_b), *all_acts)
    back_x = to_x(b16(keep_b[0] + f32(came_b[0])))
    u_terms, d_terms, upb_g = call(
        weights_kernel,
        [VM] * 4,
        [AN, AN, VM],
        [shape_of((2, 4, 96, width), bf), shape_of((2, 4, 96, width), bf), shape_of((1, width), fl)],
        [pltpu.VMEM((2, width, width), bf), dma((16,))],
        flops=3 * 10**9,
        vmem=12, moved=6 * 10**6,
    )(*all_acts)
    back_x, u_terms, d_terms, keep_b = fence(back_x, u_terms, d_terms, keep_b)
    u_came = to_y(u_terms[1])
    back_y = to_x(b16(keep_b[1] + f32(came_b[1])))
    grad_first, grad_attended, dw_out, vec_g = call(
        post_kernel,
        [VM] * 8,
        [VM] * 4,
        [
            shape_of((tok, width), fl),
            shape_of((tok, width), bf),
            shape_of((width, width), fl),
            shape_of((8, width), fl),
        ],
        vmem=12,
        flops=10**9,
        moved=4 * 10**6,
    )(residual, keep_a, came_a, back_x, grad_y, vec, w_out, attended)
    back_scratch = [
        pltpu.VMEM((keys, 2 * tok), fl),
    ]
    qa_other, qa_mine, dq_a, dkv_a = call(
        back_a_kernel,
        [VM] * 7,
        [AN] * 2 + [VM] * 2,
        [
            shape_of((2, 2, 4, 120, width // 2), bf),
            shape_of((2, 2, 4, 120, width // 2), bf),
            shape_of((tok, width // 2), bf),
            shape_of((keys, width), bf),
        ],
        back_scratch + [pltpu.VMEM((2, 2, 8, 120, width // 2), bf), dma((32,))],
        flops=5 * 10**9,
        vmem=16, moved=10 * 10**6,
    )(start, queries, kv, normed, lse, grad_attended, dw_out)

    def both(mine, came):
        return lambda *index: f32(mine[index]) + f32(came[index])

    def z_sum(part, *came):
        return b16(part(0) + sum(f32(v) for v in came))

    dq_a, qa_other, u_came, back_y, d_send = fence(
        dq_a, qa_other, u_came, back_y, d_terms[1]
    )
    d_came, qa_came = to_y(d_send), to_core(qa_other)
    u_part = both(u_terms[0], u_came)
    u_z = [to_z(b16(u_part(step)), step) for step in (1, 2, 3)]
    dq_b, dkv_b, p_own, p_y, p_z, sums = call(
        back_b_kernel,
        [VM] * 14 + [AN] * 13,
        [VM] * 6,
        [
            shape_of((tok, width // 2), bf),
            shape_of((keys, width), bf),
            shape_of((tok, width), fl),
            shape_of((2, tok, width), bf),
            shape_of((2, tok, width), bf),
            shape_of((8, 8, 256), fl),
        ],
        [pltpu.VMEM((width, 3 * width), bf)] + back_scratch + [dma((1 + 28,))],
        flops=6 * 10**9,
        vmem=20, moved=10 * 10**6,
    )(
        start, queries, kv, lse, grad_attended, vec_g, upb_g, dq_a, dkv_a,
        own_tokens, x1, x2, x3, x4, query_key_value_weight, *got_q,
    )
    dq_b, qa_came, d_came, p_y, *u_z = fence(dq_b, qa_came, d_came, p_y, *u_z)
    p_came = to_y(p_y)
    qa_1 = both(qa_mine, qa_came)
    qa_x = to_x(b16(qa_1(1)))
    d_part = both(d_terms[0], d_came)
    d_z2 = to_z(b16(d_part(2)), 1)
    qb_other, qb_mine = call(
        back_c_kernel,
        [VM] * 4,
        [AN] * 2,
        [
            shape_of((2, 2, 4, 80, width // 2), bf),
            shape_of((2, 2, 4, 80, width // 2), bf),
        ],
        [pltpu.VMEM((2, 2, 8, 80, width // 2), bf), dma((32,))],
        flops=3 * 10**9,
        vmem=12, moved=6 * 10**6,
    )(normed, dq_b, dkv_b, sums)
    qb_came = [to_core(qb_other[k]) for k in range(2)]
    *qb_came, qa_x, p_came, d_z2 = fence(*qb_came, qa_x, p_came, d_z2)
    even = y == 0
    sum_own = p_own + jnp.where(even, f32(p_came[0]), 0.0)
    sum_4 = b16(f32(p_z[1]) + jnp.where(even, 0.0, f32(p_came[1])))
    sum_2 = f32(p_z[0]) + jnp.where(even, f32(p_came[1]), f32(p_came[0]))
    def qa_2(*index):
        return qa_1(0, *index) + f32(qa_x[index])

    def qb_1(side, *index):
        return f32(qb_mine[(side,) + index]) + f32(qb_came[side][index])

    qb_x, qa_y, hop, d_z1, d_z3 = fence(
        to_x(b16(qb_1(1))),
        to_y(b16(qa_2(1))),
        to_z(sum_4, 3),
        to_z(b16(d_part(1) + f32(d_z2)), 1),
        to_z(b16(d_part(3)), 3),
    )

    def qb_2(*index):
        return qb_1(0, *index) + f32(qb_x[index])

    f_tot = join(z_sum(u_part, *u_z), z_sum(d_part, d_z1, d_z3))
    f_tot, hop = fence(f_tot, hop)
    qb_y, back_2, f_x = fence(to_y(b16(qb_2(1))), to_z(b16(sum_2 + f32(hop)), 3), to_x(f_tot))

    def q_3(*index):
        first = qa_2(0, *index) + f32(qa_y[index])
        return jnp.concatenate([first, qb_2(0, *index) + f32(qb_y[index])], axis=-2)

    f_tot, f_x, back_2, qb_y = fence(f_tot, f_x, back_2, qb_y)
    grad_tokens = call(
        tokens_kernel, [VM] * 5, VM, shape_of((tok, width), fl), vmem=4, moved=3 * 10**6
    )(sum_own, back_2, grad_first, own_tokens, vec)
    *q_z, f_tot, f_x = fence(*(to_z(b16(q_3(step)), step) for step in (1, 2, 3)), f_tot, f_x)
    q_sum = z_sum(q_3, *q_z)
    q_fx, q_fc, q_fxc = to_x(q_sum), to_core(q_sum), swap_rep(q_sum, 3)
    grad_up, grad_down = call(
        finish_f_kernel,
        [VM] * 4,
        [VM] * 2,
        [shape_of(up_weight.shape, fl), shape_of(down_weight.shape, fl)],
        [pltpu.VMEM((4, 96, width), bf)],
        vmem=8,
        moved=4 * 10**6,
    )(f_tot, f_x, to_core(f_tot), to_core(f_x))
    q_fx, q_fc, q_fxc, grad_up, grad_down = fence(q_fx, q_fc, q_fxc, grad_up, grad_down)
    result = b16(residual + vec[7:8] + keep_a[1] + f32(came_a[1]) + f32(back_y))
    grad_qkv, grad_out = call(
        finish_q_kernel,
        [VM] * 4,
        [VM] * 2,
        [shape_of(query_key_value_weight.shape, fl), shape_of(output_weight.shape, fl)],
        vmem=8, moved=3 * 10**6,
    )(q_sum, q_fx, q_fc, q_fxc)
    sums = f32(q_sum[192:200, :256])
    part = ln_gains.shape[1]
    return (
        result[None],
        grad_tokens[None],
        grad_qkv,
        grad_out,
        grad_up,
        grad_down,
        sums[0:2, :part],
        sums[2:4, :part],
        sums[4:8, :part],
        sums[0:4, 128 : 128 + part].reshape(4 * part),
    )


def solution(mesh):
    placed = (
        P("rep", "seq", None),
        P("rep", "seq"),
        P("seq", None),
        P("seq", None),
        P("seq", None),
        P("seq", None),
        P(None, "seq"),
        P(None, "seq"),
        P(None, "seq"),
        P("seq"),
        P("rep", "seq", None),
    )
    shape = dict(mesh.shape)
    small_slice = shape["rep"] == 4 and shape["seq"] == 8
    return jax.shard_map(
        on_device_fast if small_slice else on_device,
        mesh=mesh,
        in_specs=placed,
        out_specs=(
            P("rep", "seq", None),
            P("rep", "seq", None),
            P("seq", None),
            P("seq", None),
            P("seq", None),
            P("seq", None),
            P(None, "seq"),
            P(None, "seq"),
            P(None, "seq"),
            P("seq"),
        ),
        check_vma=False,
    )
```

```python
import math

import jax
import jax.numpy as jnp
from jax import lax
from jax.experimental import pallas as pl
from jax.experimental.pallas import tpu as pltpu
from jax.sharding import PartitionSpec as P

HEADS = 12
HD = 64


norm_eps = 1e-05
floor_score = -1e30


def layer_norm(values, gain, shift):
    center = values - jnp.mean(values, axis=-1, keepdims=True)
    spread = jnp.mean(center * center, axis=-1, keepdims=True)
    return center * lax.rsqrt(spread + norm_eps) * gain + shift


def head_split(matrix):
    return matrix.reshape(matrix.shape[0], HEADS, HD)


def masked_scores(queries, query_seg, query_pos, key_piece, seg_piece, offset):
    rows = key_piece.shape[0]
    scores = jnp.einsum(
        "qhd,khd->hqk", queries, head_split(key_piece), preferred_element_type=jnp.float32
    ) * HD ** (-0.5)
    key_pos = offset + jnp.arange(rows, dtype=jnp.int32)
    allowed = (query_seg[:, None] == seg_piece[None, :]) & (key_pos[None, :] <= query_pos[:, None])
    return (jnp.where(allowed[None], scores, floor_score), allowed)


def forward_block(running, pieces, offset, queries, query_seg, query_pos):
    top_run, total_run, accum = running
    key_piece, value_piece, seg_piece = pieces
    scores, allowed = masked_scores(queries, query_seg, query_pos, key_piece, seg_piece, offset)
    top_new = jnp.maximum(top_run, jnp.max(scores, axis=-1))
    probs = jnp.where(allowed[None], jnp.exp(scores - top_new[:, :, None]), 0.0)
    factor = jnp.exp(top_run - top_new)
    total_new = total_run * factor + jnp.sum(probs, axis=-1)
    update = jnp.einsum(
        "hqk,khd->qhd",
        probs.astype(jnp.bfloat16),
        head_split(value_piece),
        preferred_element_type=jnp.float32,
    )
    return (top_new, total_new, accum * factor.T[:, :, None] + update)


def in_blocks(block_fn, running, pieces):
    rows = pieces[0].shape[0]
    size = math.gcd(rows, 1024)
    stacked = tuple((member.reshape((rows // size, size) + member.shape[1:]) for member in pieces))
    offsets = jnp.arange(rows // size, dtype=jnp.int32) * size

    def scan_step(state_now, element):
        return (block_fn(state_now, element[0], element[1]), None)

    running, _unused = lax.scan(scan_step, running, (stacked, offsets))
    return running


def backward_block(
    number,
    state_now,
    whole,
    queries,
    query_seg,
    query_pos,
    grad_heads,
    log_total,
    delta,
    block_rows,
):
    grad_query, term = state_now
    offset = number * block_rows
    key_piece = lax.dynamic_slice_in_dim(whole[0], offset, block_rows, 0)
    value_piece = lax.dynamic_slice_in_dim(whole[1], offset, block_rows, 0)
    seg_piece = lax.dynamic_slice_in_dim(whole[2], offset, block_rows, 0)
    scores, allowed = masked_scores(queries, query_seg, query_pos, key_piece, seg_piece, offset)
    probs = jnp.where(allowed[None], jnp.exp(scores - log_total[:, :, None]), 0.0)
    grad_probs = jnp.einsum(
        "qhd,khd->hqk", grad_heads, head_split(value_piece), preferred_element_type=jnp.float32
    )
    grad_scores = (probs * (grad_probs - delta[:, :, None])).astype(jnp.bfloat16)
    grad_query = grad_query + jnp.einsum(
        "hqk,khd->qhd", grad_scores, head_split(key_piece), preferred_element_type=jnp.float32
    )
    grad_key = jnp.einsum(
        "hqk,qhd->khd", grad_scores, queries, preferred_element_type=jnp.float32
    ) * HD ** (-0.5)
    grad_value = jnp.einsum(
        "hqk,qhd->khd", probs.astype(jnp.bfloat16), grad_heads, preferred_element_type=jnp.float32
    )
    joined = jnp.concatenate(
        [grad_key.reshape(block_rows, -1), grad_value.reshape(block_rows, -1)], axis=1
    )
    term = lax.dynamic_update_slice_in_dim(term, joined, offset, 0)
    return (grad_query, term)


def on_device(
    tokens,
    segment_ids,
    query_key_value_weight,
    output_weight,
    up_weight,
    down_weight,
    ln_gains,
    ln_biases,
    biases,
    up_projection_bias,
    cotangent,
):
    gathered = (
        lax.all_gather(query_key_value_weight, "seq", axis=0, tiled=True),
        lax.all_gather(output_weight, "seq", axis=0, tiled=True),
        lax.all_gather(up_weight, "seq", axis=0, tiled=True),
        lax.all_gather(down_weight, "seq", axis=0, tiled=True),
        lax.all_gather(ln_gains, "seq", axis=1, tiled=True),
        lax.all_gather(ln_biases, "seq", axis=1, tiled=True),
        lax.all_gather(biases, "seq", axis=1, tiled=True),
        lax.all_gather(up_projection_bias, "seq", axis=0, tiled=True),
    )
    full_qkv, full_out, full_up, full_down, gains_all, shifts_all, biases_all, up_shift = gathered
    gains_f = gains_all.astype(jnp.float32)
    shifts_f = shifts_all.astype(jnp.float32)
    biases_f = biases_all.astype(jnp.float32)
    up_shift_f = up_shift.astype(jnp.float32)
    tokens_f = tokens[0].astype(jnp.float32)
    seg_local = segment_ids[0]
    tok_rows = tokens_f.shape[0]
    width = tokens_f.shape[1]
    seqlen = tok_rows * lax.axis_size("seq")
    query_pos = lax.axis_index("seq") * tok_rows + jnp.arange(tok_rows, dtype=jnp.int32)
    hidden_first = layer_norm(tokens_f, gains_f[0], shifts_f[0]).astype(jnp.bfloat16)
    query_key_value_bias = jnp.concatenate(
        [biases_f[0], jnp.zeros((width,), jnp.float32), biases_f[1]]
    )
    projected_rows = (
        jnp.dot(hidden_first, full_qkv, preferred_element_type=jnp.float32) + query_key_value_bias
    ).astype(jnp.bfloat16)
    queries = head_split(projected_rows[:, :width])
    key_rows = projected_rows[:, width : 2 * width]
    value_rows = projected_rows[:, 2 * width :]
    initial = (
        jnp.full((HEADS, tok_rows), floor_score, jnp.float32),
        jnp.zeros((HEADS, tok_rows), jnp.float32),
        jnp.zeros((tok_rows, HEADS, HD), jnp.float32),
    )

    def block_fn(running, pieces, offset):
        return forward_block(running, pieces, offset, queries, seg_local, query_pos)

    block_rows = math.gcd(seqlen, 1024)
    key_end = (lax.axis_index("seq") + 1) * tok_rows
    block_count = (key_end + block_rows - 1) // block_rows
    top_run, total_run, accum = in_blocks(
        block_fn,
        initial,
        (
            lax.all_gather(key_rows, "seq", axis=0, tiled=True),
            lax.all_gather(value_rows, "seq", axis=0, tiled=True),
            lax.all_gather(seg_local, "seq", axis=0, tiled=True),
        ),
    )
    log_total = top_run + jnp.log(total_run)
    attended_f = accum / total_run.T[:, :, None]
    attention_result = attended_f.reshape(tok_rows, width).astype(jnp.bfloat16)
    residual_first = (
        tokens_f
        + jnp.dot(attention_result, full_out, preferred_element_type=jnp.float32)
        + biases_f[2]
    )
    hidden_second = layer_norm(residual_first, gains_f[1], shifts_f[1]).astype(jnp.bfloat16)
    upward_rows = jnp.dot(hidden_second, full_up, preferred_element_type=jnp.float32) + up_shift_f
    activated_f, gelu_back = jax.vjp(jax.nn.gelu, upward_rows)
    activation_values = activated_f.astype(jnp.bfloat16)
    result = (
        residual_first
        + jnp.dot(activation_values, full_down, preferred_element_type=jnp.float32)
        + biases_f[3]
    )
    grad_y = cotangent[0]
    grad_y_f = grad_y.astype(jnp.float32)
    grad_down = jnp.einsum(
        "tf,td->fd", activation_values, grad_y, preferred_element_type=jnp.float32
    )
    grad_act = jnp.einsum("td,fd->tf", grad_y, full_down, preferred_element_type=jnp.float32)
    grad_up_pre = gelu_back(grad_act)[0].astype(jnp.bfloat16)
    grad_up = jnp.einsum(
        "td,tf->df", hidden_second, grad_up_pre, preferred_element_type=jnp.float32
    )
    grad_hidden_two = jnp.einsum(
        "tf,df->td", grad_up_pre, full_up, preferred_element_type=jnp.float32
    )
    _unused, norm_two_back = jax.vjp(layer_norm, residual_first, gains_f[1], shifts_f[1])
    grad_sum_part, grad_gain_two, grad_shift_two = norm_two_back(grad_hidden_two)
    grad_first = grad_y_f + grad_sum_part
    grad_first_bf = grad_first.astype(jnp.bfloat16)
    grad_out_w = jnp.einsum(
        "td,te->de", attention_result, grad_first_bf, preferred_element_type=jnp.float32
    )
    grad_attended = jnp.einsum(
        "te,de->td", grad_first_bf, full_out, preferred_element_type=jnp.float32
    ).astype(jnp.bfloat16)
    grad_heads = head_split(grad_attended)
    delta = jnp.einsum("qhd,qhd->hq", grad_heads.astype(jnp.float32), attended_f)
    whole = (
        lax.all_gather(key_rows, "seq", axis=0, tiled=True),
        lax.all_gather(value_rows, "seq", axis=0, tiled=True),
        lax.all_gather(seg_local, "seq", axis=0, tiled=True),
    )

    def backward_step(number, state_now):
        return backward_block(
            number,
            state_now,
            whole,
            queries,
            seg_local,
            query_pos,
            grad_heads,
            log_total,
            delta,
            block_rows,
        )

    start_state = (
        jnp.zeros((tok_rows, HEADS, HD), jnp.float32),
        jnp.zeros((seqlen, 2 * width), jnp.float32),
    )
    grad_query, term = lax.fori_loop(0, block_count, backward_step, start_state)
    grad_kv = lax.psum_scatter(term, "seq", scatter_dimension=0, tiled=True).astype(jnp.bfloat16)
    grad_q = (grad_query * HD ** (-0.5)).reshape(tok_rows, width).astype(jnp.bfloat16)
    grad_proj = jnp.concatenate([grad_q, grad_kv], axis=1)
    grad_qkv_w = jnp.einsum(
        "td,te->de", hidden_first, grad_proj, preferred_element_type=jnp.float32
    )
    grad_hidden_one = jnp.einsum(
        "te,de->td", grad_proj, full_qkv, preferred_element_type=jnp.float32
    )
    _unused_two, norm_one_back = jax.vjp(layer_norm, tokens_f, gains_f[0], shifts_f[0])
    grad_in_part, grad_gain_one, grad_shift_one = norm_one_back(grad_hidden_one)
    grad_tokens = grad_first + grad_in_part
    grad_proj_f = grad_proj.astype(jnp.float32)
    grad_bias_rows = jnp.stack(
        [
            jnp.sum(grad_proj_f[:, :width], axis=0),
            jnp.sum(grad_proj_f[:, 2 * width :], axis=0),
            jnp.sum(grad_first, axis=0),
            jnp.sum(grad_y_f, axis=0),
        ]
    )
    grad_up_shift = jnp.sum(grad_up_pre.astype(jnp.float32), axis=0)
    grad_gains = jnp.stack([grad_gain_one, grad_gain_two])
    grad_shifts = jnp.stack([grad_shift_one, grad_shift_two])
    shares = (
        lax.psum_scatter(grad_qkv_w, "seq", scatter_dimension=0, tiled=True),
        lax.psum_scatter(grad_out_w, "seq", scatter_dimension=0, tiled=True),
        lax.psum_scatter(grad_up, "seq", scatter_dimension=0, tiled=True),
        lax.psum_scatter(grad_down, "seq", scatter_dimension=0, tiled=True),
        lax.psum_scatter(grad_gains, "seq", scatter_dimension=1, tiled=True),
        lax.psum_scatter(grad_shifts, "seq", scatter_dimension=1, tiled=True),
        lax.psum_scatter(grad_bias_rows, "seq", scatter_dimension=1, tiled=True),
        lax.psum_scatter(grad_up_shift, "seq", scatter_dimension=0, tiled=True),
    )
    totals = (
        lax.psum(shares[0].astype(jnp.bfloat16), "rep").astype(jnp.float32),
        lax.psum(shares[1].astype(jnp.bfloat16), "rep").astype(jnp.float32),
        lax.psum(shares[2].astype(jnp.bfloat16), "rep").astype(jnp.float32),
        lax.psum(shares[3].astype(jnp.bfloat16), "rep").astype(jnp.float32),
        lax.psum(shares[4].astype(jnp.bfloat16), "rep").astype(jnp.float32),
        lax.psum(shares[5].astype(jnp.bfloat16), "rep").astype(jnp.float32),
        lax.psum(shares[6].astype(jnp.bfloat16), "rep").astype(jnp.float32),
        lax.psum(shares[7].astype(jnp.bfloat16), "rep").astype(jnp.float32),
    )
    return (
        result.astype(jnp.bfloat16)[None],
        grad_tokens[None],
        totals[0],
        totals[1],
        totals[2],
        totals[3],
        totals[4],
        totals[5],
        totals[6],
        totals[7],
    )


def f32(value):
    return value.astype(jnp.float32)


def b16(value):
    return value.astype(jnp.bfloat16)


def dot_nn(left, right):
    return jnp.dot(left, right, preferred_element_type=jnp.float32)


def dot_nt(left, right):
    return lax.dot_general(
        left, right, (((1,), (1,)), ((), ())), preferred_element_type=jnp.float32
    )


def dot_tn(left, right):
    return lax.dot_general(
        left, right, (((0,), (0,)), ((), ())), preferred_element_type=jnp.float32
    )


def norm_parts(values):
    center = values - jnp.mean(values, axis=-1, keepdims=True)
    rate = lax.rsqrt(jnp.mean(center * center, axis=-1, keepdims=True) + norm_eps)
    return center * rate, rate


def norm_back(grad, hat, rate, gain):
    scaled = grad * gain
    return rate * (
        scaled
        - jnp.mean(scaled, axis=-1, keepdims=True)
        - hat * jnp.mean(scaled * hat, axis=-1, keepdims=True)
    )


def place():
    rep, seq = lax.axis_index("rep"), lax.axis_index("seq")
    return lax.div(rep, 2), lax.rem(rep, 2), lax.rem(seq, 2), lax.div(seq, 2)


def piece_shard(number, y, z):
    if number < 3:
        return 2 * lax.rem(z + 3 - number, 4) + y
    return 2 * lax.rem(z + 7 - number, 4) + 1 - y


def pack96(parts):
    lane = lax.broadcasted_iota(jnp.int32, parts[0].shape, 1)
    one, two, three = (pltpu.roll(parts[k], 128 - 32 * k, 1) for k in (1, 2, 3))
    return jnp.concatenate(
        [
            jnp.where(lane < 96, parts[0], one),
            jnp.where(lane < 64, one, two),
            jnp.where(lane < 32, two, three),
        ],
        axis=1,
    )


def unpack96(block):
    tiles = [block[:, 128 * k : 128 * k + 128] for k in range(3)]
    lane = lax.broadcasted_iota(jnp.int32, tiles[0].shape, 1)
    return [
        tiles[0],
        jnp.where(lane < 32, pltpu.roll(tiles[0], 32, 1), pltpu.roll(tiles[1], 32, 1)),
        jnp.where(lane < 64, pltpu.roll(tiles[1], 64, 1), pltpu.roll(tiles[2], 64, 1)),
        pltpu.roll(tiles[2], 96, 1),
    ]


def choose(parts, index):
    out = parts[0]
    for number in range(1, len(parts)):
        out = jnp.where(index == number, parts[number], out)
    return out


class Copies:
    def __init__(self, sems, first=0):
        self.sems = sems
        self.first = first
        self.held = []

    def add(self, source, target):
        copy = pltpu.make_async_copy(source, target, self.sems.at[self.first + len(self.held)])
        copy.start()
        self.held.append(copy)

    def wait(self):
        for copy in self.held:
            copy.wait()
        self.held = []


def corners(x, c):
    return ((x, c), (1 - x, c), (x, 1 - c), (1 - x, 1 - c))


def fetch_qkv(copies, own, groups, full, full_out=None, own_out=None):
    x, c, y, z = place()
    rows = own.shape[0]
    half, width = rows // 2, own.shape[1] // 3
    row = pl.multiple_of((2 * z + y) * rows, 16)
    copies.add(own, full.at[pl.ds(row, rows), :])
    if full_out is not None:
        copies.add(own_out, full_out.at[pl.ds(row, rows), :])
    wide, side = 3 * width // 2, width // 2
    for number in range(7):
        for (xx, cc), group in zip(corners(x, c), groups, strict=True):
            piece = piece_of(group, number)
            at = pl.ds(pl.multiple_of(piece_shard(number, y, z) * rows + half * cc, 16), half)
            copies.add(
                piece.at[pl.ds(0, half), pl.ds(0, wide)],
                full.at[at, pl.ds(pl.multiple_of(wide * xx, 128), wide)],
            )
            if full_out is not None:
                copies.add(
                    piece.at[pl.ds(0, half), pl.ds(wide, side)],
                    full_out.at[at, pl.ds(pl.multiple_of(side * xx, 128), side)],
                )


def piece_of(group, number):
    behind, across, behind_across = group
    if number < 3:
        return behind.at[number]
    return across.at[0] if number == 3 else behind_across.at[number - 4]


def mask_bias(start, me, tok, target):
    keys, lanes = target.shape
    key_pos = (me - 4) * tok + lax.broadcasted_iota(jnp.int32, (keys, lanes), 0)
    lane = lax.broadcasted_iota(jnp.int32, (keys, lanes), 1)
    query_pos = me * tok + jnp.where(lane >= tok, lane - tok, lane)
    target[...] = jnp.where((key_pos >= start) & (key_pos <= query_pos), 0.0, floor_score)


def pair_stack(rows):
    lane = lax.broadcasted_iota(jnp.int32, rows.shape, 1)
    zero = jnp.zeros_like(rows)
    return jnp.concatenate([jnp.where(lane < HD, rows, zero), jnp.where(lane < HD, zero, rows)], axis=0)


def pair_join(transposed):
    both = transposed.T
    tok = both.shape[0] // 2
    lane = lax.broadcasted_iota(jnp.int32, (tok, 2 * HD), 1)
    return jnp.where(lane < HD, both[:tok], both[tok:])


def prep_kernel(
    tokens, segs, qkv, out, up, down, gains, shifts, biases, up_bias,
    t_out, q_out, f_out, fu_out, fd_out,
    scratch, wide, held_g, held_s, held_b, ids, line, sems,
):
    x, c, _y, _z = place()
    tok, width = tokens.shape[1:]
    rows = qkv.shape[0]
    half, side = rows // 2, width // 2
    p = 2 * x + c
    at = pl.ds(pl.multiple_of(half * c, 16), half)
    copies, others = Copies(sems), Copies(sems, 5)
    for source, target in ((gains, held_g), (shifts, held_s), (biases, held_b)):
        copies.add(source, target)
    copies.add(segs, ids)
    copies.add(up_bias, line)
    others.add(up, wide)
    wide_cols = 3 * side
    others.add(
        qkv.at[at, pl.ds(pl.multiple_of(wide_cols * x, 128), wide_cols)],
        q_out.at[pl.ds(0, half), pl.ds(0, wide_cols)],
    )
    others.add(
        out.at[at, pl.ds(pl.multiple_of(side * x, 128), side)],
        q_out.at[pl.ds(0, half), pl.ds(wide_cols, side)],
    )
    others.add(tokens.at[0], t_out.at[pl.ds(0, tok), :])
    own_rows = down.at[pl.ds(pl.multiple_of(rows * p, 16), rows), :]
    others.add(own_rows, f_out.at[pl.ds(rows, rows), :])
    others.add(own_rows, fd_out)
    copies.wait()
    scratch[...] = jnp.zeros_like(scratch)
    for first, held in ((0, held_g), (2, held_s), (4, held_b)):
        scratch[pl.ds(first, held.shape[0]), pl.ds(0, rows)] = f32(held[...])
    parts = unpack96(jnp.broadcast_to(f32(line[...]).reshape(1, line.shape[0]), (8, line.shape[0])))
    lane = lax.broadcasted_iota(jnp.int32, (8, 128), 1)
    row = lax.broadcasted_iota(jnp.int32, (8, 128), 0)
    ups = jnp.zeros((8, 128), jnp.float32)
    for number in range(4):
        ups = jnp.where((row == number) & (lane < rows), parts[number], ups)
    smalls = b16(jnp.concatenate([scratch[:, pl.ds(0, 128)], ups], axis=0))
    q_out[pl.ds(0, 16), pl.ds(2 * width, 128)] = smalls
    q_out[pl.ds(16, half - 16), pl.ds(2 * width, 128)] = jnp.zeros((half - 16, 128), jnp.bfloat16)
    scratch[...] = jnp.zeros_like(scratch)
    scratch[pl.ds(0, 1), pl.ds(0, tok)] = f32(ids[...])
    t_out[pl.ds(tok, 8), :] = b16(scratch[...])
    others.wait()
    for group in range(2):
        parts = []
        for shard in range(4 * group, 4 * group + 4):
            parts.append(choose(unpack96(f32(wide[:, pl.ds(384 * shard, 384)])), p))
        packed = b16(pack96(parts))
        f_out[pl.ds(0, rows), pl.ds(384 * group, 384)] = packed
        fu_out[:, pl.ds(384 * group, 384)] = packed


def front_kernel(
    seg, xo, x1, x2, x3, x4, first, own, own_o,
    g0, g1, g2, g3, g4, g5, g6, g7, g8, g9, g10, g11,
    q_out, kv_out, h_out, a_out, lse_out, start_out, vec_out, upb_out, wo_out, r_out, h2_out,
    full, small, bias, sems, vsems,
):
    x, c, y, z = place()
    me = 2 * z + y
    p = 2 * x + c
    tok, width = q_out.shape
    copies, vcopies = Copies(sems), Copies(vsems)
    vcopies.add(first.at[pl.ds(0, 16), pl.ds(2 * width, 128)], small.at[me])
    for number in range(7):
        source = piece_of((g0, g1, g2), number)
        vcopies.add(source.at[pl.ds(0, 16), pl.ds(2 * width, 128)], small.at[piece_shard(number, y, z)])
    groups = ((g0, g1, g2), (g3, g4, g5), (g6, g7, g8), (g9, g10, g11))
    fetch_qkv(copies, own, groups, full, wo_out, own_o)
    blocks = (xo, x1, x2, x3, x4)
    lane1 = lax.broadcasted_iota(jnp.int32, (1, tok), 1)
    start = jnp.full(seg.shape, 1 << 30, jnp.int32)
    for number in range(4):
        first_pos = jnp.full((1, 1), 1 << 30, jnp.int32)
        for back in range(5):
            ids = f32(blocks[back][pl.ds(tok, 8), pl.ds(0, tok)])[:1]
            pos = (me - back) * tok + lane1
            hit = (ids == float(number)) & (pos >= 0)
            first_pos = jnp.minimum(
                first_pos, jnp.min(jnp.where(hit, pos, 1 << 30), axis=1, keepdims=True)
            )
        start = jnp.where(seg[...] == number, first_pos, start)
    start_out[...] = start
    mask_bias(start, me, tok, bias)
    vcopies.wait()
    for group in range(2):
        held = [f32(small[4 * group + k]) for k in range(4)]
        vec_out[:, pl.ds(384 * group, 384)] = pack96([block[:8] for block in held])
        upb_out[:, pl.ds(384 * group, 384)] = pack96(
            [choose([jnp.broadcast_to(block[k : k + 1], (8, 128)) for k in range(8, 12)], p) for block in held]
        )
    vec = vec_out[...]
    for back in range(5):
        hat, _rate = norm_parts(f32(blocks[back][pl.ds(0, tok), :]))
        h_out[pl.ds((4 - back) * tok, tok), :] = b16(hat * vec[0:1] + vec[2:3])
    copies.wait()
    q_out[...] = b16(dot_nn(h_out[pl.ds(4 * tok, tok), :], full[:, pl.ds(0, width)]) + vec[4:5])

    def project(number, carry):
        col = pl.multiple_of(number * 256, 256)
        shift = jnp.where(number >= width // 256, 1.0, 0.0)
        bias_at = lax.rem(number, width // 256)
        piece = vec_out[pl.ds(5, 1), pl.ds(pl.multiple_of(bias_at * 256, 256), 256)]
        kv_out[:, pl.ds(col, 256)] = b16(
            dot_nn(h_out[...], full[:, pl.ds(pl.multiple_of(width + col, 256), 256)]) + piece * shift
        )
        return carry

    lax.fori_loop(0, 2 * width // 256, project, 0)

    def pair(number, carry):
        col = pl.multiple_of(number * 128, 128)
        queries = pair_stack(q_out[:, pl.ds(col, 128)] * jnp.bfloat16(0.125))
        scores = dot_nt(kv_out[:, pl.ds(col, 128)], queries) + bias[...]
        top = jnp.max(scores, axis=0, keepdims=True)
        probs = jnp.exp(scores - top)
        total = jnp.sum(probs, axis=0, keepdims=True)
        mixed = dot_tn(kv_out[:, pl.ds(pl.multiple_of(width + col, 128), 128)], b16(probs))
        a_out[:, pl.ds(col, 128)] = b16(pair_join(mixed / total))
        lse_out[number] = top + jnp.log(total)
        return carry

    lax.fori_loop(0, width // 128, pair, 0)
    residual = f32(xo[pl.ds(0, tok), :]) + dot_nn(a_out[...], wo_out[...]) + vec[6:7]
    r_out[...] = residual
    hat, _rate = norm_parts(residual)
    h2_out[...] = b16(hat * vec[1:2] + vec[3:4])


def feed_tokens(h2, dy, w_up, w_down, upb, act_out, du_out, y_acc, dh_acc):
    root = math.sqrt(2.0 / math.pi)
    chunk = 256

    def feed(number, carry):
        col = pl.multiple_of(number * chunk, chunk)
        pre = dot_nn(h2[...], w_up[:, pl.ds(col, chunk)]) + upb[pl.ds(0, 1), pl.ds(col, chunk)]
        square = pre * pre
        bend = jnp.tanh(root * pre * (1.0 + 0.044715 * square))
        act = b16(0.5 * pre * (1.0 + bend))
        slope = 0.5 * (1.0 + bend) + 0.5 * pre * (1.0 - bend * bend) * (
            root * (1.0 + 3.0 * 0.044715 * square)
        )
        low = b16(dot_nt(dy[...], w_down[pl.ds(col, chunk), :]) * slope)
        act_out[:, pl.ds(col, chunk)] = act
        du_out[:, pl.ds(col, chunk)] = low
        return carry

    lax.fori_loop(0, w_up.shape[1] // chunk, feed, 0)
    dh_acc[...] = dot_nt(du_out[...], w_up[...])
    y_acc[...] = dot_nn(act_out[...], w_down[...])


def assemble_kernel(own, z1, z2, z3u, z3d, y0, y13, wu_out, wd_out, sems):
    _x, _c, y, z = place()
    rows = own.shape[0] // 2
    copies = Copies(sems)
    pieces = [(own, 2 * z + y)]
    for number, ref in ((0, z1), (1, z2), (3, y0)):
        pieces.append((ref, piece_shard(number, y, z)))
    for number, first in ((4, 0), (6, 2 * rows)):
        pieces.append((y13.at[pl.ds(first, 2 * rows), :], piece_shard(number, y, z)))
    for ref, shard in pieces:
        at = pl.ds(pl.multiple_of(shard * rows, 16), rows)
        copies.add(ref.at[pl.ds(0, rows), :], wu_out.at[at, :])
        copies.add(ref.at[pl.ds(rows, rows), :], wd_out.at[at, :])
    at = pl.ds(pl.multiple_of(piece_shard(2, y, z) * rows, 16), rows)
    copies.add(z3u, wu_out.at[at, :])
    copies.add(z3d, wd_out.at[at, :])
    copies.wait()


def near_kernel(
    h_own, h_c, dy_own, dy_c, upb, y2, _wu, _wd,
    h2, dy, act_out, du_out, keep_out, send_out, wu_out, wd_out,
    y_acc, dh_acc, sems,
):
    _x, _c, y, z = place()
    tok, width = h_own.shape
    rows = width // 8
    copies = Copies(sems)
    at = pl.ds(pl.multiple_of(piece_shard(5, y, z) * rows, 16), rows)
    copies.add(y2.at[pl.ds(0, rows), :], wu_out.at[at, :])
    copies.add(y2.at[pl.ds(rows, rows), :], wd_out.at[at, :])
    h2[pl.ds(0, tok), :] = h_own[...]
    h2[pl.ds(tok, tok), :] = h_c[...]
    dy[pl.ds(0, tok), :] = dy_own[...]
    dy[pl.ds(tok, tok), :] = dy_c[...]
    copies.wait()
    feed_tokens(h2, dy, wu_out, wd_out, upb, act_out, du_out, y_acc, dh_acc)
    keep_out[0] = dh_acc[pl.ds(0, tok), :]
    keep_out[1] = y_acc[pl.ds(0, tok), :]
    send_out[0] = b16(dh_acc[pl.ds(tok, tok), :])
    send_out[1] = b16(y_acc[pl.ds(tok, tok), :])


def far_kernel(
    h_x, h_xc, dy_x, dy_xc, upb, w_up, w_down, h_near, dy_near, act_near, du_near,
    hs, dys, acts, dus, keep_out, send_out,
    y_acc, dh_acc, sems,
):
    tok = dy_x.shape[0]
    copies = Copies(sems)
    for source, target in ((h_near, hs), (dy_near, dys), (act_near, acts), (du_near, dus)):
        copies.add(source, target.at[pl.ds(0, 2 * tok), :])
    later = pl.ds(2 * tok, 2 * tok)
    hs[pl.ds(2 * tok, tok), :] = h_x[...]
    hs[pl.ds(3 * tok, tok), :] = h_xc[...]
    dys[pl.ds(2 * tok, tok), :] = dy_x[...]
    dys[pl.ds(3 * tok, tok), :] = dy_xc[...]
    feed_tokens(
        hs.at[later, :], dys.at[later, :], w_up, w_down, upb, acts.at[later, :], dus.at[later, :], y_acc, dh_acc
    )
    keep_out[0] = dh_acc[pl.ds(0, tok), :]
    keep_out[1] = y_acc[pl.ds(0, tok), :]
    send_out[0] = b16(dh_acc[pl.ds(tok, tok), :])
    send_out[1] = b16(y_acc[pl.ds(tok, tok), :])
    copies.wait()


def weights_kernel(hs, dys, acts, dus, u_out, d_out, upb_out, stage, sems):
    _x, _c, y, z = place()
    width = hs.shape[1]
    rows = width // 8
    upb_out[...] = jnp.sum(f32(dus[...]), axis=0, keepdims=True)

    def weight(number, carry):
        col = pl.multiple_of(number * 256, 256)
        stage[0, pl.ds(col, 256), :] = b16(dot_tn(hs[:, pl.ds(col, 256)], dus[...]))
        stage[1, pl.ds(col, 256), :] = b16(dot_tn(acts[:, pl.ds(col, 256)], dys[...]))
        return carry

    lax.fori_loop(0, width // 256, weight, 0)
    outs = Copies(sems)
    for shard in range(8):
        zz = lax.rem(shard // 2 + 4 - z, 4)
        yy = jnp.where(y == shard % 2, 0, 1)
        outs.add(stage.at[0, pl.ds(shard * rows, rows), :], u_out.at[yy, zz])
        outs.add(stage.at[1, pl.ds(shard * rows, rows), :], d_out.at[yy, zz])
    outs.wait()


def scatter(stage, other, mine, sems):
    x, c, y, z = place()
    outs = Copies(sems)
    for shard in range(8):
        zz = lax.rem(shard // 2 + 4 - z, 4)
        yy = jnp.where(y == shard % 2, 0, 1)
        for xx in range(2):
            far = jnp.where(x == xx, 0, 1)
            outs.add(stage.at[1 - c, xx, shard], other.at[far, yy, zz])
            outs.add(stage.at[c, xx, shard], mine.at[far, yy, zz])
    outs.wait()


def post_kernel(
    residual, own, near, across, dy_in, vec_in, w_out, a_in,
    dr_out, da_out, dw_out, vec_out,
):
    vec = vec_in[...]
    grad_hidden = own[0] + f32(near[0]) + f32(across[...])
    hat, rate = norm_parts(residual[...])
    dy = f32(dy_in[...])
    grad_first = dy + norm_back(grad_hidden, hat, rate, vec[1:2])
    dr_out[...] = grad_first
    low = b16(grad_first)
    da_out[...] = b16(dot_nt(low, w_out[...]))
    dw_out[...] = dot_tn(a_in[...], low)
    zero = jnp.zeros((1, dy.shape[1]), jnp.float32)
    vec_out[...] = jnp.concatenate(
        [
            zero,
            jnp.sum(grad_hidden * hat, axis=0, keepdims=True),
            zero,
            jnp.sum(grad_hidden, axis=0, keepdims=True),
            zero,
            zero,
            jnp.sum(grad_first, axis=0, keepdims=True),
            jnp.sum(dy, axis=0, keepdims=True),
        ],
        axis=0,
    )


def back_pairs(first, q_in, kv_in, lse_in, da_in, bias, dq, dkv):
    width = q_in.shape[1]

    def pair(number, carry):
        col = pl.multiple_of((first + number) * 128, 128)
        vcol = pl.multiple_of(width + col, 128)
        to = pl.multiple_of(number * 128, 128)
        queries = pair_stack(q_in[:, pl.ds(col, 128)] * jnp.bfloat16(0.125))
        grads = pair_stack(da_in[:, pl.ds(col, 128)])
        keys = kv_in[:, pl.ds(col, 128)]
        probs = jnp.exp(dot_nt(keys, queries) + bias[...] - lse_in[first + number])
        dkv[:, pl.ds(pl.multiple_of(width // 2 + to, 128), 128)] = b16(dot_nn(b16(probs), grads))
        term = probs * dot_nt(kv_in[:, pl.ds(vcol, 128)], grads)
        low = b16(term - probs * jnp.sum(term, axis=0, keepdims=True))
        dkv[:, pl.ds(to, 128)] = b16(dot_nn(low, queries))
        dq[:, pl.ds(to, 128)] = b16(pair_join(dot_tn(keys, low)) * 0.125)
        return carry

    lax.fori_loop(0, 3, pair, 0, unroll=first == 0)


def qkv_weight(h_in, dq, dkv, stage, tail):
    tok, part = dq.shape
    keys = h_in.shape[0]

    def weight(number, carry):
        col = pl.multiple_of(number * 384, 384)
        key = dot_tn(h_in[:, pl.ds(col, 384)], dkv[...])
        query = dot_tn(h_in[pl.ds(keys - tok, tok), pl.ds(col, 384)], dq[...])
        for shard in range(4):
            for cc in range(2):
                for xx in range(2):
                    rows = slice(96 * shard + 48 * cc + 24 * xx, 96 * shard + 48 * cc + 24 * xx + 24)
                    blocks = [query[rows], key[rows, :part], key[rows, part:]] + tail(4 * number + shard, 48 * cc + 24 * xx)
                    stage[cc, xx, 4 * number + shard] = b16(jnp.concatenate(blocks, axis=0))
        return carry

    lax.fori_loop(0, 2, weight, 0)


def back_a_kernel(
    start_in, q_in, kv_in, h_in, lse_in, da_in, dw_in,
    other, mine, dq_out, dkv_out,
    bias, stage, sems,
):
    _x, _c, y, z = place()
    mask_bias(start_in[...], 2 * z + y, q_in.shape[0], bias)
    back_pairs(0, q_in, kv_in, lse_in, da_in, bias, dq_out, dkv_out)
    side = q_in.shape[1] // 2

    def out_rows(shard, row):
        rows = dw_in[pl.ds(pl.multiple_of(96 * shard + row, 8), 24), :]
        return [rows[:, :side], rows[:, side:]]

    qkv_weight(h_in, dq_out, dkv_out, stage, out_rows)
    scatter(stage, other, mine, sems)


def back_b_kernel(
    start_in, q_in, kv_in, lse_in, da_in, vec_in, upb_in, dq_a, dkv_a, xo, x1, x2, x3, x4,
    own, g0, g1, g2, g3, g4, g5, g6, g7, g8, g9, g10, g11,
    dq_out, dkv_out, p_own, p_y, p_z, sums_out,
    full, bias, sems,
):
    x, c, y, z = place()
    p = 2 * x + c
    tok, width = q_in.shape
    side = width // 2
    copies = Copies(sems)
    groups = ((g0, g1, g2), (g3, g4, g5), (g6, g7, g8), (g9, g10, g11))
    fetch_qkv(copies, own, groups, full)
    mask_bias(start_in[...], 2 * z + y, tok, bias)
    back_pairs(3, q_in, kv_in, lse_in, da_in, bias, dq_out, dkv_out)
    copies.wait()
    gain_sum = jnp.zeros((1, width), jnp.float32)
    shift_sum = jnp.zeros((1, width), jnp.float32)
    for back, block in enumerate((xo, x1, x2, x3, x4)):
        rows = pl.ds((4 - back) * tok, tok)
        grad = jnp.zeros((tok, width), jnp.float32)
        for number, (dq, dkv) in enumerate(((dq_a, dkv_a), (dq_out, dkv_out))):
            at = number * side
            grad = grad + dot_nt(dkv[rows, pl.ds(0, side)], full[:, pl.ds(width + at, side)])
            grad = grad + dot_nt(dkv[rows, pl.ds(side, side)], full[:, pl.ds(2 * width + at, side)])
            if back == 0:
                grad = grad + dot_nt(dq[...], full[:, pl.ds(at, side)])
        if back == 0:
            p_own[...] = grad
        elif back in (1, 3):
            p_y[back // 2] = b16(grad)
        else:
            p_z[back // 2 - 1] = b16(grad)
        hat, _rate = norm_parts(f32(block[pl.ds(0, tok), :]))
        gain_sum = gain_sum + jnp.sum(grad * hat, axis=0, keepdims=True)
        shift_sum = shift_sum + jnp.sum(grad, axis=0, keepdims=True)
    zero = jnp.zeros((1, width), jnp.float32)
    bias_q = jnp.concatenate([jnp.sum(f32(d[...]), axis=0, keepdims=True) for d in (dq_a, dq_out)], axis=1)
    bias_v = jnp.concatenate(
        [jnp.sum(f32(d[:, pl.ds(side, side)]), axis=0, keepdims=True) for d in (dkv_a, dkv_out)], axis=1
    )
    vec = vec_in[...] + jnp.concatenate(
        [gain_sum, zero, shift_sum, zero, bias_q, bias_v, zero, zero], axis=0
    )
    lane = lax.broadcasted_iota(jnp.int32, (8, 128), 1)
    line = lax.broadcasted_iota(jnp.int32, (8, 128), 0)
    for group in range(2):
        cols = pl.ds(384 * group, 384)
        vec_parts = unpack96(vec[:, 384 * group : 384 * group + 384])
        upb_parts = unpack96(jnp.broadcast_to(upb_in[:, cols], (8, 384)))
        for k in range(4):
            sums_out[4 * group + k] = jnp.concatenate(
                [
                    jnp.where(lane < 96, vec_parts[k], 0.0),
                    jnp.where((lane < 96) & (line == p), upb_parts[k], 0.0),
                ],
                axis=1,
            )


def back_c_kernel(h_in, dq, dkv, sums_in, other, mine, stage, sems):
    blank = jnp.zeros((8, 128), jnp.float32)
    qkv_weight(
        h_in, dq, dkv, stage, lambda shard, _row: [jnp.concatenate([sums_in[shard], blank], axis=1)]
    )
    scatter(stage, other, mine, sems)


def tokens_kernel(own, near, dr, xo, vec_in, grad_out):
    tok = own.shape[0]
    hat, rate = norm_parts(f32(xo[pl.ds(0, tok), :]))
    grad = own[...] + f32(near[...])
    grad_out[...] = dr[...] + norm_back(grad, hat, rate, vec_in[0:1, :])


def finish_f_kernel(f0, fx, fc, fcx, up, down, held):
    x, c, _y, _z = place()
    rows = f0.shape[0] // 2
    for (xx, cc), f in zip(corners(x, c), (f0, fx, fc, fcx), strict=True):
        p = 2 * xx + cc
        held[p] = f[pl.ds(0, rows), :]
        down[pl.ds(pl.multiple_of(rows * p, 16), rows), :] = f32(f[pl.ds(rows, rows), :])
    for group in range(2):
        parts = [unpack96(f32(held[k, :, pl.ds(384 * group, 384)])) for k in range(4)]
        for shard in range(4):
            up[:, pl.ds(384 * (4 * group + shard), 384)] = pack96([part[shard] for part in parts])


def finish_q_kernel(f0, fx, fc, fcx, qkv, out):
    x, c, _y, _z = place()
    side = out.shape[1] // 2
    for (xx, cc), piece in zip(corners(x, c), (f0, fx, fc, fcx), strict=True):
        rows = pl.ds(pl.multiple_of(48 * cc + 24 * xx, 8), 24)
        blocks = f32(piece[...])
        for number in range(3):
            first, second = 24 * number, 24 * (number + 5)
            qkv[rows, pl.ds(2 * side * number, side)] = blocks[first : first + 24]
            qkv[rows, pl.ds(2 * side * number + side, side)] = blocks[second : second + 24]
        out[rows, pl.ds(0, side)] = blocks[72:96]
        out[rows, pl.ds(side, side)] = blocks[96:120]


HB = pl.BlockSpec(memory_space=pltpu.HBM)
VM = pl.BlockSpec(memory_space=pltpu.VMEM)
AN = pl.BlockSpec(memory_space=pl.ANY)


def shape_of(shape, dtype):
    return jax.ShapeDtypeStruct(shape, dtype)


def call(kernel, ins, outs, out_shape, scratch=(), vmem=40, flops=0, moved=0, aliases=None):
    return pl.pallas_call(
        kernel,
        in_specs=ins,
        out_specs=outs,
        out_shape=out_shape,
        scratch_shapes=list(scratch),
        input_output_aliases=aliases or {},
        compiler_params=pltpu.CompilerParams(vmem_limit_bytes=vmem << 20),
        cost_estimate=pl.CostEstimate(flops=flops, bytes_accessed=moved, transcendentals=0),
    )


def fence(*values):
    return lax.optimization_barrier(values)


def swap_rep(value, bit):
    return lax.ppermute(value, "rep", [(k, k ^ bit) for k in range(4)])


def to_core(value):
    return swap_rep(value, 1)


def to_x(value):
    return swap_rep(value, 2)


def to_y(value):
    return lax.ppermute(value, "seq", [(k, k ^ 1) for k in range(8)])


def to_z(value, steps):
    return lax.ppermute(value, "seq", [(k, (k + 2 * steps) % 8) for k in range(8)])


def join(*parts):
    return jnp.concatenate(parts, axis=0)


def on_device_fast(
    tokens,
    segment_ids,
    query_key_value_weight,
    output_weight,
    up_weight,
    down_weight,
    ln_gains,
    ln_biases,
    biases,
    up_projection_bias,
    cotangent,
):
    seq = lax.axis_index("seq")
    y = seq % 2
    tok, width = tokens.shape[1:]
    hidden = up_weight.shape[1]
    keys = 5 * tok
    bf, fl = jnp.bfloat16, jnp.float32
    dma = pltpu.SemaphoreType.DMA
    grad_y = cotangent[0]
    own_tokens, piece_q, piece_f, piece_u, piece_d = call(
        prep_kernel,
        [HB] * 10,
        [VM] * 5,
        [
            shape_of((tok + 8, width), bf),
            shape_of((48, 2 * width + 128), bf),
            shape_of((192, width), bf),
            shape_of((96, width), bf),
            shape_of((96, width), bf),
        ],
        [
            pltpu.VMEM((8, width), fl),
            pltpu.VMEM((96, hidden), bf),
            pltpu.VMEM((2, 96), bf),
            pltpu.VMEM((2, 96), bf),
            pltpu.VMEM((4, 96), bf),
            pltpu.VMEM((1, tok), jnp.int32),
            pltpu.VMEM((384,), bf),
            dma((11,)),
        ],
        vmem=60, moved=4 * 10**6,
    )(
        tokens, segment_ids, query_key_value_weight, output_weight, up_weight, down_weight,
        ln_gains, ln_biases, biases, up_projection_bias,
    )

    q1, q3, q_y0, dy_x = fence(to_z(piece_q, 1), to_z(piece_q, 3), to_y(piece_q), to_x(grad_y))
    own_tokens, piece_f, q1, q_y0 = fence(own_tokens, piece_f, q1, q_y0, q3, dy_x)[:4]
    q2, x2, q_xy0, f_y0 = fence(to_z(q1, 1), to_z(own_tokens, 1), to_x(q_y0), to_y(piece_f))
    q_z = join(q1, q2, q3)
    q_z, x2, piece_d = fence(q_z, x2, piece_d, q_xy0, f_y0)[:3]
    q_y, q_xz, x4, f3d = fence(to_y(q_z), to_x(q_z), to_z(x2, 1), to_z(piece_d, 3))
    near = jnp.where(y == 0, own_tokens, x2)
    far = jnp.where(y == 0, x2, x4)
    near_far, q_y, piece_f, piece_u = fence(
        jnp.stack([near, far]), q_y, piece_f, piece_u, q_xz, f3d
    )[:4]
    crossed, q_xy, f1, f3u = fence(to_y(near_far), to_x(q_y), to_z(piece_f, 1), to_z(piece_u, 3))
    x1, x3 = crossed[0], crossed[1]
    q_z, q_y0, q_y, q_xz, q_xy0, q_xy = fence(q_z, q_y0, q_y, q_xz, q_xy0, q_xy, f1, f3u, crossed)[:6]
    q_cz, q_cy0, q_cy, q_cxz, q_cxy0, q_cxy = fence(
        *(to_core(v) for v in (q_z, q_y0, q_y, q_xz, q_xy0, q_xy))
    )
    f_13, f_1, q_cz = fence(join(f1, f3u, f3d), f1, q_cz, q_cy0, q_cy, q_cxz, q_cxy0, q_cxy)[:3]
    f_y13, f2 = to_y(f_13), to_z(f_1, 1)
    dy_c, dy_xc = to_core(grad_y), to_core(dy_x)

    def pieces(value):
        return value.reshape(value.shape[0] // 48, 48, value.shape[1])

    got_q = [
        pieces(v)
        for v in (q_z, q_y0, q_y, q_xz, q_xy0, q_xy, q_cz, q_cy0, q_cy, q_cxz, q_cxy0, q_cxy)
    ]
    seg = jnp.concatenate([segment_ids, segment_ids], axis=1)
    front = call(
        front_kernel,
        [VM] * 6 + [AN] * 15,
        [VM] * 11,
        [
            shape_of((tok, width), bf),
            shape_of((keys, 2 * width), bf),
            shape_of((keys, width), bf),
            shape_of((tok, width), bf),
            shape_of((width // 128, 1, 2 * tok), fl),
            shape_of((1, 2 * tok), jnp.int32),
            shape_of((8, width), fl),
            shape_of((8, width), fl),
            shape_of((width, width), bf),
            shape_of((tok, width), fl),
            shape_of((tok, width), bf),
        ],
        [
            pltpu.VMEM((width, 3 * width), bf),
            pltpu.VMEM((8, 16, 128), bf),
            pltpu.VMEM((keys, 2 * tok), fl),
            dma((2 + 56,)),
            dma((8,)),
        ],
        flops=7 * 10**9,
        vmem=16, moved=12 * 10**6,
    )(
        seg, own_tokens, x1, x2, x3, x4, piece_q, query_key_value_weight, output_weight, *got_q,
    )
    *front, f_y13, f2, dy_c, dy_xc = fence(*front, f_y13, f2, dy_c, dy_xc)
    queries, kv, normed, attended, lse, start, vec, upb, w_out, residual, hidden_2 = front
    w_half = call(
        assemble_kernel,
        [AN] * 7,
        [VM] * 2,
        [shape_of((width, width), bf)] * 2,
        [dma((14,))],
        vmem=4,
        moved=5 * 10**6,
    )(piece_f, f1, f2, f3u, f3d, f_y0, f_y13)
    h_x, h_c, f_y2, *w_half = fence(to_x(hidden_2), to_core(hidden_2), to_y(f2), *w_half)
    act = shape_of((2 * tok, width), bf)
    acts = shape_of((4 * tok, width), bf)
    feed_shapes = [shape_of((2, tok, width), fl), shape_of((2, tok, width), bf)]
    feed_scratch = [pltpu.VMEM((2 * tok, width), fl), pltpu.VMEM((2 * tok, width), fl)]
    *near_acts, keep_a, send_a, w_up, w_down = call(
        near_kernel,
        [VM] * 5 + [AN] + [VM] * 2,
        [VM] * 8,
        [act] * 4 + feed_shapes + [shape_of((width, width), bf)] * 2,
        feed_scratch + [dma((2,))],
        flops=3 * 10**9,
        vmem=8,
        moved=6 * 10**6,
        aliases={6: 6, 7: 7},
    )(hidden_2, h_c, grad_y, dy_c, upb, f_y2, *w_half)
    h_xc = to_core(h_x)
    keep_a, send_a, h_xc, w_up = fence(keep_a, send_a, h_xc, w_up)
    came_a = to_core(send_a)
    *all_acts, keep_b, send_b = call(
        far_kernel,
        [VM] * 7 + [AN] * 4,
        [VM] * 6,
        [acts] * 4 + feed_shapes,
        feed_scratch + [dma((4,))],
        flops=3 * 10**9,
        vmem=8, moved=6 * 10**6,
    )(h_x, h_xc, dy_x, dy_xc, upb, w_up, w_down, *near_acts)
    keep_b, send_b, came_a = fence(keep_b, send_b, came_a)
    keep_b, came_b, *all_acts = fence(keep_b, to_core(send_b), *all_acts)
    back_x = to_x(b16(keep_b[0] + f32(came_b[0])))
    u_terms, d_terms, upb_g = call(
        weights_kernel,
        [VM] * 4,
        [AN, AN, VM],
        [shape_of((2, 4, 96, width), bf), shape_of((2, 4, 96, width), bf), shape_of((1, width), fl)],
        [pltpu.VMEM((2, width, width), bf), dma((16,))],
        flops=3 * 10**9,
        vmem=12, moved=6 * 10**6,
    )(*all_acts)
    back_x, u_terms, d_terms, keep_b = fence(back_x, u_terms, d_terms, keep_b)
    u_came = to_y(u_terms[1])
    back_y = to_x(b16(keep_b[1] + f32(came_b[1])))
    grad_first, grad_attended, dw_out, vec_g = call(
        post_kernel,
        [VM] * 8,
        [VM] * 4,
        [
            shape_of((tok, width), fl),
            shape_of((tok, width), bf),
            shape_of((width, width), fl),
            shape_of((8, width), fl),
        ],
        vmem=12,
        flops=10**9,
        moved=4 * 10**6,
    )(residual, keep_a, came_a, back_x, grad_y, vec, w_out, attended)
    back_scratch = [
        pltpu.VMEM((keys, 2 * tok), fl),
    ]
    qa_other, qa_mine, dq_a, dkv_a = call(
        back_a_kernel,
        [VM] * 7,
        [AN] * 2 + [VM] * 2,
        [
            shape_of((2, 2, 4, 120, width // 2), bf),
            shape_of((2, 2, 4, 120, width // 2), bf),
            shape_of((tok, width // 2), bf),
            shape_of((keys, width), bf),
        ],
        back_scratch + [pltpu.VMEM((2, 2, 8, 120, width // 2), bf), dma((32,))],
        flops=5 * 10**9,
        vmem=16, moved=10 * 10**6,
    )(start, queries, kv, normed, lse, grad_attended, dw_out)

    def both(mine, came):
        return lambda *index: f32(mine[index]) + f32(came[index])

    def z_sum(part, *came):
        return b16(part(0) + sum(f32(v) for v in came))

    dq_a, qa_other, u_came, back_y, d_send = fence(
        dq_a, qa_other, u_came, back_y, d_terms[1]
    )
    d_came, qa_came = to_y(d_send), to_core(qa_other)
    u_part = both(u_terms[0], u_came)
    u_z = [to_z(b16(u_part(step)), step) for step in (1, 2, 3)]
    dq_b, dkv_b, p_own, p_y, p_z, sums = call(
        back_b_kernel,
        [VM] * 14 + [AN] * 13,
        [VM] * 6,
        [
            shape_of((tok, width // 2), bf),
            shape_of((keys, width), bf),
            shape_of((tok, width), fl),
            shape_of((2, tok, width), bf),
            shape_of((2, tok, width), bf),
            shape_of((8, 8, 256), fl),
        ],
        [pltpu.VMEM((width, 3 * width), bf)] + back_scratch + [dma((1 + 28,))],
        flops=6 * 10**9,
        vmem=20, moved=10 * 10**6,
    )(
        start, queries, kv, lse, grad_attended, vec_g, upb_g, dq_a, dkv_a,
        own_tokens, x1, x2, x3, x4, query_key_value_weight, *got_q,
    )
    dq_b, qa_came, d_came, p_y, *u_z = fence(dq_b, qa_came, d_came, p_y, *u_z)
    p_came = to_y(p_y)
    qa_1 = both(qa_mine, qa_came)
    qa_x = to_x(b16(qa_1(1)))
    d_part = both(d_terms[0], d_came)
    d_z2 = to_z(b16(d_part(2)), 1)
    qb_other, qb_mine = call(
        back_c_kernel,
        [VM] * 4,
        [AN] * 2,
        [
            shape_of((2, 2, 4, 80, width // 2), bf),
            shape_of((2, 2, 4, 80, width // 2), bf),
        ],
        [pltpu.VMEM((2, 2, 8, 80, width // 2), bf), dma((32,))],
        flops=3 * 10**9,
        vmem=12, moved=6 * 10**6,
    )(normed, dq_b, dkv_b, sums)
    qb_came = [to_core(qb_other[k]) for k in range(2)]
    *qb_came, qa_x, p_came, d_z2 = fence(*qb_came, qa_x, p_came, d_z2)
    even = y == 0
    sum_own = p_own + jnp.where(even, f32(p_came[0]), 0.0)
    sum_4 = b16(f32(p_z[1]) + jnp.where(even, 0.0, f32(p_came[1])))
    sum_2 = f32(p_z[0]) + jnp.where(even, f32(p_came[1]), f32(p_came[0]))
    def qa_2(*index):
        return qa_1(0, *index) + f32(qa_x[index])

    def qb_1(side, *index):
        return f32(qb_mine[(side,) + index]) + f32(qb_came[side][index])

    qb_x, qa_y, hop, d_z1, d_z3 = fence(
        to_x(b16(qb_1(1))),
        to_y(b16(qa_2(1))),
        to_z(sum_4, 3),
        to_z(b16(d_part(1) + f32(d_z2)), 1),
        to_z(b16(d_part(3)), 3),
    )

    def qb_2(*index):
        return qb_1(0, *index) + f32(qb_x[index])

    f_tot = join(z_sum(u_part, *u_z), z_sum(d_part, d_z1, d_z3))
    qb_y, back_2, f_tot = fence(to_y(b16(qb_2(1))), to_z(b16(sum_2 + f32(hop)), 3), f_tot)

    def q_3(*index):
        first = qa_2(0, *index) + f32(qa_y[index])
        return jnp.concatenate([first, qb_2(0, *index) + f32(qb_y[index])], axis=-2)

    grad_tokens = call(
        tokens_kernel, [VM] * 5, VM, shape_of((tok, width), fl), vmem=4, moved=3 * 10**6
    )(sum_own, back_2, grad_first, own_tokens, vec)
    *q_z, f_x, f_tot = fence(*(to_z(b16(q_3(step)), step) for step in (1, 2, 3)), to_x(f_tot), f_tot)
    q_sum = z_sum(q_3, *q_z)
    q_fx, q_fc, q_fxc = to_x(q_sum), to_core(q_sum), swap_rep(q_sum, 3)
    grad_up, grad_down = call(
        finish_f_kernel,
        [VM] * 4,
        [VM] * 2,
        [shape_of(up_weight.shape, fl), shape_of(down_weight.shape, fl)],
        [pltpu.VMEM((4, 96, width), bf)],
        vmem=8,
        moved=4 * 10**6,
    )(f_tot, f_x, to_core(f_tot), to_core(f_x))
    q_fx, q_fc, q_fxc, grad_up, grad_down = fence(q_fx, q_fc, q_fxc, grad_up, grad_down)
    result = b16(residual + vec[7:8] + keep_a[1] + f32(came_a[1]) + f32(back_y))
    grad_qkv, grad_out = call(
        finish_q_kernel,
        [VM] * 4,
        [VM] * 2,
        [shape_of(query_key_value_weight.shape, fl), shape_of(output_weight.shape, fl)],
        vmem=8, moved=3 * 10**6,
    )(q_sum, q_fx, q_fc, q_fxc)
    sums = f32(q_sum[192:200, :256])
    part = ln_gains.shape[1]
    return (
        result[None],
        grad_tokens[None],
        grad_qkv,
        grad_out,
        grad_up,
        grad_down,
        sums[0:2, :part],
        sums[2:4, :part],
        sums[4:8, :part],
        sums[0:4, 128 : 128 + part].reshape(4 * part),
    )


def solution(mesh):
    placed = (
        P("rep", "seq", None),
        P("rep", "seq"),
        P("seq", None),
        P("seq", None),
        P("seq", None),
        P("seq", None),
        P(None, "seq"),
        P(None, "seq"),
        P(None, "seq"),
        P("seq"),
        P("rep", "seq", None),
    )
    shape = dict(mesh.shape)
    small_slice = shape["rep"] == 4 and shape["seq"] == 8
    return jax.shard_map(
        on_device_fast if small_slice else on_device,
        mesh=mesh,
        in_specs=placed,
        out_specs=(
            P("rep", "seq", None),
            P("rep", "seq", None),
            P("seq", None),
            P("seq", None),
            P("seq", None),
            P("seq", None),
            P(None, "seq"),
            P(None, "seq"),
            P(None, "seq"),
            P("seq"),
        ),
        check_vma=False,
    )
```

```python
import math

import jax
import jax.numpy as jnp
from jax import lax
from jax.experimental import pallas as pl
from jax.experimental.pallas import tpu as pltpu
from jax.sharding import PartitionSpec as P

HEADS = 12
HD = 64


norm_eps = 1e-05
floor_score = -1e30


def layer_norm(values, gain, shift):
    center = values - jnp.mean(values, axis=-1, keepdims=True)
    spread = jnp.mean(center * center, axis=-1, keepdims=True)
    return center * lax.rsqrt(spread + norm_eps) * gain + shift


def head_split(matrix):
    return matrix.reshape(matrix.shape[0], HEADS, HD)


def masked_scores(queries, query_seg, query_pos, key_piece, seg_piece, offset):
    rows = key_piece.shape[0]
    scores = jnp.einsum(
        "qhd,khd->hqk", queries, head_split(key_piece), preferred_element_type=jnp.float32
    ) * HD ** (-0.5)
    key_pos = offset + jnp.arange(rows, dtype=jnp.int32)
    allowed = (query_seg[:, None] == seg_piece[None, :]) & (key_pos[None, :] <= query_pos[:, None])
    return (jnp.where(allowed[None], scores, floor_score), allowed)


def forward_block(running, pieces, offset, queries, query_seg, query_pos):
    top_run, total_run, accum = running
    key_piece, value_piece, seg_piece = pieces
    scores, allowed = masked_scores(queries, query_seg, query_pos, key_piece, seg_piece, offset)
    top_new = jnp.maximum(top_run, jnp.max(scores, axis=-1))
    probs = jnp.where(allowed[None], jnp.exp(scores - top_new[:, :, None]), 0.0)
    factor = jnp.exp(top_run - top_new)
    total_new = total_run * factor + jnp.sum(probs, axis=-1)
    update = jnp.einsum(
        "hqk,khd->qhd",
        probs.astype(jnp.bfloat16),
        head_split(value_piece),
        preferred_element_type=jnp.float32,
    )
    return (top_new, total_new, accum * factor.T[:, :, None] + update)


def in_blocks(block_fn, running, pieces):
    rows = pieces[0].shape[0]
    size = math.gcd(rows, 1024)
    stacked = tuple((member.reshape((rows // size, size) + member.shape[1:]) for member in pieces))
    offsets = jnp.arange(rows // size, dtype=jnp.int32) * size

    def scan_step(state_now, element):
        return (block_fn(state_now, element[0], element[1]), None)

    running, _unused = lax.scan(scan_step, running, (stacked, offsets))
    return running


def backward_block(
    number,
    state_now,
    whole,
    queries,
    query_seg,
    query_pos,
    grad_heads,
    log_total,
    delta,
    block_rows,
):
    grad_query, term = state_now
    offset = number * block_rows
    key_piece = lax.dynamic_slice_in_dim(whole[0], offset, block_rows, 0)
    value_piece = lax.dynamic_slice_in_dim(whole[1], offset, block_rows, 0)
    seg_piece = lax.dynamic_slice_in_dim(whole[2], offset, block_rows, 0)
    scores, allowed = masked_scores(queries, query_seg, query_pos, key_piece, seg_piece, offset)
    probs = jnp.where(allowed[None], jnp.exp(scores - log_total[:, :, None]), 0.0)
    grad_probs = jnp.einsum(
        "qhd,khd->hqk", grad_heads, head_split(value_piece), preferred_element_type=jnp.float32
    )
    grad_scores = (probs * (grad_probs - delta[:, :, None])).astype(jnp.bfloat16)
    grad_query = grad_query + jnp.einsum(
        "hqk,khd->qhd", grad_scores, head_split(key_piece), preferred_element_type=jnp.float32
    )
    grad_key = jnp.einsum(
        "hqk,qhd->khd", grad_scores, queries, preferred_element_type=jnp.float32
    ) * HD ** (-0.5)
    grad_value = jnp.einsum(
        "hqk,qhd->khd", probs.astype(jnp.bfloat16), grad_heads, preferred_element_type=jnp.float32
    )
    joined = jnp.concatenate(
        [grad_key.reshape(block_rows, -1), grad_value.reshape(block_rows, -1)], axis=1
    )
    term = lax.dynamic_update_slice_in_dim(term, joined, offset, 0)
    return (grad_query, term)


def on_device(
    tokens,
    segment_ids,
    query_key_value_weight,
    output_weight,
    up_weight,
    down_weight,
    ln_gains,
    ln_biases,
    biases,
    up_projection_bias,
    cotangent,
):
    gathered = (
        lax.all_gather(query_key_value_weight, "seq", axis=0, tiled=True),
        lax.all_gather(output_weight, "seq", axis=0, tiled=True),
        lax.all_gather(up_weight, "seq", axis=0, tiled=True),
        lax.all_gather(down_weight, "seq", axis=0, tiled=True),
        lax.all_gather(ln_gains, "seq", axis=1, tiled=True),
        lax.all_gather(ln_biases, "seq", axis=1, tiled=True),
        lax.all_gather(biases, "seq", axis=1, tiled=True),
        lax.all_gather(up_projection_bias, "seq", axis=0, tiled=True),
    )
    full_qkv, full_out, full_up, full_down, gains_all, shifts_all, biases_all, up_shift = gathered
    gains_f = gains_all.astype(jnp.float32)
    shifts_f = shifts_all.astype(jnp.float32)
    biases_f = biases_all.astype(jnp.float32)
    up_shift_f = up_shift.astype(jnp.float32)
    tokens_f = tokens[0].astype(jnp.float32)
    seg_local = segment_ids[0]
    tok_rows = tokens_f.shape[0]
    width = tokens_f.shape[1]
    seqlen = tok_rows * lax.axis_size("seq")
    query_pos = lax.axis_index("seq") * tok_rows + jnp.arange(tok_rows, dtype=jnp.int32)
    hidden_first = layer_norm(tokens_f, gains_f[0], shifts_f[0]).astype(jnp.bfloat16)
    query_key_value_bias = jnp.concatenate(
        [biases_f[0], jnp.zeros((width,), jnp.float32), biases_f[1]]
    )
    projected_rows = (
        jnp.dot(hidden_first, full_qkv, preferred_element_type=jnp.float32) + query_key_value_bias
    ).astype(jnp.bfloat16)
    queries = head_split(projected_rows[:, :width])
    key_rows = projected_rows[:, width : 2 * width]
    value_rows = projected_rows[:, 2 * width :]
    initial = (
        jnp.full((HEADS, tok_rows), floor_score, jnp.float32),
        jnp.zeros((HEADS, tok_rows), jnp.float32),
        jnp.zeros((tok_rows, HEADS, HD), jnp.float32),
    )

    def block_fn(running, pieces, offset):
        return forward_block(running, pieces, offset, queries, seg_local, query_pos)

    block_rows = math.gcd(seqlen, 1024)
    key_end = (lax.axis_index("seq") + 1) * tok_rows
    block_count = (key_end + block_rows - 1) // block_rows
    top_run, total_run, accum = in_blocks(
        block_fn,
        initial,
        (
            lax.all_gather(key_rows, "seq", axis=0, tiled=True),
            lax.all_gather(value_rows, "seq", axis=0, tiled=True),
            lax.all_gather(seg_local, "seq", axis=0, tiled=True),
        ),
    )
    log_total = top_run + jnp.log(total_run)
    attended_f = accum / total_run.T[:, :, None]
    attention_result = attended_f.reshape(tok_rows, width).astype(jnp.bfloat16)
    residual_first = (
        tokens_f
        + jnp.dot(attention_result, full_out, preferred_element_type=jnp.float32)
        + biases_f[2]
    )
    hidden_second = layer_norm(residual_first, gains_f[1], shifts_f[1]).astype(jnp.bfloat16)
    upward_rows = jnp.dot(hidden_second, full_up, preferred_element_type=jnp.float32) + up_shift_f
    activated_f, gelu_back = jax.vjp(jax.nn.gelu, upward_rows)
    activation_values = activated_f.astype(jnp.bfloat16)
    result = (
        residual_first
        + jnp.dot(activation_values, full_down, preferred_element_type=jnp.float32)
        + biases_f[3]
    )
    grad_y = cotangent[0]
    grad_y_f = grad_y.astype(jnp.float32)
    grad_down = jnp.einsum(
        "tf,td->fd", activation_values, grad_y, preferred_element_type=jnp.float32
    )
    grad_act = jnp.einsum("td,fd->tf", grad_y, full_down, preferred_element_type=jnp.float32)
    grad_up_pre = gelu_back(grad_act)[0].astype(jnp.bfloat16)
    grad_up = jnp.einsum(
        "td,tf->df", hidden_second, grad_up_pre, preferred_element_type=jnp.float32
    )
    grad_hidden_two = jnp.einsum(
        "tf,df->td", grad_up_pre, full_up, preferred_element_type=jnp.float32
    )
    _unused, norm_two_back = jax.vjp(layer_norm, residual_first, gains_f[1], shifts_f[1])
    grad_sum_part, grad_gain_two, grad_shift_two = norm_two_back(grad_hidden_two)
    grad_first = grad_y_f + grad_sum_part
    grad_first_bf = grad_first.astype(jnp.bfloat16)
    grad_out_w = jnp.einsum(
        "td,te->de", attention_result, grad_first_bf, preferred_element_type=jnp.float32
    )
    grad_attended = jnp.einsum(
        "te,de->td", grad_first_bf, full_out, preferred_element_type=jnp.float32
    ).astype(jnp.bfloat16)
    grad_heads = head_split(grad_attended)
    delta = jnp.einsum("qhd,qhd->hq", grad_heads.astype(jnp.float32), attended_f)
    whole = (
        lax.all_gather(key_rows, "seq", axis=0, tiled=True),
        lax.all_gather(value_rows, "seq", axis=0, tiled=True),
        lax.all_gather(seg_local, "seq", axis=0, tiled=True),
    )

    def backward_step(number, state_now):
        return backward_block(
            number,
            state_now,
            whole,
            queries,
            seg_local,
            query_pos,
            grad_heads,
            log_total,
            delta,
            block_rows,
        )

    start_state = (
        jnp.zeros((tok_rows, HEADS, HD), jnp.float32),
        jnp.zeros((seqlen, 2 * width), jnp.float32),
    )
    grad_query, term = lax.fori_loop(0, block_count, backward_step, start_state)
    grad_kv = lax.psum_scatter(term, "seq", scatter_dimension=0, tiled=True).astype(jnp.bfloat16)
    grad_q = (grad_query * HD ** (-0.5)).reshape(tok_rows, width).astype(jnp.bfloat16)
    grad_proj = jnp.concatenate([grad_q, grad_kv], axis=1)
    grad_qkv_w = jnp.einsum(
        "td,te->de", hidden_first, grad_proj, preferred_element_type=jnp.float32
    )
    grad_hidden_one = jnp.einsum(
        "te,de->td", grad_proj, full_qkv, preferred_element_type=jnp.float32
    )
    _unused_two, norm_one_back = jax.vjp(layer_norm, tokens_f, gains_f[0], shifts_f[0])
    grad_in_part, grad_gain_one, grad_shift_one = norm_one_back(grad_hidden_one)
    grad_tokens = grad_first + grad_in_part
    grad_proj_f = grad_proj.astype(jnp.float32)
    grad_bias_rows = jnp.stack(
        [
            jnp.sum(grad_proj_f[:, :width], axis=0),
            jnp.sum(grad_proj_f[:, 2 * width :], axis=0),
            jnp.sum(grad_first, axis=0),
            jnp.sum(grad_y_f, axis=0),
        ]
    )
    grad_up_shift = jnp.sum(grad_up_pre.astype(jnp.float32), axis=0)
    grad_gains = jnp.stack([grad_gain_one, grad_gain_two])
    grad_shifts = jnp.stack([grad_shift_one, grad_shift_two])
    shares = (
        lax.psum_scatter(grad_qkv_w, "seq", scatter_dimension=0, tiled=True),
        lax.psum_scatter(grad_out_w, "seq", scatter_dimension=0, tiled=True),
        lax.psum_scatter(grad_up, "seq", scatter_dimension=0, tiled=True),
        lax.psum_scatter(grad_down, "seq", scatter_dimension=0, tiled=True),
        lax.psum_scatter(grad_gains, "seq", scatter_dimension=1, tiled=True),
        lax.psum_scatter(grad_shifts, "seq", scatter_dimension=1, tiled=True),
        lax.psum_scatter(grad_bias_rows, "seq", scatter_dimension=1, tiled=True),
        lax.psum_scatter(grad_up_shift, "seq", scatter_dimension=0, tiled=True),
    )
    totals = (
        lax.psum(shares[0].astype(jnp.bfloat16), "rep").astype(jnp.float32),
        lax.psum(shares[1].astype(jnp.bfloat16), "rep").astype(jnp.float32),
        lax.psum(shares[2].astype(jnp.bfloat16), "rep").astype(jnp.float32),
        lax.psum(shares[3].astype(jnp.bfloat16), "rep").astype(jnp.float32),
        lax.psum(shares[4].astype(jnp.bfloat16), "rep").astype(jnp.float32),
        lax.psum(shares[5].astype(jnp.bfloat16), "rep").astype(jnp.float32),
        lax.psum(shares[6].astype(jnp.bfloat16), "rep").astype(jnp.float32),
        lax.psum(shares[7].astype(jnp.bfloat16), "rep").astype(jnp.float32),
    )
    return (
        result.astype(jnp.bfloat16)[None],
        grad_tokens[None],
        totals[0],
        totals[1],
        totals[2],
        totals[3],
        totals[4],
        totals[5],
        totals[6],
        totals[7],
    )


def f32(value):
    return value.astype(jnp.float32)


def b16(value):
    return value.astype(jnp.bfloat16)


def dot_nn(left, right):
    return jnp.dot(left, right, preferred_element_type=jnp.float32)


def dot_nt(left, right):
    return lax.dot_general(
        left, right, (((1,), (1,)), ((), ())), preferred_element_type=jnp.float32
    )


def dot_tn(left, right):
    return lax.dot_general(
        left, right, (((0,), (0,)), ((), ())), preferred_element_type=jnp.float32
    )


def norm_parts(values):
    center = values - jnp.mean(values, axis=-1, keepdims=True)
    rate = lax.rsqrt(jnp.mean(center * center, axis=-1, keepdims=True) + norm_eps)
    return center * rate, rate


def norm_back(grad, hat, rate, gain):
    scaled = grad * gain
    return rate * (
        scaled
        - jnp.mean(scaled, axis=-1, keepdims=True)
        - hat * jnp.mean(scaled * hat, axis=-1, keepdims=True)
    )


def place():
    rep, seq = lax.axis_index("rep"), lax.axis_index("seq")
    return lax.div(rep, 2), lax.rem(rep, 2), lax.rem(seq, 2), lax.div(seq, 2)


def piece_shard(number, y, z):
    if number < 3:
        return 2 * lax.rem(z + 3 - number, 4) + y
    return 2 * lax.rem(z + 7 - number, 4) + 1 - y


def pack96(parts):
    lane = lax.broadcasted_iota(jnp.int32, parts[0].shape, 1)
    one, two, three = (pltpu.roll(parts[k], 128 - 32 * k, 1) for k in (1, 2, 3))
    return jnp.concatenate(
        [
            jnp.where(lane < 96, parts[0], one),
            jnp.where(lane < 64, one, two),
            jnp.where(lane < 32, two, three),
        ],
        axis=1,
    )


def unpack96(block):
    tiles = [block[:, 128 * k : 128 * k + 128] for k in range(3)]
    lane = lax.broadcasted_iota(jnp.int32, tiles[0].shape, 1)
    return [
        tiles[0],
        jnp.where(lane < 32, pltpu.roll(tiles[0], 32, 1), pltpu.roll(tiles[1], 32, 1)),
        jnp.where(lane < 64, pltpu.roll(tiles[1], 64, 1), pltpu.roll(tiles[2], 64, 1)),
        pltpu.roll(tiles[2], 96, 1),
    ]


def choose(parts, index):
    out = parts[0]
    for number in range(1, len(parts)):
        out = jnp.where(index == number, parts[number], out)
    return out


class Copies:
    def __init__(self, sems, first=0):
        self.sems = sems
        self.first = first
        self.held = []

    def add(self, source, target):
        copy = pltpu.make_async_copy(source, target, self.sems.at[self.first + len(self.held)])
        copy.start()
        self.held.append(copy)

    def wait(self):
        for copy in self.held:
            copy.wait()
        self.held = []


def corners(x, c):
    return ((x, c), (1 - x, c), (x, 1 - c), (1 - x, 1 - c))


def fetch_qkv(copies, own, groups, full, full_out=None, own_out=None):
    x, c, y, z = place()
    rows = own.shape[0]
    half, width = rows // 2, own.shape[1] // 3
    row = pl.multiple_of((2 * z + y) * rows, 16)
    copies.add(own, full.at[pl.ds(row, rows), :])
    if full_out is not None:
        copies.add(own_out, full_out.at[pl.ds(row, rows), :])
    wide, side = 3 * width // 2, width // 2
    for number in range(7):
        for (xx, cc), group in zip(corners(x, c), groups, strict=True):
            piece = piece_of(group, number)
            at = pl.ds(pl.multiple_of(piece_shard(number, y, z) * rows + half * cc, 16), half)
            copies.add(
                piece.at[pl.ds(0, half), pl.ds(0, wide)],
                full.at[at, pl.ds(pl.multiple_of(wide * xx, 128), wide)],
            )
            if full_out is not None:
                copies.add(
                    piece.at[pl.ds(0, half), pl.ds(wide, side)],
                    full_out.at[at, pl.ds(pl.multiple_of(side * xx, 128), side)],
                )


def piece_of(group, number):
    behind, across, behind_across = group
    if number < 3:
        return behind.at[number]
    return across.at[0] if number == 3 else behind_across.at[number - 4]


def mask_bias(start, me, tok, target):
    keys, lanes = target.shape
    key_pos = (me - 4) * tok + lax.broadcasted_iota(jnp.int32, (keys, lanes), 0)
    lane = lax.broadcasted_iota(jnp.int32, (keys, lanes), 1)
    query_pos = me * tok + jnp.where(lane >= tok, lane - tok, lane)
    target[...] = jnp.where((key_pos >= start) & (key_pos <= query_pos), 0.0, floor_score)


def pair_stack(rows):
    lane = lax.broadcasted_iota(jnp.int32, rows.shape, 1)
    zero = jnp.zeros_like(rows)
    return jnp.concatenate([jnp.where(lane < HD, rows, zero), jnp.where(lane < HD, zero, rows)], axis=0)


def pair_join(transposed):
    both = transposed.T
    tok = both.shape[0] // 2
    lane = lax.broadcasted_iota(jnp.int32, (tok, 2 * HD), 1)
    return jnp.where(lane < HD, both[:tok], both[tok:])


def prep_kernel(
    tokens, segs, qkv, out, up, down, gains, shifts, biases, up_bias,
    t_out, q_out, f_out, fu_out, fd_out,
    scratch, wide, held_g, held_s, held_b, ids, line, sems,
):
    x, c, _y, _z = place()
    tok, width = tokens.shape[1:]
    rows = qkv.shape[0]
    half, side = rows // 2, width // 2
    p = 2 * x + c
    at = pl.ds(pl.multiple_of(half * c, 16), half)
    copies, others = Copies(sems), Copies(sems, 5)
    for source, target in ((gains, held_g), (shifts, held_s), (biases, held_b)):
        copies.add(source, target)
    copies.add(segs, ids)
    copies.add(up_bias, line)
    others.add(up, wide)
    wide_cols = 3 * side
    others.add(
        qkv.at[at, pl.ds(pl.multiple_of(wide_cols * x, 128), wide_cols)],
        q_out.at[pl.ds(0, half), pl.ds(0, wide_cols)],
    )
    others.add(
        out.at[at, pl.ds(pl.multiple_of(side * x, 128), side)],
        q_out.at[pl.ds(0, half), pl.ds(wide_cols, side)],
    )
    others.add(tokens.at[0], t_out.at[pl.ds(0, tok), :])
    own_rows = down.at[pl.ds(pl.multiple_of(rows * p, 16), rows), :]
    others.add(own_rows, f_out.at[pl.ds(rows, rows), :])
    others.add(own_rows, fd_out)
    copies.wait()
    scratch[...] = jnp.zeros_like(scratch)
    for first, held in ((0, held_g), (2, held_s), (4, held_b)):
        scratch[pl.ds(first, held.shape[0]), pl.ds(0, rows)] = f32(held[...])
    parts = unpack96(jnp.broadcast_to(f32(line[...]).reshape(1, line.shape[0]), (8, line.shape[0])))
    lane = lax.broadcasted_iota(jnp.int32, (8, 128), 1)
    row = lax.broadcasted_iota(jnp.int32, (8, 128), 0)
    ups = jnp.zeros((8, 128), jnp.float32)
    for number in range(4):
        ups = jnp.where((row == number) & (lane < rows), parts[number], ups)
    smalls = b16(jnp.concatenate([scratch[:, pl.ds(0, 128)], ups], axis=0))
    q_out[pl.ds(0, 16), pl.ds(2 * width, 128)] = smalls
    q_out[pl.ds(16, half - 16), pl.ds(2 * width, 128)] = jnp.zeros((half - 16, 128), jnp.bfloat16)
    scratch[...] = jnp.zeros_like(scratch)
    scratch[pl.ds(0, 1), pl.ds(0, tok)] = f32(ids[...])
    t_out[pl.ds(tok, 8), :] = b16(scratch[...])
    others.wait()
    for group in range(2):
        parts = []
        for shard in range(4 * group, 4 * group + 4):
            parts.append(choose(unpack96(f32(wide[:, pl.ds(384 * shard, 384)])), p))
        packed = b16(pack96(parts))
        f_out[pl.ds(0, rows), pl.ds(384 * group, 384)] = packed
        fu_out[:, pl.ds(384 * group, 384)] = packed


def front_kernel(
    seg, xo, x1, x2, x3, x4, first, own, own_o,
    g0, g1, g2, g3, g4, g5, g6, g7, g8, g9, g10, g11,
    q_out, kv_out, h_out, a_out, lse_out, start_out, vec_out, upb_out, wo_out, r_out, h2_out,
    full, small, bias, sems, vsems,
):
    x, c, y, z = place()
    me = 2 * z + y
    p = 2 * x + c
    tok, width = q_out.shape
    copies, vcopies = Copies(sems), Copies(vsems)
    vcopies.add(first.at[pl.ds(0, 16), pl.ds(2 * width, 128)], small.at[me])
    for number in range(7):
        source = piece_of((g0, g1, g2), number)
        vcopies.add(source.at[pl.ds(0, 16), pl.ds(2 * width, 128)], small.at[piece_shard(number, y, z)])
    groups = ((g0, g1, g2), (g3, g4, g5), (g6, g7, g8), (g9, g10, g11))
    fetch_qkv(copies, own, groups, full, wo_out, own_o)
    blocks = (xo, x1, x2, x3, x4)
    lane1 = lax.broadcasted_iota(jnp.int32, (1, tok), 1)
    start = jnp.full(seg.shape, 1 << 30, jnp.int32)
    for number in range(4):
        first_pos = jnp.full((1, 1), 1 << 30, jnp.int32)
        for back in range(5):
            ids = f32(blocks[back][pl.ds(tok, 8), pl.ds(0, tok)])[:1]
            pos = (me - back) * tok + lane1
            hit = (ids == float(number)) & (pos >= 0)
            first_pos = jnp.minimum(
                first_pos, jnp.min(jnp.where(hit, pos, 1 << 30), axis=1, keepdims=True)
            )
        start = jnp.where(seg[...] == number, first_pos, start)
    start_out[...] = start
    mask_bias(start, me, tok, bias)
    vcopies.wait()
    for group in range(2):
        held = [f32(small[4 * group + k]) for k in range(4)]
        vec_out[:, pl.ds(384 * group, 384)] = pack96([block[:8] for block in held])
        upb_out[:, pl.ds(384 * group, 384)] = pack96(
            [choose([jnp.broadcast_to(block[k : k + 1], (8, 128)) for k in range(8, 12)], p) for block in held]
        )
    vec = vec_out[...]
    for back in range(5):
        hat, _rate = norm_parts(f32(blocks[back][pl.ds(0, tok), :]))
        h_out[pl.ds((4 - back) * tok, tok), :] = b16(hat * vec[0:1] + vec[2:3])
    copies.wait()
    q_out[...] = b16(dot_nn(h_out[pl.ds(4 * tok, tok), :], full[:, pl.ds(0, width)]) + vec[4:5])

    def project(number, carry):
        col = pl.multiple_of(number * 256, 256)
        shift = jnp.where(number >= width // 256, 1.0, 0.0)
        bias_at = lax.rem(number, width // 256)
        piece = vec_out[pl.ds(5, 1), pl.ds(pl.multiple_of(bias_at * 256, 256), 256)]
        kv_out[:, pl.ds(col, 256)] = b16(
            dot_nn(h_out[...], full[:, pl.ds(pl.multiple_of(width + col, 256), 256)]) + piece * shift
        )
        return carry

    lax.fori_loop(0, 2 * width // 256, project, 0)

    def pair(number, carry):
        col = pl.multiple_of(number * 128, 128)
        queries = pair_stack(q_out[:, pl.ds(col, 128)] * jnp.bfloat16(0.125))
        scores = dot_nt(kv_out[:, pl.ds(col, 128)], queries) + bias[...]
        top = jnp.max(scores, axis=0, keepdims=True)
        probs = jnp.exp(scores - top)
        total = jnp.sum(probs, axis=0, keepdims=True)
        mixed = dot_tn(kv_out[:, pl.ds(pl.multiple_of(width + col, 128), 128)], b16(probs))
        a_out[:, pl.ds(col, 128)] = b16(pair_join(mixed / total))
        lse_out[number] = top + jnp.log(total)
        return carry

    lax.fori_loop(0, width // 128, pair, 0)
    residual = f32(xo[pl.ds(0, tok), :]) + dot_nn(a_out[...], wo_out[...]) + vec[6:7]
    r_out[...] = residual
    hat, _rate = norm_parts(residual)
    h2_out[...] = b16(hat * vec[1:2] + vec[3:4])


def feed_tokens(h2, dy, w_up, w_down, upb, act_out, du_out):
    root = math.sqrt(2.0 / math.pi)
    chunk = 256

    def feed(number, carry):
        col = pl.multiple_of(number * chunk, chunk)
        pre = dot_nn(h2[...], w_up[:, pl.ds(col, chunk)]) + upb[pl.ds(0, 1), pl.ds(col, chunk)]
        square = pre * pre
        bend = jnp.tanh(root * pre * (1.0 + 0.044715 * square))
        act = b16(0.5 * pre * (1.0 + bend))
        slope = 0.5 * (1.0 + bend) + 0.5 * pre * (1.0 - bend * bend) * (
            root * (1.0 + 3.0 * 0.044715 * square)
        )
        low = b16(dot_nt(dy[...], w_down[pl.ds(col, chunk), :]) * slope)
        act_out[:, pl.ds(col, chunk)] = act
        du_out[:, pl.ds(col, chunk)] = low
        return carry

    lax.fori_loop(0, w_up.shape[1] // chunk, feed, 0)
    return dot_nt(du_out[...], w_up[...])


def assemble_kernel(own, z1, z2, z3u, z3d, y0, y13, wu_out, wd_out, sems):
    _x, _c, y, z = place()
    rows = own.shape[0] // 2
    copies = Copies(sems)
    pieces = [(own, 2 * z + y)]
    for number, ref in ((0, z1), (1, z2), (3, y0)):
        pieces.append((ref, piece_shard(number, y, z)))
    for number, first in ((4, 0), (6, 2 * rows)):
        pieces.append((y13.at[pl.ds(first, 2 * rows), :], piece_shard(number, y, z)))
    for ref, shard in pieces:
        at = pl.ds(pl.multiple_of(shard * rows, 16), rows)
        copies.add(ref.at[pl.ds(0, rows), :], wu_out.at[at, :])
        copies.add(ref.at[pl.ds(rows, rows), :], wd_out.at[at, :])
    at = pl.ds(pl.multiple_of(piece_shard(2, y, z) * rows, 16), rows)
    copies.add(z3u, wu_out.at[at, :])
    copies.add(z3d, wd_out.at[at, :])
    copies.wait()


def near_kernel(
    h_own, h_c, dy_own, dy_c, upb, y2, _wu, _wd,
    h2, dy, act_out, du_out, keep_out, send_out, wu_out, wd_out,
    sems,
):
    _x, _c, y, z = place()
    tok, width = h_own.shape
    rows = width // 8
    copies = Copies(sems)
    at = pl.ds(pl.multiple_of(piece_shard(5, y, z) * rows, 16), rows)
    copies.add(y2.at[pl.ds(0, rows), :], wu_out.at[at, :])
    copies.add(y2.at[pl.ds(rows, rows), :], wd_out.at[at, :])
    h2[pl.ds(0, tok), :] = h_own[...]
    h2[pl.ds(tok, tok), :] = h_c[...]
    dy[pl.ds(0, tok), :] = dy_own[...]
    dy[pl.ds(tok, tok), :] = dy_c[...]
    copies.wait()
    grad = feed_tokens(h2, dy, wu_out, wd_out, upb, act_out, du_out)
    keep_out[...] = grad[:tok]
    send_out[...] = b16(grad[tok:])


def far_c_kernel(
    h_xc, dy_xc, upb, w_up, w_down, h_near, dy_near, act_near, du_near,
    hs, dys, acts, dus, send_out,
    sems,
):
    tok = dy_xc.shape[0]
    copies = Copies(sems)
    for source, target in ((h_near, hs), (dy_near, dys), (act_near, acts), (du_near, dus)):
        copies.add(source, target.at[pl.ds(0, 2 * tok), :])
    last = pl.ds(3 * tok, tok)
    hs[last, :] = h_xc[...]
    dys[last, :] = dy_xc[...]
    send_out[...] = b16(
        feed_tokens(h_xc, dy_xc, w_up, w_down, upb, acts.at[last, :], dus.at[last, :])
    )
    copies.wait()


def far_x_kernel(
    h_x, dy_x, upb, w_up, w_down, _hs, _dys, _acts, _dus,
    hs, dys, acts, dus, keep_out,
):
    tok = dy_x.shape[0]
    third = pl.ds(2 * tok, tok)
    hs[third, :] = h_x[...]
    dys[third, :] = dy_x[...]
    keep_out[...] = feed_tokens(h_x, dy_x, w_up, w_down, upb, acts.at[third, :], dus.at[third, :])


def weights_kernel(
    hs, dys, acts, dus, w_down,
    u_out, d_out, upb_out, keep_out, send_out,
    stage, sems,
):
    _x, _c, y, z = place()
    width = hs.shape[1]
    rows = width // 8
    upb_out[...] = jnp.sum(f32(dus[...]), axis=0, keepdims=True)

    def weight(number, carry):
        col = pl.multiple_of(number * 256, 256)
        stage[0, pl.ds(col, 256), :] = b16(dot_tn(hs[:, pl.ds(col, 256)], dus[...]))
        stage[1, pl.ds(col, 256), :] = b16(dot_tn(acts[:, pl.ds(col, 256)], dys[...]))
        return carry

    lax.fori_loop(0, width // 256, weight, 0)
    outs = Copies(sems)
    for shard in range(8):
        zz = lax.rem(shard // 2 + 4 - z, 4)
        yy = jnp.where(y == shard % 2, 0, 1)
        outs.add(stage.at[0, pl.ds(shard * rows, rows), :], u_out.at[yy, zz])
        outs.add(stage.at[1, pl.ds(shard * rows, rows), :], d_out.at[yy, zz])
    tok = hs.shape[0] // 4
    for number in range(4):
        part = dot_nn(acts[pl.ds(number * tok, tok), :], w_down[...])
        if number % 2:
            send_out[number // 2] = b16(part)
        else:
            keep_out[number // 2] = part
    outs.wait()


def scatter(stage, other, mine, sems):
    x, c, y, z = place()
    outs = Copies(sems)
    for shard in range(8):
        zz = lax.rem(shard // 2 + 4 - z, 4)
        yy = jnp.where(y == shard % 2, 0, 1)
        for xx in range(2):
            far = jnp.where(x == xx, 0, 1)
            outs.add(stage.at[1 - c, xx, shard], other.at[far, yy, zz])
            outs.add(stage.at[c, xx, shard], mine.at[far, yy, zz])
    outs.wait()


def post_kernel(
    residual, own, near, across, dy_in, vec_in, w_out, a_in,
    dr_out, da_out, dw_out, vec_out,
):
    vec = vec_in[...]
    grad_hidden = own[...] + f32(near[...]) + f32(across[...])
    hat, rate = norm_parts(residual[...])
    dy = f32(dy_in[...])
    grad_first = dy + norm_back(grad_hidden, hat, rate, vec[1:2])
    dr_out[...] = grad_first
    low = b16(grad_first)
    da_out[...] = b16(dot_nt(low, w_out[...]))
    dw_out[...] = dot_tn(a_in[...], low)
    zero = jnp.zeros((1, dy.shape[1]), jnp.float32)
    vec_out[...] = jnp.concatenate(
        [
            zero,
            jnp.sum(grad_hidden * hat, axis=0, keepdims=True),
            zero,
            jnp.sum(grad_hidden, axis=0, keepdims=True),
            zero,
            zero,
            jnp.sum(grad_first, axis=0, keepdims=True),
            jnp.sum(dy, axis=0, keepdims=True),
        ],
        axis=0,
    )


def back_pairs(first, q_in, kv_in, lse_in, da_in, bias, dq, dkv):
    width = q_in.shape[1]

    def pair(number, carry):
        col = pl.multiple_of((first + number) * 128, 128)
        vcol = pl.multiple_of(width + col, 128)
        to = pl.multiple_of(number * 128, 128)
        queries = pair_stack(q_in[:, pl.ds(col, 128)] * jnp.bfloat16(0.125))
        grads = pair_stack(da_in[:, pl.ds(col, 128)])
        keys = kv_in[:, pl.ds(col, 128)]
        probs = jnp.exp(dot_nt(keys, queries) + bias[...] - lse_in[first + number])
        dkv[:, pl.ds(pl.multiple_of(width // 2 + to, 128), 128)] = b16(dot_nn(b16(probs), grads))
        term = probs * dot_nt(kv_in[:, pl.ds(vcol, 128)], grads)
        low = b16(term - probs * jnp.sum(term, axis=0, keepdims=True))
        dkv[:, pl.ds(to, 128)] = b16(dot_nn(low, queries))
        dq[:, pl.ds(to, 128)] = b16(pair_join(dot_tn(keys, low)) * 0.125)
        return carry

    lax.fori_loop(0, 3, pair, 0, unroll=first == 0)


def qkv_weight(h_in, dq, dkv, stage, tail):
    tok, part = dq.shape
    keys = h_in.shape[0]

    def weight(number, carry):
        col = pl.multiple_of(number * 384, 384)
        key = dot_tn(h_in[:, pl.ds(col, 384)], dkv[...])
        query = dot_tn(h_in[pl.ds(keys - tok, tok), pl.ds(col, 384)], dq[...])
        for shard in range(4):
            for cc in range(2):
                for xx in range(2):
                    rows = slice(96 * shard + 48 * cc + 24 * xx, 96 * shard + 48 * cc + 24 * xx + 24)
                    blocks = [query[rows], key[rows, :part], key[rows, part:]] + tail(4 * number + shard, 48 * cc + 24 * xx)
                    stage[cc, xx, 4 * number + shard] = b16(jnp.concatenate(blocks, axis=0))
        return carry

    lax.fori_loop(0, 2, weight, 0)


def back_a_kernel(
    start_in, q_in, kv_in, h_in, lse_in, da_in, dw_in,
    other, mine, dq_out, dkv_out,
    bias, stage, sems,
):
    _x, _c, y, z = place()
    mask_bias(start_in[...], 2 * z + y, q_in.shape[0], bias)
    back_pairs(0, q_in, kv_in, lse_in, da_in, bias, dq_out, dkv_out)
    side = q_in.shape[1] // 2

    def out_rows(shard, row):
        rows = dw_in[pl.ds(pl.multiple_of(96 * shard + row, 8), 24), :]
        return [rows[:, :side], rows[:, side:]]

    qkv_weight(h_in, dq_out, dkv_out, stage, out_rows)
    scatter(stage, other, mine, sems)


def back_b_kernel(
    start_in, q_in, kv_in, lse_in, da_in, vec_in, upb_in, dq_a, dkv_a, xo, x1, x2, x3, x4,
    own, g0, g1, g2, g3, g4, g5, g6, g7, g8, g9, g10, g11,
    dq_out, dkv_out, p_own, p_y, p_z, sums_out,
    full, bias, sems,
):
    x, c, y, z = place()
    p = 2 * x + c
    tok, width = q_in.shape
    side = width // 2
    copies = Copies(sems)
    groups = ((g0, g1, g2), (g3, g4, g5), (g6, g7, g8), (g9, g10, g11))
    fetch_qkv(copies, own, groups, full)
    mask_bias(start_in[...], 2 * z + y, tok, bias)
    back_pairs(3, q_in, kv_in, lse_in, da_in, bias, dq_out, dkv_out)
    copies.wait()
    gain_sum = jnp.zeros((1, width), jnp.float32)
    shift_sum = jnp.zeros((1, width), jnp.float32)
    for back, block in enumerate((xo, x1, x2, x3, x4)):
        rows = pl.ds((4 - back) * tok, tok)
        grad = jnp.zeros((tok, width), jnp.float32)
        for number, (dq, dkv) in enumerate(((dq_a, dkv_a), (dq_out, dkv_out))):
            at = number * side
            grad = grad + dot_nt(dkv[rows, pl.ds(0, side)], full[:, pl.ds(width + at, side)])
            grad = grad + dot_nt(dkv[rows, pl.ds(side, side)], full[:, pl.ds(2 * width + at, side)])
            if back == 0:
                grad = grad + dot_nt(dq[...], full[:, pl.ds(at, side)])
        if back == 0:
            p_own[...] = grad
        elif back in (1, 3):
            p_y[back // 2] = b16(grad)
        else:
            p_z[back // 2 - 1] = b16(grad)
        hat, _rate = norm_parts(f32(block[pl.ds(0, tok), :]))
        gain_sum = gain_sum + jnp.sum(grad * hat, axis=0, keepdims=True)
        shift_sum = shift_sum + jnp.sum(grad, axis=0, keepdims=True)
    zero = jnp.zeros((1, width), jnp.float32)
    bias_q = jnp.concatenate([jnp.sum(f32(d[...]), axis=0, keepdims=True) for d in (dq_a, dq_out)], axis=1)
    bias_v = jnp.concatenate(
        [jnp.sum(f32(d[:, pl.ds(side, side)]), axis=0, keepdims=True) for d in (dkv_a, dkv_out)], axis=1
    )
    vec = vec_in[...] + jnp.concatenate(
        [gain_sum, zero, shift_sum, zero, bias_q, bias_v, zero, zero], axis=0
    )
    lane = lax.broadcasted_iota(jnp.int32, (8, 128), 1)
    line = lax.broadcasted_iota(jnp.int32, (8, 128), 0)
    for group in range(2):
        cols = pl.ds(384 * group, 384)
        vec_parts = unpack96(vec[:, 384 * group : 384 * group + 384])
        upb_parts = unpack96(jnp.broadcast_to(upb_in[:, cols], (8, 384)))
        for k in range(4):
            sums_out[4 * group + k] = jnp.concatenate(
                [
                    jnp.where(lane < 96, vec_parts[k], 0.0),
                    jnp.where((lane < 96) & (line == p), upb_parts[k], 0.0),
                ],
                axis=1,
            )


def back_c_kernel(h_in, dq, dkv, sums_in, other, mine, stage, sems):
    blank = jnp.zeros((8, 128), jnp.float32)
    qkv_weight(
        h_in, dq, dkv, stage, lambda shard, _row: [jnp.concatenate([sums_in[shard], blank], axis=1)]
    )
    scatter(stage, other, mine, sems)


def tokens_kernel(own, near, dr, xo, vec_in, grad_out):
    tok = own.shape[0]
    hat, rate = norm_parts(f32(xo[pl.ds(0, tok), :]))
    grad = own[...] + f32(near[...])
    grad_out[...] = dr[...] + norm_back(grad, hat, rate, vec_in[0:1, :])


def finish_f_kernel(f0, fx, fc, fcx, up, down, held):
    x, c, _y, _z = place()
    rows = f0.shape[0] // 2
    for (xx, cc), f in zip(corners(x, c), (f0, fx, fc, fcx), strict=True):
        p = 2 * xx + cc
        held[p] = f[pl.ds(0, rows), :]
        down[pl.ds(pl.multiple_of(rows * p, 16), rows), :] = f32(f[pl.ds(rows, rows), :])
    for group in range(2):
        parts = [unpack96(f32(held[k, :, pl.ds(384 * group, 384)])) for k in range(4)]
        for shard in range(4):
            up[:, pl.ds(384 * (4 * group + shard), 384)] = pack96([part[shard] for part in parts])


def finish_q_kernel(f0, fx, fc, fcx, qkv, out):
    x, c, _y, _z = place()
    side = out.shape[1] // 2
    for (xx, cc), piece in zip(corners(x, c), (f0, fx, fc, fcx), strict=True):
        rows = pl.ds(pl.multiple_of(48 * cc + 24 * xx, 8), 24)
        blocks = f32(piece[...])
        for number in range(3):
            first, second = 24 * number, 24 * (number + 5)
            qkv[rows, pl.ds(2 * side * number, side)] = blocks[first : first + 24]
            qkv[rows, pl.ds(2 * side * number + side, side)] = blocks[second : second + 24]
        out[rows, pl.ds(0, side)] = blocks[72:96]
        out[rows, pl.ds(side, side)] = blocks[96:120]


HB = pl.BlockSpec(memory_space=pltpu.HBM)
VM = pl.BlockSpec(memory_space=pltpu.VMEM)
AN = pl.BlockSpec(memory_space=pl.ANY)


def shape_of(shape, dtype):
    return jax.ShapeDtypeStruct(shape, dtype)


def call(kernel, ins, outs, out_shape, scratch=(), vmem=40, flops=0, moved=0, aliases=None):
    return pl.pallas_call(
        kernel,
        in_specs=ins,
        out_specs=outs,
        out_shape=out_shape,
        scratch_shapes=list(scratch),
        input_output_aliases=aliases or {},
        compiler_params=pltpu.CompilerParams(vmem_limit_bytes=vmem << 20),
        cost_estimate=pl.CostEstimate(flops=flops, bytes_accessed=moved, transcendentals=0),
    )


def fence(*values):
    return lax.optimization_barrier(values)


def swap_rep(value, bit):
    return lax.ppermute(value, "rep", [(k, k ^ bit) for k in range(4)])


def to_core(value):
    return swap_rep(value, 1)


def to_x(value):
    return swap_rep(value, 2)


def to_y(value):
    return lax.ppermute(value, "seq", [(k, k ^ 1) for k in range(8)])


def to_z(value, steps):
    return lax.ppermute(value, "seq", [(k, (k + 2 * steps) % 8) for k in range(8)])


def join(*parts):
    return jnp.concatenate(parts, axis=0)


def on_device_fast(
    tokens,
    segment_ids,
    query_key_value_weight,
    output_weight,
    up_weight,
    down_weight,
    ln_gains,
    ln_biases,
    biases,
    up_projection_bias,
    cotangent,
):
    seq = lax.axis_index("seq")
    y = seq % 2
    tok, width = tokens.shape[1:]
    hidden = up_weight.shape[1]
    keys = 5 * tok
    bf, fl = jnp.bfloat16, jnp.float32
    dma = pltpu.SemaphoreType.DMA
    grad_y = cotangent[0]
    own_tokens, piece_q, piece_f, piece_u, piece_d = call(
        prep_kernel,
        [HB] * 10,
        [VM] * 5,
        [
            shape_of((tok + 8, width), bf),
            shape_of((48, 2 * width + 128), bf),
            shape_of((192, width), bf),
            shape_of((96, width), bf),
            shape_of((96, width), bf),
        ],
        [
            pltpu.VMEM((8, width), fl),
            pltpu.VMEM((96, hidden), bf),
            pltpu.VMEM((2, 96), bf),
            pltpu.VMEM((2, 96), bf),
            pltpu.VMEM((4, 96), bf),
            pltpu.VMEM((1, tok), jnp.int32),
            pltpu.VMEM((384,), bf),
            dma((11,)),
        ],
        vmem=60, moved=4 * 10**6,
    )(
        tokens, segment_ids, query_key_value_weight, output_weight, up_weight, down_weight,
        ln_gains, ln_biases, biases, up_projection_bias,
    )

    q1, q3, q_y0, dy_x = fence(to_z(piece_q, 1), to_z(piece_q, 3), to_y(piece_q), to_x(grad_y))
    own_tokens, piece_f, q1, q_y0 = fence(own_tokens, piece_f, q1, q_y0, q3, dy_x)[:4]
    q2, x2, q_xy0, f_y0 = fence(to_z(q1, 1), to_z(own_tokens, 1), to_x(q_y0), to_y(piece_f))
    q_z = join(q1, q2, q3)
    q_z, x2, piece_d = fence(q_z, x2, piece_d, q_xy0, f_y0)[:3]
    q_y, q_xz, x4, f3d = fence(to_y(q_z), to_x(q_z), to_z(x2, 1), to_z(piece_d, 3))
    near = jnp.where(y == 0, own_tokens, x2)
    far = jnp.where(y == 0, x2, x4)
    near_far, q_y, piece_f, piece_u = fence(
        jnp.stack([near, far]), q_y, piece_f, piece_u, q_xz, f3d
    )[:4]
    crossed, q_xy, f1, f3u = fence(to_y(near_far), to_x(q_y), to_z(piece_f, 1), to_z(piece_u, 3))
    x1, x3 = crossed[0], crossed[1]
    q_z, q_y0, q_y, q_xz, q_xy0, q_xy = fence(q_z, q_y0, q_y, q_xz, q_xy0, q_xy, f1, f3u, crossed)[:6]
    q_cz, q_cy0, q_cy, q_cxz, q_cxy0, q_cxy = fence(
        *(to_core(v) for v in (q_z, q_y0, q_y, q_xz, q_xy0, q_xy))
    )
    f_13, f_1, q_cz = fence(join(f1, f3u, f3d), f1, q_cz, q_cy0, q_cy, q_cxz, q_cxy0, q_cxy)[:3]
    f_y13, f2 = to_y(f_13), to_z(f_1, 1)
    dy_c, dy_xc = to_core(grad_y), to_core(dy_x)

    def pieces(value):
        return value.reshape(value.shape[0] // 48, 48, value.shape[1])

    got_q = [
        pieces(v)
        for v in (q_z, q_y0, q_y, q_xz, q_xy0, q_xy, q_cz, q_cy0, q_cy, q_cxz, q_cxy0, q_cxy)
    ]
    seg = jnp.concatenate([segment_ids, segment_ids], axis=1)
    front = call(
        front_kernel,
        [VM] * 6 + [AN] * 15,
        [VM] * 11,
        [
            shape_of((tok, width), bf),
            shape_of((keys, 2 * width), bf),
            shape_of((keys, width), bf),
            shape_of((tok, width), bf),
            shape_of((width // 128, 1, 2 * tok), fl),
            shape_of((1, 2 * tok), jnp.int32),
            shape_of((8, width), fl),
            shape_of((8, width), fl),
            shape_of((width, width), bf),
            shape_of((tok, width), fl),
            shape_of((tok, width), bf),
        ],
        [
            pltpu.VMEM((width, 3 * width), bf),
            pltpu.VMEM((8, 16, 128), bf),
            pltpu.VMEM((keys, 2 * tok), fl),
            dma((2 + 56,)),
            dma((8,)),
        ],
        flops=7 * 10**9,
        vmem=16, moved=12 * 10**6,
    )(
        seg, own_tokens, x1, x2, x3, x4, piece_q, query_key_value_weight, output_weight, *got_q,
    )
    *front, f_y13, f2, dy_c, dy_xc = fence(*front, f_y13, f2, dy_c, dy_xc)
    queries, kv, normed, attended, lse, start, vec, upb, w_out, residual, hidden_2 = front
    w_half = call(
        assemble_kernel,
        [AN] * 7,
        [VM] * 2,
        [shape_of((width, width), bf)] * 2,
        [dma((14,))],
        vmem=4,
        moved=5 * 10**6,
    )(piece_f, f1, f2, f3u, f3d, f_y0, f_y13)
    h_x, h_c, f_y2, *w_half = fence(to_x(hidden_2), to_core(hidden_2), to_y(f2), *w_half)
    act = shape_of((2 * tok, width), bf)
    acts = shape_of((4 * tok, width), bf)
    feed_shapes = [shape_of((tok, width), fl), shape_of((tok, width), bf)]
    *near_acts, keep_a, send_a, w_up, w_down = call(
        near_kernel,
        [VM] * 5 + [AN] + [VM] * 2,
        [VM] * 8,
        [act] * 4 + feed_shapes + [shape_of((width, width), bf)] * 2,
        [dma((2,))],
        flops=3 * 10**9,
        vmem=8,
        moved=6 * 10**6,
        aliases={6: 6, 7: 7},
    )(hidden_2, h_c, grad_y, dy_c, upb, f_y2, *w_half)
    h_xc = to_core(h_x)
    keep_a, send_a, h_xc, w_up = fence(keep_a, send_a, h_xc, w_up)
    came_a = to_core(send_a)
    *all_acts, send_b = call(
        far_c_kernel,
        [VM] * 5 + [AN] * 4,
        [VM] * 5,
        [acts] * 4 + feed_shapes[1:],
        [dma((4,))],
        flops=15 * 10**8,
        vmem=8,
        moved=6 * 10**6,
    )(h_xc, dy_xc, upb, w_up, w_down, *near_acts)
    send_b, came_a, h_x = fence(send_b, came_a, h_x)
    came_b = to_core(send_b)
    *all_acts, keep_b = call(
        far_x_kernel,
        [VM] * 9,
        [VM] * 5,
        [acts] * 4 + feed_shapes[:1],
        flops=3 * 10**9,
        vmem=8,
        moved=6 * 10**6,
        aliases={5: 0, 6: 1, 7: 2, 8: 3},
    )(h_x, dy_x, upb, w_up, w_down, *all_acts)
    keep_b, came_b, *all_acts = fence(keep_b, came_b, *all_acts)
    back_x = to_x(b16(keep_b + f32(came_b)))
    u_terms, d_terms, upb_g, y_keep, y_send = call(
        weights_kernel,
        [VM] * 5,
        [AN, AN] + [VM] * 3,
        [
            shape_of((2, 4, 96, width), bf),
            shape_of((2, 4, 96, width), bf),
            shape_of((1, width), fl),
            shape_of((2, tok, width), fl),
            shape_of((2, tok, width), bf),
        ],
        [pltpu.VMEM((2, width, width), bf), dma((16,))],
        flops=3 * 10**9,
        vmem=12,
        moved=6 * 10**6,
    )(*all_acts, w_down)
    back_x, u_terms, d_terms, y_send = fence(back_x, u_terms, d_terms, y_send)
    u_came = to_y(u_terms[1])
    came_y = to_core(y_send)
    grad_first, grad_attended, dw_out, vec_g = call(
        post_kernel,
        [VM] * 8,
        [VM] * 4,
        [
            shape_of((tok, width), fl),
            shape_of((tok, width), bf),
            shape_of((width, width), fl),
            shape_of((8, width), fl),
        ],
        vmem=12,
        flops=10**9,
        moved=4 * 10**6,
    )(residual, keep_a, came_a, back_x, grad_y, vec, w_out, attended)
    back_scratch = [
        pltpu.VMEM((keys, 2 * tok), fl),
    ]
    qa_other, qa_mine, dq_a, dkv_a = call(
        back_a_kernel,
        [VM] * 7,
        [AN] * 2 + [VM] * 2,
        [
            shape_of((2, 2, 4, 120, width // 2), bf),
            shape_of((2, 2, 4, 120, width // 2), bf),
            shape_of((tok, width // 2), bf),
            shape_of((keys, width), bf),
        ],
        back_scratch + [pltpu.VMEM((2, 2, 8, 120, width // 2), bf), dma((32,))],
        flops=5 * 10**9,
        vmem=16, moved=10 * 10**6,
    )(start, queries, kv, normed, lse, grad_attended, dw_out)

    def both(mine, came):
        return lambda *index: f32(mine[index]) + f32(came[index])

    def z_sum(part, *came):
        return b16(part(0) + sum(f32(v) for v in came))

    dq_a, qa_other, u_came, came_y, d_send = fence(
        dq_a, qa_other, u_came, came_y, d_terms[1]
    )
    d_came, qa_came = to_y(d_send), to_core(qa_other)
    u_part = both(u_terms[0], u_came)
    u_z = [to_z(b16(u_part(step)), step) for step in (1, 2, 3)]
    dq_b, dkv_b, p_own, p_y, p_z, sums = call(
        back_b_kernel,
        [VM] * 14 + [AN] * 13,
        [VM] * 6,
        [
            shape_of((tok, width // 2), bf),
            shape_of((keys, width), bf),
            shape_of((tok, width), fl),
            shape_of((2, tok, width), bf),
            shape_of((2, tok, width), bf),
            shape_of((8, 8, 256), fl),
        ],
        [pltpu.VMEM((width, 3 * width), bf)] + back_scratch + [dma((1 + 28,))],
        flops=6 * 10**9,
        vmem=20, moved=10 * 10**6,
    )(
        start, queries, kv, lse, grad_attended, vec_g, upb_g, dq_a, dkv_a,
        own_tokens, x1, x2, x3, x4, query_key_value_weight, *got_q,
    )
    dq_b, qa_came, d_came, p_y, *u_z = fence(dq_b, qa_came, d_came, p_y, *u_z)
    p_came = to_y(p_y)
    qa_1 = both(qa_mine, qa_came)
    qa_x = to_x(b16(qa_1(1)))
    d_part = both(d_terms[0], d_came)
    d_z2 = to_z(b16(d_part(2)), 1)
    qb_other, qb_mine = call(
        back_c_kernel,
        [VM] * 4,
        [AN] * 2,
        [
            shape_of((2, 2, 4, 80, width // 2), bf),
            shape_of((2, 2, 4, 80, width // 2), bf),
        ],
        [pltpu.VMEM((2, 2, 8, 80, width // 2), bf), dma((32,))],
        flops=3 * 10**9,
        vmem=12, moved=6 * 10**6,
    )(normed, dq_b, dkv_b, sums)
    qb_came = [to_core(qb_other[k]) for k in range(2)]
    *qb_came, qa_x, p_came, d_z2 = fence(*qb_came, qa_x, p_came, d_z2)
    even = y == 0
    sum_own = p_own + jnp.where(even, f32(p_came[0]), 0.0)
    sum_4 = b16(f32(p_z[1]) + jnp.where(even, 0.0, f32(p_came[1])))
    sum_2 = f32(p_z[0]) + jnp.where(even, f32(p_came[1]), f32(p_came[0]))
    def qa_2(*index):
        return qa_1(0, *index) + f32(qa_x[index])

    def qb_1(side, *index):
        return f32(qb_mine[(side,) + index]) + f32(qb_came[side][index])

    qb_x, qa_y, hop, d_z1, d_z3 = fence(
        to_x(b16(qb_1(1))),
        to_y(b16(qa_2(1))),
        to_z(sum_4, 3),
        to_z(b16(d_part(1) + f32(d_z2)), 1),
        to_z(b16(d_part(3)), 3),
    )

    def qb_2(*index):
        return qb_1(0, *index) + f32(qb_x[index])

    f_tot = join(z_sum(u_part, *u_z), z_sum(d_part, d_z1, d_z3))
    fy_tot = join(f_tot, b16(y_keep[1] + f32(came_y[1])))
    qb_y, back_2, f_tot, fy_tot = fence(
        to_y(b16(qb_2(1))), to_z(b16(sum_2 + f32(hop)), 3), f_tot, fy_tot
    )

    def q_3(*index):
        first = qa_2(0, *index) + f32(qa_y[index])
        return jnp.concatenate([first, qb_2(0, *index) + f32(qb_y[index])], axis=-2)

    grad_tokens = call(
        tokens_kernel, [VM] * 5, VM, shape_of((tok, width), fl), vmem=4, moved=3 * 10**6
    )(sum_own, back_2, grad_first, own_tokens, vec)
    *q_z, over_x, f_tot = fence(*(to_z(b16(q_3(step)), step) for step in (1, 2, 3)), to_x(fy_tot), f_tot)
    f_x, back_y = over_x[:tok], over_x[tok:]
    q_sum = z_sum(q_3, *q_z)
    q_fx, q_fc, q_fxc = to_x(q_sum), to_core(q_sum), swap_rep(q_sum, 3)
    grad_up, grad_down = call(
        finish_f_kernel,
        [VM] * 4,
        [VM] * 2,
        [shape_of(up_weight.shape, fl), shape_of(down_weight.shape, fl)],
        [pltpu.VMEM((4, 96, width), bf)],
        vmem=8,
        moved=4 * 10**6,
    )(f_tot, f_x, to_core(f_tot), to_core(f_x))
    q_fx, q_fc, q_fxc, grad_up, grad_down = fence(q_fx, q_fc, q_fxc, grad_up, grad_down)
    result = b16(residual + vec[7:8] + y_keep[0] + f32(came_y[0]) + f32(back_y))
    grad_qkv, grad_out = call(
        finish_q_kernel,
        [VM] * 4,
        [VM] * 2,
        [shape_of(query_key_value_weight.shape, fl), shape_of(output_weight.shape, fl)],
        vmem=8, moved=3 * 10**6,
    )(q_sum, q_fx, q_fc, q_fxc)
    sums = f32(q_sum[192:200, :256])
    part = ln_gains.shape[1]
    return (
        result[None],
        grad_tokens[None],
        grad_qkv,
        grad_out,
        grad_up,
        grad_down,
        sums[0:2, :part],
        sums[2:4, :part],
        sums[4:8, :part],
        sums[0:4, 128 : 128 + part].reshape(4 * part),
    )


def solution(mesh):
    placed = (
        P("rep", "seq", None),
        P("rep", "seq"),
        P("seq", None),
        P("seq", None),
        P("seq", None),
        P("seq", None),
        P(None, "seq"),
        P(None, "seq"),
        P(None, "seq"),
        P("seq"),
        P("rep", "seq", None),
    )
    shape = dict(mesh.shape)
    small_slice = shape["rep"] == 4 and shape["seq"] == 8
    return jax.shard_map(
        on_device_fast if small_slice else on_device,
        mesh=mesh,
        in_specs=placed,
        out_specs=(
            P("rep", "seq", None),
            P("rep", "seq", None),
            P("seq", None),
            P("seq", None),
            P("seq", None),
            P("seq", None),
            P(None, "seq"),
            P(None, "seq"),
            P(None, "seq"),
            P("seq"),
        ),
        check_vma=False,
    )
```

```python
import math

import jax
import jax.numpy as jnp
from jax import lax
from jax.experimental import pallas as pl
from jax.experimental.pallas import tpu as pltpu
from jax.sharding import PartitionSpec as P

HEADS = 12
HD = 64


norm_eps = 1e-05
floor_score = -1e30


def layer_norm(values, gain, shift):
    center = values - jnp.mean(values, axis=-1, keepdims=True)
    spread = jnp.mean(center * center, axis=-1, keepdims=True)
    return center * lax.rsqrt(spread + norm_eps) * gain + shift


def head_split(matrix):
    return matrix.reshape(matrix.shape[0], HEADS, HD)


def masked_scores(queries, query_seg, query_pos, key_piece, seg_piece, offset):
    rows = key_piece.shape[0]
    scores = jnp.einsum(
        "qhd,khd->hqk", queries, head_split(key_piece), preferred_element_type=jnp.float32
    ) * HD ** (-0.5)
    key_pos = offset + jnp.arange(rows, dtype=jnp.int32)
    allowed = (query_seg[:, None] == seg_piece[None, :]) & (key_pos[None, :] <= query_pos[:, None])
    return (jnp.where(allowed[None], scores, floor_score), allowed)


def forward_block(running, pieces, offset, queries, query_seg, query_pos):
    top_run, total_run, accum = running
    key_piece, value_piece, seg_piece = pieces
    scores, allowed = masked_scores(queries, query_seg, query_pos, key_piece, seg_piece, offset)
    top_new = jnp.maximum(top_run, jnp.max(scores, axis=-1))
    probs = jnp.where(allowed[None], jnp.exp(scores - top_new[:, :, None]), 0.0)
    factor = jnp.exp(top_run - top_new)
    total_new = total_run * factor + jnp.sum(probs, axis=-1)
    update = jnp.einsum(
        "hqk,khd->qhd",
        probs.astype(jnp.bfloat16),
        head_split(value_piece),
        preferred_element_type=jnp.float32,
    )
    return (top_new, total_new, accum * factor.T[:, :, None] + update)


def in_blocks(block_fn, running, pieces):
    rows = pieces[0].shape[0]
    size = math.gcd(rows, 1024)
    stacked = tuple((member.reshape((rows // size, size) + member.shape[1:]) for member in pieces))
    offsets = jnp.arange(rows // size, dtype=jnp.int32) * size

    def scan_step(state_now, element):
        return (block_fn(state_now, element[0], element[1]), None)

    running, _unused = lax.scan(scan_step, running, (stacked, offsets))
    return running


def backward_block(
    number,
    state_now,
    whole,
    queries,
    query_seg,
    query_pos,
    grad_heads,
    log_total,
    delta,
    block_rows,
):
    grad_query, term = state_now
    offset = number * block_rows
    key_piece = lax.dynamic_slice_in_dim(whole[0], offset, block_rows, 0)
    value_piece = lax.dynamic_slice_in_dim(whole[1], offset, block_rows, 0)
    seg_piece = lax.dynamic_slice_in_dim(whole[2], offset, block_rows, 0)
    scores, allowed = masked_scores(queries, query_seg, query_pos, key_piece, seg_piece, offset)
    probs = jnp.where(allowed[None], jnp.exp(scores - log_total[:, :, None]), 0.0)
    grad_probs = jnp.einsum(
        "qhd,khd->hqk", grad_heads, head_split(value_piece), preferred_element_type=jnp.float32
    )
    grad_scores = (probs * (grad_probs - delta[:, :, None])).astype(jnp.bfloat16)
    grad_query = grad_query + jnp.einsum(
        "hqk,khd->qhd", grad_scores, head_split(key_piece), preferred_element_type=jnp.float32
    )
    grad_key = jnp.einsum(
        "hqk,qhd->khd", grad_scores, queries, preferred_element_type=jnp.float32
    ) * HD ** (-0.5)
    grad_value = jnp.einsum(
        "hqk,qhd->khd", probs.astype(jnp.bfloat16), grad_heads, preferred_element_type=jnp.float32
    )
    joined = jnp.concatenate(
        [grad_key.reshape(block_rows, -1), grad_value.reshape(block_rows, -1)], axis=1
    )
    term = lax.dynamic_update_slice_in_dim(term, joined, offset, 0)
    return (grad_query, term)


def on_device(
    tokens,
    segment_ids,
    query_key_value_weight,
    output_weight,
    up_weight,
    down_weight,
    ln_gains,
    ln_biases,
    biases,
    up_projection_bias,
    cotangent,
):
    gathered = (
        lax.all_gather(query_key_value_weight, "seq", axis=0, tiled=True),
        lax.all_gather(output_weight, "seq", axis=0, tiled=True),
        lax.all_gather(up_weight, "seq", axis=0, tiled=True),
        lax.all_gather(down_weight, "seq", axis=0, tiled=True),
        lax.all_gather(ln_gains, "seq", axis=1, tiled=True),
        lax.all_gather(ln_biases, "seq", axis=1, tiled=True),
        lax.all_gather(biases, "seq", axis=1, tiled=True),
        lax.all_gather(up_projection_bias, "seq", axis=0, tiled=True),
    )
    full_qkv, full_out, full_up, full_down, gains_all, shifts_all, biases_all, up_shift = gathered
    gains_f = gains_all.astype(jnp.float32)
    shifts_f = shifts_all.astype(jnp.float32)
    biases_f = biases_all.astype(jnp.float32)
    up_shift_f = up_shift.astype(jnp.float32)
    tokens_f = tokens[0].astype(jnp.float32)
    seg_local = segment_ids[0]
    tok_rows = tokens_f.shape[0]
    width = tokens_f.shape[1]
    seqlen = tok_rows * lax.axis_size("seq")
    query_pos = lax.axis_index("seq") * tok_rows + jnp.arange(tok_rows, dtype=jnp.int32)
    hidden_first = layer_norm(tokens_f, gains_f[0], shifts_f[0]).astype(jnp.bfloat16)
    query_key_value_bias = jnp.concatenate(
        [biases_f[0], jnp.zeros((width,), jnp.float32), biases_f[1]]
    )
    projected_rows = (
        jnp.dot(hidden_first, full_qkv, preferred_element_type=jnp.float32) + query_key_value_bias
    ).astype(jnp.bfloat16)
    queries = head_split(projected_rows[:, :width])
    key_rows = projected_rows[:, width : 2 * width]
    value_rows = projected_rows[:, 2 * width :]
    initial = (
        jnp.full((HEADS, tok_rows), floor_score, jnp.float32),
        jnp.zeros((HEADS, tok_rows), jnp.float32),
        jnp.zeros((tok_rows, HEADS, HD), jnp.float32),
    )

    def block_fn(running, pieces, offset):
        return forward_block(running, pieces, offset, queries, seg_local, query_pos)

    block_rows = math.gcd(seqlen, 1024)
    key_end = (lax.axis_index("seq") + 1) * tok_rows
    block_count = (key_end + block_rows - 1) // block_rows
    top_run, total_run, accum = in_blocks(
        block_fn,
        initial,
        (
            lax.all_gather(key_rows, "seq", axis=0, tiled=True),
            lax.all_gather(value_rows, "seq", axis=0, tiled=True),
            lax.all_gather(seg_local, "seq", axis=0, tiled=True),
        ),
    )
    log_total = top_run + jnp.log(total_run)
    attended_f = accum / total_run.T[:, :, None]
    attention_result = attended_f.reshape(tok_rows, width).astype(jnp.bfloat16)
    residual_first = (
        tokens_f
        + jnp.dot(attention_result, full_out, preferred_element_type=jnp.float32)
        + biases_f[2]
    )
    hidden_second = layer_norm(residual_first, gains_f[1], shifts_f[1]).astype(jnp.bfloat16)
    upward_rows = jnp.dot(hidden_second, full_up, preferred_element_type=jnp.float32) + up_shift_f
    activated_f, gelu_back = jax.vjp(jax.nn.gelu, upward_rows)
    activation_values = activated_f.astype(jnp.bfloat16)
    result = (
        residual_first
        + jnp.dot(activation_values, full_down, preferred_element_type=jnp.float32)
        + biases_f[3]
    )
    grad_y = cotangent[0]
    grad_y_f = grad_y.astype(jnp.float32)
    grad_down = jnp.einsum(
        "tf,td->fd", activation_values, grad_y, preferred_element_type=jnp.float32
    )
    grad_act = jnp.einsum("td,fd->tf", grad_y, full_down, preferred_element_type=jnp.float32)
    grad_up_pre = gelu_back(grad_act)[0].astype(jnp.bfloat16)
    grad_up = jnp.einsum(
        "td,tf->df", hidden_second, grad_up_pre, preferred_element_type=jnp.float32
    )
    grad_hidden_two = jnp.einsum(
        "tf,df->td", grad_up_pre, full_up, preferred_element_type=jnp.float32
    )
    _unused, norm_two_back = jax.vjp(layer_norm, residual_first, gains_f[1], shifts_f[1])
    grad_sum_part, grad_gain_two, grad_shift_two = norm_two_back(grad_hidden_two)
    grad_first = grad_y_f + grad_sum_part
    grad_first_bf = grad_first.astype(jnp.bfloat16)
    grad_out_w = jnp.einsum(
        "td,te->de", attention_result, grad_first_bf, preferred_element_type=jnp.float32
    )
    grad_attended = jnp.einsum(
        "te,de->td", grad_first_bf, full_out, preferred_element_type=jnp.float32
    ).astype(jnp.bfloat16)
    grad_heads = head_split(grad_attended)
    delta = jnp.einsum("qhd,qhd->hq", grad_heads.astype(jnp.float32), attended_f)
    whole = (
        lax.all_gather(key_rows, "seq", axis=0, tiled=True),
        lax.all_gather(value_rows, "seq", axis=0, tiled=True),
        lax.all_gather(seg_local, "seq", axis=0, tiled=True),
    )

    def backward_step(number, state_now):
        return backward_block(
            number,
            state_now,
            whole,
            queries,
            seg_local,
            query_pos,
            grad_heads,
            log_total,
            delta,
            block_rows,
        )

    start_state = (
        jnp.zeros((tok_rows, HEADS, HD), jnp.float32),
        jnp.zeros((seqlen, 2 * width), jnp.float32),
    )
    grad_query, term = lax.fori_loop(0, block_count, backward_step, start_state)
    grad_kv = lax.psum_scatter(term, "seq", scatter_dimension=0, tiled=True).astype(jnp.bfloat16)
    grad_q = (grad_query * HD ** (-0.5)).reshape(tok_rows, width).astype(jnp.bfloat16)
    grad_proj = jnp.concatenate([grad_q, grad_kv], axis=1)
    grad_qkv_w = jnp.einsum(
        "td,te->de", hidden_first, grad_proj, preferred_element_type=jnp.float32
    )
    grad_hidden_one = jnp.einsum(
        "te,de->td", grad_proj, full_qkv, preferred_element_type=jnp.float32
    )
    _unused_two, norm_one_back = jax.vjp(layer_norm, tokens_f, gains_f[0], shifts_f[0])
    grad_in_part, grad_gain_one, grad_shift_one = norm_one_back(grad_hidden_one)
    grad_tokens = grad_first + grad_in_part
    grad_proj_f = grad_proj.astype(jnp.float32)
    grad_bias_rows = jnp.stack(
        [
            jnp.sum(grad_proj_f[:, :width], axis=0),
            jnp.sum(grad_proj_f[:, 2 * width :], axis=0),
            jnp.sum(grad_first, axis=0),
            jnp.sum(grad_y_f, axis=0),
        ]
    )
    grad_up_shift = jnp.sum(grad_up_pre.astype(jnp.float32), axis=0)
    grad_gains = jnp.stack([grad_gain_one, grad_gain_two])
    grad_shifts = jnp.stack([grad_shift_one, grad_shift_two])
    shares = (
        lax.psum_scatter(grad_qkv_w, "seq", scatter_dimension=0, tiled=True),
        lax.psum_scatter(grad_out_w, "seq", scatter_dimension=0, tiled=True),
        lax.psum_scatter(grad_up, "seq", scatter_dimension=0, tiled=True),
        lax.psum_scatter(grad_down, "seq", scatter_dimension=0, tiled=True),
        lax.psum_scatter(grad_gains, "seq", scatter_dimension=1, tiled=True),
        lax.psum_scatter(grad_shifts, "seq", scatter_dimension=1, tiled=True),
        lax.psum_scatter(grad_bias_rows, "seq", scatter_dimension=1, tiled=True),
        lax.psum_scatter(grad_up_shift, "seq", scatter_dimension=0, tiled=True),
    )
    totals = (
        lax.psum(shares[0].astype(jnp.bfloat16), "rep").astype(jnp.float32),
        lax.psum(shares[1].astype(jnp.bfloat16), "rep").astype(jnp.float32),
        lax.psum(shares[2].astype(jnp.bfloat16), "rep").astype(jnp.float32),
        lax.psum(shares[3].astype(jnp.bfloat16), "rep").astype(jnp.float32),
        lax.psum(shares[4].astype(jnp.bfloat16), "rep").astype(jnp.float32),
        lax.psum(shares[5].astype(jnp.bfloat16), "rep").astype(jnp.float32),
        lax.psum(shares[6].astype(jnp.bfloat16), "rep").astype(jnp.float32),
        lax.psum(shares[7].astype(jnp.bfloat16), "rep").astype(jnp.float32),
    )
    return (
        result.astype(jnp.bfloat16)[None],
        grad_tokens[None],
        totals[0],
        totals[1],
        totals[2],
        totals[3],
        totals[4],
        totals[5],
        totals[6],
        totals[7],
    )


def f32(value):
    return value.astype(jnp.float32)


def b16(value):
    return value.astype(jnp.bfloat16)


def dot_nn(left, right):
    return jnp.dot(left, right, preferred_element_type=jnp.float32)


def dot_nt(left, right):
    return lax.dot_general(
        left, right, (((1,), (1,)), ((), ())), preferred_element_type=jnp.float32
    )


def dot_tn(left, right):
    return lax.dot_general(
        left, right, (((0,), (0,)), ((), ())), preferred_element_type=jnp.float32
    )


def norm_parts(values):
    center = values - jnp.mean(values, axis=-1, keepdims=True)
    rate = lax.rsqrt(jnp.mean(center * center, axis=-1, keepdims=True) + norm_eps)
    return center * rate, rate


def norm_back(grad, hat, rate, gain):
    scaled = grad * gain
    return rate * (
        scaled
        - jnp.mean(scaled, axis=-1, keepdims=True)
        - hat * jnp.mean(scaled * hat, axis=-1, keepdims=True)
    )


def place():
    rep, seq = lax.axis_index("rep"), lax.axis_index("seq")
    return lax.div(rep, 2), lax.rem(rep, 2), lax.rem(seq, 2), lax.div(seq, 2)


def piece_shard(number, y, z):
    if number < 3:
        return 2 * lax.rem(z + 3 - number, 4) + y
    return 2 * lax.rem(z + 7 - number, 4) + 1 - y


def pack96(parts):
    lane = lax.broadcasted_iota(jnp.int32, parts[0].shape, 1)
    one, two, three = (pltpu.roll(parts[k], 128 - 32 * k, 1) for k in (1, 2, 3))
    return jnp.concatenate(
        [
            jnp.where(lane < 96, parts[0], one),
            jnp.where(lane < 64, one, two),
            jnp.where(lane < 32, two, three),
        ],
        axis=1,
    )


def unpack96(block):
    tiles = [block[:, 128 * k : 128 * k + 128] for k in range(3)]
    lane = lax.broadcasted_iota(jnp.int32, tiles[0].shape, 1)
    return [
        tiles[0],
        jnp.where(lane < 32, pltpu.roll(tiles[0], 32, 1), pltpu.roll(tiles[1], 32, 1)),
        jnp.where(lane < 64, pltpu.roll(tiles[1], 64, 1), pltpu.roll(tiles[2], 64, 1)),
        pltpu.roll(tiles[2], 96, 1),
    ]


def choose(parts, index):
    out = parts[0]
    for number in range(1, len(parts)):
        out = jnp.where(index == number, parts[number], out)
    return out


class Copies:
    def __init__(self, sems, first=0):
        self.sems = sems
        self.first = first
        self.held = []

    def add(self, source, target):
        copy = pltpu.make_async_copy(source, target, self.sems.at[self.first + len(self.held)])
        copy.start()
        self.held.append(copy)

    def wait(self):
        for copy in self.held:
            copy.wait()
        self.held = []


def corners(x, c):
    return ((x, c), (1 - x, c), (x, 1 - c), (1 - x, 1 - c))


def fetch_qkv(copies, own, groups, full, full_out=None, own_out=None):
    x, c, y, z = place()
    rows = own.shape[0]
    half, width = rows // 2, own.shape[1] // 3
    row = pl.multiple_of((2 * z + y) * rows, 16)
    copies.add(own, full.at[pl.ds(row, rows), :])
    if full_out is not None:
        copies.add(own_out, full_out.at[pl.ds(row, rows), :])
    wide, side = 3 * width // 2, width // 2
    for number in range(7):
        for (xx, cc), group in zip(corners(x, c), groups, strict=True):
            piece = piece_of(group, number)
            at = pl.ds(pl.multiple_of(piece_shard(number, y, z) * rows + half * cc, 16), half)
            copies.add(
                piece.at[pl.ds(0, half), pl.ds(0, wide)],
                full.at[at, pl.ds(pl.multiple_of(wide * xx, 128), wide)],
            )
            if full_out is not None:
                copies.add(
                    piece.at[pl.ds(0, half), pl.ds(wide, side)],
                    full_out.at[at, pl.ds(pl.multiple_of(side * xx, 128), side)],
                )


def piece_of(group, number):
    behind, across, behind_across = group
    if number < 3:
        return behind.at[number]
    return across.at[0] if number == 3 else behind_across.at[number - 4]


def mask_bias(start, me, tok, target):
    keys, lanes = target.shape
    key_pos = (me - 4) * tok + lax.broadcasted_iota(jnp.int32, (keys, lanes), 0)
    lane = lax.broadcasted_iota(jnp.int32, (keys, lanes), 1)
    query_pos = me * tok + jnp.where(lane >= tok, lane - tok, lane)
    target[...] = jnp.where((key_pos >= start) & (key_pos <= query_pos), 0.0, floor_score)


def pair_stack(rows):
    lane = lax.broadcasted_iota(jnp.int32, rows.shape, 1)
    zero = jnp.zeros_like(rows)
    return jnp.concatenate([jnp.where(lane < HD, rows, zero), jnp.where(lane < HD, zero, rows)], axis=0)


def pair_join(transposed):
    both = transposed.T
    tok = both.shape[0] // 2
    lane = lax.broadcasted_iota(jnp.int32, (tok, 2 * HD), 1)
    return jnp.where(lane < HD, both[:tok], both[tok:])


def prep_kernel(
    tokens, segs, qkv, out, up, down, gains, shifts, biases, up_bias,
    t_out, q_out, f_out, fu_out, fd_out,
    scratch, wide, held_g, held_s, held_b, ids, line, sems,
):
    x, c, _y, _z = place()
    tok, width = tokens.shape[1:]
    rows = qkv.shape[0]
    half, side = rows // 2, width // 2
    p = 2 * x + c
    at = pl.ds(pl.multiple_of(half * c, 16), half)
    copies, others = Copies(sems), Copies(sems, 5)
    for source, target in ((gains, held_g), (shifts, held_s), (biases, held_b)):
        copies.add(source, target)
    copies.add(segs, ids)
    copies.add(up_bias, line)
    others.add(up, wide)
    wide_cols = 3 * side
    others.add(
        qkv.at[at, pl.ds(pl.multiple_of(wide_cols * x, 128), wide_cols)],
        q_out.at[pl.ds(0, half), pl.ds(0, wide_cols)],
    )
    others.add(
        out.at[at, pl.ds(pl.multiple_of(side * x, 128), side)],
        q_out.at[pl.ds(0, half), pl.ds(wide_cols, side)],
    )
    others.add(tokens.at[0], t_out.at[pl.ds(0, tok), :])
    own_rows = down.at[pl.ds(pl.multiple_of(rows * p, 16), rows), :]
    others.add(own_rows, f_out.at[pl.ds(rows, rows), :])
    others.add(own_rows, fd_out)
    copies.wait()
    scratch[...] = jnp.zeros_like(scratch)
    for first, held in ((0, held_g), (2, held_s), (4, held_b)):
        scratch[pl.ds(first, held.shape[0]), pl.ds(0, rows)] = f32(held[...])
    parts = unpack96(jnp.broadcast_to(f32(line[...]).reshape(1, line.shape[0]), (8, line.shape[0])))
    lane = lax.broadcasted_iota(jnp.int32, (8, 128), 1)
    row = lax.broadcasted_iota(jnp.int32, (8, 128), 0)
    ups = jnp.zeros((8, 128), jnp.float32)
    for number in range(4):
        ups = jnp.where((row == number) & (lane < rows), parts[number], ups)
    smalls = b16(jnp.concatenate([scratch[:, pl.ds(0, 128)], ups], axis=0))
    q_out[pl.ds(0, 16), pl.ds(2 * width, 128)] = smalls
    q_out[pl.ds(16, half - 16), pl.ds(2 * width, 128)] = jnp.zeros((half - 16, 128), jnp.bfloat16)
    scratch[...] = jnp.zeros_like(scratch)
    scratch[pl.ds(0, 1), pl.ds(0, tok)] = f32(ids[...])
    t_out[pl.ds(tok, 8), :] = b16(scratch[...])
    others.wait()
    for group in range(2):
        parts = []
        for shard in range(4 * group, 4 * group + 4):
            parts.append(choose(unpack96(f32(wide[:, pl.ds(384 * shard, 384)])), p))
        packed = b16(pack96(parts))
        f_out[pl.ds(0, rows), pl.ds(384 * group, 384)] = packed
        fu_out[:, pl.ds(384 * group, 384)] = packed


def front_kernel(
    seg, xo, x1, x2, x3, x4, first, own, own_o,
    g0, g1, g2, g3, g4, g5, g6, g7, g8, g9, g10, g11,
    q_out, kv_out, h_out, a_out, lse_out, start_out, vec_out, upb_out, wo_out, r_out, h2_out,
    full, small, bias, sems, vsems,
):
    x, c, y, z = place()
    me = 2 * z + y
    p = 2 * x + c
    tok, width = q_out.shape
    copies, vcopies = Copies(sems), Copies(vsems)
    vcopies.add(first.at[pl.ds(0, 16), pl.ds(2 * width, 128)], small.at[me])
    for number in range(7):
        source = piece_of((g0, g1, g2), number)
        vcopies.add(source.at[pl.ds(0, 16), pl.ds(2 * width, 128)], small.at[piece_shard(number, y, z)])
    groups = ((g0, g1, g2), (g3, g4, g5), (g6, g7, g8), (g9, g10, g11))
    fetch_qkv(copies, own, groups, full, wo_out, own_o)
    blocks = (xo, x1, x2, x3, x4)
    lane1 = lax.broadcasted_iota(jnp.int32, (1, tok), 1)
    start = jnp.full(seg.shape, 1 << 30, jnp.int32)
    for number in range(4):
        first_pos = jnp.full((1, 1), 1 << 30, jnp.int32)
        for back in range(5):
            ids = f32(blocks[back][pl.ds(tok, 8), pl.ds(0, tok)])[:1]
            pos = (me - back) * tok + lane1
            hit = (ids == float(number)) & (pos >= 0)
            first_pos = jnp.minimum(
                first_pos, jnp.min(jnp.where(hit, pos, 1 << 30), axis=1, keepdims=True)
            )
        start = jnp.where(seg[...] == number, first_pos, start)
    start_out[...] = start
    mask_bias(start, me, tok, bias)
    vcopies.wait()
    for group in range(2):
        held = [f32(small[4 * group + k]) for k in range(4)]
        vec_out[:, pl.ds(384 * group, 384)] = pack96([block[:8] for block in held])
        upb_out[:, pl.ds(384 * group, 384)] = pack96(
            [choose([jnp.broadcast_to(block[k : k + 1], (8, 128)) for k in range(8, 12)], p) for block in held]
        )
    vec = vec_out[...]
    for back in range(5):
        hat, _rate = norm_parts(f32(blocks[back][pl.ds(0, tok), :]))
        h_out[pl.ds((4 - back) * tok, tok), :] = b16(hat * vec[0:1] + vec[2:3])
    copies.wait()
    q_out[...] = b16(dot_nn(h_out[pl.ds(4 * tok, tok), :], full[:, pl.ds(0, width)]) + vec[4:5])

    def project(number, carry):
        col = pl.multiple_of(number * 256, 256)
        shift = jnp.where(number >= width // 256, 1.0, 0.0)
        bias_at = lax.rem(number, width // 256)
        piece = vec_out[pl.ds(5, 1), pl.ds(pl.multiple_of(bias_at * 256, 256), 256)]
        kv_out[:, pl.ds(col, 256)] = b16(
            dot_nn(h_out[...], full[:, pl.ds(pl.multiple_of(width + col, 256), 256)]) + piece * shift
        )
        return carry

    lax.fori_loop(0, 2 * width // 256, project, 0)

    def pair(number, carry):
        col = pl.multiple_of(number * 128, 128)
        queries = pair_stack(q_out[:, pl.ds(col, 128)] * jnp.bfloat16(0.125))
        scores = dot_nt(kv_out[:, pl.ds(col, 128)], queries) + bias[...]
        top = jnp.max(scores, axis=0, keepdims=True)
        probs = jnp.exp(scores - top)
        total = jnp.sum(probs, axis=0, keepdims=True)
        mixed = dot_tn(kv_out[:, pl.ds(pl.multiple_of(width + col, 128), 128)], b16(probs))
        a_out[:, pl.ds(col, 128)] = b16(pair_join(mixed / total))
        lse_out[number] = top + jnp.log(total)
        return carry

    lax.fori_loop(0, width // 128, pair, 0)
    residual = f32(xo[pl.ds(0, tok), :]) + dot_nn(a_out[...], wo_out[...]) + vec[6:7]
    r_out[...] = residual
    hat, _rate = norm_parts(residual)
    h2_out[...] = b16(hat * vec[1:2] + vec[3:4])


def feed_tokens(h2, dy, w_up, w_down, upb, act_out, du_out):
    root = math.sqrt(2.0 / math.pi)
    chunk = 256

    def feed(number, carry):
        col = pl.multiple_of(number * chunk, chunk)
        pre = dot_nn(h2[...], w_up[:, pl.ds(col, chunk)]) + upb[pl.ds(0, 1), pl.ds(col, chunk)]
        square = pre * pre
        bend = jnp.tanh(root * pre * (1.0 + 0.044715 * square))
        act = b16(0.5 * pre * (1.0 + bend))
        slope = 0.5 * (1.0 + bend) + 0.5 * pre * (1.0 - bend * bend) * (
            root * (1.0 + 3.0 * 0.044715 * square)
        )
        low = b16(dot_nt(dy[...], w_down[pl.ds(col, chunk), :]) * slope)
        act_out[:, pl.ds(col, chunk)] = act
        du_out[:, pl.ds(col, chunk)] = low
        return carry

    lax.fori_loop(0, w_up.shape[1] // chunk, feed, 0, unroll=True)
    return dot_nt(du_out[...], w_up[...])


def assemble_kernel(own, z1, z2, z3u, z3d, y0, y13, wu_out, wd_out, sems):
    _x, _c, y, z = place()
    rows = own.shape[0] // 2
    copies = Copies(sems)
    pieces = [(own, 2 * z + y)]
    for number, ref in ((0, z1), (1, z2), (3, y0)):
        pieces.append((ref, piece_shard(number, y, z)))
    for number, first in ((4, 0), (6, 2 * rows)):
        pieces.append((y13.at[pl.ds(first, 2 * rows), :], piece_shard(number, y, z)))
    for ref, shard in pieces:
        at = pl.ds(pl.multiple_of(shard * rows, 16), rows)
        copies.add(ref.at[pl.ds(0, rows), :], wu_out.at[at, :])
        copies.add(ref.at[pl.ds(rows, rows), :], wd_out.at[at, :])
    at = pl.ds(pl.multiple_of(piece_shard(2, y, z) * rows, 16), rows)
    copies.add(z3u, wu_out.at[at, :])
    copies.add(z3d, wd_out.at[at, :])
    copies.wait()


def near_kernel(
    h_own, h_c, dy_own, dy_c, upb, y2, _wu, _wd,
    h2, dy, act_out, du_out, keep_out, send_out, wu_out, wd_out,
    sems,
):
    _x, _c, y, z = place()
    tok, width = h_own.shape
    rows = width // 8
    copies = Copies(sems)
    at = pl.ds(pl.multiple_of(piece_shard(5, y, z) * rows, 16), rows)
    copies.add(y2.at[pl.ds(0, rows), :], wu_out.at[at, :])
    copies.add(y2.at[pl.ds(rows, rows), :], wd_out.at[at, :])
    h2[pl.ds(0, tok), :] = h_own[...]
    h2[pl.ds(tok, tok), :] = h_c[...]
    dy[pl.ds(0, tok), :] = dy_own[...]
    dy[pl.ds(tok, tok), :] = dy_c[...]
    copies.wait()
    grad = feed_tokens(h2, dy, wu_out, wd_out, upb, act_out, du_out)
    keep_out[...] = grad[:tok]
    send_out[...] = b16(grad[tok:])


def far_c_kernel(
    h_xc, dy_xc, upb, w_up, w_down, h_near, dy_near, act_near, du_near,
    hs, dys, acts, dus, send_out,
    sems,
):
    tok = dy_xc.shape[0]
    copies = Copies(sems)
    for source, target in ((h_near, hs), (dy_near, dys), (act_near, acts), (du_near, dus)):
        copies.add(source, target.at[pl.ds(0, 2 * tok), :])
    last = pl.ds(3 * tok, tok)
    hs[last, :] = h_xc[...]
    dys[last, :] = dy_xc[...]
    send_out[...] = b16(
        feed_tokens(h_xc, dy_xc, w_up, w_down, upb, acts.at[last, :], dus.at[last, :])
    )
    copies.wait()


def far_x_kernel(
    h_x, dy_x, upb, w_up, w_down, _hs, _dys, _acts, _dus,
    hs, dys, acts, dus, keep_out,
):
    tok = dy_x.shape[0]
    third = pl.ds(2 * tok, tok)
    hs[third, :] = h_x[...]
    dys[third, :] = dy_x[...]
    keep_out[...] = feed_tokens(h_x, dy_x, w_up, w_down, upb, acts.at[third, :], dus.at[third, :])


def weights_kernel(
    hs, dys, acts, dus, w_down,
    u_out, d_out, upb_out, keep_out, send_out,
    stage, sems,
):
    _x, _c, y, z = place()
    width = hs.shape[1]
    rows = width // 8
    upb_out[...] = jnp.sum(f32(dus[...]), axis=0, keepdims=True)

    def weight(number, carry):
        col = pl.multiple_of(number * 256, 256)
        stage[0, pl.ds(col, 256), :] = b16(dot_tn(hs[:, pl.ds(col, 256)], dus[...]))
        stage[1, pl.ds(col, 256), :] = b16(dot_tn(acts[:, pl.ds(col, 256)], dys[...]))
        return carry

    lax.fori_loop(0, width // 256, weight, 0)
    outs = Copies(sems)
    for shard in range(8):
        zz = lax.rem(shard // 2 + 4 - z, 4)
        yy = jnp.where(y == shard % 2, 0, 1)
        outs.add(stage.at[0, pl.ds(shard * rows, rows), :], u_out.at[yy, zz])
        outs.add(stage.at[1, pl.ds(shard * rows, rows), :], d_out.at[yy, zz])
    tok = hs.shape[0] // 4
    for number in range(4):
        part = dot_nn(acts[pl.ds(number * tok, tok), :], w_down[...])
        if number % 2:
            send_out[number // 2] = b16(part)
        else:
            keep_out[number // 2] = part
    outs.wait()


def scatter(stage, other, mine, sems):
    x, c, y, z = place()
    outs = Copies(sems)
    for shard in range(8):
        zz = lax.rem(shard // 2 + 4 - z, 4)
        yy = jnp.where(y == shard % 2, 0, 1)
        for xx in range(2):
            far = jnp.where(x == xx, 0, 1)
            outs.add(stage.at[1 - c, xx, shard], other.at[far, yy, zz])
            outs.add(stage.at[c, xx, shard], mine.at[far, yy, zz])
    outs.wait()


def post_kernel(
    residual, own, near, across, dy_in, vec_in, w_out, a_in,
    dr_out, da_out, dw_out, vec_out,
):
    vec = vec_in[...]
    grad_hidden = own[...] + f32(near[...]) + f32(across[...])
    hat, rate = norm_parts(residual[...])
    dy = f32(dy_in[...])
    grad_first = dy + norm_back(grad_hidden, hat, rate, vec[1:2])
    dr_out[...] = grad_first
    low = b16(grad_first)
    da_out[...] = b16(dot_nt(low, w_out[...]))
    dw_out[...] = dot_tn(a_in[...], low)
    zero = jnp.zeros((1, dy.shape[1]), jnp.float32)
    vec_out[...] = jnp.concatenate(
        [
            zero,
            jnp.sum(grad_hidden * hat, axis=0, keepdims=True),
            zero,
            jnp.sum(grad_hidden, axis=0, keepdims=True),
            zero,
            zero,
            jnp.sum(grad_first, axis=0, keepdims=True),
            jnp.sum(dy, axis=0, keepdims=True),
        ],
        axis=0,
    )


def back_pairs(first, q_in, kv_in, lse_in, da_in, bias, dq, dkv):
    width = q_in.shape[1]

    def pair(number, carry):
        col = pl.multiple_of((first + number) * 128, 128)
        vcol = pl.multiple_of(width + col, 128)
        to = pl.multiple_of(number * 128, 128)
        queries = pair_stack(q_in[:, pl.ds(col, 128)] * jnp.bfloat16(0.125))
        grads = pair_stack(da_in[:, pl.ds(col, 128)])
        keys = kv_in[:, pl.ds(col, 128)]
        probs = jnp.exp(dot_nt(keys, queries) + bias[...] - lse_in[first + number])
        dkv[:, pl.ds(pl.multiple_of(width // 2 + to, 128), 128)] = b16(dot_nn(b16(probs), grads))
        term = probs * dot_nt(kv_in[:, pl.ds(vcol, 128)], grads)
        low = b16(term - probs * jnp.sum(term, axis=0, keepdims=True))
        dkv[:, pl.ds(to, 128)] = b16(dot_nn(low, queries))
        dq[:, pl.ds(to, 128)] = b16(pair_join(dot_tn(keys, low)) * 0.125)
        return carry

    lax.fori_loop(0, 3, pair, 0, unroll=first == 0)


def qkv_weight(h_in, dq, dkv, stage, tail):
    tok, part = dq.shape
    keys = h_in.shape[0]

    def weight(number, carry):
        col = pl.multiple_of(number * 384, 384)
        key = dot_tn(h_in[:, pl.ds(col, 384)], dkv[...])
        query = dot_tn(h_in[pl.ds(keys - tok, tok), pl.ds(col, 384)], dq[...])
        for shard in range(4):
            for cc in range(2):
                for xx in range(2):
                    rows = slice(96 * shard + 48 * cc + 24 * xx, 96 * shard + 48 * cc + 24 * xx + 24)
                    blocks = [query[rows], key[rows, :part], key[rows, part:]] + tail(4 * number + shard, 48 * cc + 24 * xx)
                    stage[cc, xx, 4 * number + shard] = b16(jnp.concatenate(blocks, axis=0))
        return carry

    lax.fori_loop(0, 2, weight, 0)


def back_a_kernel(
    start_in, q_in, kv_in, h_in, lse_in, da_in, dw_in,
    other, mine, dq_out, dkv_out,
    bias, stage, sems,
):
    _x, _c, y, z = place()
    mask_bias(start_in[...], 2 * z + y, q_in.shape[0], bias)
    back_pairs(0, q_in, kv_in, lse_in, da_in, bias, dq_out, dkv_out)
    side = q_in.shape[1] // 2

    def out_rows(shard, row):
        rows = dw_in[pl.ds(pl.multiple_of(96 * shard + row, 8), 24), :]
        return [rows[:, :side], rows[:, side:]]

    qkv_weight(h_in, dq_out, dkv_out, stage, out_rows)
    scatter(stage, other, mine, sems)


def back_b_kernel(
    start_in, q_in, kv_in, lse_in, da_in, vec_in, upb_in, dq_a, dkv_a, xo, x1, x2, x3, x4,
    own, g0, g1, g2, g3, g4, g5, g6, g7, g8, g9, g10, g11,
    dq_out, dkv_out, p_own, p_y, p_z, sums_out,
    full, bias, sems,
):
    x, c, y, z = place()
    p = 2 * x + c
    tok, width = q_in.shape
    side = width // 2
    copies = Copies(sems)
    groups = ((g0, g1, g2), (g3, g4, g5), (g6, g7, g8), (g9, g10, g11))
    fetch_qkv(copies, own, groups, full)
    mask_bias(start_in[...], 2 * z + y, tok, bias)
    back_pairs(3, q_in, kv_in, lse_in, da_in, bias, dq_out, dkv_out)
    copies.wait()
    gain_sum = jnp.zeros((1, width), jnp.float32)
    shift_sum = jnp.zeros((1, width), jnp.float32)
    for back, block in enumerate((xo, x1, x2, x3, x4)):
        rows = pl.ds((4 - back) * tok, tok)
        grad = jnp.zeros((tok, width), jnp.float32)
        for number, (dq, dkv) in enumerate(((dq_a, dkv_a), (dq_out, dkv_out))):
            at = number * side
            grad = grad + dot_nt(dkv[rows, pl.ds(0, side)], full[:, pl.ds(width + at, side)])
            grad = grad + dot_nt(dkv[rows, pl.ds(side, side)], full[:, pl.ds(2 * width + at, side)])
            if back == 0:
                grad = grad + dot_nt(dq[...], full[:, pl.ds(at, side)])
        if back == 0:
            p_own[...] = grad
        elif back in (1, 3):
            p_y[back // 2] = b16(grad)
        else:
            p_z[back // 2 - 1] = b16(grad)
        hat, _rate = norm_parts(f32(block[pl.ds(0, tok), :]))
        gain_sum = gain_sum + jnp.sum(grad * hat, axis=0, keepdims=True)
        shift_sum = shift_sum + jnp.sum(grad, axis=0, keepdims=True)
    zero = jnp.zeros((1, width), jnp.float32)
    bias_q = jnp.concatenate([jnp.sum(f32(d[...]), axis=0, keepdims=True) for d in (dq_a, dq_out)], axis=1)
    bias_v = jnp.concatenate(
        [jnp.sum(f32(d[:, pl.ds(side, side)]), axis=0, keepdims=True) for d in (dkv_a, dkv_out)], axis=1
    )
    vec = vec_in[...] + jnp.concatenate(
        [gain_sum, zero, shift_sum, zero, bias_q, bias_v, zero, zero], axis=0
    )
    lane = lax.broadcasted_iota(jnp.int32, (8, 128), 1)
    line = lax.broadcasted_iota(jnp.int32, (8, 128), 0)
    for group in range(2):
        cols = pl.ds(384 * group, 384)
        vec_parts = unpack96(vec[:, 384 * group : 384 * group + 384])
        upb_parts = unpack96(jnp.broadcast_to(upb_in[:, cols], (8, 384)))
        for k in range(4):
            sums_out[4 * group + k] = jnp.concatenate(
                [
                    jnp.where(lane < 96, vec_parts[k], 0.0),
                    jnp.where((lane < 96) & (line == p), upb_parts[k], 0.0),
                ],
                axis=1,
            )


def back_c_kernel(h_in, dq, dkv, sums_in, other, mine, stage, sems):
    blank = jnp.zeros((8, 128), jnp.float32)
    qkv_weight(
        h_in, dq, dkv, stage, lambda shard, _row: [jnp.concatenate([sums_in[shard], blank], axis=1)]
    )
    scatter(stage, other, mine, sems)


def tokens_kernel(own, near, dr, xo, vec_in, grad_out):
    tok = own.shape[0]
    hat, rate = norm_parts(f32(xo[pl.ds(0, tok), :]))
    grad = own[...] + f32(near[...])
    grad_out[...] = dr[...] + norm_back(grad, hat, rate, vec_in[0:1, :])


def finish_f_kernel(f0, fx, fc, fcx, up, down, held):
    x, c, _y, _z = place()
    rows = f0.shape[0] // 2
    for (xx, cc), f in zip(corners(x, c), (f0, fx, fc, fcx), strict=True):
        p = 2 * xx + cc
        held[p] = f[pl.ds(0, rows), :]
        down[pl.ds(pl.multiple_of(rows * p, 16), rows), :] = f32(f[pl.ds(rows, rows), :])
    for group in range(2):
        parts = [unpack96(f32(held[k, :, pl.ds(384 * group, 384)])) for k in range(4)]
        for shard in range(4):
            up[:, pl.ds(384 * (4 * group + shard), 384)] = pack96([part[shard] for part in parts])


def finish_q_kernel(f0, fx, fc, fcx, qkv, out):
    x, c, _y, _z = place()
    side = out.shape[1] // 2
    for (xx, cc), piece in zip(corners(x, c), (f0, fx, fc, fcx), strict=True):
        rows = pl.ds(pl.multiple_of(48 * cc + 24 * xx, 8), 24)
        blocks = f32(piece[...])
        for number in range(3):
            first, second = 24 * number, 24 * (number + 5)
            qkv[rows, pl.ds(2 * side * number, side)] = blocks[first : first + 24]
            qkv[rows, pl.ds(2 * side * number + side, side)] = blocks[second : second + 24]
        out[rows, pl.ds(0, side)] = blocks[72:96]
        out[rows, pl.ds(side, side)] = blocks[96:120]


HB = pl.BlockSpec(memory_space=pltpu.HBM)
VM = pl.BlockSpec(memory_space=pltpu.VMEM)
AN = pl.BlockSpec(memory_space=pl.ANY)


def shape_of(shape, dtype):
    return jax.ShapeDtypeStruct(shape, dtype)


def call(kernel, ins, outs, out_shape, scratch=(), vmem=40, flops=0, moved=0, aliases=None):
    return pl.pallas_call(
        kernel,
        in_specs=ins,
        out_specs=outs,
        out_shape=out_shape,
        scratch_shapes=list(scratch),
        input_output_aliases=aliases or {},
        compiler_params=pltpu.CompilerParams(vmem_limit_bytes=vmem << 20),
        cost_estimate=pl.CostEstimate(flops=flops, bytes_accessed=moved, transcendentals=0),
    )


def fence(*values):
    return lax.optimization_barrier(values)


def swap_rep(value, bit):
    return lax.ppermute(value, "rep", [(k, k ^ bit) for k in range(4)])


def to_core(value):
    return swap_rep(value, 1)


def to_x(value):
    return swap_rep(value, 2)


def to_y(value):
    return lax.ppermute(value, "seq", [(k, k ^ 1) for k in range(8)])


def to_z(value, steps):
    return lax.ppermute(value, "seq", [(k, (k + 2 * steps) % 8) for k in range(8)])


def join(*parts):
    return jnp.concatenate(parts, axis=0)


def on_device_fast(
    tokens,
    segment_ids,
    query_key_value_weight,
    output_weight,
    up_weight,
    down_weight,
    ln_gains,
    ln_biases,
    biases,
    up_projection_bias,
    cotangent,
):
    seq = lax.axis_index("seq")
    y = seq % 2
    tok, width = tokens.shape[1:]
    hidden = up_weight.shape[1]
    keys = 5 * tok
    bf, fl = jnp.bfloat16, jnp.float32
    dma = pltpu.SemaphoreType.DMA
    grad_y = cotangent[0]
    own_tokens, piece_q, piece_f, piece_u, piece_d = call(
        prep_kernel,
        [HB] * 10,
        [VM] * 5,
        [
            shape_of((tok + 8, width), bf),
            shape_of((48, 2 * width + 128), bf),
            shape_of((192, width), bf),
            shape_of((96, width), bf),
            shape_of((96, width), bf),
        ],
        [
            pltpu.VMEM((8, width), fl),
            pltpu.VMEM((96, hidden), bf),
            pltpu.VMEM((2, 96), bf),
            pltpu.VMEM((2, 96), bf),
            pltpu.VMEM((4, 96), bf),
            pltpu.VMEM((1, tok), jnp.int32),
            pltpu.VMEM((384,), bf),
            dma((11,)),
        ],
        vmem=60, moved=4 * 10**6,
    )(
        tokens, segment_ids, query_key_value_weight, output_weight, up_weight, down_weight,
        ln_gains, ln_biases, biases, up_projection_bias,
    )

    q1, q3, q_y0, dy_x = fence(to_z(piece_q, 1), to_z(piece_q, 3), to_y(piece_q), to_x(grad_y))
    own_tokens, piece_f, q1, q_y0 = fence(own_tokens, piece_f, q1, q_y0, q3, dy_x)[:4]
    q2, x2, q_xy0, f_y0 = fence(to_z(q1, 1), to_z(own_tokens, 1), to_x(q_y0), to_y(piece_f))
    q_z = join(q1, q2, q3)
    q_z, x2, piece_d = fence(q_z, x2, piece_d, q_xy0, f_y0)[:3]
    q_y, q_xz, x4, f3d = fence(to_y(q_z), to_x(q_z), to_z(x2, 1), to_z(piece_d, 3))
    near = jnp.where(y == 0, own_tokens, x2)
    far = jnp.where(y == 0, x2, x4)
    near_far, q_y, piece_f, piece_u = fence(
        jnp.stack([near, far]), q_y, piece_f, piece_u, q_xz, f3d
    )[:4]
    crossed, q_xy, f1, f3u = fence(to_y(near_far), to_x(q_y), to_z(piece_f, 1), to_z(piece_u, 3))
    x1, x3 = crossed[0], crossed[1]
    q_z, q_y0, q_y, q_xz, q_xy0, q_xy = fence(q_z, q_y0, q_y, q_xz, q_xy0, q_xy, f1, f3u, crossed)[:6]
    q_cz, q_cy0, q_cy, q_cxz, q_cxy0, q_cxy = fence(
        *(to_core(v) for v in (q_z, q_y0, q_y, q_xz, q_xy0, q_xy))
    )
    f_13, f_1, q_cz = fence(join(f1, f3u, f3d), f1, q_cz, q_cy0, q_cy, q_cxz, q_cxy0, q_cxy)[:3]
    f_y13, f2 = to_y(f_13), to_z(f_1, 1)
    dy_c, dy_xc = to_core(grad_y), to_core(dy_x)

    def pieces(value):
        return value.reshape(value.shape[0] // 48, 48, value.shape[1])

    got_q = [
        pieces(v)
        for v in (q_z, q_y0, q_y, q_xz, q_xy0, q_xy, q_cz, q_cy0, q_cy, q_cxz, q_cxy0, q_cxy)
    ]
    seg = jnp.concatenate([segment_ids, segment_ids], axis=1)
    front = call(
        front_kernel,
        [VM] * 6 + [AN] * 15,
        [VM] * 11,
        [
            shape_of((tok, width), bf),
            shape_of((keys, 2 * width), bf),
            shape_of((keys, width), bf),
            shape_of((tok, width), bf),
            shape_of((width // 128, 1, 2 * tok), fl),
            shape_of((1, 2 * tok), jnp.int32),
            shape_of((8, width), fl),
            shape_of((8, width), fl),
            shape_of((width, width), bf),
            shape_of((tok, width), fl),
            shape_of((tok, width), bf),
        ],
        [
            pltpu.VMEM((width, 3 * width), bf),
            pltpu.VMEM((8, 16, 128), bf),
            pltpu.VMEM((keys, 2 * tok), fl),
            dma((2 + 56,)),
            dma((8,)),
        ],
        flops=7 * 10**9,
        vmem=16, moved=12 * 10**6,
    )(
        seg, own_tokens, x1, x2, x3, x4, piece_q, query_key_value_weight, output_weight, *got_q,
    )
    *front, f_y13, f2, dy_c, dy_xc = fence(*front, f_y13, f2, dy_c, dy_xc)
    queries, kv, normed, attended, lse, start, vec, upb, w_out, residual, hidden_2 = front
    w_half = call(
        assemble_kernel,
        [AN] * 7,
        [VM] * 2,
        [shape_of((width, width), bf)] * 2,
        [dma((14,))],
        vmem=4,
        moved=5 * 10**6,
    )(piece_f, f1, f2, f3u, f3d, f_y0, f_y13)
    h_x, h_c, f_y2, *w_half = fence(to_x(hidden_2), to_core(hidden_2), to_y(f2), *w_half)
    act = shape_of((2 * tok, width), bf)
    acts = shape_of((4 * tok, width), bf)
    feed_shapes = [shape_of((tok, width), fl), shape_of((tok, width), bf)]
    *near_acts, keep_a, send_a, w_up, w_down = call(
        near_kernel,
        [VM] * 5 + [AN] + [VM] * 2,
        [VM] * 8,
        [act] * 4 + feed_shapes + [shape_of((width, width), bf)] * 2,
        [dma((2,))],
        flops=3 * 10**9,
        vmem=8,
        moved=6 * 10**6,
        aliases={6: 6, 7: 7},
    )(hidden_2, h_c, grad_y, dy_c, upb, f_y2, *w_half)
    h_xc = to_core(h_x)
    keep_a, send_a, h_xc, w_up = fence(keep_a, send_a, h_xc, w_up)
    came_a = to_core(send_a)
    *all_acts, send_b = call(
        far_c_kernel,
        [VM] * 5 + [AN] * 4,
        [VM] * 5,
        [acts] * 4 + feed_shapes[1:],
        [dma((4,))],
        flops=15 * 10**8,
        vmem=8,
        moved=6 * 10**6,
    )(h_xc, dy_xc, upb, w_up, w_down, *near_acts)
    send_b, came_a, h_x = fence(send_b, came_a, h_x)
    came_b = to_core(send_b)
    *all_acts, keep_b = call(
        far_x_kernel,
        [VM] * 9,
        [VM] * 5,
        [acts] * 4 + feed_shapes[:1],
        flops=3 * 10**9,
        vmem=8,
        moved=6 * 10**6,
        aliases={5: 0, 6: 1, 7: 2, 8: 3},
    )(h_x, dy_x, upb, w_up, w_down, *all_acts)
    keep_b, came_b, *all_acts = fence(keep_b, came_b, *all_acts)
    back_x = to_x(b16(keep_b + f32(came_b)))
    u_terms, d_terms, upb_g, y_keep, y_send = call(
        weights_kernel,
        [VM] * 5,
        [AN, AN] + [VM] * 3,
        [
            shape_of((2, 4, 96, width), bf),
            shape_of((2, 4, 96, width), bf),
            shape_of((1, width), fl),
            shape_of((2, tok, width), fl),
            shape_of((2, tok, width), bf),
        ],
        [pltpu.VMEM((2, width, width), bf), dma((16,))],
        flops=3 * 10**9,
        vmem=12,
        moved=6 * 10**6,
    )(*all_acts, w_down)
    back_x, u_terms, d_terms, y_send = fence(back_x, u_terms, d_terms, y_send)
    u_came = to_y(u_terms[1])
    came_y = to_core(y_send)
    grad_first, grad_attended, dw_out, vec_g = call(
        post_kernel,
        [VM] * 8,
        [VM] * 4,
        [
            shape_of((tok, width), fl),
            shape_of((tok, width), bf),
            shape_of((width, width), fl),
            shape_of((8, width), fl),
        ],
        vmem=12,
        flops=10**9,
        moved=4 * 10**6,
    )(residual, keep_a, came_a, back_x, grad_y, vec, w_out, attended)
    back_scratch = [
        pltpu.VMEM((keys, 2 * tok), fl),
    ]
    qa_other, qa_mine, dq_a, dkv_a = call(
        back_a_kernel,
        [VM] * 7,
        [AN] * 2 + [VM] * 2,
        [
            shape_of((2, 2, 4, 120, width // 2), bf),
            shape_of((2, 2, 4, 120, width // 2), bf),
            shape_of((tok, width // 2), bf),
            shape_of((keys, width), bf),
        ],
        back_scratch + [pltpu.VMEM((2, 2, 8, 120, width // 2), bf), dma((32,))],
        flops=5 * 10**9,
        vmem=16, moved=10 * 10**6,
    )(start, queries, kv, normed, lse, grad_attended, dw_out)

    def both(mine, came):
        return lambda *index: f32(mine[index]) + f32(came[index])

    def z_sum(part, *came):
        return b16(part(0) + sum(f32(v) for v in came))

    dq_a, qa_other, u_came, came_y, d_send = fence(
        dq_a, qa_other, u_came, came_y, d_terms[1]
    )
    d_came, qa_came = to_y(d_send), to_core(qa_other)
    u_part = both(u_terms[0], u_came)
    u_z = [to_z(b16(u_part(step)), step) for step in (1, 2, 3)]
    dq_b, dkv_b, p_own, p_y, p_z, sums = call(
        back_b_kernel,
        [VM] * 14 + [AN] * 13,
        [VM] * 6,
        [
            shape_of((tok, width // 2), bf),
            shape_of((keys, width), bf),
            shape_of((tok, width), fl),
            shape_of((2, tok, width), bf),
            shape_of((2, tok, width), bf),
            shape_of((8, 8, 256), fl),
        ],
        [pltpu.VMEM((width, 3 * width), bf)] + back_scratch + [dma((1 + 28,))],
        flops=6 * 10**9,
        vmem=20, moved=10 * 10**6,
    )(
        start, queries, kv, lse, grad_attended, vec_g, upb_g, dq_a, dkv_a,
        own_tokens, x1, x2, x3, x4, query_key_value_weight, *got_q,
    )
    dq_b, qa_came, d_came, p_y, *u_z = fence(dq_b, qa_came, d_came, p_y, *u_z)
    p_came = to_y(p_y)
    qa_1 = both(qa_mine, qa_came)
    qa_x = to_x(b16(qa_1(1)))
    d_part = both(d_terms[0], d_came)
    d_z2 = to_z(b16(d_part(2)), 1)
    qb_other, qb_mine = call(
        back_c_kernel,
        [VM] * 4,
        [AN] * 2,
        [
            shape_of((2, 2, 4, 80, width // 2), bf),
            shape_of((2, 2, 4, 80, width // 2), bf),
        ],
        [pltpu.VMEM((2, 2, 8, 80, width // 2), bf), dma((32,))],
        flops=3 * 10**9,
        vmem=12, moved=6 * 10**6,
    )(normed, dq_b, dkv_b, sums)
    qb_came = [to_core(qb_other[k]) for k in range(2)]
    *qb_came, qa_x, p_came, d_z2 = fence(*qb_came, qa_x, p_came, d_z2)
    even = y == 0
    sum_own = p_own + jnp.where(even, f32(p_came[0]), 0.0)
    sum_4 = b16(f32(p_z[1]) + jnp.where(even, 0.0, f32(p_came[1])))
    sum_2 = f32(p_z[0]) + jnp.where(even, f32(p_came[1]), f32(p_came[0]))
    def qa_2(*index):
        return qa_1(0, *index) + f32(qa_x[index])

    def qb_1(side, *index):
        return f32(qb_mine[(side,) + index]) + f32(qb_came[side][index])

    qb_x, qa_y, hop, d_z1, d_z3 = fence(
        to_x(b16(qb_1(1))),
        to_y(b16(qa_2(1))),
        to_z(sum_4, 3),
        to_z(b16(d_part(1) + f32(d_z2)), 1),
        to_z(b16(d_part(3)), 3),
    )

    def qb_2(*index):
        return qb_1(0, *index) + f32(qb_x[index])

    f_tot = join(z_sum(u_part, *u_z), z_sum(d_part, d_z1, d_z3))
    fy_tot = join(f_tot, b16(y_keep[1] + f32(came_y[1])))
    qb_y, back_2, f_tot, fy_tot = fence(
        to_y(b16(qb_2(1))), to_z(b16(sum_2 + f32(hop)), 3), f_tot, fy_tot
    )

    def q_3(*index):
        first = qa_2(0, *index) + f32(qa_y[index])
        return jnp.concatenate([first, qb_2(0, *index) + f32(qb_y[index])], axis=-2)

    grad_tokens = call(
        tokens_kernel, [VM] * 5, VM, shape_of((tok, width), fl), vmem=4, moved=3 * 10**6
    )(sum_own, back_2, grad_first, own_tokens, vec)
    *q_z, over_x, f_tot = fence(*(to_z(b16(q_3(step)), step) for step in (1, 2, 3)), to_x(fy_tot), f_tot)
    f_x, back_y = over_x[:tok], over_x[tok:]
    q_sum = z_sum(q_3, *q_z)
    q_fx, q_fc, q_fxc = to_x(q_sum), to_core(q_sum), swap_rep(q_sum, 3)
    grad_up, grad_down = call(
        finish_f_kernel,
        [VM] * 4,
        [VM] * 2,
        [shape_of(up_weight.shape, fl), shape_of(down_weight.shape, fl)],
        [pltpu.VMEM((4, 96, width), bf)],
        vmem=8,
        moved=4 * 10**6,
    )(f_tot, f_x, to_core(f_tot), to_core(f_x))
    q_fx, q_fc, q_fxc, grad_up, grad_down = fence(q_fx, q_fc, q_fxc, grad_up, grad_down)
    result = b16(residual + vec[7:8] + y_keep[0] + f32(came_y[0]) + f32(back_y))
    grad_qkv, grad_out = call(
        finish_q_kernel,
        [VM] * 4,
        [VM] * 2,
        [shape_of(query_key_value_weight.shape, fl), shape_of(output_weight.shape, fl)],
        vmem=8, moved=3 * 10**6,
    )(q_sum, q_fx, q_fc, q_fxc)
    sums = f32(q_sum[192:200, :256])
    part = ln_gains.shape[1]
    return (
        result[None],
        grad_tokens[None],
        grad_qkv,
        grad_out,
        grad_up,
        grad_down,
        sums[0:2, :part],
        sums[2:4, :part],
        sums[4:8, :part],
        sums[0:4, 128 : 128 + part].reshape(4 * part),
    )


def solution(mesh):
    placed = (
        P("rep", "seq", None),
        P("rep", "seq"),
        P("seq", None),
        P("seq", None),
        P("seq", None),
        P("seq", None),
        P(None, "seq"),
        P(None, "seq"),
        P(None, "seq"),
        P("seq"),
        P("rep", "seq", None),
    )
    shape = dict(mesh.shape)
    small_slice = shape["rep"] == 4 and shape["seq"] == 8
    return jax.shard_map(
        on_device_fast if small_slice else on_device,
        mesh=mesh,
        in_specs=placed,
        out_specs=(
            P("rep", "seq", None),
            P("rep", "seq", None),
            P("seq", None),
            P("seq", None),
            P("seq", None),
            P("seq", None),
            P(None, "seq"),
            P(None, "seq"),
            P(None, "seq"),
            P("seq"),
        ),
        check_vma=False,
    )
```

```python
import math

import jax
import jax.numpy as jnp
from jax import lax
from jax.experimental import pallas as pl
from jax.experimental.pallas import tpu as pltpu
from jax.sharding import PartitionSpec as P

HEADS = 12
HD = 64


norm_eps = 1e-05
floor_score = -1e30


def layer_norm(values, gain, shift):
    center = values - jnp.mean(values, axis=-1, keepdims=True)
    spread = jnp.mean(center * center, axis=-1, keepdims=True)
    return center * lax.rsqrt(spread + norm_eps) * gain + shift


def head_split(matrix):
    return matrix.reshape(matrix.shape[0], HEADS, HD)


def masked_scores(queries, query_seg, query_pos, key_piece, seg_piece, offset):
    rows = key_piece.shape[0]
    scores = jnp.einsum(
        "qhd,khd->hqk", queries, head_split(key_piece), preferred_element_type=jnp.float32
    ) * HD ** (-0.5)
    key_pos = offset + jnp.arange(rows, dtype=jnp.int32)
    allowed = (query_seg[:, None] == seg_piece[None, :]) & (key_pos[None, :] <= query_pos[:, None])
    return (jnp.where(allowed[None], scores, floor_score), allowed)


def forward_block(running, pieces, offset, queries, query_seg, query_pos):
    top_run, total_run, accum = running
    key_piece, value_piece, seg_piece = pieces
    scores, allowed = masked_scores(queries, query_seg, query_pos, key_piece, seg_piece, offset)
    top_new = jnp.maximum(top_run, jnp.max(scores, axis=-1))
    probs = jnp.where(allowed[None], jnp.exp(scores - top_new[:, :, None]), 0.0)
    factor = jnp.exp(top_run - top_new)
    total_new = total_run * factor + jnp.sum(probs, axis=-1)
    update = jnp.einsum(
        "hqk,khd->qhd",
        probs.astype(jnp.bfloat16),
        head_split(value_piece),
        preferred_element_type=jnp.float32,
    )
    return (top_new, total_new, accum * factor.T[:, :, None] + update)


def in_blocks(block_fn, running, pieces):
    rows = pieces[0].shape[0]
    size = math.gcd(rows, 1024)
    stacked = tuple((member.reshape((rows // size, size) + member.shape[1:]) for member in pieces))
    offsets = jnp.arange(rows // size, dtype=jnp.int32) * size

    def scan_step(state_now, element):
        return (block_fn(state_now, element[0], element[1]), None)

    running, _unused = lax.scan(scan_step, running, (stacked, offsets))
    return running


def backward_block(
    number,
    state_now,
    whole,
    queries,
    query_seg,
    query_pos,
    grad_heads,
    log_total,
    delta,
    block_rows,
):
    grad_query, term = state_now
    offset = number * block_rows
    key_piece = lax.dynamic_slice_in_dim(whole[0], offset, block_rows, 0)
    value_piece = lax.dynamic_slice_in_dim(whole[1], offset, block_rows, 0)
    seg_piece = lax.dynamic_slice_in_dim(whole[2], offset, block_rows, 0)
    scores, allowed = masked_scores(queries, query_seg, query_pos, key_piece, seg_piece, offset)
    probs = jnp.where(allowed[None], jnp.exp(scores - log_total[:, :, None]), 0.0)
    grad_probs = jnp.einsum(
        "qhd,khd->hqk", grad_heads, head_split(value_piece), preferred_element_type=jnp.float32
    )
    grad_scores = (probs * (grad_probs - delta[:, :, None])).astype(jnp.bfloat16)
    grad_query = grad_query + jnp.einsum(
        "hqk,khd->qhd", grad_scores, head_split(key_piece), preferred_element_type=jnp.float32
    )
    grad_key = jnp.einsum(
        "hqk,qhd->khd", grad_scores, queries, preferred_element_type=jnp.float32
    ) * HD ** (-0.5)
    grad_value = jnp.einsum(
        "hqk,qhd->khd", probs.astype(jnp.bfloat16), grad_heads, preferred_element_type=jnp.float32
    )
    joined = jnp.concatenate(
        [grad_key.reshape(block_rows, -1), grad_value.reshape(block_rows, -1)], axis=1
    )
    term = lax.dynamic_update_slice_in_dim(term, joined, offset, 0)
    return (grad_query, term)


def on_device(
    tokens,
    segment_ids,
    query_key_value_weight,
    output_weight,
    up_weight,
    down_weight,
    ln_gains,
    ln_biases,
    biases,
    up_projection_bias,
    cotangent,
):
    gathered = (
        lax.all_gather(query_key_value_weight, "seq", axis=0, tiled=True),
        lax.all_gather(output_weight, "seq", axis=0, tiled=True),
        lax.all_gather(up_weight, "seq", axis=0, tiled=True),
        lax.all_gather(down_weight, "seq", axis=0, tiled=True),
        lax.all_gather(ln_gains, "seq", axis=1, tiled=True),
        lax.all_gather(ln_biases, "seq", axis=1, tiled=True),
        lax.all_gather(biases, "seq", axis=1, tiled=True),
        lax.all_gather(up_projection_bias, "seq", axis=0, tiled=True),
    )
    full_qkv, full_out, full_up, full_down, gains_all, shifts_all, biases_all, up_shift = gathered
    gains_f = gains_all.astype(jnp.float32)
    shifts_f = shifts_all.astype(jnp.float32)
    biases_f = biases_all.astype(jnp.float32)
    up_shift_f = up_shift.astype(jnp.float32)
    tokens_f = tokens[0].astype(jnp.float32)
    seg_local = segment_ids[0]
    tok_rows = tokens_f.shape[0]
    width = tokens_f.shape[1]
    seqlen = tok_rows * lax.axis_size("seq")
    query_pos = lax.axis_index("seq") * tok_rows + jnp.arange(tok_rows, dtype=jnp.int32)
    hidden_first = layer_norm(tokens_f, gains_f[0], shifts_f[0]).astype(jnp.bfloat16)
    query_key_value_bias = jnp.concatenate(
        [biases_f[0], jnp.zeros((width,), jnp.float32), biases_f[1]]
    )
    projected_rows = (
        jnp.dot(hidden_first, full_qkv, preferred_element_type=jnp.float32) + query_key_value_bias
    ).astype(jnp.bfloat16)
    queries = head_split(projected_rows[:, :width])
    key_rows = projected_rows[:, width : 2 * width]
    value_rows = projected_rows[:, 2 * width :]
    initial = (
        jnp.full((HEADS, tok_rows), floor_score, jnp.float32),
        jnp.zeros((HEADS, tok_rows), jnp.float32),
        jnp.zeros((tok_rows, HEADS, HD), jnp.float32),
    )

    def block_fn(running, pieces, offset):
        return forward_block(running, pieces, offset, queries, seg_local, query_pos)

    block_rows = math.gcd(seqlen, 1024)
    key_end = (lax.axis_index("seq") + 1) * tok_rows
    block_count = (key_end + block_rows - 1) // block_rows
    top_run, total_run, accum = in_blocks(
        block_fn,
        initial,
        (
            lax.all_gather(key_rows, "seq", axis=0, tiled=True),
            lax.all_gather(value_rows, "seq", axis=0, tiled=True),
            lax.all_gather(seg_local, "seq", axis=0, tiled=True),
        ),
    )
    log_total = top_run + jnp.log(total_run)
    attended_f = accum / total_run.T[:, :, None]
    attention_result = attended_f.reshape(tok_rows, width).astype(jnp.bfloat16)
    residual_first = (
        tokens_f
        + jnp.dot(attention_result, full_out, preferred_element_type=jnp.float32)
        + biases_f[2]
    )
    hidden_second = layer_norm(residual_first, gains_f[1], shifts_f[1]).astype(jnp.bfloat16)
    upward_rows = jnp.dot(hidden_second, full_up, preferred_element_type=jnp.float32) + up_shift_f
    activated_f, gelu_back = jax.vjp(jax.nn.gelu, upward_rows)
    activation_values = activated_f.astype(jnp.bfloat16)
    result = (
        residual_first
        + jnp.dot(activation_values, full_down, preferred_element_type=jnp.float32)
        + biases_f[3]
    )
    grad_y = cotangent[0]
    grad_y_f = grad_y.astype(jnp.float32)
    grad_down = jnp.einsum(
        "tf,td->fd", activation_values, grad_y, preferred_element_type=jnp.float32
    )
    grad_act = jnp.einsum("td,fd->tf", grad_y, full_down, preferred_element_type=jnp.float32)
    grad_up_pre = gelu_back(grad_act)[0].astype(jnp.bfloat16)
    grad_up = jnp.einsum(
        "td,tf->df", hidden_second, grad_up_pre, preferred_element_type=jnp.float32
    )
    grad_hidden_two = jnp.einsum(
        "tf,df->td", grad_up_pre, full_up, preferred_element_type=jnp.float32
    )
    _unused, norm_two_back = jax.vjp(layer_norm, residual_first, gains_f[1], shifts_f[1])
    grad_sum_part, grad_gain_two, grad_shift_two = norm_two_back(grad_hidden_two)
    grad_first = grad_y_f + grad_sum_part
    grad_first_bf = grad_first.astype(jnp.bfloat16)
    grad_out_w = jnp.einsum(
        "td,te->de", attention_result, grad_first_bf, preferred_element_type=jnp.float32
    )
    grad_attended = jnp.einsum(
        "te,de->td", grad_first_bf, full_out, preferred_element_type=jnp.float32
    ).astype(jnp.bfloat16)
    grad_heads = head_split(grad_attended)
    delta = jnp.einsum("qhd,qhd->hq", grad_heads.astype(jnp.float32), attended_f)
    whole = (
        lax.all_gather(key_rows, "seq", axis=0, tiled=True),
        lax.all_gather(value_rows, "seq", axis=0, tiled=True),
        lax.all_gather(seg_local, "seq", axis=0, tiled=True),
    )

    def backward_step(number, state_now):
        return backward_block(
            number,
            state_now,
            whole,
            queries,
            seg_local,
            query_pos,
            grad_heads,
            log_total,
            delta,
            block_rows,
        )

    start_state = (
        jnp.zeros((tok_rows, HEADS, HD), jnp.float32),
        jnp.zeros((seqlen, 2 * width), jnp.float32),
    )
    grad_query, term = lax.fori_loop(0, block_count, backward_step, start_state)
    grad_kv = lax.psum_scatter(term, "seq", scatter_dimension=0, tiled=True).astype(jnp.bfloat16)
    grad_q = (grad_query * HD ** (-0.5)).reshape(tok_rows, width).astype(jnp.bfloat16)
    grad_proj = jnp.concatenate([grad_q, grad_kv], axis=1)
    grad_qkv_w = jnp.einsum(
        "td,te->de", hidden_first, grad_proj, preferred_element_type=jnp.float32
    )
    grad_hidden_one = jnp.einsum(
        "te,de->td", grad_proj, full_qkv, preferred_element_type=jnp.float32
    )
    _unused_two, norm_one_back = jax.vjp(layer_norm, tokens_f, gains_f[0], shifts_f[0])
    grad_in_part, grad_gain_one, grad_shift_one = norm_one_back(grad_hidden_one)
    grad_tokens = grad_first + grad_in_part
    grad_proj_f = grad_proj.astype(jnp.float32)
    grad_bias_rows = jnp.stack(
        [
            jnp.sum(grad_proj_f[:, :width], axis=0),
            jnp.sum(grad_proj_f[:, 2 * width :], axis=0),
            jnp.sum(grad_first, axis=0),
            jnp.sum(grad_y_f, axis=0),
        ]
    )
    grad_up_shift = jnp.sum(grad_up_pre.astype(jnp.float32), axis=0)
    grad_gains = jnp.stack([grad_gain_one, grad_gain_two])
    grad_shifts = jnp.stack([grad_shift_one, grad_shift_two])
    shares = (
        lax.psum_scatter(grad_qkv_w, "seq", scatter_dimension=0, tiled=True),
        lax.psum_scatter(grad_out_w, "seq", scatter_dimension=0, tiled=True),
        lax.psum_scatter(grad_up, "seq", scatter_dimension=0, tiled=True),
        lax.psum_scatter(grad_down, "seq", scatter_dimension=0, tiled=True),
        lax.psum_scatter(grad_gains, "seq", scatter_dimension=1, tiled=True),
        lax.psum_scatter(grad_shifts, "seq", scatter_dimension=1, tiled=True),
        lax.psum_scatter(grad_bias_rows, "seq", scatter_dimension=1, tiled=True),
        lax.psum_scatter(grad_up_shift, "seq", scatter_dimension=0, tiled=True),
    )
    totals = (
        lax.psum(shares[0].astype(jnp.bfloat16), "rep").astype(jnp.float32),
        lax.psum(shares[1].astype(jnp.bfloat16), "rep").astype(jnp.float32),
        lax.psum(shares[2].astype(jnp.bfloat16), "rep").astype(jnp.float32),
        lax.psum(shares[3].astype(jnp.bfloat16), "rep").astype(jnp.float32),
        lax.psum(shares[4].astype(jnp.bfloat16), "rep").astype(jnp.float32),
        lax.psum(shares[5].astype(jnp.bfloat16), "rep").astype(jnp.float32),
        lax.psum(shares[6].astype(jnp.bfloat16), "rep").astype(jnp.float32),
        lax.psum(shares[7].astype(jnp.bfloat16), "rep").astype(jnp.float32),
    )
    return (
        result.astype(jnp.bfloat16)[None],
        grad_tokens[None],
        totals[0],
        totals[1],
        totals[2],
        totals[3],
        totals[4],
        totals[5],
        totals[6],
        totals[7],
    )


def f32(value):
    return value.astype(jnp.float32)


def b16(value):
    return value.astype(jnp.bfloat16)


def dot_nn(left, right):
    return jnp.dot(left, right, preferred_element_type=jnp.float32)


def dot_nt(left, right):
    return lax.dot_general(
        left, right, (((1,), (1,)), ((), ())), preferred_element_type=jnp.float32
    )


def dot_tn(left, right):
    return lax.dot_general(
        left, right, (((0,), (0,)), ((), ())), preferred_element_type=jnp.float32
    )


def norm_parts(values):
    center = values - jnp.mean(values, axis=-1, keepdims=True)
    rate = lax.rsqrt(jnp.mean(center * center, axis=-1, keepdims=True) + norm_eps)
    return center * rate, rate


def norm_back(grad, hat, rate, gain):
    scaled = grad * gain
    return rate * (
        scaled
        - jnp.mean(scaled, axis=-1, keepdims=True)
        - hat * jnp.mean(scaled * hat, axis=-1, keepdims=True)
    )


def place():
    rep, seq = lax.axis_index("rep"), lax.axis_index("seq")
    return lax.div(rep, 2), lax.rem(rep, 2), lax.rem(seq, 2), lax.div(seq, 2)


def piece_shard(number, y, z):
    if number < 3:
        return 2 * lax.rem(z + 3 - number, 4) + y
    return 2 * lax.rem(z + 7 - number, 4) + 1 - y


def pack96(parts):
    lane = lax.broadcasted_iota(jnp.int32, parts[0].shape, 1)
    one, two, three = (pltpu.roll(parts[k], 128 - 32 * k, 1) for k in (1, 2, 3))
    return jnp.concatenate(
        [
            jnp.where(lane < 96, parts[0], one),
            jnp.where(lane < 64, one, two),
            jnp.where(lane < 32, two, three),
        ],
        axis=1,
    )


def unpack96(block):
    tiles = [block[:, 128 * k : 128 * k + 128] for k in range(3)]
    lane = lax.broadcasted_iota(jnp.int32, tiles[0].shape, 1)
    return [
        tiles[0],
        jnp.where(lane < 32, pltpu.roll(tiles[0], 32, 1), pltpu.roll(tiles[1], 32, 1)),
        jnp.where(lane < 64, pltpu.roll(tiles[1], 64, 1), pltpu.roll(tiles[2], 64, 1)),
        pltpu.roll(tiles[2], 96, 1),
    ]


def choose(parts, index):
    out = parts[0]
    for number in range(1, len(parts)):
        out = jnp.where(index == number, parts[number], out)
    return out


class Copies:
    def __init__(self, sems, first=0):
        self.sems = sems
        self.first = first
        self.held = []

    def add(self, source, target):
        copy = pltpu.make_async_copy(source, target, self.sems.at[self.first + len(self.held)])
        copy.start()
        self.held.append(copy)

    def wait(self):
        for copy in self.held:
            copy.wait()
        self.held = []


def corners(x, c):
    return ((x, c), (1 - x, c), (x, 1 - c), (1 - x, 1 - c))


def fetch_qkv(copies, own, groups, full, full_out=None, own_out=None):
    x, c, y, z = place()
    rows = own.shape[0]
    half, width = rows // 2, own.shape[1] // 3
    row = pl.multiple_of((2 * z + y) * rows, 16)
    copies.add(own, full.at[pl.ds(row, rows), :])
    if full_out is not None:
        copies.add(own_out, full_out.at[pl.ds(row, rows), :])
    wide, side = 3 * width // 2, width // 2
    for number in range(7):
        for (xx, cc), group in zip(corners(x, c), groups, strict=True):
            piece = piece_of(group, number)
            at = pl.ds(pl.multiple_of(piece_shard(number, y, z) * rows + half * cc, 16), half)
            copies.add(
                piece.at[pl.ds(0, half), pl.ds(0, wide)],
                full.at[at, pl.ds(pl.multiple_of(wide * xx, 128), wide)],
            )
            if full_out is not None:
                copies.add(
                    piece.at[pl.ds(0, half), pl.ds(wide, side)],
                    full_out.at[at, pl.ds(pl.multiple_of(side * xx, 128), side)],
                )


def piece_of(group, number):
    behind, across, behind_across = group
    if number < 3:
        return behind.at[number]
    return across.at[0] if number == 3 else behind_across.at[number - 4]


def mask_bias(start, me, tok, target):
    keys, lanes = target.shape
    key_pos = (me - 4) * tok + lax.broadcasted_iota(jnp.int32, (keys, lanes), 0)
    lane = lax.broadcasted_iota(jnp.int32, (keys, lanes), 1)
    query_pos = me * tok + jnp.where(lane >= tok, lane - tok, lane)
    target[...] = jnp.where((key_pos >= start) & (key_pos <= query_pos), 0.0, floor_score)


def pair_stack(rows):
    lane = lax.broadcasted_iota(jnp.int32, rows.shape, 1)
    zero = jnp.zeros_like(rows)
    return jnp.concatenate([jnp.where(lane < HD, rows, zero), jnp.where(lane < HD, zero, rows)], axis=0)


def pair_join(transposed):
    both = transposed.T
    tok = both.shape[0] // 2
    lane = lax.broadcasted_iota(jnp.int32, (tok, 2 * HD), 1)
    return jnp.where(lane < HD, both[:tok], both[tok:])


def prep_kernel(
    tokens, segs, qkv, out, up, down, gains, shifts, biases, up_bias,
    t_out, q_out, f_out, fu_out, fd_out,
    scratch, wide, held_g, held_s, held_b, ids, line, sems,
):
    x, c, _y, _z = place()
    tok, width = tokens.shape[1:]
    rows = qkv.shape[0]
    half, side = rows // 2, width // 2
    p = 2 * x + c
    at = pl.ds(pl.multiple_of(half * c, 16), half)
    copies, others = Copies(sems), Copies(sems, 5)
    for source, target in ((gains, held_g), (shifts, held_s), (biases, held_b)):
        copies.add(source, target)
    copies.add(segs, ids)
    copies.add(up_bias, line)
    others.add(up, wide)
    wide_cols = 3 * side
    others.add(
        qkv.at[at, pl.ds(pl.multiple_of(wide_cols * x, 128), wide_cols)],
        q_out.at[pl.ds(0, half), pl.ds(0, wide_cols)],
    )
    others.add(
        out.at[at, pl.ds(pl.multiple_of(side * x, 128), side)],
        q_out.at[pl.ds(0, half), pl.ds(wide_cols, side)],
    )
    others.add(tokens.at[0], t_out.at[pl.ds(0, tok), :])
    own_rows = down.at[pl.ds(pl.multiple_of(rows * p, 16), rows), :]
    others.add(own_rows, f_out.at[pl.ds(rows, rows), :])
    others.add(own_rows, fd_out)
    copies.wait()
    scratch[...] = jnp.zeros_like(scratch)
    for first, held in ((0, held_g), (2, held_s), (4, held_b)):
        scratch[pl.ds(first, held.shape[0]), pl.ds(0, rows)] = f32(held[...])
    parts = unpack96(jnp.broadcast_to(f32(line[...]).reshape(1, line.shape[0]), (8, line.shape[0])))
    lane = lax.broadcasted_iota(jnp.int32, (8, 128), 1)
    row = lax.broadcasted_iota(jnp.int32, (8, 128), 0)
    ups = jnp.zeros((8, 128), jnp.float32)
    for number in range(4):
        ups = jnp.where((row == number) & (lane < rows), parts[number], ups)
    smalls = b16(jnp.concatenate([scratch[:, pl.ds(0, 128)], ups], axis=0))
    q_out[pl.ds(0, 16), pl.ds(2 * width, 128)] = smalls
    q_out[pl.ds(16, half - 16), pl.ds(2 * width, 128)] = jnp.zeros((half - 16, 128), jnp.bfloat16)
    scratch[...] = jnp.zeros_like(scratch)
    scratch[pl.ds(0, 1), pl.ds(0, tok)] = f32(ids[...])
    t_out[pl.ds(tok, 8), :] = b16(scratch[...])
    others.wait()
    for group in range(2):
        parts = []
        for shard in range(4 * group, 4 * group + 4):
            parts.append(choose(unpack96(f32(wide[:, pl.ds(384 * shard, 384)])), p))
        packed = b16(pack96(parts))
        f_out[pl.ds(0, rows), pl.ds(384 * group, 384)] = packed
        fu_out[:, pl.ds(384 * group, 384)] = packed


def front_kernel(
    seg, xo, x1, x2, x3, x4, first, own, own_o,
    g0, g1, g2, g3, g4, g5, g6, g7, g8, g9, g10, g11,
    q_out, kv_out, h_out, a_out, lse_out, start_out, vec_out, upb_out, wo_out, r_out, h2_out,
    full, small, bias, sems, vsems,
):
    x, c, y, z = place()
    me = 2 * z + y
    p = 2 * x + c
    tok, width = q_out.shape
    copies, vcopies = Copies(sems), Copies(vsems)
    vcopies.add(first.at[pl.ds(0, 16), pl.ds(2 * width, 128)], small.at[me])
    for number in range(7):
        source = piece_of((g0, g1, g2), number)
        vcopies.add(source.at[pl.ds(0, 16), pl.ds(2 * width, 128)], small.at[piece_shard(number, y, z)])
    groups = ((g0, g1, g2), (g3, g4, g5), (g6, g7, g8), (g9, g10, g11))
    fetch_qkv(copies, own, groups, full, wo_out, own_o)
    blocks = (xo, x1, x2, x3, x4)
    lane1 = lax.broadcasted_iota(jnp.int32, (1, tok), 1)
    start = jnp.full(seg.shape, 1 << 30, jnp.int32)
    for number in range(4):
        first_pos = jnp.full((1, 1), 1 << 30, jnp.int32)
        for back in range(5):
            ids = f32(blocks[back][pl.ds(tok, 8), pl.ds(0, tok)])[:1]
            pos = (me - back) * tok + lane1
            hit = (ids == float(number)) & (pos >= 0)
            first_pos = jnp.minimum(
                first_pos, jnp.min(jnp.where(hit, pos, 1 << 30), axis=1, keepdims=True)
            )
        start = jnp.where(seg[...] == number, first_pos, start)
    start_out[...] = start
    mask_bias(start, me, tok, bias)
    vcopies.wait()
    for group in range(2):
        held = [f32(small[4 * group + k]) for k in range(4)]
        vec_out[:, pl.ds(384 * group, 384)] = pack96([block[:8] for block in held])
        upb_out[:, pl.ds(384 * group, 384)] = pack96(
            [choose([jnp.broadcast_to(block[k : k + 1], (8, 128)) for k in range(8, 12)], p) for block in held]
        )
    vec = vec_out[...]
    for back in range(5):
        hat, _rate = norm_parts(f32(blocks[back][pl.ds(0, tok), :]))
        h_out[pl.ds((4 - back) * tok, tok), :] = b16(hat * vec[0:1] + vec[2:3])
    copies.wait()
    q_out[...] = b16(dot_nn(h_out[pl.ds(4 * tok, tok), :], full[:, pl.ds(0, width)]) + vec[4:5])

    def project(number, carry):
        col = pl.multiple_of(number * 256, 256)
        shift = jnp.where(number >= width // 256, 1.0, 0.0)
        bias_at = lax.rem(number, width // 256)
        piece = vec_out[pl.ds(5, 1), pl.ds(pl.multiple_of(bias_at * 256, 256), 256)]
        kv_out[:, pl.ds(col, 256)] = b16(
            dot_nn(h_out[...], full[:, pl.ds(pl.multiple_of(width + col, 256), 256)]) + piece * shift
        )
        return carry

    lax.fori_loop(0, 2 * width // 256, project, 0)

    def pair(number, carry):
        col = pl.multiple_of(number * 128, 128)
        queries = pair_stack(q_out[:, pl.ds(col, 128)] * jnp.bfloat16(0.125))
        scores = dot_nt(kv_out[:, pl.ds(col, 128)], queries) + bias[...]
        top = jnp.max(scores, axis=0, keepdims=True)
        probs = jnp.exp(scores - top)
        total = jnp.sum(probs, axis=0, keepdims=True)
        mixed = dot_tn(kv_out[:, pl.ds(pl.multiple_of(width + col, 128), 128)], b16(probs))
        a_out[:, pl.ds(col, 128)] = b16(pair_join(mixed / total))
        lse_out[number] = top + jnp.log(total)
        return carry

    lax.fori_loop(0, width // 128, pair, 0)
    residual = f32(xo[pl.ds(0, tok), :]) + dot_nn(a_out[...], wo_out[...]) + vec[6:7]
    r_out[...] = residual
    hat, _rate = norm_parts(residual)
    h2_out[...] = b16(hat * vec[1:2] + vec[3:4])


def feed_tokens(h2, dy, w_up, w_down, upb, act_out, du_out):
    root = math.sqrt(2.0 / math.pi)
    chunk = 256

    def feed(number, carry):
        col = pl.multiple_of(number * chunk, chunk)
        pre = dot_nn(h2[...], w_up[:, pl.ds(col, chunk)]) + upb[pl.ds(0, 1), pl.ds(col, chunk)]
        square = pre * pre
        bend = jnp.tanh(root * pre * (1.0 + 0.044715 * square))
        act = b16(0.5 * pre * (1.0 + bend))
        slope = 0.5 * (1.0 + bend) + 0.5 * pre * (1.0 - bend * bend) * (
            root * (1.0 + 3.0 * 0.044715 * square)
        )
        low = b16(dot_nt(dy[...], w_down[pl.ds(col, chunk), :]) * slope)
        act_out[:, pl.ds(col, chunk)] = act
        du_out[:, pl.ds(col, chunk)] = low
        return carry

    lax.fori_loop(0, w_up.shape[1] // chunk, feed, 0, unroll=True)
    return dot_nt(du_out[...], w_up[...])


def assemble_kernel(own, z1, z2, z3u, z3d, y0, y13, wu_out, wd_out, sems):
    _x, _c, y, z = place()
    rows = own.shape[0] // 2
    copies = Copies(sems)
    pieces = [(own, 2 * z + y)]
    for number, ref in ((0, z1), (1, z2), (3, y0)):
        pieces.append((ref, piece_shard(number, y, z)))
    for number, first in ((4, 0), (6, 2 * rows)):
        pieces.append((y13.at[pl.ds(first, 2 * rows), :], piece_shard(number, y, z)))
    for ref, shard in pieces:
        at = pl.ds(pl.multiple_of(shard * rows, 16), rows)
        copies.add(ref.at[pl.ds(0, rows), :], wu_out.at[at, :])
        copies.add(ref.at[pl.ds(rows, rows), :], wd_out.at[at, :])
    at = pl.ds(pl.multiple_of(piece_shard(2, y, z) * rows, 16), rows)
    copies.add(z3u, wu_out.at[at, :])
    copies.add(z3d, wd_out.at[at, :])
    copies.wait()


def near_kernel(
    h_own, h_c, dy_own, dy_c, upb, y2, _wu, _wd,
    h2, dy, act_out, du_out, keep_out, send_out, wu_out, wd_out,
    sems,
):
    _x, _c, y, z = place()
    tok, width = h_own.shape
    rows = width // 8
    copies = Copies(sems)
    at = pl.ds(pl.multiple_of(piece_shard(5, y, z) * rows, 16), rows)
    copies.add(y2.at[pl.ds(0, rows), :], wu_out.at[at, :])
    copies.add(y2.at[pl.ds(rows, rows), :], wd_out.at[at, :])
    h2[pl.ds(0, tok), :] = h_own[...]
    h2[pl.ds(tok, tok), :] = h_c[...]
    dy[pl.ds(0, tok), :] = dy_own[...]
    dy[pl.ds(tok, tok), :] = dy_c[...]
    copies.wait()
    grad = feed_tokens(h2, dy, wu_out, wd_out, upb, act_out, du_out)
    keep_out[...] = grad[:tok]
    send_out[...] = b16(grad[tok:])


def far_c_kernel(
    h_xc, dy_xc, upb, w_up, w_down, h_near, dy_near, act_near, du_near,
    hs, dys, acts, dus, send_out,
    sems,
):
    tok = dy_xc.shape[0]
    copies = Copies(sems)
    for source, target in ((h_near, hs), (dy_near, dys), (act_near, acts), (du_near, dus)):
        copies.add(source, target.at[pl.ds(0, 2 * tok), :])
    last = pl.ds(3 * tok, tok)
    hs[last, :] = h_xc[...]
    dys[last, :] = dy_xc[...]
    send_out[...] = b16(
        feed_tokens(h_xc, dy_xc, w_up, w_down, upb, acts.at[last, :], dus.at[last, :])
    )
    copies.wait()


def far_x_kernel(
    h_x, dy_x, upb, w_up, w_down, _hs, _dys, _acts, _dus,
    hs, dys, acts, dus, keep_out,
):
    tok = dy_x.shape[0]
    third = pl.ds(2 * tok, tok)
    hs[third, :] = h_x[...]
    dys[third, :] = dy_x[...]
    keep_out[...] = feed_tokens(h_x, dy_x, w_up, w_down, upb, acts.at[third, :], dus.at[third, :])


def weights_kernel(
    hs, dys, acts, dus, w_down,
    u_out, d_out, upb_out, keep_out, send_out,
    stage, sems,
):
    _x, _c, y, z = place()
    width = hs.shape[1]
    rows = width // 8
    upb_out[...] = jnp.sum(f32(dus[...]), axis=0, keepdims=True)

    def weight(number, carry):
        col = pl.multiple_of(number * 256, 256)
        stage[0, pl.ds(col, 256), :] = b16(dot_tn(hs[:, pl.ds(col, 256)], dus[...]))
        stage[1, pl.ds(col, 256), :] = b16(dot_tn(acts[:, pl.ds(col, 256)], dys[...]))
        return carry

    lax.fori_loop(0, width // 256, weight, 0)
    outs = Copies(sems)
    for shard in range(8):
        zz = lax.rem(shard // 2 + 4 - z, 4)
        yy = jnp.where(y == shard % 2, 0, 1)
        outs.add(stage.at[0, pl.ds(shard * rows, rows), :], u_out.at[yy, zz])
        outs.add(stage.at[1, pl.ds(shard * rows, rows), :], d_out.at[yy, zz])
    tok = hs.shape[0] // 4
    for number in range(4):
        part = dot_nn(acts[pl.ds(number * tok, tok), :], w_down[...])
        if number % 2:
            send_out[number // 2] = b16(part)
        else:
            keep_out[number // 2] = part
    outs.wait()


def scatter(stage, other, mine, sems):
    x, c, y, z = place()
    outs = Copies(sems)
    for shard in range(8):
        zz = lax.rem(shard // 2 + 4 - z, 4)
        yy = jnp.where(y == shard % 2, 0, 1)
        for xx in range(2):
            far = jnp.where(x == xx, 0, 1)
            outs.add(stage.at[1 - c, xx, shard], other.at[far, yy, zz])
            outs.add(stage.at[c, xx, shard], mine.at[far, yy, zz])
    outs.wait()


def post_kernel(
    residual, own, near, across, dy_in, vec_in, w_out, a_in,
    dr_out, da_out, dw_out, vec_out,
):
    vec = vec_in[...]
    grad_hidden = own[...] + f32(near[...]) + f32(across[...])
    hat, rate = norm_parts(residual[...])
    dy = f32(dy_in[...])
    grad_first = dy + norm_back(grad_hidden, hat, rate, vec[1:2])
    dr_out[...] = grad_first
    low = b16(grad_first)
    da_out[...] = b16(dot_nt(low, w_out[...]))
    dw_out[...] = dot_tn(a_in[...], low)
    zero = jnp.zeros((1, dy.shape[1]), jnp.float32)
    vec_out[...] = jnp.concatenate(
        [
            zero,
            jnp.sum(grad_hidden * hat, axis=0, keepdims=True),
            zero,
            jnp.sum(grad_hidden, axis=0, keepdims=True),
            zero,
            zero,
            jnp.sum(grad_first, axis=0, keepdims=True),
            jnp.sum(dy, axis=0, keepdims=True),
        ],
        axis=0,
    )


def back_pairs(first, q_in, kv_in, lse_in, da_in, bias, dq, dkv):
    width = q_in.shape[1]

    def pair(number, carry):
        col = pl.multiple_of((first + number) * 128, 128)
        vcol = pl.multiple_of(width + col, 128)
        to = pl.multiple_of(number * 128, 128)
        queries = pair_stack(q_in[:, pl.ds(col, 128)] * jnp.bfloat16(0.125))
        grads = pair_stack(da_in[:, pl.ds(col, 128)])
        keys = kv_in[:, pl.ds(col, 128)]
        probs = jnp.exp(dot_nt(keys, queries) + bias[...] - lse_in[first + number])
        dkv[:, pl.ds(pl.multiple_of(width // 2 + to, 128), 128)] = b16(dot_nn(b16(probs), grads))
        term = probs * dot_nt(kv_in[:, pl.ds(vcol, 128)], grads)
        low = b16(term - probs * jnp.sum(term, axis=0, keepdims=True))
        dkv[:, pl.ds(to, 128)] = b16(dot_nn(low, queries))
        dq[:, pl.ds(to, 128)] = b16(pair_join(dot_tn(keys, low)) * 0.125)
        return carry

    lax.fori_loop(0, 3, pair, 0, unroll=first == 0)


def qkv_weight(h_in, dq, dkv, stage, tail):
    tok, part = dq.shape
    keys = h_in.shape[0]

    def weight(number, carry):
        col = pl.multiple_of(number * 384, 384)
        key = dot_tn(h_in[:, pl.ds(col, 384)], dkv[...])
        query = dot_tn(h_in[pl.ds(keys - tok, tok), pl.ds(col, 384)], dq[...])
        for shard in range(4):
            for cc in range(2):
                for xx in range(2):
                    rows = slice(96 * shard + 48 * cc + 24 * xx, 96 * shard + 48 * cc + 24 * xx + 24)
                    blocks = [query[rows], key[rows, :part], key[rows, part:]] + tail(4 * number + shard, 48 * cc + 24 * xx)
                    stage[cc, xx, 4 * number + shard] = b16(jnp.concatenate(blocks, axis=0))
        return carry

    lax.fori_loop(0, 2, weight, 0)


def back_a_kernel(
    start_in, q_in, kv_in, h_in, lse_in, da_in, dw_in,
    other, mine, dq_out, dkv_out,
    bias, stage, sems,
):
    _x, _c, y, z = place()
    mask_bias(start_in[...], 2 * z + y, q_in.shape[0], bias)
    back_pairs(0, q_in, kv_in, lse_in, da_in, bias, dq_out, dkv_out)
    side = q_in.shape[1] // 2

    def out_rows(shard, row):
        rows = dw_in[pl.ds(pl.multiple_of(96 * shard + row, 8), 24), :]
        return [rows[:, :side], rows[:, side:]]

    qkv_weight(h_in, dq_out, dkv_out, stage, out_rows)
    scatter(stage, other, mine, sems)


def back_b_kernel(
    start_in, q_in, kv_in, lse_in, da_in, vec_in, upb_in, dq_a, dkv_a, xo, x1, x2, x3, x4,
    own, g0, g1, g2, g3, g4, g5, g6, g7, g8, g9, g10, g11,
    dq_out, dkv_out, p_own, p_y, p_z, sums_out,
    full, bias, sems,
):
    x, c, y, z = place()
    p = 2 * x + c
    tok, width = q_in.shape
    side = width // 2
    copies = Copies(sems)
    groups = ((g0, g1, g2), (g3, g4, g5), (g6, g7, g8), (g9, g10, g11))
    fetch_qkv(copies, own, groups, full)
    mask_bias(start_in[...], 2 * z + y, tok, bias)
    back_pairs(3, q_in, kv_in, lse_in, da_in, bias, dq_out, dkv_out)
    copies.wait()
    gain_sum = jnp.zeros((1, width), jnp.float32)
    shift_sum = jnp.zeros((1, width), jnp.float32)
    for back, block in enumerate((xo, x1, x2, x3, x4)):
        rows = pl.ds((4 - back) * tok, tok)
        grad = jnp.zeros((tok, width), jnp.float32)
        for number, (dq, dkv) in enumerate(((dq_a, dkv_a), (dq_out, dkv_out))):
            at = number * side
            grad = grad + dot_nt(dkv[rows, pl.ds(0, side)], full[:, pl.ds(width + at, side)])
            grad = grad + dot_nt(dkv[rows, pl.ds(side, side)], full[:, pl.ds(2 * width + at, side)])
            if back == 0:
                grad = grad + dot_nt(dq[...], full[:, pl.ds(at, side)])
        if back == 0:
            p_own[...] = grad
        elif back in (1, 3):
            p_y[back // 2] = b16(grad)
        else:
            p_z[back // 2 - 1] = b16(grad)
        hat, _rate = norm_parts(f32(block[pl.ds(0, tok), :]))
        gain_sum = gain_sum + jnp.sum(grad * hat, axis=0, keepdims=True)
        shift_sum = shift_sum + jnp.sum(grad, axis=0, keepdims=True)
    zero = jnp.zeros((1, width), jnp.float32)
    bias_q = jnp.concatenate([jnp.sum(f32(d[...]), axis=0, keepdims=True) for d in (dq_a, dq_out)], axis=1)
    bias_v = jnp.concatenate(
        [jnp.sum(f32(d[:, pl.ds(side, side)]), axis=0, keepdims=True) for d in (dkv_a, dkv_out)], axis=1
    )
    vec = vec_in[...] + jnp.concatenate(
        [gain_sum, zero, shift_sum, zero, bias_q, bias_v, zero, zero], axis=0
    )
    lane = lax.broadcasted_iota(jnp.int32, (8, 128), 1)
    line = lax.broadcasted_iota(jnp.int32, (8, 128), 0)
    for group in range(2):
        cols = pl.ds(384 * group, 384)
        vec_parts = unpack96(vec[:, 384 * group : 384 * group + 384])
        upb_parts = unpack96(jnp.broadcast_to(upb_in[:, cols], (8, 384)))
        for k in range(4):
            sums_out[4 * group + k] = jnp.concatenate(
                [
                    jnp.where(lane < 96, vec_parts[k], 0.0),
                    jnp.where((lane < 96) & (line == p), upb_parts[k], 0.0),
                ],
                axis=1,
            )


def back_c_kernel(h_in, dq, dkv, sums_in, other, mine, stage, sems):
    blank = jnp.zeros((8, 128), jnp.float32)
    qkv_weight(
        h_in, dq, dkv, stage, lambda shard, _row: [jnp.concatenate([sums_in[shard], blank], axis=1)]
    )
    scatter(stage, other, mine, sems)


def tokens_kernel(own, near, dr, xo, vec_in, grad_out):
    tok = own.shape[0]
    hat, rate = norm_parts(f32(xo[pl.ds(0, tok), :]))
    grad = own[...] + f32(near[...])
    grad_out[...] = dr[...] + norm_back(grad, hat, rate, vec_in[0:1, :])


def finish_f_kernel(f0, fx, fc, fcx, up, down, held):
    x, c, _y, _z = place()
    rows = f0.shape[0] // 2
    for (xx, cc), f in zip(corners(x, c), (f0, fx, fc, fcx), strict=True):
        p = 2 * xx + cc
        held[p] = f[pl.ds(0, rows), :]
        down[pl.ds(pl.multiple_of(rows * p, 16), rows), :] = f32(f[pl.ds(rows, rows), :])
    for group in range(2):
        parts = [unpack96(f32(held[k, :, pl.ds(384 * group, 384)])) for k in range(4)]
        for shard in range(4):
            up[:, pl.ds(384 * (4 * group + shard), 384)] = pack96([part[shard] for part in parts])


def finish_q_kernel(f0, fx, fc, fcx, qkv, out, gains, shifts, biases, up_bias):
    x, c, _y, _z = place()
    side = out.shape[1] // 2
    for (xx, cc), piece in zip(corners(x, c), (f0, fx, fc, fcx), strict=True):
        rows = pl.ds(pl.multiple_of(48 * cc + 24 * xx, 8), 24)
        blocks = f32(piece[...])
        for number in range(3):
            first, second = 24 * number, 24 * (number + 5)
            qkv[rows, pl.ds(2 * side * number, side)] = blocks[first : first + 24]
            qkv[rows, pl.ds(2 * side * number + side, side)] = blocks[second : second + 24]
        out[rows, pl.ds(0, side)] = blocks[72:96]
        out[rows, pl.ds(side, side)] = blocks[96:120]
    sums = f32(f0[...])[192:]
    part = gains.shape[1]
    gains[...] = sums[0:2, :part]
    shifts[...] = sums[2:4, :part]
    biases[...] = sums[4:8, :part]
    ups = sums[:, 128:256]
    packed = pack96([jnp.broadcast_to(ups[k : k + 1], (8, 128)) for k in range(4)])
    up_bias[...] = packed[0]


HB = pl.BlockSpec(memory_space=pltpu.HBM)
VM = pl.BlockSpec(memory_space=pltpu.VMEM)
AN = pl.BlockSpec(memory_space=pl.ANY)


def shape_of(shape, dtype):
    return jax.ShapeDtypeStruct(shape, dtype)


def call(kernel, ins, outs, out_shape, scratch=(), vmem=40, flops=0, moved=0, aliases=None):
    return pl.pallas_call(
        kernel,
        in_specs=ins,
        out_specs=outs,
        out_shape=out_shape,
        scratch_shapes=list(scratch),
        input_output_aliases=aliases or {},
        compiler_params=pltpu.CompilerParams(vmem_limit_bytes=vmem << 20),
        cost_estimate=pl.CostEstimate(flops=flops, bytes_accessed=moved, transcendentals=0),
    )


def fence(*values):
    return lax.optimization_barrier(values)


def swap_rep(value, bit):
    return lax.ppermute(value, "rep", [(k, k ^ bit) for k in range(4)])


def to_core(value):
    return swap_rep(value, 1)


def to_x(value):
    return swap_rep(value, 2)


def to_y(value):
    return lax.ppermute(value, "seq", [(k, k ^ 1) for k in range(8)])


def to_z(value, steps):
    return lax.ppermute(value, "seq", [(k, (k + 2 * steps) % 8) for k in range(8)])


def join(*parts):
    return jnp.concatenate(parts, axis=0)


def on_device_fast(
    tokens,
    segment_ids,
    query_key_value_weight,
    output_weight,
    up_weight,
    down_weight,
    ln_gains,
    ln_biases,
    biases,
    up_projection_bias,
    cotangent,
):
    seq = lax.axis_index("seq")
    y = seq % 2
    tok, width = tokens.shape[1:]
    hidden = up_weight.shape[1]
    keys = 5 * tok
    bf, fl = jnp.bfloat16, jnp.float32
    dma = pltpu.SemaphoreType.DMA
    grad_y = cotangent[0]
    own_tokens, piece_q, piece_f, piece_u, piece_d = call(
        prep_kernel,
        [HB] * 10,
        [VM] * 5,
        [
            shape_of((tok + 8, width), bf),
            shape_of((48, 2 * width + 128), bf),
            shape_of((192, width), bf),
            shape_of((96, width), bf),
            shape_of((96, width), bf),
        ],
        [
            pltpu.VMEM((8, width), fl),
            pltpu.VMEM((96, hidden), bf),
            pltpu.VMEM((2, 96), bf),
            pltpu.VMEM((2, 96), bf),
            pltpu.VMEM((4, 96), bf),
            pltpu.VMEM((1, tok), jnp.int32),
            pltpu.VMEM((384,), bf),
            dma((11,)),
        ],
        vmem=60, moved=4 * 10**6,
    )(
        tokens, segment_ids, query_key_value_weight, output_weight, up_weight, down_weight,
        ln_gains, ln_biases, biases, up_projection_bias,
    )

    q1, q3, q_y0, dy_x = fence(to_z(piece_q, 1), to_z(piece_q, 3), to_y(piece_q), to_x(grad_y))
    own_tokens, piece_f, q1, q_y0 = fence(own_tokens, piece_f, q1, q_y0, q3, dy_x)[:4]
    q2, x2, q_xy0, f_y0 = fence(to_z(q1, 1), to_z(own_tokens, 1), to_x(q_y0), to_y(piece_f))
    q_z = join(q1, q2, q3)
    q_z, x2, piece_d = fence(q_z, x2, piece_d, q_xy0, f_y0)[:3]
    q_y, q_xz, x4, f3d = fence(to_y(q_z), to_x(q_z), to_z(x2, 1), to_z(piece_d, 3))
    near = jnp.where(y == 0, own_tokens, x2)
    far = jnp.where(y == 0, x2, x4)
    near_far, q_y, piece_f, piece_u = fence(
        jnp.stack([near, far]), q_y, piece_f, piece_u, q_xz, f3d
    )[:4]
    crossed, q_xy, f1, f3u = fence(to_y(near_far), to_x(q_y), to_z(piece_f, 1), to_z(piece_u, 3))
    x1, x3 = crossed[0], crossed[1]
    q_z, q_y0, q_y, q_xz, q_xy0, q_xy = fence(q_z, q_y0, q_y, q_xz, q_xy0, q_xy, f1, f3u, crossed)[:6]
    q_cz, q_cy0, q_cy, q_cxz, q_cxy0, q_cxy = fence(
        *(to_core(v) for v in (q_z, q_y0, q_y, q_xz, q_xy0, q_xy))
    )
    f_13, f_1, q_cz = fence(join(f1, f3u, f3d), f1, q_cz, q_cy0, q_cy, q_cxz, q_cxy0, q_cxy)[:3]
    f_y13, f2 = to_y(f_13), to_z(f_1, 1)
    dy_c, dy_xc = to_core(grad_y), to_core(dy_x)

    def pieces(value):
        return value.reshape(value.shape[0] // 48, 48, value.shape[1])

    got_q = [
        pieces(v)
        for v in (q_z, q_y0, q_y, q_xz, q_xy0, q_xy, q_cz, q_cy0, q_cy, q_cxz, q_cxy0, q_cxy)
    ]
    seg = jnp.concatenate([segment_ids, segment_ids], axis=1)
    front = call(
        front_kernel,
        [VM] * 6 + [AN] * 15,
        [VM] * 11,
        [
            shape_of((tok, width), bf),
            shape_of((keys, 2 * width), bf),
            shape_of((keys, width), bf),
            shape_of((tok, width), bf),
            shape_of((width // 128, 1, 2 * tok), fl),
            shape_of((1, 2 * tok), jnp.int32),
            shape_of((8, width), fl),
            shape_of((8, width), fl),
            shape_of((width, width), bf),
            shape_of((tok, width), fl),
            shape_of((tok, width), bf),
        ],
        [
            pltpu.VMEM((width, 3 * width), bf),
            pltpu.VMEM((8, 16, 128), bf),
            pltpu.VMEM((keys, 2 * tok), fl),
            dma((2 + 56,)),
            dma((8,)),
        ],
        flops=7 * 10**9,
        vmem=16, moved=12 * 10**6,
    )(
        seg, own_tokens, x1, x2, x3, x4, piece_q, query_key_value_weight, output_weight, *got_q,
    )
    *front, f_y13, f2, dy_c, dy_xc = fence(*front, f_y13, f2, dy_c, dy_xc)
    queries, kv, normed, attended, lse, start, vec, upb, w_out, residual, hidden_2 = front
    w_half = call(
        assemble_kernel,
        [AN] * 7,
        [VM] * 2,
        [shape_of((width, width), bf)] * 2,
        [dma((14,))],
        vmem=4,
        moved=5 * 10**6,
    )(piece_f, f1, f2, f3u, f3d, f_y0, f_y13)
    h_x, h_c, f_y2, *w_half = fence(to_x(hidden_2), to_core(hidden_2), to_y(f2), *w_half)
    act = shape_of((2 * tok, width), bf)
    acts = shape_of((4 * tok, width), bf)
    feed_shapes = [shape_of((tok, width), fl), shape_of((tok, width), bf)]
    *near_acts, keep_a, send_a, w_up, w_down = call(
        near_kernel,
        [VM] * 5 + [AN] + [VM] * 2,
        [VM] * 8,
        [act] * 4 + feed_shapes + [shape_of((width, width), bf)] * 2,
        [dma((2,))],
        flops=3 * 10**9,
        vmem=8,
        moved=6 * 10**6,
        aliases={6: 6, 7: 7},
    )(hidden_2, h_c, grad_y, dy_c, upb, f_y2, *w_half)
    h_xc = to_core(h_x)
    keep_a, send_a, h_xc, w_up = fence(keep_a, send_a, h_xc, w_up)
    came_a = to_core(send_a)
    *all_acts, send_b = call(
        far_c_kernel,
        [VM] * 5 + [AN] * 4,
        [VM] * 5,
        [acts] * 4 + feed_shapes[1:],
        [dma((4,))],
        flops=15 * 10**8,
        vmem=8,
        moved=6 * 10**6,
    )(h_xc, dy_xc, upb, w_up, w_down, *near_acts)
    send_b, came_a, h_x = fence(send_b, came_a, h_x)
    came_b = to_core(send_b)
    *all_acts, keep_b = call(
        far_x_kernel,
        [VM] * 9,
        [VM] * 5,
        [acts] * 4 + feed_shapes[:1],
        flops=3 * 10**9,
        vmem=8,
        moved=6 * 10**6,
        aliases={5: 0, 6: 1, 7: 2, 8: 3},
    )(h_x, dy_x, upb, w_up, w_down, *all_acts)
    keep_b, came_b, *all_acts = fence(keep_b, came_b, *all_acts)
    back_x = to_x(b16(keep_b + f32(came_b)))
    u_terms, d_terms, upb_g, y_keep, y_send = call(
        weights_kernel,
        [VM] * 5,
        [AN, AN] + [VM] * 3,
        [
            shape_of((2, 4, 96, width), bf),
            shape_of((2, 4, 96, width), bf),
            shape_of((1, width), fl),
            shape_of((2, tok, width), fl),
            shape_of((2, tok, width), bf),
        ],
        [pltpu.VMEM((2, width, width), bf), dma((16,))],
        flops=3 * 10**9,
        vmem=12,
        moved=6 * 10**6,
    )(*all_acts, w_down)
    back_x, u_terms, d_terms, y_send = fence(back_x, u_terms, d_terms, y_send)
    u_came = to_y(u_terms[1])
    came_y = to_core(y_send)
    grad_first, grad_attended, dw_out, vec_g = call(
        post_kernel,
        [VM] * 8,
        [VM] * 4,
        [
            shape_of((tok, width), fl),
            shape_of((tok, width), bf),
            shape_of((width, width), fl),
            shape_of((8, width), fl),
        ],
        vmem=12,
        flops=10**9,
        moved=4 * 10**6,
    )(residual, keep_a, came_a, back_x, grad_y, vec, w_out, attended)
    back_scratch = [
        pltpu.VMEM((keys, 2 * tok), fl),
    ]
    qa_other, qa_mine, dq_a, dkv_a = call(
        back_a_kernel,
        [VM] * 7,
        [AN] * 2 + [VM] * 2,
        [
            shape_of((2, 2, 4, 120, width // 2), bf),
            shape_of((2, 2, 4, 120, width // 2), bf),
            shape_of((tok, width // 2), bf),
            shape_of((keys, width), bf),
        ],
        back_scratch + [pltpu.VMEM((2, 2, 8, 120, width // 2), bf), dma((32,))],
        flops=5 * 10**9,
        vmem=16, moved=10 * 10**6,
    )(start, queries, kv, normed, lse, grad_attended, dw_out)

    def both(mine, came):
        return lambda *index: f32(mine[index]) + f32(came[index])

    def z_sum(part, *came):
        return b16(part(0) + sum(f32(v) for v in came))

    dq_a, qa_other, u_came, came_y, d_send = fence(
        dq_a, qa_other, u_came, came_y, d_terms[1]
    )
    d_came, qa_came = to_y(d_send), to_core(qa_other)
    u_part = both(u_terms[0], u_came)
    u_z = [to_z(b16(u_part(step)), step) for step in (1, 2, 3)]
    dq_b, dkv_b, p_own, p_y, p_z, sums = call(
        back_b_kernel,
        [VM] * 14 + [AN] * 13,
        [VM] * 6,
        [
            shape_of((tok, width // 2), bf),
            shape_of((keys, width), bf),
            shape_of((tok, width), fl),
            shape_of((2, tok, width), bf),
            shape_of((2, tok, width), bf),
            shape_of((8, 8, 256), fl),
        ],
        [pltpu.VMEM((width, 3 * width), bf)] + back_scratch + [dma((1 + 28,))],
        flops=6 * 10**9,
        vmem=20, moved=10 * 10**6,
    )(
        start, queries, kv, lse, grad_attended, vec_g, upb_g, dq_a, dkv_a,
        own_tokens, x1, x2, x3, x4, query_key_value_weight, *got_q,
    )
    dq_b, qa_came, d_came, p_y, *u_z = fence(dq_b, qa_came, d_came, p_y, *u_z)
    p_came = to_y(p_y)
    qa_1 = both(qa_mine, qa_came)
    qa_x = to_x(b16(qa_1(1)))
    d_part = both(d_terms[0], d_came)
    d_z2 = to_z(b16(d_part(2)), 1)
    qb_other, qb_mine = call(
        back_c_kernel,
        [VM] * 4,
        [AN] * 2,
        [
            shape_of((2, 2, 4, 80, width // 2), bf),
            shape_of((2, 2, 4, 80, width // 2), bf),
        ],
        [pltpu.VMEM((2, 2, 8, 80, width // 2), bf), dma((32,))],
        flops=3 * 10**9,
        vmem=12, moved=6 * 10**6,
    )(normed, dq_b, dkv_b, sums)
    qb_came = [to_core(qb_other[k]) for k in range(2)]
    *qb_came, qa_x, p_came, d_z2 = fence(*qb_came, qa_x, p_came, d_z2)
    even = y == 0
    sum_own = p_own + jnp.where(even, f32(p_came[0]), 0.0)
    sum_4 = b16(f32(p_z[1]) + jnp.where(even, 0.0, f32(p_came[1])))
    sum_2 = f32(p_z[0]) + jnp.where(even, f32(p_came[1]), f32(p_came[0]))
    def qa_2(*index):
        return qa_1(0, *index) + f32(qa_x[index])

    def qb_1(side, *index):
        return f32(qb_mine[(side,) + index]) + f32(qb_came[side][index])

    qb_x, qa_y, hop, d_z1, d_z3 = fence(
        to_x(b16(qb_1(1))),
        to_y(b16(qa_2(1))),
        to_z(sum_4, 3),
        to_z(b16(d_part(1) + f32(d_z2)), 1),
        to_z(b16(d_part(3)), 3),
    )

    def qb_2(*index):
        return qb_1(0, *index) + f32(qb_x[index])

    f_tot = join(z_sum(u_part, *u_z), z_sum(d_part, d_z1, d_z3))
    fy_tot = join(f_tot, b16(y_keep[1] + f32(came_y[1])))
    qb_y, back_2, f_tot, fy_tot = fence(
        to_y(b16(qb_2(1))), to_z(b16(sum_2 + f32(hop)), 3), f_tot, fy_tot
    )

    def q_3(*index):
        first = qa_2(0, *index) + f32(qa_y[index])
        return jnp.concatenate([first, qb_2(0, *index) + f32(qb_y[index])], axis=-2)

    grad_tokens = call(
        tokens_kernel, [VM] * 5, VM, shape_of((tok, width), fl), vmem=4, moved=3 * 10**6
    )(sum_own, back_2, grad_first, own_tokens, vec)
    *q_z, over_x, f_tot = fence(*(to_z(b16(q_3(step)), step) for step in (1, 2, 3)), to_x(fy_tot), f_tot)
    f_x, back_y = over_x[:tok], over_x[tok:]
    q_sum = z_sum(q_3, *q_z)
    q_fx, q_fc = to_x(q_sum), to_core(q_sum)
    grad_up, grad_down = call(
        finish_f_kernel,
        [VM] * 4,
        [VM] * 2,
        [shape_of(up_weight.shape, fl), shape_of(down_weight.shape, fl)],
        [pltpu.VMEM((4, 96, width), bf)],
        vmem=8,
        moved=4 * 10**6,
    )(f_tot, f_x, to_core(f_tot), to_core(f_x))
    q_fx, q_fc, grad_up, grad_down = fence(q_fx, q_fc, grad_up, grad_down)
    q_fxc = to_core(q_fx)
    result = b16(residual + vec[7:8] + y_keep[0] + f32(came_y[0]) + f32(back_y))
    grad_qkv, grad_out, grad_gains, grad_shifts, grad_biases, grad_up_bias = call(
        finish_q_kernel,
        [VM] * 4,
        [VM] * 6,
        [
            shape_of(query_key_value_weight.shape, fl),
            shape_of(output_weight.shape, fl),
            shape_of(ln_gains.shape, fl),
            shape_of(ln_biases.shape, fl),
            shape_of(biases.shape, fl),
            shape_of(up_projection_bias.shape, fl),
        ],
        vmem=8,
        moved=3 * 10**6,
    )(q_sum, q_fx, q_fc, q_fxc)
    return (
        result[None],
        grad_tokens[None],
        grad_qkv,
        grad_out,
        grad_up,
        grad_down,
        grad_gains,
        grad_shifts,
        grad_biases,
        grad_up_bias,
    )


def solution(mesh):
    placed = (
        P("rep", "seq", None),
        P("rep", "seq"),
        P("seq", None),
        P("seq", None),
        P("seq", None),
        P("seq", None),
        P(None, "seq"),
        P(None, "seq"),
        P(None, "seq"),
        P("seq"),
        P("rep", "seq", None),
    )
    shape = dict(mesh.shape)
    small_slice = shape["rep"] == 4 and shape["seq"] == 8
    return jax.shard_map(
        on_device_fast if small_slice else on_device,
        mesh=mesh,
        in_specs=placed,
        out_specs=(
            P("rep", "seq", None),
            P("rep", "seq", None),
            P("seq", None),
            P("seq", None),
            P("seq", None),
            P("seq", None),
            P(None, "seq"),
            P(None, "seq"),
            P(None, "seq"),
            P("seq"),
        ),
        check_vma=False,
    )
```

```python
import math

import jax
import jax.numpy as jnp
from jax import lax
from jax.experimental import pallas as pl
from jax.experimental.pallas import tpu as pltpu
from jax.sharding import PartitionSpec as P

HEADS = 12
HD = 64


norm_eps = 1e-05
floor_score = -1e30


def layer_norm(values, gain, shift):
    center = values - jnp.mean(values, axis=-1, keepdims=True)
    spread = jnp.mean(center * center, axis=-1, keepdims=True)
    return center * lax.rsqrt(spread + norm_eps) * gain + shift


def head_split(matrix):
    return matrix.reshape(matrix.shape[0], HEADS, HD)


def masked_scores(queries, query_seg, query_pos, key_piece, seg_piece, offset):
    rows = key_piece.shape[0]
    scores = jnp.einsum(
        "qhd,khd->hqk", queries, head_split(key_piece), preferred_element_type=jnp.float32
    ) * HD ** (-0.5)
    key_pos = offset + jnp.arange(rows, dtype=jnp.int32)
    allowed = (query_seg[:, None] == seg_piece[None, :]) & (key_pos[None, :] <= query_pos[:, None])
    return (jnp.where(allowed[None], scores, floor_score), allowed)


def forward_block(running, pieces, offset, queries, query_seg, query_pos):
    top_run, total_run, accum = running
    key_piece, value_piece, seg_piece = pieces
    scores, allowed = masked_scores(queries, query_seg, query_pos, key_piece, seg_piece, offset)
    top_new = jnp.maximum(top_run, jnp.max(scores, axis=-1))
    probs = jnp.where(allowed[None], jnp.exp(scores - top_new[:, :, None]), 0.0)
    factor = jnp.exp(top_run - top_new)
    total_new = total_run * factor + jnp.sum(probs, axis=-1)
    update = jnp.einsum(
        "hqk,khd->qhd",
        probs.astype(jnp.bfloat16),
        head_split(value_piece),
        preferred_element_type=jnp.float32,
    )
    return (top_new, total_new, accum * factor.T[:, :, None] + update)


def in_blocks(block_fn, running, pieces):
    rows = pieces[0].shape[0]
    size = math.gcd(rows, 1024)
    stacked = tuple((member.reshape((rows // size, size) + member.shape[1:]) for member in pieces))
    offsets = jnp.arange(rows // size, dtype=jnp.int32) * size

    def scan_step(state_now, element):
        return (block_fn(state_now, element[0], element[1]), None)

    running, _unused = lax.scan(scan_step, running, (stacked, offsets))
    return running


def backward_block(
    number,
    state_now,
    whole,
    queries,
    query_seg,
    query_pos,
    grad_heads,
    log_total,
    delta,
    block_rows,
):
    grad_query, term = state_now
    offset = number * block_rows
    key_piece = lax.dynamic_slice_in_dim(whole[0], offset, block_rows, 0)
    value_piece = lax.dynamic_slice_in_dim(whole[1], offset, block_rows, 0)
    seg_piece = lax.dynamic_slice_in_dim(whole[2], offset, block_rows, 0)
    scores, allowed = masked_scores(queries, query_seg, query_pos, key_piece, seg_piece, offset)
    probs = jnp.where(allowed[None], jnp.exp(scores - log_total[:, :, None]), 0.0)
    grad_probs = jnp.einsum(
        "qhd,khd->hqk", grad_heads, head_split(value_piece), preferred_element_type=jnp.float32
    )
    grad_scores = (probs * (grad_probs - delta[:, :, None])).astype(jnp.bfloat16)
    grad_query = grad_query + jnp.einsum(
        "hqk,khd->qhd", grad_scores, head_split(key_piece), preferred_element_type=jnp.float32
    )
    grad_key = jnp.einsum(
        "hqk,qhd->khd", grad_scores, queries, preferred_element_type=jnp.float32
    ) * HD ** (-0.5)
    grad_value = jnp.einsum(
        "hqk,qhd->khd", probs.astype(jnp.bfloat16), grad_heads, preferred_element_type=jnp.float32
    )
    joined = jnp.concatenate(
        [grad_key.reshape(block_rows, -1), grad_value.reshape(block_rows, -1)], axis=1
    )
    term = lax.dynamic_update_slice_in_dim(term, joined, offset, 0)
    return (grad_query, term)


def on_device(
    tokens,
    segment_ids,
    query_key_value_weight,
    output_weight,
    up_weight,
    down_weight,
    ln_gains,
    ln_biases,
    biases,
    up_projection_bias,
    cotangent,
):
    gathered = (
        lax.all_gather(query_key_value_weight, "seq", axis=0, tiled=True),
        lax.all_gather(output_weight, "seq", axis=0, tiled=True),
        lax.all_gather(up_weight, "seq", axis=0, tiled=True),
        lax.all_gather(down_weight, "seq", axis=0, tiled=True),
        lax.all_gather(ln_gains, "seq", axis=1, tiled=True),
        lax.all_gather(ln_biases, "seq", axis=1, tiled=True),
        lax.all_gather(biases, "seq", axis=1, tiled=True),
        lax.all_gather(up_projection_bias, "seq", axis=0, tiled=True),
    )
    full_qkv, full_out, full_up, full_down, gains_all, shifts_all, biases_all, up_shift = gathered
    gains_f = gains_all.astype(jnp.float32)
    shifts_f = shifts_all.astype(jnp.float32)
    biases_f = biases_all.astype(jnp.float32)
    up_shift_f = up_shift.astype(jnp.float32)
    tokens_f = tokens[0].astype(jnp.float32)
    seg_local = segment_ids[0]
    tok_rows = tokens_f.shape[0]
    width = tokens_f.shape[1]
    seqlen = tok_rows * lax.axis_size("seq")
    query_pos = lax.axis_index("seq") * tok_rows + jnp.arange(tok_rows, dtype=jnp.int32)
    hidden_first = layer_norm(tokens_f, gains_f[0], shifts_f[0]).astype(jnp.bfloat16)
    query_key_value_bias = jnp.concatenate(
        [biases_f[0], jnp.zeros((width,), jnp.float32), biases_f[1]]
    )
    projected_rows = (
        jnp.dot(hidden_first, full_qkv, preferred_element_type=jnp.float32) + query_key_value_bias
    ).astype(jnp.bfloat16)
    queries = head_split(projected_rows[:, :width])
    key_rows = projected_rows[:, width : 2 * width]
    value_rows = projected_rows[:, 2 * width :]
    initial = (
        jnp.full((HEADS, tok_rows), floor_score, jnp.float32),
        jnp.zeros((HEADS, tok_rows), jnp.float32),
        jnp.zeros((tok_rows, HEADS, HD), jnp.float32),
    )

    def block_fn(running, pieces, offset):
        return forward_block(running, pieces, offset, queries, seg_local, query_pos)

    block_rows = math.gcd(seqlen, 1024)
    key_end = (lax.axis_index("seq") + 1) * tok_rows
    block_count = (key_end + block_rows - 1) // block_rows
    top_run, total_run, accum = in_blocks(
        block_fn,
        initial,
        (
            lax.all_gather(key_rows, "seq", axis=0, tiled=True),
            lax.all_gather(value_rows, "seq", axis=0, tiled=True),
            lax.all_gather(seg_local, "seq", axis=0, tiled=True),
        ),
    )
    log_total = top_run + jnp.log(total_run)
    attended_f = accum / total_run.T[:, :, None]
    attention_result = attended_f.reshape(tok_rows, width).astype(jnp.bfloat16)
    residual_first = (
        tokens_f
        + jnp.dot(attention_result, full_out, preferred_element_type=jnp.float32)
        + biases_f[2]
    )
    hidden_second = layer_norm(residual_first, gains_f[1], shifts_f[1]).astype(jnp.bfloat16)
    upward_rows = jnp.dot(hidden_second, full_up, preferred_element_type=jnp.float32) + up_shift_f
    activated_f, gelu_back = jax.vjp(jax.nn.gelu, upward_rows)
    activation_values = activated_f.astype(jnp.bfloat16)
    result = (
        residual_first
        + jnp.dot(activation_values, full_down, preferred_element_type=jnp.float32)
        + biases_f[3]
    )
    grad_y = cotangent[0]
    grad_y_f = grad_y.astype(jnp.float32)
    grad_down = jnp.einsum(
        "tf,td->fd", activation_values, grad_y, preferred_element_type=jnp.float32
    )
    grad_act = jnp.einsum("td,fd->tf", grad_y, full_down, preferred_element_type=jnp.float32)
    grad_up_pre = gelu_back(grad_act)[0].astype(jnp.bfloat16)
    grad_up = jnp.einsum(
        "td,tf->df", hidden_second, grad_up_pre, preferred_element_type=jnp.float32
    )
    grad_hidden_two = jnp.einsum(
        "tf,df->td", grad_up_pre, full_up, preferred_element_type=jnp.float32
    )
    _unused, norm_two_back = jax.vjp(layer_norm, residual_first, gains_f[1], shifts_f[1])
    grad_sum_part, grad_gain_two, grad_shift_two = norm_two_back(grad_hidden_two)
    grad_first = grad_y_f + grad_sum_part
    grad_first_bf = grad_first.astype(jnp.bfloat16)
    grad_out_w = jnp.einsum(
        "td,te->de", attention_result, grad_first_bf, preferred_element_type=jnp.float32
    )
    grad_attended = jnp.einsum(
        "te,de->td", grad_first_bf, full_out, preferred_element_type=jnp.float32
    ).astype(jnp.bfloat16)
    grad_heads = head_split(grad_attended)
    delta = jnp.einsum("qhd,qhd->hq", grad_heads.astype(jnp.float32), attended_f)
    whole = (
        lax.all_gather(key_rows, "seq", axis=0, tiled=True),
        lax.all_gather(value_rows, "seq", axis=0, tiled=True),
        lax.all_gather(seg_local, "seq", axis=0, tiled=True),
    )

    def backward_step(number, state_now):
        return backward_block(
            number,
            state_now,
            whole,
            queries,
            seg_local,
            query_pos,
            grad_heads,
            log_total,
            delta,
            block_rows,
        )

    start_state = (
        jnp.zeros((tok_rows, HEADS, HD), jnp.float32),
        jnp.zeros((seqlen, 2 * width), jnp.float32),
    )
    grad_query, term = lax.fori_loop(0, block_count, backward_step, start_state)
    grad_kv = lax.psum_scatter(term, "seq", scatter_dimension=0, tiled=True).astype(jnp.bfloat16)
    grad_q = (grad_query * HD ** (-0.5)).reshape(tok_rows, width).astype(jnp.bfloat16)
    grad_proj = jnp.concatenate([grad_q, grad_kv], axis=1)
    grad_qkv_w = jnp.einsum(
        "td,te->de", hidden_first, grad_proj, preferred_element_type=jnp.float32
    )
    grad_hidden_one = jnp.einsum(
        "te,de->td", grad_proj, full_qkv, preferred_element_type=jnp.float32
    )
    _unused_two, norm_one_back = jax.vjp(layer_norm, tokens_f, gains_f[0], shifts_f[0])
    grad_in_part, grad_gain_one, grad_shift_one = norm_one_back(grad_hidden_one)
    grad_tokens = grad_first + grad_in_part
    grad_proj_f = grad_proj.astype(jnp.float32)
    grad_bias_rows = jnp.stack(
        [
            jnp.sum(grad_proj_f[:, :width], axis=0),
            jnp.sum(grad_proj_f[:, 2 * width :], axis=0),
            jnp.sum(grad_first, axis=0),
            jnp.sum(grad_y_f, axis=0),
        ]
    )
    grad_up_shift = jnp.sum(grad_up_pre.astype(jnp.float32), axis=0)
    grad_gains = jnp.stack([grad_gain_one, grad_gain_two])
    grad_shifts = jnp.stack([grad_shift_one, grad_shift_two])
    shares = (
        lax.psum_scatter(grad_qkv_w, "seq", scatter_dimension=0, tiled=True),
        lax.psum_scatter(grad_out_w, "seq", scatter_dimension=0, tiled=True),
        lax.psum_scatter(grad_up, "seq", scatter_dimension=0, tiled=True),
        lax.psum_scatter(grad_down, "seq", scatter_dimension=0, tiled=True),
        lax.psum_scatter(grad_gains, "seq", scatter_dimension=1, tiled=True),
        lax.psum_scatter(grad_shifts, "seq", scatter_dimension=1, tiled=True),
        lax.psum_scatter(grad_bias_rows, "seq", scatter_dimension=1, tiled=True),
        lax.psum_scatter(grad_up_shift, "seq", scatter_dimension=0, tiled=True),
    )
    totals = (
        lax.psum(shares[0].astype(jnp.bfloat16), "rep").astype(jnp.float32),
        lax.psum(shares[1].astype(jnp.bfloat16), "rep").astype(jnp.float32),
        lax.psum(shares[2].astype(jnp.bfloat16), "rep").astype(jnp.float32),
        lax.psum(shares[3].astype(jnp.bfloat16), "rep").astype(jnp.float32),
        lax.psum(shares[4].astype(jnp.bfloat16), "rep").astype(jnp.float32),
        lax.psum(shares[5].astype(jnp.bfloat16), "rep").astype(jnp.float32),
        lax.psum(shares[6].astype(jnp.bfloat16), "rep").astype(jnp.float32),
        lax.psum(shares[7].astype(jnp.bfloat16), "rep").astype(jnp.float32),
    )
    return (
        result.astype(jnp.bfloat16)[None],
        grad_tokens[None],
        totals[0],
        totals[1],
        totals[2],
        totals[3],
        totals[4],
        totals[5],
        totals[6],
        totals[7],
    )


def f32(value):
    return value.astype(jnp.float32)


def b16(value):
    return value.astype(jnp.bfloat16)


def dot_nn(left, right):
    return jnp.dot(left, right, preferred_element_type=jnp.float32)


def dot_nt(left, right):
    return lax.dot_general(
        left, right, (((1,), (1,)), ((), ())), preferred_element_type=jnp.float32
    )


def dot_tn(left, right):
    return lax.dot_general(
        left, right, (((0,), (0,)), ((), ())), preferred_element_type=jnp.float32
    )


def norm_parts(values):
    center = values - jnp.mean(values, axis=-1, keepdims=True)
    rate = lax.rsqrt(jnp.mean(center * center, axis=-1, keepdims=True) + norm_eps)
    return center * rate, rate


def norm_back(grad, hat, rate, gain):
    scaled = grad * gain
    return rate * (
        scaled
        - jnp.mean(scaled, axis=-1, keepdims=True)
        - hat * jnp.mean(scaled * hat, axis=-1, keepdims=True)
    )


def place():
    rep, seq = lax.axis_index("rep"), lax.axis_index("seq")
    return lax.div(rep, 2), lax.rem(rep, 2), lax.rem(seq, 2), lax.div(seq, 2)


def piece_shard(number, y, z):
    if number < 3:
        return 2 * lax.rem(z + 3 - number, 4) + y
    return 2 * lax.rem(z + 7 - number, 4) + 1 - y


def pack96(parts):
    lane = lax.broadcasted_iota(jnp.int32, parts[0].shape, 1)
    one, two, three = (pltpu.roll(parts[k], 128 - 32 * k, 1) for k in (1, 2, 3))
    return jnp.concatenate(
        [
            jnp.where(lane < 96, parts[0], one),
            jnp.where(lane < 64, one, two),
            jnp.where(lane < 32, two, three),
        ],
        axis=1,
    )


def unpack96(block):
    tiles = [block[:, 128 * k : 128 * k + 128] for k in range(3)]
    lane = lax.broadcasted_iota(jnp.int32, tiles[0].shape, 1)
    return [
        tiles[0],
        jnp.where(lane < 32, pltpu.roll(tiles[0], 32, 1), pltpu.roll(tiles[1], 32, 1)),
        jnp.where(lane < 64, pltpu.roll(tiles[1], 64, 1), pltpu.roll(tiles[2], 64, 1)),
        pltpu.roll(tiles[2], 96, 1),
    ]


def choose(parts, index):
    out = parts[0]
    for number in range(1, len(parts)):
        out = jnp.where(index == number, parts[number], out)
    return out


class Copies:
    def __init__(self, sems, first=0):
        self.sems = sems
        self.first = first
        self.held = []

    def add(self, source, target):
        copy = pltpu.make_async_copy(source, target, self.sems.at[self.first + len(self.held)])
        copy.start()
        self.held.append(copy)

    def wait(self):
        for copy in self.held:
            copy.wait()
        self.held = []


def corners(x, c):
    return ((x, c), (1 - x, c), (x, 1 - c), (1 - x, 1 - c))


def fetch_qkv(copies, own, groups, full, full_out=None, own_out=None):
    x, c, y, z = place()
    rows = own.shape[0]
    half, width = rows // 2, own.shape[1] // 3
    row = pl.multiple_of((2 * z + y) * rows, 16)
    copies.add(own, full.at[pl.ds(row, rows), :])
    if full_out is not None:
        copies.add(own_out, full_out.at[pl.ds(row, rows), :])
    wide, side = 3 * width // 2, width // 2
    for number in range(7):
        for (xx, cc), group in zip(corners(x, c), groups, strict=True):
            piece = piece_of(group, number)
            at = pl.ds(pl.multiple_of(piece_shard(number, y, z) * rows + half * cc, 16), half)
            copies.add(
                piece.at[pl.ds(0, half), pl.ds(0, wide)],
                full.at[at, pl.ds(pl.multiple_of(wide * xx, 128), wide)],
            )
            if full_out is not None:
                copies.add(
                    piece.at[pl.ds(0, half), pl.ds(wide, side)],
                    full_out.at[at, pl.ds(pl.multiple_of(side * xx, 128), side)],
                )


def piece_of(group, number):
    behind, across, behind_across = group
    if number < 3:
        return behind.at[number]
    return across.at[0] if number == 3 else behind_across.at[number - 4]


def mask_bias(start, me, tok, target):
    keys, lanes = target.shape
    key_pos = (me - 4) * tok + lax.broadcasted_iota(jnp.int32, (keys, lanes), 0)
    lane = lax.broadcasted_iota(jnp.int32, (keys, lanes), 1)
    query_pos = me * tok + jnp.where(lane >= tok, lane - tok, lane)
    target[...] = jnp.where((key_pos >= start) & (key_pos <= query_pos), 0.0, floor_score)


def pair_stack(rows):
    lane = lax.broadcasted_iota(jnp.int32, rows.shape, 1)
    zero = jnp.zeros_like(rows)
    return jnp.concatenate([jnp.where(lane < HD, rows, zero), jnp.where(lane < HD, zero, rows)], axis=0)


def pair_join(transposed):
    both = transposed.T
    tok = both.shape[0] // 2
    lane = lax.broadcasted_iota(jnp.int32, (tok, 2 * HD), 1)
    return jnp.where(lane < HD, both[:tok], both[tok:])


def prep_kernel(
    tokens, segs, qkv, out, up, down, gains, shifts, biases, up_bias,
    t_out, q_out, f_out, fu_out, fd_out,
    scratch, wide, held_g, held_s, held_b, ids, line, sems,
):
    x, c, _y, _z = place()
    tok, width = tokens.shape[1:]
    rows = qkv.shape[0]
    half, side = rows // 2, width // 2
    p = 2 * x + c
    at = pl.ds(pl.multiple_of(half * c, 16), half)
    copies, others = Copies(sems), Copies(sems, 5)
    for source, target in ((gains, held_g), (shifts, held_s), (biases, held_b)):
        copies.add(source, target)
    copies.add(segs, ids)
    copies.add(up_bias, line)
    others.add(up, wide)
    wide_cols = 3 * side
    others.add(
        qkv.at[at, pl.ds(pl.multiple_of(wide_cols * x, 128), wide_cols)],
        q_out.at[pl.ds(0, half), pl.ds(0, wide_cols)],
    )
    others.add(
        out.at[at, pl.ds(pl.multiple_of(side * x, 128), side)],
        q_out.at[pl.ds(0, half), pl.ds(wide_cols, side)],
    )
    others.add(tokens.at[0], t_out.at[pl.ds(0, tok), :])
    own_rows = down.at[pl.ds(pl.multiple_of(rows * p, 16), rows), :]
    others.add(own_rows, f_out.at[pl.ds(rows, rows), :])
    others.add(own_rows, fd_out)
    copies.wait()
    scratch[...] = jnp.zeros_like(scratch)
    for first, held in ((0, held_g), (2, held_s), (4, held_b)):
        scratch[pl.ds(first, held.shape[0]), pl.ds(0, rows)] = f32(held[...])
    parts = unpack96(jnp.broadcast_to(f32(line[...]).reshape(1, line.shape[0]), (8, line.shape[0])))
    lane = lax.broadcasted_iota(jnp.int32, (8, 128), 1)
    row = lax.broadcasted_iota(jnp.int32, (8, 128), 0)
    ups = jnp.zeros((8, 128), jnp.float32)
    for number in range(4):
        ups = jnp.where((row == number) & (lane < rows), parts[number], ups)
    smalls = b16(jnp.concatenate([scratch[:, pl.ds(0, 128)], ups], axis=0))
    q_out[pl.ds(0, 16), pl.ds(2 * width, 128)] = smalls
    q_out[pl.ds(16, half - 16), pl.ds(2 * width, 128)] = jnp.zeros((half - 16, 128), jnp.bfloat16)
    scratch[...] = jnp.zeros_like(scratch)
    scratch[pl.ds(0, 1), pl.ds(0, tok)] = f32(ids[...])
    t_out[pl.ds(tok, 8), :] = b16(scratch[...])
    others.wait()
    for group in range(2):
        parts = []
        for shard in range(4 * group, 4 * group + 4):
            parts.append(choose(unpack96(f32(wide[:, pl.ds(384 * shard, 384)])), p))
        packed = b16(pack96(parts))
        f_out[pl.ds(0, rows), pl.ds(384 * group, 384)] = packed
        fu_out[:, pl.ds(384 * group, 384)] = packed


def front_kernel(
    seg, xo, x1, x2, x3, x4, first, own, own_o,
    g0, g1, g2, g3, g4, g5, g6, g7, g8, g9, g10, g11,
    q_out, kv_out, h_out, a_out, lse_out, start_out, vec_out, upb_out, wo_out, r_out, h2_out,
    full, small, bias, sems, vsems,
):
    x, c, y, z = place()
    me = 2 * z + y
    p = 2 * x + c
    tok, width = q_out.shape
    copies, vcopies = Copies(sems), Copies(vsems)
    vcopies.add(first.at[pl.ds(0, 16), pl.ds(2 * width, 128)], small.at[me])
    for number in range(7):
        source = piece_of((g0, g1, g2), number)
        vcopies.add(source.at[pl.ds(0, 16), pl.ds(2 * width, 128)], small.at[piece_shard(number, y, z)])
    groups = ((g0, g1, g2), (g3, g4, g5), (g6, g7, g8), (g9, g10, g11))
    fetch_qkv(copies, own, groups, full, wo_out, own_o)
    blocks = (xo, x1, x2, x3, x4)
    lane1 = lax.broadcasted_iota(jnp.int32, (1, tok), 1)
    start = jnp.full(seg.shape, 1 << 30, jnp.int32)
    for number in range(4):
        first_pos = jnp.full((1, 1), 1 << 30, jnp.int32)
        for back in range(5):
            ids = f32(blocks[back][pl.ds(tok, 8), pl.ds(0, tok)])[:1]
            pos = (me - back) * tok + lane1
            hit = (ids == float(number)) & (pos >= 0)
            first_pos = jnp.minimum(
                first_pos, jnp.min(jnp.where(hit, pos, 1 << 30), axis=1, keepdims=True)
            )
        start = jnp.where(seg[...] == number, first_pos, start)
    start_out[...] = start
    mask_bias(start, me, tok, bias)
    vcopies.wait()
    for group in range(2):
        held = [f32(small[4 * group + k]) for k in range(4)]
        vec_out[:, pl.ds(384 * group, 384)] = pack96([block[:8] for block in held])
        upb_out[:, pl.ds(384 * group, 384)] = pack96(
            [choose([jnp.broadcast_to(block[k : k + 1], (8, 128)) for k in range(8, 12)], p) for block in held]
        )
    vec = vec_out[...]
    for back in range(5):
        hat, _rate = norm_parts(f32(blocks[back][pl.ds(0, tok), :]))
        h_out[pl.ds((4 - back) * tok, tok), :] = b16(hat * vec[0:1] + vec[2:3])
    copies.wait()
    q_out[...] = b16(dot_nn(h_out[pl.ds(4 * tok, tok), :], full[:, pl.ds(0, width)]) + vec[4:5])

    def project(number, carry):
        col = pl.multiple_of(number * 256, 256)
        shift = jnp.where(number >= width // 256, 1.0, 0.0)
        bias_at = lax.rem(number, width // 256)
        piece = vec_out[pl.ds(5, 1), pl.ds(pl.multiple_of(bias_at * 256, 256), 256)]
        kv_out[:, pl.ds(col, 256)] = b16(
            dot_nn(h_out[...], full[:, pl.ds(pl.multiple_of(width + col, 256), 256)]) + piece * shift
        )
        return carry

    lax.fori_loop(0, 2 * width // 256, project, 0)

    def pair(number, carry):
        col = pl.multiple_of(number * 128, 128)
        queries = pair_stack(q_out[:, pl.ds(col, 128)] * jnp.bfloat16(0.125))
        scores = dot_nt(kv_out[:, pl.ds(col, 128)], queries) + bias[...]
        top = jnp.max(scores, axis=0, keepdims=True)
        probs = jnp.exp(scores - top)
        total = jnp.sum(probs, axis=0, keepdims=True)
        mixed = dot_tn(kv_out[:, pl.ds(pl.multiple_of(width + col, 128), 128)], b16(probs))
        a_out[:, pl.ds(col, 128)] = b16(pair_join(mixed / total))
        lse_out[number] = top + jnp.log(total)
        return carry

    lax.fori_loop(0, width // 128, pair, 0)
    residual = f32(xo[pl.ds(0, tok), :]) + dot_nn(a_out[...], wo_out[...]) + vec[6:7]
    r_out[...] = residual
    hat, _rate = norm_parts(residual)
    h2_out[...] = b16(hat * vec[1:2] + vec[3:4])


def feed_tokens(h2, dy, w_up, w_down, upb, act_out, du_out):
    root = math.sqrt(2.0 / math.pi)
    chunk = 256

    def feed(number, carry):
        col = pl.multiple_of(number * chunk, chunk)
        pre = dot_nn(h2[...], w_up[:, pl.ds(col, chunk)]) + upb[pl.ds(0, 1), pl.ds(col, chunk)]
        square = pre * pre
        bend = jnp.tanh(root * pre * (1.0 + 0.044715 * square))
        act = b16(0.5 * pre * (1.0 + bend))
        slope = 0.5 * (1.0 + bend) + 0.5 * pre * (1.0 - bend * bend) * (
            root * (1.0 + 3.0 * 0.044715 * square)
        )
        low = b16(dot_nt(dy[...], w_down[pl.ds(col, chunk), :]) * slope)
        act_out[:, pl.ds(col, chunk)] = act
        du_out[:, pl.ds(col, chunk)] = low
        return carry

    lax.fori_loop(0, w_up.shape[1] // chunk, feed, 0, unroll=True)
    return dot_nt(du_out[...], w_up[...])


def assemble_kernel(own, z1, z2, z3u, z3d, y0, y13, wu_out, wd_out, sems):
    _x, _c, y, z = place()
    rows = own.shape[0] // 2
    copies = Copies(sems)
    pieces = [(own, 2 * z + y)]
    for number, ref in ((0, z1), (1, z2), (3, y0)):
        pieces.append((ref, piece_shard(number, y, z)))
    for number, first in ((4, 0), (6, 2 * rows)):
        pieces.append((y13.at[pl.ds(first, 2 * rows), :], piece_shard(number, y, z)))
    for ref, shard in pieces:
        at = pl.ds(pl.multiple_of(shard * rows, 16), rows)
        copies.add(ref.at[pl.ds(0, rows), :], wu_out.at[at, :])
        copies.add(ref.at[pl.ds(rows, rows), :], wd_out.at[at, :])
    at = pl.ds(pl.multiple_of(piece_shard(2, y, z) * rows, 16), rows)
    copies.add(z3u, wu_out.at[at, :])
    copies.add(z3d, wd_out.at[at, :])
    copies.wait()


def near_kernel(
    h_own, h_c, dy_own, dy_c, upb, y2u, y2d, _wu, _wd,
    h2, dy, act_out, du_out, keep_out, send_out, wu_out, wd_out,
    sems,
):
    _x, _c, y, z = place()
    tok, width = h_own.shape
    rows = width // 8
    copies = Copies(sems)
    at = pl.ds(pl.multiple_of(piece_shard(5, y, z) * rows, 16), rows)
    copies.add(y2u, wu_out.at[at, :])
    copies.add(y2d, wd_out.at[at, :])
    h2[pl.ds(0, tok), :] = h_own[...]
    h2[pl.ds(tok, tok), :] = h_c[...]
    dy[pl.ds(0, tok), :] = dy_own[...]
    dy[pl.ds(tok, tok), :] = dy_c[...]
    copies.wait()
    grad = feed_tokens(h2, dy, wu_out, wd_out, upb, act_out, du_out)
    keep_out[...] = grad[:tok]
    send_out[...] = b16(grad[tok:])


def far_c_kernel(
    h_xc, dy_xc, upb, w_up, w_down, h_near, dy_near, act_near, du_near,
    hs, dys, acts, dus, send_out,
    sems,
):
    tok = dy_xc.shape[0]
    copies = Copies(sems)
    for source, target in ((h_near, hs), (dy_near, dys), (act_near, acts), (du_near, dus)):
        copies.add(source, target.at[pl.ds(0, 2 * tok), :])
    last = pl.ds(3 * tok, tok)
    hs[last, :] = h_xc[...]
    dys[last, :] = dy_xc[...]
    send_out[...] = b16(
        feed_tokens(h_xc, dy_xc, w_up, w_down, upb, acts.at[last, :], dus.at[last, :])
    )
    copies.wait()


def far_x_kernel(
    h_x, dy_x, upb, w_up, w_down, _hs, _dys, _acts, _dus,
    hs, dys, acts, dus, keep_out,
):
    tok = dy_x.shape[0]
    third = pl.ds(2 * tok, tok)
    hs[third, :] = h_x[...]
    dys[third, :] = dy_x[...]
    keep_out[...] = feed_tokens(h_x, dy_x, w_up, w_down, upb, acts.at[third, :], dus.at[third, :])


def weights_kernel(
    hs, dys, acts, dus, w_down,
    u_out, d_out, upb_out, keep_out, send_out,
    stage, sems,
):
    _x, _c, y, z = place()
    width = hs.shape[1]
    rows = width // 8
    upb_out[...] = jnp.sum(f32(dus[...]), axis=0, keepdims=True)

    def weight(number, carry):
        col = pl.multiple_of(number * 256, 256)
        stage[0, pl.ds(col, 256), :] = b16(dot_tn(hs[:, pl.ds(col, 256)], dus[...]))
        stage[1, pl.ds(col, 256), :] = b16(dot_tn(acts[:, pl.ds(col, 256)], dys[...]))
        return carry

    lax.fori_loop(0, width // 256, weight, 0)
    outs = Copies(sems)
    for shard in range(8):
        zz = lax.rem(shard // 2 + 4 - z, 4)
        yy = jnp.where(y == shard % 2, 0, 1)
        outs.add(stage.at[0, pl.ds(shard * rows, rows), :], u_out.at[yy, zz])
        outs.add(stage.at[1, pl.ds(shard * rows, rows), :], d_out.at[yy, zz])
    tok = hs.shape[0] // 4
    for number in range(4):
        part = dot_nn(acts[pl.ds(number * tok, tok), :], w_down[...])
        if number % 2:
            send_out[number // 2] = b16(part)
        else:
            keep_out[number // 2] = part
    outs.wait()


def scatter(stage, other, mine, sems):
    x, c, y, z = place()
    outs = Copies(sems)
    for shard in range(8):
        zz = lax.rem(shard // 2 + 4 - z, 4)
        yy = jnp.where(y == shard % 2, 0, 1)
        for xx in range(2):
            far = jnp.where(x == xx, 0, 1)
            outs.add(stage.at[1 - c, xx, shard], other.at[far, yy, zz])
            outs.add(stage.at[c, xx, shard], mine.at[far, yy, zz])
    outs.wait()


def post_kernel(
    residual, own, near, across, dy_in, vec_in, w_out, a_in,
    dr_out, da_out, dw_out, vec_out,
):
    vec = vec_in[...]
    grad_hidden = own[...] + f32(near[...]) + f32(across[...])
    hat, rate = norm_parts(residual[...])
    dy = f32(dy_in[...])
    grad_first = dy + norm_back(grad_hidden, hat, rate, vec[1:2])
    dr_out[...] = grad_first
    low = b16(grad_first)
    da_out[...] = b16(dot_nt(low, w_out[...]))
    dw_out[...] = dot_tn(a_in[...], low)
    zero = jnp.zeros((1, dy.shape[1]), jnp.float32)
    vec_out[...] = jnp.concatenate(
        [
            zero,
            jnp.sum(grad_hidden * hat, axis=0, keepdims=True),
            zero,
            jnp.sum(grad_hidden, axis=0, keepdims=True),
            zero,
            zero,
            jnp.sum(grad_first, axis=0, keepdims=True),
            jnp.sum(dy, axis=0, keepdims=True),
        ],
        axis=0,
    )


def back_pairs(first, q_in, kv_in, lse_in, da_in, bias, dq, dkv):
    width = q_in.shape[1]

    def pair(number, carry):
        col = pl.multiple_of((first + number) * 128, 128)
        vcol = pl.multiple_of(width + col, 128)
        to = pl.multiple_of(number * 128, 128)
        queries = pair_stack(q_in[:, pl.ds(col, 128)] * jnp.bfloat16(0.125))
        grads = pair_stack(da_in[:, pl.ds(col, 128)])
        keys = kv_in[:, pl.ds(col, 128)]
        probs = jnp.exp(dot_nt(keys, queries) + bias[...] - lse_in[first + number])
        dkv[:, pl.ds(pl.multiple_of(width // 2 + to, 128), 128)] = b16(dot_nn(b16(probs), grads))
        term = probs * dot_nt(kv_in[:, pl.ds(vcol, 128)], grads)
        low = b16(term - probs * jnp.sum(term, axis=0, keepdims=True))
        dkv[:, pl.ds(to, 128)] = b16(dot_nn(low, queries))
        dq[:, pl.ds(to, 128)] = b16(pair_join(dot_tn(keys, low)) * 0.125)
        return carry

    lax.fori_loop(0, 3, pair, 0, unroll=first == 0)


def qkv_weight(h_in, dq, dkv, stage, tail):
    tok, part = dq.shape
    keys = h_in.shape[0]

    def weight(number, carry):
        col = pl.multiple_of(number * 384, 384)
        key = dot_tn(h_in[:, pl.ds(col, 384)], dkv[...])
        query = dot_tn(h_in[pl.ds(keys - tok, tok), pl.ds(col, 384)], dq[...])
        for shard in range(4):
            for cc in range(2):
                for xx in range(2):
                    rows = slice(96 * shard + 48 * cc + 24 * xx, 96 * shard + 48 * cc + 24 * xx + 24)
                    blocks = [query[rows], key[rows, :part], key[rows, part:]] + tail(4 * number + shard, 48 * cc + 24 * xx)
                    stage[cc, xx, 4 * number + shard] = b16(jnp.concatenate(blocks, axis=0))
        return carry

    lax.fori_loop(0, 2, weight, 0)


def back_a_kernel(
    start_in, q_in, kv_in, h_in, lse_in, da_in, dw_in,
    other, mine, dq_out, dkv_out,
    bias, stage, sems,
):
    _x, _c, y, z = place()
    mask_bias(start_in[...], 2 * z + y, q_in.shape[0], bias)
    back_pairs(0, q_in, kv_in, lse_in, da_in, bias, dq_out, dkv_out)
    side = q_in.shape[1] // 2

    def out_rows(shard, row):
        rows = dw_in[pl.ds(pl.multiple_of(96 * shard + row, 8), 24), :]
        return [rows[:, :side], rows[:, side:]]

    qkv_weight(h_in, dq_out, dkv_out, stage, out_rows)
    scatter(stage, other, mine, sems)


def back_b_kernel(
    start_in, q_in, kv_in, lse_in, da_in, vec_in, upb_in, dq_a, dkv_a, xo, x1, x2, x3, x4,
    own, g0, g1, g2, g3, g4, g5, g6, g7, g8, g9, g10, g11,
    dq_out, dkv_out, p_own, p_y, p_z, sums_out,
    full, bias, sems,
):
    x, c, y, z = place()
    p = 2 * x + c
    tok, width = q_in.shape
    side = width // 2
    copies = Copies(sems)
    groups = ((g0, g1, g2), (g3, g4, g5), (g6, g7, g8), (g9, g10, g11))
    fetch_qkv(copies, own, groups, full)
    mask_bias(start_in[...], 2 * z + y, tok, bias)
    back_pairs(3, q_in, kv_in, lse_in, da_in, bias, dq_out, dkv_out)
    copies.wait()
    gain_sum = jnp.zeros((1, width), jnp.float32)
    shift_sum = jnp.zeros((1, width), jnp.float32)
    for back, block in enumerate((xo, x1, x2, x3, x4)):
        rows = pl.ds((4 - back) * tok, tok)
        grad = jnp.zeros((tok, width), jnp.float32)
        for number, (dq, dkv) in enumerate(((dq_a, dkv_a), (dq_out, dkv_out))):
            at = number * side
            grad = grad + dot_nt(dkv[rows, pl.ds(0, side)], full[:, pl.ds(width + at, side)])
            grad = grad + dot_nt(dkv[rows, pl.ds(side, side)], full[:, pl.ds(2 * width + at, side)])
            if back == 0:
                grad = grad + dot_nt(dq[...], full[:, pl.ds(at, side)])
        if back == 0:
            p_own[...] = grad
        elif back in (1, 3):
            p_y[back // 2] = b16(grad)
        else:
            p_z[back // 2 - 1] = b16(grad)
        hat, _rate = norm_parts(f32(block[pl.ds(0, tok), :]))
        gain_sum = gain_sum + jnp.sum(grad * hat, axis=0, keepdims=True)
        shift_sum = shift_sum + jnp.sum(grad, axis=0, keepdims=True)
    zero = jnp.zeros((1, width), jnp.float32)
    bias_q = jnp.concatenate([jnp.sum(f32(d[...]), axis=0, keepdims=True) for d in (dq_a, dq_out)], axis=1)
    bias_v = jnp.concatenate(
        [jnp.sum(f32(d[:, pl.ds(side, side)]), axis=0, keepdims=True) for d in (dkv_a, dkv_out)], axis=1
    )
    vec = vec_in[...] + jnp.concatenate(
        [gain_sum, zero, shift_sum, zero, bias_q, bias_v, zero, zero], axis=0
    )
    lane = lax.broadcasted_iota(jnp.int32, (8, 128), 1)
    line = lax.broadcasted_iota(jnp.int32, (8, 128), 0)
    for group in range(2):
        cols = pl.ds(384 * group, 384)
        vec_parts = unpack96(vec[:, 384 * group : 384 * group + 384])
        upb_parts = unpack96(jnp.broadcast_to(upb_in[:, cols], (8, 384)))
        for k in range(4):
            sums_out[4 * group + k] = jnp.concatenate(
                [
                    jnp.where(lane < 96, vec_parts[k], 0.0),
                    jnp.where((lane < 96) & (line == p), upb_parts[k], 0.0),
                ],
                axis=1,
            )


def back_c_kernel(h_in, dq, dkv, sums_in, other, mine, stage, sems):
    blank = jnp.zeros((8, 128), jnp.float32)
    qkv_weight(
        h_in, dq, dkv, stage, lambda shard, _row: [jnp.concatenate([sums_in[shard], blank], axis=1)]
    )
    scatter(stage, other, mine, sems)


def tokens_kernel(own, near, dr, xo, vec_in, grad_out):
    tok = own.shape[0]
    hat, rate = norm_parts(f32(xo[pl.ds(0, tok), :]))
    grad = own[...] + f32(near[...])
    grad_out[...] = dr[...] + norm_back(grad, hat, rate, vec_in[0:1, :])


def finish_f_kernel(f0, fx, fc, fcx, up, down, held):
    x, c, _y, _z = place()
    rows = f0.shape[0] // 2
    for (xx, cc), f in zip(corners(x, c), (f0, fx, fc, fcx), strict=True):
        p = 2 * xx + cc
        held[p] = f[pl.ds(0, rows), :]
        down[pl.ds(pl.multiple_of(rows * p, 16), rows), :] = f32(f[pl.ds(rows, rows), :])
    for group in range(2):
        parts = [unpack96(f32(held[k, :, pl.ds(384 * group, 384)])) for k in range(4)]
        for shard in range(4):
            up[:, pl.ds(384 * (4 * group + shard), 384)] = pack96([part[shard] for part in parts])


def finish_q_kernel(f0, fx, fc, fcx, qkv, out, gains, shifts, biases, up_bias):
    x, c, _y, _z = place()
    side = out.shape[1] // 2
    for (xx, cc), piece in zip(corners(x, c), (f0, fx, fc, fcx), strict=True):
        rows = pl.ds(pl.multiple_of(48 * cc + 24 * xx, 8), 24)
        blocks = f32(piece[...])
        for number in range(3):
            first, second = 24 * number, 24 * (number + 5)
            qkv[rows, pl.ds(2 * side * number, side)] = blocks[first : first + 24]
            qkv[rows, pl.ds(2 * side * number + side, side)] = blocks[second : second + 24]
        out[rows, pl.ds(0, side)] = blocks[72:96]
        out[rows, pl.ds(side, side)] = blocks[96:120]
    sums = f32(f0[...])[192:]
    part = gains.shape[1]
    gains[...] = sums[0:2, :part]
    shifts[...] = sums[2:4, :part]
    biases[...] = sums[4:8, :part]
    ups = sums[:, 128:256]
    packed = pack96([jnp.broadcast_to(ups[k : k + 1], (8, 128)) for k in range(4)])
    up_bias[...] = packed[0]


HB = pl.BlockSpec(memory_space=pltpu.HBM)
VM = pl.BlockSpec(memory_space=pltpu.VMEM)
AN = pl.BlockSpec(memory_space=pl.ANY)


def shape_of(shape, dtype):
    return jax.ShapeDtypeStruct(shape, dtype)


def call(kernel, ins, outs, out_shape, scratch=(), vmem=40, flops=0, moved=0, aliases=None):
    return pl.pallas_call(
        kernel,
        in_specs=ins,
        out_specs=outs,
        out_shape=out_shape,
        scratch_shapes=list(scratch),
        input_output_aliases=aliases or {},
        compiler_params=pltpu.CompilerParams(vmem_limit_bytes=vmem << 20),
        cost_estimate=pl.CostEstimate(flops=flops, bytes_accessed=moved, transcendentals=0),
    )


def fence(*values):
    return lax.optimization_barrier(values)


def swap_rep(value, bit):
    return lax.ppermute(value, "rep", [(k, k ^ bit) for k in range(4)])


def to_core(value):
    return swap_rep(value, 1)


def to_x(value):
    return swap_rep(value, 2)


def to_y(value):
    return lax.ppermute(value, "seq", [(k, k ^ 1) for k in range(8)])


def to_z(value, steps):
    return lax.ppermute(value, "seq", [(k, (k + 2 * steps) % 8) for k in range(8)])


def join(*parts):
    return jnp.concatenate(parts, axis=0)


def on_device_fast(
    tokens,
    segment_ids,
    query_key_value_weight,
    output_weight,
    up_weight,
    down_weight,
    ln_gains,
    ln_biases,
    biases,
    up_projection_bias,
    cotangent,
):
    seq = lax.axis_index("seq")
    y = seq % 2
    tok, width = tokens.shape[1:]
    hidden = up_weight.shape[1]
    keys = 5 * tok
    bf, fl = jnp.bfloat16, jnp.float32
    dma = pltpu.SemaphoreType.DMA
    grad_y = cotangent[0]
    own_tokens, piece_q, piece_f, piece_u, piece_d = call(
        prep_kernel,
        [HB] * 10,
        [VM] * 5,
        [
            shape_of((tok + 8, width), bf),
            shape_of((48, 2 * width + 128), bf),
            shape_of((192, width), bf),
            shape_of((96, width), bf),
            shape_of((96, width), bf),
        ],
        [
            pltpu.VMEM((8, width), fl),
            pltpu.VMEM((96, hidden), bf),
            pltpu.VMEM((2, 96), bf),
            pltpu.VMEM((2, 96), bf),
            pltpu.VMEM((4, 96), bf),
            pltpu.VMEM((1, tok), jnp.int32),
            pltpu.VMEM((384,), bf),
            dma((11,)),
        ],
        vmem=60, moved=4 * 10**6,
    )(
        tokens, segment_ids, query_key_value_weight, output_weight, up_weight, down_weight,
        ln_gains, ln_biases, biases, up_projection_bias,
    )

    q1, q3, q_y0, dy_x = fence(to_z(piece_q, 1), to_z(piece_q, 3), to_y(piece_q), to_x(grad_y))
    own_tokens, piece_f, q1, q_y0 = fence(own_tokens, piece_f, q1, q_y0, q3, dy_x)[:4]
    q2, x2, q_xy0, f_y0 = fence(to_z(q1, 1), to_z(own_tokens, 1), to_x(q_y0), to_y(piece_f))
    q_z = join(q1, q2, q3)
    q_z, x2, piece_d = fence(q_z, x2, piece_d, q_xy0, f_y0)[:3]
    q_y, q_xz, x4, f3d = fence(to_y(q_z), to_x(q_z), to_z(x2, 1), to_z(piece_d, 3))
    near = jnp.where(y == 0, own_tokens, x2)
    far = jnp.where(y == 0, x2, x4)
    near_far, q_y, piece_f, piece_u = fence(
        jnp.stack([near, far]), q_y, piece_f, piece_u, q_xz, f3d
    )[:4]
    crossed, q_xy, f1, f3u = fence(to_y(near_far), to_x(q_y), to_z(piece_f, 1), to_z(piece_u, 3))
    x1, x3 = crossed[0], crossed[1]
    q_z, q_y0, q_y, q_xz, q_xy0, q_xy = fence(q_z, q_y0, q_y, q_xz, q_xy0, q_xy, f1, f3u, crossed)[:6]
    q_cz, q_cy0, q_cy, q_cxz, q_cxy0, q_cxy = fence(
        *(to_core(v) for v in (q_z, q_y0, q_y, q_xz, q_xy0, q_xy))
    )
    f_13, f_1, q_cz = fence(join(f1, f3u, f3d), f1, q_cz, q_cy0, q_cy, q_cxz, q_cxy0, q_cxy)[:3]
    f_y13, f2 = to_y(f_13), to_z(f_1, 1)
    dy_c, dy_xc = to_core(grad_y), to_core(dy_x)

    def pieces(value):
        return value.reshape(value.shape[0] // 48, 48, value.shape[1])

    got_q = [
        pieces(v)
        for v in (q_z, q_y0, q_y, q_xz, q_xy0, q_xy, q_cz, q_cy0, q_cy, q_cxz, q_cxy0, q_cxy)
    ]
    seg = jnp.concatenate([segment_ids, segment_ids], axis=1)
    front = call(
        front_kernel,
        [VM] * 6 + [AN] * 15,
        [VM] * 11,
        [
            shape_of((tok, width), bf),
            shape_of((keys, 2 * width), bf),
            shape_of((keys, width), bf),
            shape_of((tok, width), bf),
            shape_of((width // 128, 1, 2 * tok), fl),
            shape_of((1, 2 * tok), jnp.int32),
            shape_of((8, width), fl),
            shape_of((8, width), fl),
            shape_of((width, width), bf),
            shape_of((tok, width), fl),
            shape_of((tok, width), bf),
        ],
        [
            pltpu.VMEM((width, 3 * width), bf),
            pltpu.VMEM((8, 16, 128), bf),
            pltpu.VMEM((keys, 2 * tok), fl),
            dma((2 + 56,)),
            dma((8,)),
        ],
        flops=7 * 10**9,
        vmem=16, moved=12 * 10**6,
    )(
        seg, own_tokens, x1, x2, x3, x4, piece_q, query_key_value_weight, output_weight, *got_q,
    )
    *front, f_y13, f2, dy_c, dy_xc = fence(*front, f_y13, f2, dy_c, dy_xc)
    queries, kv, normed, attended, lse, start, vec, upb, w_out, residual, hidden_2 = front
    w_half = call(
        assemble_kernel,
        [AN] * 7,
        [VM] * 2,
        [shape_of((width, width), bf)] * 2,
        [dma((14,))],
        vmem=4,
        moved=5 * 10**6,
    )(piece_f, f1, f2, f3u, f3d, f_y0, f_y13)
    h_x, h_c, f_y2u, f_y2d, *w_half = fence(
        to_x(hidden_2), to_core(hidden_2), to_y(f2[:96]), to_z(f_y13[96:192], 1), *w_half
    )
    act = shape_of((2 * tok, width), bf)
    acts = shape_of((4 * tok, width), bf)
    feed_shapes = [shape_of((tok, width), fl), shape_of((tok, width), bf)]
    *near_acts, keep_a, send_a, w_up, w_down = call(
        near_kernel,
        [VM] * 5 + [AN] * 2 + [VM] * 2,
        [VM] * 8,
        [act] * 4 + feed_shapes + [shape_of((width, width), bf)] * 2,
        [dma((2,))],
        flops=3 * 10**9,
        vmem=8,
        moved=6 * 10**6,
        aliases={7: 6, 8: 7},
    )(hidden_2, h_c, grad_y, dy_c, upb, f_y2u, f_y2d, *w_half)
    h_xc = to_core(h_x)
    keep_a, send_a, h_xc, w_up = fence(keep_a, send_a, h_xc, w_up)
    came_a = to_core(send_a)
    *all_acts, send_b = call(
        far_c_kernel,
        [VM] * 5 + [AN] * 4,
        [VM] * 5,
        [acts] * 4 + feed_shapes[1:],
        [dma((4,))],
        flops=15 * 10**8,
        vmem=8,
        moved=6 * 10**6,
    )(h_xc, dy_xc, upb, w_up, w_down, *near_acts)
    send_b, came_a, h_x = fence(send_b, came_a, h_x)
    came_b = to_core(send_b)
    *all_acts, keep_b = call(
        far_x_kernel,
        [VM] * 9,
        [VM] * 5,
        [acts] * 4 + feed_shapes[:1],
        flops=3 * 10**9,
        vmem=8,
        moved=6 * 10**6,
        aliases={5: 0, 6: 1, 7: 2, 8: 3},
    )(h_x, dy_x, upb, w_up, w_down, *all_acts)
    keep_b, came_b, *all_acts = fence(keep_b, came_b, *all_acts)
    back_x = to_x(b16(keep_b + f32(came_b)))
    u_terms, d_terms, upb_g, y_keep, y_send = call(
        weights_kernel,
        [VM] * 5,
        [AN, AN] + [VM] * 3,
        [
            shape_of((2, 4, 96, width), bf),
            shape_of((2, 4, 96, width), bf),
            shape_of((1, width), fl),
            shape_of((2, tok, width), fl),
            shape_of((2, tok, width), bf),
        ],
        [pltpu.VMEM((2, width, width), bf), dma((16,))],
        flops=3 * 10**9,
        vmem=12,
        moved=6 * 10**6,
    )(*all_acts, w_down)
    back_x, u_terms, d_terms, y_send = fence(back_x, u_terms, d_terms, y_send)
    u_came = to_y(u_terms[1])
    came_y = to_core(y_send)
    grad_first, grad_attended, dw_out, vec_g = call(
        post_kernel,
        [VM] * 8,
        [VM] * 4,
        [
            shape_of((tok, width), fl),
            shape_of((tok, width), bf),
            shape_of((width, width), fl),
            shape_of((8, width), fl),
        ],
        vmem=12,
        flops=10**9,
        moved=4 * 10**6,
    )(residual, keep_a, came_a, back_x, grad_y, vec, w_out, attended)
    back_scratch = [
        pltpu.VMEM((keys, 2 * tok), fl),
    ]
    qa_other, qa_mine, dq_a, dkv_a = call(
        back_a_kernel,
        [VM] * 7,
        [AN] * 2 + [VM] * 2,
        [
            shape_of((2, 2, 4, 120, width // 2), bf),
            shape_of((2, 2, 4, 120, width // 2), bf),
            shape_of((tok, width // 2), bf),
            shape_of((keys, width), bf),
        ],
        back_scratch + [pltpu.VMEM((2, 2, 8, 120, width // 2), bf), dma((32,))],
        flops=5 * 10**9,
        vmem=16, moved=10 * 10**6,
    )(start, queries, kv, normed, lse, grad_attended, dw_out)

    def both(mine, came):
        return lambda *index: f32(mine[index]) + f32(came[index])

    def z_sum(part, *came):
        return b16(part(0) + sum(f32(v) for v in came))

    dq_a, qa_other, u_came, came_y, d_send = fence(
        dq_a, qa_other, u_came, came_y, d_terms[1]
    )
    d_came, qa_came = to_y(d_send), to_core(qa_other)
    u_part = both(u_terms[0], u_came)
    u_z = [to_z(b16(u_part(step)), step) for step in (1, 2, 3)]
    dq_b, dkv_b, p_own, p_y, p_z, sums = call(
        back_b_kernel,
        [VM] * 14 + [AN] * 13,
        [VM] * 6,
        [
            shape_of((tok, width // 2), bf),
            shape_of((keys, width), bf),
            shape_of((tok, width), fl),
            shape_of((2, tok, width), bf),
            shape_of((2, tok, width), bf),
            shape_of((8, 8, 256), fl),
        ],
        [pltpu.VMEM((width, 3 * width), bf)] + back_scratch + [dma((1 + 28,))],
        flops=6 * 10**9,
        vmem=20, moved=10 * 10**6,
    )(
        start, queries, kv, lse, grad_attended, vec_g, upb_g, dq_a, dkv_a,
        own_tokens, x1, x2, x3, x4, query_key_value_weight, *got_q,
    )
    dq_b, qa_came, d_came, p_y, *u_z = fence(dq_b, qa_came, d_came, p_y, *u_z)
    p_came = to_y(p_y)
    qa_1 = both(qa_mine, qa_came)
    qa_x = to_x(b16(qa_1(1)))
    d_part = both(d_terms[0], d_came)
    d_z2 = to_z(b16(d_part(2)), 1)
    qb_other, qb_mine = call(
        back_c_kernel,
        [VM] * 4,
        [AN] * 2,
        [
            shape_of((2, 2, 4, 80, width // 2), bf),
            shape_of((2, 2, 4, 80, width // 2), bf),
        ],
        [pltpu.VMEM((2, 2, 8, 80, width // 2), bf), dma((32,))],
        flops=3 * 10**9,
        vmem=12, moved=6 * 10**6,
    )(normed, dq_b, dkv_b, sums)
    qb_came = [to_core(qb_other[k]) for k in range(2)]
    *qb_came, qa_x, p_came, d_z2 = fence(*qb_came, qa_x, p_came, d_z2)
    even = y == 0
    sum_own = p_own + jnp.where(even, f32(p_came[0]), 0.0)
    sum_4 = b16(f32(p_z[1]) + jnp.where(even, 0.0, f32(p_came[1])))
    sum_2 = f32(p_z[0]) + jnp.where(even, f32(p_came[1]), f32(p_came[0]))
    def qa_2(*index):
        return qa_1(0, *index) + f32(qa_x[index])

    def qb_1(side, *index):
        return f32(qb_mine[(side,) + index]) + f32(qb_came[side][index])

    qb_x, qa_y, hop, d_z1, d_z3 = fence(
        to_x(b16(qb_1(1))),
        to_y(b16(qa_2(1))),
        to_z(sum_4, 3),
        to_z(b16(d_part(1) + f32(d_z2)), 1),
        to_z(b16(d_part(3)), 3),
    )

    def qb_2(*index):
        return qb_1(0, *index) + f32(qb_x[index])

    f_tot = join(z_sum(u_part, *u_z), z_sum(d_part, d_z1, d_z3))
    fy_tot = join(f_tot, b16(y_keep[1] + f32(came_y[1])))
    qb_y, back_2, f_tot, fy_tot = fence(
        to_y(b16(qb_2(1))), to_z(b16(sum_2 + f32(hop)), 3), f_tot, fy_tot
    )

    def q_3(*index):
        first = qa_2(0, *index) + f32(qa_y[index])
        return jnp.concatenate([first, qb_2(0, *index) + f32(qb_y[index])], axis=-2)

    grad_tokens = call(
        tokens_kernel, [VM] * 5, VM, shape_of((tok, width), fl), vmem=4, moved=3 * 10**6
    )(sum_own, back_2, grad_first, own_tokens, vec)
    *q_z, over_x, f_tot = fence(*(to_z(b16(q_3(step)), step) for step in (1, 2, 3)), to_x(fy_tot), f_tot)
    f_x, back_y = over_x[:tok], over_x[tok:]
    q_sum = z_sum(q_3, *q_z)
    q_fx, q_fc = to_x(q_sum), to_core(q_sum)
    grad_up, grad_down = call(
        finish_f_kernel,
        [VM] * 4,
        [VM] * 2,
        [shape_of(up_weight.shape, fl), shape_of(down_weight.shape, fl)],
        [pltpu.VMEM((4, 96, width), bf)],
        vmem=8,
        moved=4 * 10**6,
    )(f_tot, f_x, to_core(f_tot), to_core(f_x))
    q_fx, q_fc, grad_up, grad_down = fence(q_fx, q_fc, grad_up, grad_down)
    q_fxc = to_core(q_fx)
    result = b16(residual + vec[7:8] + y_keep[0] + f32(came_y[0]) + f32(back_y))
    grad_qkv, grad_out, grad_gains, grad_shifts, grad_biases, grad_up_bias = call(
        finish_q_kernel,
        [VM] * 4,
        [VM] * 6,
        [
            shape_of(query_key_value_weight.shape, fl),
            shape_of(output_weight.shape, fl),
            shape_of(ln_gains.shape, fl),
            shape_of(ln_biases.shape, fl),
            shape_of(biases.shape, fl),
            shape_of(up_projection_bias.shape, fl),
        ],
        vmem=8,
        moved=3 * 10**6,
    )(q_sum, q_fx, q_fc, q_fxc)
    return (
        result[None],
        grad_tokens[None],
        grad_qkv,
        grad_out,
        grad_up,
        grad_down,
        grad_gains,
        grad_shifts,
        grad_biases,
        grad_up_bias,
    )


def solution(mesh):
    placed = (
        P("rep", "seq", None),
        P("rep", "seq"),
        P("seq", None),
        P("seq", None),
        P("seq", None),
        P("seq", None),
        P(None, "seq"),
        P(None, "seq"),
        P(None, "seq"),
        P("seq"),
        P("rep", "seq", None),
    )
    shape = dict(mesh.shape)
    small_slice = shape["rep"] == 4 and shape["seq"] == 8
    return jax.shard_map(
        on_device_fast if small_slice else on_device,
        mesh=mesh,
        in_specs=placed,
        out_specs=(
            P("rep", "seq", None),
            P("rep", "seq", None),
            P("seq", None),
            P("seq", None),
            P("seq", None),
            P("seq", None),
            P(None, "seq"),
            P(None, "seq"),
            P(None, "seq"),
            P("seq"),
        ),
        check_vma=False,
    )
```

```python
import math

import jax
import jax.numpy as jnp
from jax import lax
from jax.experimental import pallas as pl
from jax.experimental.pallas import tpu as pltpu
from jax.sharding import PartitionSpec as P

HEADS = 12
HD = 64


norm_eps = 1e-05
floor_score = -1e30


def layer_norm(values, gain, shift):
    center = values - jnp.mean(values, axis=-1, keepdims=True)
    spread = jnp.mean(center * center, axis=-1, keepdims=True)
    return center * lax.rsqrt(spread + norm_eps) * gain + shift


def head_split(matrix):
    return matrix.reshape(matrix.shape[0], HEADS, HD)


def masked_scores(queries, query_seg, query_pos, key_piece, seg_piece, offset):
    rows = key_piece.shape[0]
    scores = jnp.einsum(
        "qhd,khd->hqk", queries, head_split(key_piece), preferred_element_type=jnp.float32
    ) * HD ** (-0.5)
    key_pos = offset + jnp.arange(rows, dtype=jnp.int32)
    allowed = (query_seg[:, None] == seg_piece[None, :]) & (key_pos[None, :] <= query_pos[:, None])
    return (jnp.where(allowed[None], scores, floor_score), allowed)


def forward_block(running, pieces, offset, queries, query_seg, query_pos):
    top_run, total_run, accum = running
    key_piece, value_piece, seg_piece = pieces
    scores, allowed = masked_scores(queries, query_seg, query_pos, key_piece, seg_piece, offset)
    top_new = jnp.maximum(top_run, jnp.max(scores, axis=-1))
    probs = jnp.where(allowed[None], jnp.exp(scores - top_new[:, :, None]), 0.0)
    factor = jnp.exp(top_run - top_new)
    total_new = total_run * factor + jnp.sum(probs, axis=-1)
    update = jnp.einsum(
        "hqk,khd->qhd",
        probs.astype(jnp.bfloat16),
        head_split(value_piece),
        preferred_element_type=jnp.float32,
    )
    return (top_new, total_new, accum * factor.T[:, :, None] + update)


def in_blocks(block_fn, running, pieces):
    rows = pieces[0].shape[0]
    size = math.gcd(rows, 1024)
    stacked = tuple((member.reshape((rows // size, size) + member.shape[1:]) for member in pieces))
    offsets = jnp.arange(rows // size, dtype=jnp.int32) * size

    def scan_step(state_now, element):
        return (block_fn(state_now, element[0], element[1]), None)

    running, _unused = lax.scan(scan_step, running, (stacked, offsets))
    return running


def backward_block(
    number,
    state_now,
    whole,
    queries,
    query_seg,
    query_pos,
    grad_heads,
    log_total,
    delta,
    block_rows,
):
    grad_query, term = state_now
    offset = number * block_rows
    key_piece = lax.dynamic_slice_in_dim(whole[0], offset, block_rows, 0)
    value_piece = lax.dynamic_slice_in_dim(whole[1], offset, block_rows, 0)
    seg_piece = lax.dynamic_slice_in_dim(whole[2], offset, block_rows, 0)
    scores, allowed = masked_scores(queries, query_seg, query_pos, key_piece, seg_piece, offset)
    probs = jnp.where(allowed[None], jnp.exp(scores - log_total[:, :, None]), 0.0)
    grad_probs = jnp.einsum(
        "qhd,khd->hqk", grad_heads, head_split(value_piece), preferred_element_type=jnp.float32
    )
    grad_scores = (probs * (grad_probs - delta[:, :, None])).astype(jnp.bfloat16)
    grad_query = grad_query + jnp.einsum(
        "hqk,khd->qhd", grad_scores, head_split(key_piece), preferred_element_type=jnp.float32
    )
    grad_key = jnp.einsum(
        "hqk,qhd->khd", grad_scores, queries, preferred_element_type=jnp.float32
    ) * HD ** (-0.5)
    grad_value = jnp.einsum(
        "hqk,qhd->khd", probs.astype(jnp.bfloat16), grad_heads, preferred_element_type=jnp.float32
    )
    joined = jnp.concatenate(
        [grad_key.reshape(block_rows, -1), grad_value.reshape(block_rows, -1)], axis=1
    )
    term = lax.dynamic_update_slice_in_dim(term, joined, offset, 0)
    return (grad_query, term)


def on_device(
    tokens,
    segment_ids,
    query_key_value_weight,
    output_weight,
    up_weight,
    down_weight,
    ln_gains,
    ln_biases,
    biases,
    up_projection_bias,
    cotangent,
):
    gathered = (
        lax.all_gather(query_key_value_weight, "seq", axis=0, tiled=True),
        lax.all_gather(output_weight, "seq", axis=0, tiled=True),
        lax.all_gather(up_weight, "seq", axis=0, tiled=True),
        lax.all_gather(down_weight, "seq", axis=0, tiled=True),
        lax.all_gather(ln_gains, "seq", axis=1, tiled=True),
        lax.all_gather(ln_biases, "seq", axis=1, tiled=True),
        lax.all_gather(biases, "seq", axis=1, tiled=True),
        lax.all_gather(up_projection_bias, "seq", axis=0, tiled=True),
    )
    full_qkv, full_out, full_up, full_down, gains_all, shifts_all, biases_all, up_shift = gathered
    gains_f = gains_all.astype(jnp.float32)
    shifts_f = shifts_all.astype(jnp.float32)
    biases_f = biases_all.astype(jnp.float32)
    up_shift_f = up_shift.astype(jnp.float32)
    tokens_f = tokens[0].astype(jnp.float32)
    seg_local = segment_ids[0]
    tok_rows = tokens_f.shape[0]
    width = tokens_f.shape[1]
    seqlen = tok_rows * lax.axis_size("seq")
    query_pos = lax.axis_index("seq") * tok_rows + jnp.arange(tok_rows, dtype=jnp.int32)
    hidden_first = layer_norm(tokens_f, gains_f[0], shifts_f[0]).astype(jnp.bfloat16)
    query_key_value_bias = jnp.concatenate(
        [biases_f[0], jnp.zeros((width,), jnp.float32), biases_f[1]]
    )
    projected_rows = (
        jnp.dot(hidden_first, full_qkv, preferred_element_type=jnp.float32) + query_key_value_bias
    ).astype(jnp.bfloat16)
    queries = head_split(projected_rows[:, :width])
    key_rows = projected_rows[:, width : 2 * width]
    value_rows = projected_rows[:, 2 * width :]
    initial = (
        jnp.full((HEADS, tok_rows), floor_score, jnp.float32),
        jnp.zeros((HEADS, tok_rows), jnp.float32),
        jnp.zeros((tok_rows, HEADS, HD), jnp.float32),
    )

    def block_fn(running, pieces, offset):
        return forward_block(running, pieces, offset, queries, seg_local, query_pos)

    block_rows = math.gcd(seqlen, 1024)
    key_end = (lax.axis_index("seq") + 1) * tok_rows
    block_count = (key_end + block_rows - 1) // block_rows
    top_run, total_run, accum = in_blocks(
        block_fn,
        initial,
        (
            lax.all_gather(key_rows, "seq", axis=0, tiled=True),
            lax.all_gather(value_rows, "seq", axis=0, tiled=True),
            lax.all_gather(seg_local, "seq", axis=0, tiled=True),
        ),
    )
    log_total = top_run + jnp.log(total_run)
    attended_f = accum / total_run.T[:, :, None]
    attention_result = attended_f.reshape(tok_rows, width).astype(jnp.bfloat16)
    residual_first = (
        tokens_f
        + jnp.dot(attention_result, full_out, preferred_element_type=jnp.float32)
        + biases_f[2]
    )
    hidden_second = layer_norm(residual_first, gains_f[1], shifts_f[1]).astype(jnp.bfloat16)
    upward_rows = jnp.dot(hidden_second, full_up, preferred_element_type=jnp.float32) + up_shift_f
    activated_f, gelu_back = jax.vjp(jax.nn.gelu, upward_rows)
    activation_values = activated_f.astype(jnp.bfloat16)
    result = (
        residual_first
        + jnp.dot(activation_values, full_down, preferred_element_type=jnp.float32)
        + biases_f[3]
    )
    grad_y = cotangent[0]
    grad_y_f = grad_y.astype(jnp.float32)
    grad_down = jnp.einsum(
        "tf,td->fd", activation_values, grad_y, preferred_element_type=jnp.float32
    )
    grad_act = jnp.einsum("td,fd->tf", grad_y, full_down, preferred_element_type=jnp.float32)
    grad_up_pre = gelu_back(grad_act)[0].astype(jnp.bfloat16)
    grad_up = jnp.einsum(
        "td,tf->df", hidden_second, grad_up_pre, preferred_element_type=jnp.float32
    )
    grad_hidden_two = jnp.einsum(
        "tf,df->td", grad_up_pre, full_up, preferred_element_type=jnp.float32
    )
    _unused, norm_two_back = jax.vjp(layer_norm, residual_first, gains_f[1], shifts_f[1])
    grad_sum_part, grad_gain_two, grad_shift_two = norm_two_back(grad_hidden_two)
    grad_first = grad_y_f + grad_sum_part
    grad_first_bf = grad_first.astype(jnp.bfloat16)
    grad_out_w = jnp.einsum(
        "td,te->de", attention_result, grad_first_bf, preferred_element_type=jnp.float32
    )
    grad_attended = jnp.einsum(
        "te,de->td", grad_first_bf, full_out, preferred_element_type=jnp.float32
    ).astype(jnp.bfloat16)
    grad_heads = head_split(grad_attended)
    delta = jnp.einsum("qhd,qhd->hq", grad_heads.astype(jnp.float32), attended_f)
    whole = (
        lax.all_gather(key_rows, "seq", axis=0, tiled=True),
        lax.all_gather(value_rows, "seq", axis=0, tiled=True),
        lax.all_gather(seg_local, "seq", axis=0, tiled=True),
    )

    def backward_step(number, state_now):
        return backward_block(
            number,
            state_now,
            whole,
            queries,
            seg_local,
            query_pos,
            grad_heads,
            log_total,
            delta,
            block_rows,
        )

    start_state = (
        jnp.zeros((tok_rows, HEADS, HD), jnp.float32),
        jnp.zeros((seqlen, 2 * width), jnp.float32),
    )
    grad_query, term = lax.fori_loop(0, block_count, backward_step, start_state)
    grad_kv = lax.psum_scatter(term, "seq", scatter_dimension=0, tiled=True).astype(jnp.bfloat16)
    grad_q = (grad_query * HD ** (-0.5)).reshape(tok_rows, width).astype(jnp.bfloat16)
    grad_proj = jnp.concatenate([grad_q, grad_kv], axis=1)
    grad_qkv_w = jnp.einsum(
        "td,te->de", hidden_first, grad_proj, preferred_element_type=jnp.float32
    )
    grad_hidden_one = jnp.einsum(
        "te,de->td", grad_proj, full_qkv, preferred_element_type=jnp.float32
    )
    _unused_two, norm_one_back = jax.vjp(layer_norm, tokens_f, gains_f[0], shifts_f[0])
    grad_in_part, grad_gain_one, grad_shift_one = norm_one_back(grad_hidden_one)
    grad_tokens = grad_first + grad_in_part
    grad_proj_f = grad_proj.astype(jnp.float32)
    grad_bias_rows = jnp.stack(
        [
            jnp.sum(grad_proj_f[:, :width], axis=0),
            jnp.sum(grad_proj_f[:, 2 * width :], axis=0),
            jnp.sum(grad_first, axis=0),
            jnp.sum(grad_y_f, axis=0),
        ]
    )
    grad_up_shift = jnp.sum(grad_up_pre.astype(jnp.float32), axis=0)
    grad_gains = jnp.stack([grad_gain_one, grad_gain_two])
    grad_shifts = jnp.stack([grad_shift_one, grad_shift_two])
    shares = (
        lax.psum_scatter(grad_qkv_w, "seq", scatter_dimension=0, tiled=True),
        lax.psum_scatter(grad_out_w, "seq", scatter_dimension=0, tiled=True),
        lax.psum_scatter(grad_up, "seq", scatter_dimension=0, tiled=True),
        lax.psum_scatter(grad_down, "seq", scatter_dimension=0, tiled=True),
        lax.psum_scatter(grad_gains, "seq", scatter_dimension=1, tiled=True),
        lax.psum_scatter(grad_shifts, "seq", scatter_dimension=1, tiled=True),
        lax.psum_scatter(grad_bias_rows, "seq", scatter_dimension=1, tiled=True),
        lax.psum_scatter(grad_up_shift, "seq", scatter_dimension=0, tiled=True),
    )
    totals = (
        lax.psum(shares[0].astype(jnp.bfloat16), "rep").astype(jnp.float32),
        lax.psum(shares[1].astype(jnp.bfloat16), "rep").astype(jnp.float32),
        lax.psum(shares[2].astype(jnp.bfloat16), "rep").astype(jnp.float32),
        lax.psum(shares[3].astype(jnp.bfloat16), "rep").astype(jnp.float32),
        lax.psum(shares[4].astype(jnp.bfloat16), "rep").astype(jnp.float32),
        lax.psum(shares[5].astype(jnp.bfloat16), "rep").astype(jnp.float32),
        lax.psum(shares[6].astype(jnp.bfloat16), "rep").astype(jnp.float32),
        lax.psum(shares[7].astype(jnp.bfloat16), "rep").astype(jnp.float32),
    )
    return (
        result.astype(jnp.bfloat16)[None],
        grad_tokens[None],
        totals[0],
        totals[1],
        totals[2],
        totals[3],
        totals[4],
        totals[5],
        totals[6],
        totals[7],
    )


def f32(value):
    return value.astype(jnp.float32)


def b16(value):
    return value.astype(jnp.bfloat16)


def dot_nn(left, right):
    return jnp.dot(left, right, preferred_element_type=jnp.float32)


def dot_nt(left, right):
    return lax.dot_general(
        left, right, (((1,), (1,)), ((), ())), preferred_element_type=jnp.float32
    )


def dot_tn(left, right):
    return lax.dot_general(
        left, right, (((0,), (0,)), ((), ())), preferred_element_type=jnp.float32
    )


def norm_parts(values):
    center = values - jnp.mean(values, axis=-1, keepdims=True)
    rate = lax.rsqrt(jnp.mean(center * center, axis=-1, keepdims=True) + norm_eps)
    return center * rate, rate


def norm_back(grad, hat, rate, gain):
    scaled = grad * gain
    return rate * (
        scaled
        - jnp.mean(scaled, axis=-1, keepdims=True)
        - hat * jnp.mean(scaled * hat, axis=-1, keepdims=True)
    )


def place():
    rep, seq = lax.axis_index("rep"), lax.axis_index("seq")
    return lax.div(rep, 2), lax.rem(rep, 2), lax.rem(seq, 2), lax.div(seq, 2)


def piece_shard(number, y, z):
    if number < 3:
        return 2 * lax.rem(z + 3 - number, 4) + y
    return 2 * lax.rem(z + 7 - number, 4) + 1 - y


def pack96(parts):
    lane = lax.broadcasted_iota(jnp.int32, parts[0].shape, 1)
    one, two, three = (pltpu.roll(parts[k], 128 - 32 * k, 1) for k in (1, 2, 3))
    return jnp.concatenate(
        [
            jnp.where(lane < 96, parts[0], one),
            jnp.where(lane < 64, one, two),
            jnp.where(lane < 32, two, three),
        ],
        axis=1,
    )


def unpack96(block):
    tiles = [block[:, 128 * k : 128 * k + 128] for k in range(3)]
    lane = lax.broadcasted_iota(jnp.int32, tiles[0].shape, 1)
    return [
        tiles[0],
        jnp.where(lane < 32, pltpu.roll(tiles[0], 32, 1), pltpu.roll(tiles[1], 32, 1)),
        jnp.where(lane < 64, pltpu.roll(tiles[1], 64, 1), pltpu.roll(tiles[2], 64, 1)),
        pltpu.roll(tiles[2], 96, 1),
    ]


def choose(parts, index):
    out = parts[0]
    for number in range(1, len(parts)):
        out = jnp.where(index == number, parts[number], out)
    return out


class Copies:
    def __init__(self, sems, first=0):
        self.sems = sems
        self.first = first
        self.held = []

    def add(self, source, target):
        copy = pltpu.make_async_copy(source, target, self.sems.at[self.first + len(self.held)])
        copy.start()
        self.held.append(copy)

    def wait(self):
        for copy in self.held:
            copy.wait()
        self.held = []


def corners(x, c):
    return ((x, c), (1 - x, c), (x, 1 - c), (1 - x, 1 - c))


def fetch_qkv(copies, own, groups, full, full_out=None, own_out=None):
    x, c, y, z = place()
    rows = own.shape[0]
    half, width = rows // 2, own.shape[1] // 3
    row = pl.multiple_of((2 * z + y) * rows, 16)
    copies.add(own, full.at[pl.ds(row, rows), :])
    if full_out is not None:
        copies.add(own_out, full_out.at[pl.ds(row, rows), :])
    wide, side = 3 * width // 2, width // 2
    for number in range(7):
        for (xx, cc), group in zip(corners(x, c), groups, strict=True):
            piece = piece_of(group, number)
            at = pl.ds(pl.multiple_of(piece_shard(number, y, z) * rows + half * cc, 16), half)
            copies.add(
                piece.at[pl.ds(0, half), pl.ds(0, wide)],
                full.at[at, pl.ds(pl.multiple_of(wide * xx, 128), wide)],
            )
            if full_out is not None:
                copies.add(
                    piece.at[pl.ds(0, half), pl.ds(wide, side)],
                    full_out.at[at, pl.ds(pl.multiple_of(side * xx, 128), side)],
                )


def piece_of(group, number):
    behind, across, behind_across = group
    if number < 3:
        return behind.at[number]
    return across.at[0] if number == 3 else behind_across.at[number - 4]


def mask_bias(start, me, tok, target):
    keys, lanes = target.shape
    key_pos = (me - 4) * tok + lax.broadcasted_iota(jnp.int32, (keys, lanes), 0)
    lane = lax.broadcasted_iota(jnp.int32, (keys, lanes), 1)
    query_pos = me * tok + jnp.where(lane >= tok, lane - tok, lane)
    target[...] = jnp.where((key_pos >= start) & (key_pos <= query_pos), 0.0, floor_score)


def pair_stack(rows):
    lane = lax.broadcasted_iota(jnp.int32, rows.shape, 1)
    zero = jnp.zeros_like(rows)
    return jnp.concatenate([jnp.where(lane < HD, rows, zero), jnp.where(lane < HD, zero, rows)], axis=0)


def pair_join(transposed):
    both = transposed.T
    tok = both.shape[0] // 2
    lane = lax.broadcasted_iota(jnp.int32, (tok, 2 * HD), 1)
    return jnp.where(lane < HD, both[:tok], both[tok:])


def prep_kernel(
    tokens, segs, qkv, out, up, down, gains, shifts, biases, up_bias,
    t_out, q_out, f_out, fu_out, fd_out,
    scratch, wide, held_g, held_s, held_b, ids, line, sems,
):
    x, c, _y, _z = place()
    tok, width = tokens.shape[1:]
    rows = qkv.shape[0]
    half, side = rows // 2, width // 2
    p = 2 * x + c
    at = pl.ds(pl.multiple_of(half * c, 16), half)
    copies, others = Copies(sems), Copies(sems, 5)
    for source, target in ((gains, held_g), (shifts, held_s), (biases, held_b)):
        copies.add(source, target)
    copies.add(segs, ids)
    copies.add(up_bias, line)
    others.add(up, wide)
    wide_cols = 3 * side
    others.add(
        qkv.at[at, pl.ds(pl.multiple_of(wide_cols * x, 128), wide_cols)],
        q_out.at[pl.ds(0, half), pl.ds(0, wide_cols)],
    )
    others.add(
        out.at[at, pl.ds(pl.multiple_of(side * x, 128), side)],
        q_out.at[pl.ds(0, half), pl.ds(wide_cols, side)],
    )
    others.add(tokens.at[0], t_out.at[pl.ds(0, tok), :])
    own_rows = down.at[pl.ds(pl.multiple_of(rows * p, 16), rows), :]
    others.add(own_rows, f_out.at[pl.ds(rows, rows), :])
    others.add(own_rows, fd_out)
    copies.wait()
    scratch[...] = jnp.zeros_like(scratch)
    for first, held in ((0, held_g), (2, held_s), (4, held_b)):
        scratch[pl.ds(first, held.shape[0]), pl.ds(0, rows)] = f32(held[...])
    parts = unpack96(jnp.broadcast_to(f32(line[...]).reshape(1, line.shape[0]), (8, line.shape[0])))
    lane = lax.broadcasted_iota(jnp.int32, (8, 128), 1)
    row = lax.broadcasted_iota(jnp.int32, (8, 128), 0)
    ups = jnp.zeros((8, 128), jnp.float32)
    for number in range(4):
        ups = jnp.where((row == number) & (lane < rows), parts[number], ups)
    smalls = b16(jnp.concatenate([scratch[:, pl.ds(0, 128)], ups], axis=0))
    q_out[pl.ds(0, 16), pl.ds(2 * width, 128)] = smalls
    q_out[pl.ds(16, half - 16), pl.ds(2 * width, 128)] = jnp.zeros((half - 16, 128), jnp.bfloat16)
    scratch[...] = jnp.zeros_like(scratch)
    scratch[pl.ds(0, 1), pl.ds(0, tok)] = f32(ids[...])
    t_out[pl.ds(tok, 8), :] = b16(scratch[...])
    others.wait()
    for group in range(2):
        parts = []
        for shard in range(4 * group, 4 * group + 4):
            parts.append(choose(unpack96(f32(wide[:, pl.ds(384 * shard, 384)])), p))
        packed = b16(pack96(parts))
        f_out[pl.ds(0, rows), pl.ds(384 * group, 384)] = packed
        fu_out[:, pl.ds(384 * group, 384)] = packed


def front_kernel(
    seg, xo, x1, x2, x3, x4, first, own, own_o,
    g0, g1, g2, g3, g4, g5, g6, g7, g8, g9, g10, g11,
    q_out, kv_out, h_out, a_out, lse_out, start_out, vec_out, upb_out, wo_out, r_out, h2_out,
    full, small, bias, sems, vsems,
):
    x, c, y, z = place()
    me = 2 * z + y
    p = 2 * x + c
    tok, width = q_out.shape
    copies, vcopies = Copies(sems), Copies(vsems)
    vcopies.add(first.at[pl.ds(0, 16), pl.ds(2 * width, 128)], small.at[me])
    for number in range(7):
        source = piece_of((g0, g1, g2), number)
        vcopies.add(source.at[pl.ds(0, 16), pl.ds(2 * width, 128)], small.at[piece_shard(number, y, z)])
    groups = ((g0, g1, g2), (g3, g4, g5), (g6, g7, g8), (g9, g10, g11))
    fetch_qkv(copies, own, groups, full, wo_out, own_o)
    blocks = (xo, x1, x2, x3, x4)
    lane1 = lax.broadcasted_iota(jnp.int32, (1, tok), 1)
    start = jnp.full(seg.shape, 1 << 30, jnp.int32)
    for number in range(4):
        first_pos = jnp.full((1, 1), 1 << 30, jnp.int32)
        for back in range(5):
            ids = f32(blocks[back][pl.ds(tok, 8), pl.ds(0, tok)])[:1]
            pos = (me - back) * tok + lane1
            hit = (ids == float(number)) & (pos >= 0)
            first_pos = jnp.minimum(
                first_pos, jnp.min(jnp.where(hit, pos, 1 << 30), axis=1, keepdims=True)
            )
        start = jnp.where(seg[...] == number, first_pos, start)
    start_out[...] = start
    mask_bias(start, me, tok, bias)
    vcopies.wait()
    for group in range(2):
        held = [f32(small[4 * group + k]) for k in range(4)]
        vec_out[:, pl.ds(384 * group, 384)] = pack96([block[:8] for block in held])
        upb_out[:, pl.ds(384 * group, 384)] = pack96(
            [choose([jnp.broadcast_to(block[k : k + 1], (8, 128)) for k in range(8, 12)], p) for block in held]
        )
    vec = vec_out[...]
    for back in range(5):
        hat, _rate = norm_parts(f32(blocks[back][pl.ds(0, tok), :]))
        h_out[pl.ds((4 - back) * tok, tok), :] = b16(hat * vec[0:1] + vec[2:3])
    copies.wait()
    q_out[...] = b16(dot_nn(h_out[pl.ds(4 * tok, tok), :], full[:, pl.ds(0, width)]) + vec[4:5])

    def project(number, carry):
        col = pl.multiple_of(number * 256, 256)
        shift = jnp.where(number >= width // 256, 1.0, 0.0)
        bias_at = lax.rem(number, width // 256)
        piece = vec_out[pl.ds(5, 1), pl.ds(pl.multiple_of(bias_at * 256, 256), 256)]
        kv_out[:, pl.ds(col, 256)] = b16(
            dot_nn(h_out[...], full[:, pl.ds(pl.multiple_of(width + col, 256), 256)]) + piece * shift
        )
        return carry

    lax.fori_loop(0, 2 * width // 256, project, 0)

    def pair(number, carry):
        col = pl.multiple_of(number * 128, 128)
        queries = pair_stack(q_out[:, pl.ds(col, 128)] * jnp.bfloat16(0.125))
        scores = dot_nt(kv_out[:, pl.ds(col, 128)], queries) + bias[...]
        top = jnp.max(scores, axis=0, keepdims=True)
        probs = jnp.exp(scores - top)
        total = jnp.sum(probs, axis=0, keepdims=True)
        mixed = dot_tn(kv_out[:, pl.ds(pl.multiple_of(width + col, 128), 128)], b16(probs))
        a_out[:, pl.ds(col, 128)] = b16(pair_join(mixed / total))
        lse_out[number] = top + jnp.log(total)
        return carry

    lax.fori_loop(0, width // 128, pair, 0, unroll=2)
    residual = f32(xo[pl.ds(0, tok), :]) + dot_nn(a_out[...], wo_out[...]) + vec[6:7]
    r_out[...] = residual
    hat, _rate = norm_parts(residual)
    h2_out[...] = b16(hat * vec[1:2] + vec[3:4])


def feed_tokens(h2, dy, w_up, w_down, upb, act_out, du_out):
    root = math.sqrt(2.0 / math.pi)
    chunk = 256

    def feed(number, carry):
        col = pl.multiple_of(number * chunk, chunk)
        pre = dot_nn(h2[...], w_up[:, pl.ds(col, chunk)]) + upb[pl.ds(0, 1), pl.ds(col, chunk)]
        square = pre * pre
        bend = jnp.tanh(root * pre * (1.0 + 0.044715 * square))
        act = b16(0.5 * pre * (1.0 + bend))
        slope = 0.5 * (1.0 + bend) + 0.5 * pre * (1.0 - bend * bend) * (
            root * (1.0 + 3.0 * 0.044715 * square)
        )
        low = b16(dot_nt(dy[...], w_down[pl.ds(col, chunk), :]) * slope)
        act_out[:, pl.ds(col, chunk)] = act
        du_out[:, pl.ds(col, chunk)] = low
        return carry

    lax.fori_loop(0, w_up.shape[1] // chunk, feed, 0, unroll=True)
    return dot_nt(du_out[...], w_up[...])


def assemble_kernel(own, z1, z2, z3u, z3d, y0, y13, wu_out, wd_out, sems):
    _x, _c, y, z = place()
    rows = own.shape[0] // 2
    copies = Copies(sems)
    pieces = [(own, 2 * z + y)]
    for number, ref in ((0, z1), (1, z2), (3, y0)):
        pieces.append((ref, piece_shard(number, y, z)))
    for number, first in ((4, 0), (6, 2 * rows)):
        pieces.append((y13.at[pl.ds(first, 2 * rows), :], piece_shard(number, y, z)))
    for ref, shard in pieces:
        at = pl.ds(pl.multiple_of(shard * rows, 16), rows)
        copies.add(ref.at[pl.ds(0, rows), :], wu_out.at[at, :])
        copies.add(ref.at[pl.ds(rows, rows), :], wd_out.at[at, :])
    at = pl.ds(pl.multiple_of(piece_shard(2, y, z) * rows, 16), rows)
    copies.add(z3u, wu_out.at[at, :])
    copies.add(z3d, wd_out.at[at, :])
    copies.wait()


def near_kernel(
    h_own, h_c, dy_own, dy_c, upb, y2u, y2d, _wu, _wd,
    h2, dy, act_out, du_out, keep_out, send_out, wu_out, wd_out,
    sems,
):
    _x, _c, y, z = place()
    tok, width = h_own.shape
    rows = width // 8
    copies = Copies(sems)
    at = pl.ds(pl.multiple_of(piece_shard(5, y, z) * rows, 16), rows)
    copies.add(y2u, wu_out.at[at, :])
    copies.add(y2d, wd_out.at[at, :])
    h2[pl.ds(0, tok), :] = h_own[...]
    h2[pl.ds(tok, tok), :] = h_c[...]
    dy[pl.ds(0, tok), :] = dy_own[...]
    dy[pl.ds(tok, tok), :] = dy_c[...]
    copies.wait()
    grad = feed_tokens(h2, dy, wu_out, wd_out, upb, act_out, du_out)
    keep_out[...] = grad[:tok]
    send_out[...] = b16(grad[tok:])


def far_c_kernel(
    h_xc, dy_xc, upb, w_up, w_down, h_near, dy_near, act_near, du_near,
    hs, dys, acts, dus, send_out,
    sems,
):
    tok = dy_xc.shape[0]
    copies = Copies(sems)
    for source, target in ((h_near, hs), (dy_near, dys), (act_near, acts), (du_near, dus)):
        copies.add(source, target.at[pl.ds(0, 2 * tok), :])
    last = pl.ds(3 * tok, tok)
    hs[last, :] = h_xc[...]
    dys[last, :] = dy_xc[...]
    send_out[...] = b16(
        feed_tokens(h_xc, dy_xc, w_up, w_down, upb, acts.at[last, :], dus.at[last, :])
    )
    copies.wait()


def far_x_kernel(
    h_x, dy_x, upb, w_up, w_down, _hs, _dys, _acts, _dus,
    hs, dys, acts, dus, keep_out,
):
    tok = dy_x.shape[0]
    third = pl.ds(2 * tok, tok)
    hs[third, :] = h_x[...]
    dys[third, :] = dy_x[...]
    keep_out[...] = feed_tokens(h_x, dy_x, w_up, w_down, upb, acts.at[third, :], dus.at[third, :])


def weights_kernel(
    hs, dys, acts, dus, w_down,
    u_out, d_out, upb_out, keep_out, send_out,
    stage, sems,
):
    _x, _c, y, z = place()
    width = hs.shape[1]
    rows = width // 8
    upb_out[...] = jnp.sum(f32(dus[...]), axis=0, keepdims=True)

    def weight(number, carry):
        col = pl.multiple_of(number * 256, 256)
        stage[0, pl.ds(col, 256), :] = b16(dot_tn(hs[:, pl.ds(col, 256)], dus[...]))
        stage[1, pl.ds(col, 256), :] = b16(dot_tn(acts[:, pl.ds(col, 256)], dys[...]))
        return carry

    lax.fori_loop(0, width // 256, weight, 0)
    outs = Copies(sems)
    for shard in range(8):
        zz = lax.rem(shard // 2 + 4 - z, 4)
        yy = jnp.where(y == shard % 2, 0, 1)
        outs.add(stage.at[0, pl.ds(shard * rows, rows), :], u_out.at[yy, zz])
        outs.add(stage.at[1, pl.ds(shard * rows, rows), :], d_out.at[yy, zz])
    tok = hs.shape[0] // 4
    for number in range(4):
        part = dot_nn(acts[pl.ds(number * tok, tok), :], w_down[...])
        if number % 2:
            send_out[number // 2] = b16(part)
        else:
            keep_out[number // 2] = part
    outs.wait()


def scatter(stage, other, mine, sems):
    x, c, y, z = place()
    outs = Copies(sems)
    for shard in range(8):
        zz = lax.rem(shard // 2 + 4 - z, 4)
        yy = jnp.where(y == shard % 2, 0, 1)
        for xx in range(2):
            far = jnp.where(x == xx, 0, 1)
            outs.add(stage.at[1 - c, xx, shard], other.at[far, yy, zz])
            outs.add(stage.at[c, xx, shard], mine.at[far, yy, zz])
    outs.wait()


def post_kernel(
    residual, own, near, across, dy_in, vec_in, w_out, a_in,
    dr_out, da_out, dw_out, vec_out,
):
    vec = vec_in[...]
    grad_hidden = own[...] + f32(near[...]) + f32(across[...])
    hat, rate = norm_parts(residual[...])
    dy = f32(dy_in[...])
    grad_first = dy + norm_back(grad_hidden, hat, rate, vec[1:2])
    dr_out[...] = grad_first
    low = b16(grad_first)
    da_out[...] = b16(dot_nt(low, w_out[...]))
    dw_out[...] = dot_tn(a_in[...], low)
    zero = jnp.zeros((1, dy.shape[1]), jnp.float32)
    vec_out[...] = jnp.concatenate(
        [
            zero,
            jnp.sum(grad_hidden * hat, axis=0, keepdims=True),
            zero,
            jnp.sum(grad_hidden, axis=0, keepdims=True),
            zero,
            zero,
            jnp.sum(grad_first, axis=0, keepdims=True),
            jnp.sum(dy, axis=0, keepdims=True),
        ],
        axis=0,
    )


def back_pairs(first, q_in, kv_in, lse_in, da_in, bias, dq, dkv):
    width = q_in.shape[1]

    def pair(number, carry):
        col = pl.multiple_of((first + number) * 128, 128)
        vcol = pl.multiple_of(width + col, 128)
        to = pl.multiple_of(number * 128, 128)
        queries = pair_stack(q_in[:, pl.ds(col, 128)] * jnp.bfloat16(0.125))
        grads = pair_stack(da_in[:, pl.ds(col, 128)])
        keys = kv_in[:, pl.ds(col, 128)]
        probs = jnp.exp(dot_nt(keys, queries) + bias[...] - lse_in[first + number])
        dkv[:, pl.ds(pl.multiple_of(width // 2 + to, 128), 128)] = b16(dot_nn(b16(probs), grads))
        term = probs * dot_nt(kv_in[:, pl.ds(vcol, 128)], grads)
        low = b16(term - probs * jnp.sum(term, axis=0, keepdims=True))
        dkv[:, pl.ds(to, 128)] = b16(dot_nn(low, queries))
        dq[:, pl.ds(to, 128)] = b16(pair_join(dot_tn(keys, low)) * 0.125)
        return carry

    lax.fori_loop(0, 3, pair, 0, unroll=first == 0)


def qkv_weight(h_in, dq, dkv, stage, tail):
    tok, part = dq.shape
    keys = h_in.shape[0]

    def weight(number, carry):
        col = pl.multiple_of(number * 384, 384)
        key = dot_tn(h_in[:, pl.ds(col, 384)], dkv[...])
        query = dot_tn(h_in[pl.ds(keys - tok, tok), pl.ds(col, 384)], dq[...])
        for shard in range(4):
            for cc in range(2):
                for xx in range(2):
                    rows = slice(96 * shard + 48 * cc + 24 * xx, 96 * shard + 48 * cc + 24 * xx + 24)
                    blocks = [query[rows], key[rows, :part], key[rows, part:]] + tail(4 * number + shard, 48 * cc + 24 * xx)
                    stage[cc, xx, 4 * number + shard] = b16(jnp.concatenate(blocks, axis=0))
        return carry

    lax.fori_loop(0, 2, weight, 0)


def back_a_kernel(
    start_in, q_in, kv_in, h_in, lse_in, da_in, dw_in,
    other, mine, dq_out, dkv_out,
    bias, stage, sems,
):
    _x, _c, y, z = place()
    mask_bias(start_in[...], 2 * z + y, q_in.shape[0], bias)
    back_pairs(0, q_in, kv_in, lse_in, da_in, bias, dq_out, dkv_out)
    side = q_in.shape[1] // 2

    def out_rows(shard, row):
        rows = dw_in[pl.ds(pl.multiple_of(96 * shard + row, 8), 24), :]
        return [rows[:, :side], rows[:, side:]]

    qkv_weight(h_in, dq_out, dkv_out, stage, out_rows)
    scatter(stage, other, mine, sems)


def back_b_kernel(
    start_in, q_in, kv_in, lse_in, da_in, vec_in, upb_in, dq_a, dkv_a, xo, x1, x2, x3, x4,
    own, g0, g1, g2, g3, g4, g5, g6, g7, g8, g9, g10, g11,
    dq_out, dkv_out, p_own, p_y, p_z, sums_out,
    full, bias, sems,
):
    x, c, y, z = place()
    p = 2 * x + c
    tok, width = q_in.shape
    side = width // 2
    copies = Copies(sems)
    groups = ((g0, g1, g2), (g3, g4, g5), (g6, g7, g8), (g9, g10, g11))
    fetch_qkv(copies, own, groups, full)
    mask_bias(start_in[...], 2 * z + y, tok, bias)
    back_pairs(3, q_in, kv_in, lse_in, da_in, bias, dq_out, dkv_out)
    copies.wait()
    gain_sum = jnp.zeros((1, width), jnp.float32)
    shift_sum = jnp.zeros((1, width), jnp.float32)
    for back, block in enumerate((xo, x1, x2, x3, x4)):
        rows = pl.ds((4 - back) * tok, tok)
        grad = jnp.zeros((tok, width), jnp.float32)
        for number, (dq, dkv) in enumerate(((dq_a, dkv_a), (dq_out, dkv_out))):
            at = number * side
            grad = grad + dot_nt(dkv[rows, pl.ds(0, side)], full[:, pl.ds(width + at, side)])
            grad = grad + dot_nt(dkv[rows, pl.ds(side, side)], full[:, pl.ds(2 * width + at, side)])
            if back == 0:
                grad = grad + dot_nt(dq[...], full[:, pl.ds(at, side)])
        if back == 0:
            p_own[...] = grad
        elif back in (1, 3):
            p_y[back // 2] = b16(grad)
        else:
            p_z[back // 2 - 1] = b16(grad)
        hat, _rate = norm_parts(f32(block[pl.ds(0, tok), :]))
        gain_sum = gain_sum + jnp.sum(grad * hat, axis=0, keepdims=True)
        shift_sum = shift_sum + jnp.sum(grad, axis=0, keepdims=True)
    zero = jnp.zeros((1, width), jnp.float32)
    bias_q = jnp.concatenate([jnp.sum(f32(d[...]), axis=0, keepdims=True) for d in (dq_a, dq_out)], axis=1)
    bias_v = jnp.concatenate(
        [jnp.sum(f32(d[:, pl.ds(side, side)]), axis=0, keepdims=True) for d in (dkv_a, dkv_out)], axis=1
    )
    vec = vec_in[...] + jnp.concatenate(
        [gain_sum, zero, shift_sum, zero, bias_q, bias_v, zero, zero], axis=0
    )
    lane = lax.broadcasted_iota(jnp.int32, (8, 128), 1)
    line = lax.broadcasted_iota(jnp.int32, (8, 128), 0)
    for group in range(2):
        cols = pl.ds(384 * group, 384)
        vec_parts = unpack96(vec[:, 384 * group : 384 * group + 384])
        upb_parts = unpack96(jnp.broadcast_to(upb_in[:, cols], (8, 384)))
        for k in range(4):
            sums_out[4 * group + k] = jnp.concatenate(
                [
                    jnp.where(lane < 96, vec_parts[k], 0.0),
                    jnp.where((lane < 96) & (line == p), upb_parts[k], 0.0),
                ],
                axis=1,
            )


def back_c_kernel(h_in, dq, dkv, sums_in, other, mine, stage, sems):
    blank = jnp.zeros((8, 128), jnp.float32)
    qkv_weight(
        h_in, dq, dkv, stage, lambda shard, _row: [jnp.concatenate([sums_in[shard], blank], axis=1)]
    )
    scatter(stage, other, mine, sems)


def tokens_kernel(own, near, dr, xo, vec_in, grad_out):
    tok = own.shape[0]
    hat, rate = norm_parts(f32(xo[pl.ds(0, tok), :]))
    grad = own[...] + f32(near[...])
    grad_out[...] = dr[...] + norm_back(grad, hat, rate, vec_in[0:1, :])


def finish_f_kernel(f0, fx, fc, fcx, up, down, held):
    x, c, _y, _z = place()
    rows = f0.shape[0] // 2
    for (xx, cc), f in zip(corners(x, c), (f0, fx, fc, fcx), strict=True):
        p = 2 * xx + cc
        held[p] = f[pl.ds(0, rows), :]
        down[pl.ds(pl.multiple_of(rows * p, 16), rows), :] = f32(f[pl.ds(rows, rows), :])
    for group in range(2):
        parts = [unpack96(f32(held[k, :, pl.ds(384 * group, 384)])) for k in range(4)]
        for shard in range(4):
            up[:, pl.ds(384 * (4 * group + shard), 384)] = pack96([part[shard] for part in parts])


def finish_q_kernel(f0, fx, fc, fcx, qkv, out, gains, shifts, biases, up_bias):
    x, c, _y, _z = place()
    side = out.shape[1] // 2
    for (xx, cc), piece in zip(corners(x, c), (f0, fx, fc, fcx), strict=True):
        rows = pl.ds(pl.multiple_of(48 * cc + 24 * xx, 8), 24)
        blocks = f32(piece[...])
        for number in range(3):
            first, second = 24 * number, 24 * (number + 5)
            qkv[rows, pl.ds(2 * side * number, side)] = blocks[first : first + 24]
            qkv[rows, pl.ds(2 * side * number + side, side)] = blocks[second : second + 24]
        out[rows, pl.ds(0, side)] = blocks[72:96]
        out[rows, pl.ds(side, side)] = blocks[96:120]
    sums = f32(f0[...])[192:]
    part = gains.shape[1]
    gains[...] = sums[0:2, :part]
    shifts[...] = sums[2:4, :part]
    biases[...] = sums[4:8, :part]
    ups = sums[:, 128:256]
    packed = pack96([jnp.broadcast_to(ups[k : k + 1], (8, 128)) for k in range(4)])
    up_bias[...] = packed[0]


HB = pl.BlockSpec(memory_space=pltpu.HBM)
VM = pl.BlockSpec(memory_space=pltpu.VMEM)
AN = pl.BlockSpec(memory_space=pl.ANY)


def shape_of(shape, dtype):
    return jax.ShapeDtypeStruct(shape, dtype)


def call(kernel, ins, outs, out_shape, scratch=(), vmem=40, flops=0, moved=0, aliases=None):
    return pl.pallas_call(
        kernel,
        in_specs=ins,
        out_specs=outs,
        out_shape=out_shape,
        scratch_shapes=list(scratch),
        input_output_aliases=aliases or {},
        compiler_params=pltpu.CompilerParams(vmem_limit_bytes=vmem << 20),
        cost_estimate=pl.CostEstimate(flops=flops, bytes_accessed=moved, transcendentals=0),
    )


def fence(*values):
    return lax.optimization_barrier(values)


def swap_rep(value, bit):
    return lax.ppermute(value, "rep", [(k, k ^ bit) for k in range(4)])


def to_core(value):
    return swap_rep(value, 1)


def to_x(value):
    return swap_rep(value, 2)


def to_y(value):
    return lax.ppermute(value, "seq", [(k, k ^ 1) for k in range(8)])


def to_z(value, steps):
    return lax.ppermute(value, "seq", [(k, (k + 2 * steps) % 8) for k in range(8)])


def join(*parts):
    return jnp.concatenate(parts, axis=0)


def on_device_fast(
    tokens,
    segment_ids,
    query_key_value_weight,
    output_weight,
    up_weight,
    down_weight,
    ln_gains,
    ln_biases,
    biases,
    up_projection_bias,
    cotangent,
):
    seq = lax.axis_index("seq")
    y = seq % 2
    tok, width = tokens.shape[1:]
    hidden = up_weight.shape[1]
    keys = 5 * tok
    bf, fl = jnp.bfloat16, jnp.float32
    dma = pltpu.SemaphoreType.DMA
    grad_y = cotangent[0]
    own_tokens, piece_q, piece_f, piece_u, piece_d = call(
        prep_kernel,
        [HB] * 10,
        [VM] * 5,
        [
            shape_of((tok + 8, width), bf),
            shape_of((48, 2 * width + 128), bf),
            shape_of((192, width), bf),
            shape_of((96, width), bf),
            shape_of((96, width), bf),
        ],
        [
            pltpu.VMEM((8, width), fl),
            pltpu.VMEM((96, hidden), bf),
            pltpu.VMEM((2, 96), bf),
            pltpu.VMEM((2, 96), bf),
            pltpu.VMEM((4, 96), bf),
            pltpu.VMEM((1, tok), jnp.int32),
            pltpu.VMEM((384,), bf),
            dma((11,)),
        ],
        vmem=60, moved=4 * 10**6,
    )(
        tokens, segment_ids, query_key_value_weight, output_weight, up_weight, down_weight,
        ln_gains, ln_biases, biases, up_projection_bias,
    )

    q1, q3, q_y0, dy_x = fence(to_z(piece_q, 1), to_z(piece_q, 3), to_y(piece_q), to_x(grad_y))
    own_tokens, piece_f, q1, q_y0 = fence(own_tokens, piece_f, q1, q_y0, q3, dy_x)[:4]
    q2, x2, q_xy0, f_y0 = fence(to_z(q1, 1), to_z(own_tokens, 1), to_x(q_y0), to_y(piece_f))
    q_z = join(q1, q2, q3)
    q_z, x2, piece_d = fence(q_z, x2, piece_d, q_xy0, f_y0)[:3]
    q_y, q_xz, x4, f3d = fence(to_y(q_z), to_x(q_z), to_z(x2, 1), to_z(piece_d, 3))
    near = jnp.where(y == 0, own_tokens, x2)
    far = jnp.where(y == 0, x2, x4)
    near_far, q_y, piece_f, piece_u = fence(
        jnp.stack([near, far]), q_y, piece_f, piece_u, q_xz, f3d
    )[:4]
    crossed, q_xy, f1, f3u = fence(to_y(near_far), to_x(q_y), to_z(piece_f, 1), to_z(piece_u, 3))
    x1, x3 = crossed[0], crossed[1]
    q_z, q_y0, q_y, q_xz, q_xy0, q_xy = fence(q_z, q_y0, q_y, q_xz, q_xy0, q_xy, f1, f3u, crossed)[:6]
    q_cz, q_cy0, q_cy, q_cxz, q_cxy0, q_cxy = fence(
        *(to_core(v) for v in (q_z, q_y0, q_y, q_xz, q_xy0, q_xy))
    )
    f_13, f_1, q_cz = fence(join(f1, f3u, f3d), f1, q_cz, q_cy0, q_cy, q_cxz, q_cxy0, q_cxy)[:3]
    f_y13, f2 = to_y(f_13), to_z(f_1, 1)
    dy_c, dy_xc = to_core(grad_y), to_core(dy_x)

    def pieces(value):
        return value.reshape(value.shape[0] // 48, 48, value.shape[1])

    got_q = [
        pieces(v)
        for v in (q_z, q_y0, q_y, q_xz, q_xy0, q_xy, q_cz, q_cy0, q_cy, q_cxz, q_cxy0, q_cxy)
    ]
    seg = jnp.concatenate([segment_ids, segment_ids], axis=1)
    front = call(
        front_kernel,
        [VM] * 6 + [AN] * 15,
        [VM] * 11,
        [
            shape_of((tok, width), bf),
            shape_of((keys, 2 * width), bf),
            shape_of((keys, width), bf),
            shape_of((tok, width), bf),
            shape_of((width // 128, 1, 2 * tok), fl),
            shape_of((1, 2 * tok), jnp.int32),
            shape_of((8, width), fl),
            shape_of((8, width), fl),
            shape_of((width, width), bf),
            shape_of((tok, width), fl),
            shape_of((tok, width), bf),
        ],
        [
            pltpu.VMEM((width, 3 * width), bf),
            pltpu.VMEM((8, 16, 128), bf),
            pltpu.VMEM((keys, 2 * tok), fl),
            dma((2 + 56,)),
            dma((8,)),
        ],
        flops=7 * 10**9,
        vmem=16, moved=12 * 10**6,
    )(
        seg, own_tokens, x1, x2, x3, x4, piece_q, query_key_value_weight, output_weight, *got_q,
    )
    *front, f_y13, f2, dy_c, dy_xc = fence(*front, f_y13, f2, dy_c, dy_xc)
    queries, kv, normed, attended, lse, start, vec, upb, w_out, residual, hidden_2 = front
    w_half = call(
        assemble_kernel,
        [AN] * 7,
        [VM] * 2,
        [shape_of((width, width), bf)] * 2,
        [dma((14,))],
        vmem=4,
        moved=5 * 10**6,
    )(piece_f, f1, f2, f3u, f3d, f_y0, f_y13)
    h_x, h_c, f_y2u, f_y2d, *w_half = fence(
        to_x(hidden_2), to_core(hidden_2), to_y(f2[:96]), to_z(f_y13[96:192], 1), *w_half
    )
    act = shape_of((2 * tok, width), bf)
    acts = shape_of((4 * tok, width), bf)
    feed_shapes = [shape_of((tok, width), fl), shape_of((tok, width), bf)]
    *near_acts, keep_a, send_a, w_up, w_down = call(
        near_kernel,
        [VM] * 5 + [AN] * 2 + [VM] * 2,
        [VM] * 8,
        [act] * 4 + feed_shapes + [shape_of((width, width), bf)] * 2,
        [dma((2,))],
        flops=3 * 10**9,
        vmem=8,
        moved=6 * 10**6,
        aliases={7: 6, 8: 7},
    )(hidden_2, h_c, grad_y, dy_c, upb, f_y2u, f_y2d, *w_half)
    h_xc = to_core(h_x)
    keep_a, send_a, h_xc, w_up = fence(keep_a, send_a, h_xc, w_up)
    came_a = to_core(send_a)
    *all_acts, send_b = call(
        far_c_kernel,
        [VM] * 5 + [AN] * 4,
        [VM] * 5,
        [acts] * 4 + feed_shapes[1:],
        [dma((4,))],
        flops=15 * 10**8,
        vmem=8,
        moved=6 * 10**6,
    )(h_xc, dy_xc, upb, w_up, w_down, *near_acts)
    send_b, came_a, h_x = fence(send_b, came_a, h_x)
    came_b = to_core(send_b)
    *all_acts, keep_b = call(
        far_x_kernel,
        [VM] * 9,
        [VM] * 5,
        [acts] * 4 + feed_shapes[:1],
        flops=3 * 10**9,
        vmem=8,
        moved=6 * 10**6,
        aliases={5: 0, 6: 1, 7: 2, 8: 3},
    )(h_x, dy_x, upb, w_up, w_down, *all_acts)
    keep_b, came_b, *all_acts = fence(keep_b, came_b, *all_acts)
    back_x = to_x(b16(keep_b + f32(came_b)))
    u_terms, d_terms, upb_g, y_keep, y_send = call(
        weights_kernel,
        [VM] * 5,
        [AN, AN] + [VM] * 3,
        [
            shape_of((2, 4, 96, width), bf),
            shape_of((2, 4, 96, width), bf),
            shape_of((1, width), fl),
            shape_of((2, tok, width), fl),
            shape_of((2, tok, width), bf),
        ],
        [pltpu.VMEM((2, width, width), bf), dma((16,))],
        flops=3 * 10**9,
        vmem=12,
        moved=6 * 10**6,
    )(*all_acts, w_down)
    back_x, u_terms, d_terms, y_send = fence(back_x, u_terms, d_terms, y_send)
    u_came = to_y(u_terms[1])
    came_y = to_core(y_send)
    grad_first, grad_attended, dw_out, vec_g = call(
        post_kernel,
        [VM] * 8,
        [VM] * 4,
        [
            shape_of((tok, width), fl),
            shape_of((tok, width), bf),
            shape_of((width, width), fl),
            shape_of((8, width), fl),
        ],
        vmem=12,
        flops=10**9,
        moved=4 * 10**6,
    )(residual, keep_a, came_a, back_x, grad_y, vec, w_out, attended)
    back_scratch = [
        pltpu.VMEM((keys, 2 * tok), fl),
    ]
    qa_other, qa_mine, dq_a, dkv_a = call(
        back_a_kernel,
        [VM] * 7,
        [AN] * 2 + [VM] * 2,
        [
            shape_of((2, 2, 4, 120, width // 2), bf),
            shape_of((2, 2, 4, 120, width // 2), bf),
            shape_of((tok, width // 2), bf),
            shape_of((keys, width), bf),
        ],
        back_scratch + [pltpu.VMEM((2, 2, 8, 120, width // 2), bf), dma((32,))],
        flops=5 * 10**9,
        vmem=16, moved=10 * 10**6,
    )(start, queries, kv, normed, lse, grad_attended, dw_out)

    def both(mine, came):
        return lambda *index: f32(mine[index]) + f32(came[index])

    def z_sum(part, *came):
        return b16(part(0) + sum(f32(v) for v in came))

    dq_a, qa_other, u_came, came_y, d_send = fence(
        dq_a, qa_other, u_came, came_y, d_terms[1]
    )
    d_came, qa_came = to_y(d_send), to_core(qa_other)
    u_part = both(u_terms[0], u_came)
    u_z = [to_z(b16(u_part(step)), step) for step in (1, 2, 3)]
    dq_b, dkv_b, p_own, p_y, p_z, sums = call(
        back_b_kernel,
        [VM] * 14 + [AN] * 13,
        [VM] * 6,
        [
            shape_of((tok, width // 2), bf),
            shape_of((keys, width), bf),
            shape_of((tok, width), fl),
            shape_of((2, tok, width), bf),
            shape_of((2, tok, width), bf),
            shape_of((8, 8, 256), fl),
        ],
        [pltpu.VMEM((width, 3 * width), bf)] + back_scratch + [dma((1 + 28,))],
        flops=6 * 10**9,
        vmem=20, moved=10 * 10**6,
    )(
        start, queries, kv, lse, grad_attended, vec_g, upb_g, dq_a, dkv_a,
        own_tokens, x1, x2, x3, x4, query_key_value_weight, *got_q,
    )
    dq_b, qa_came, d_came, p_y, *u_z = fence(dq_b, qa_came, d_came, p_y, *u_z)
    p_came = to_y(p_y)
    qa_1 = both(qa_mine, qa_came)
    qa_x = to_x(b16(qa_1(1)))
    d_part = both(d_terms[0], d_came)
    d_z2 = to_z(b16(d_part(2)), 1)
    qb_other, qb_mine = call(
        back_c_kernel,
        [VM] * 4,
        [AN] * 2,
        [
            shape_of((2, 2, 4, 80, width // 2), bf),
            shape_of((2, 2, 4, 80, width // 2), bf),
        ],
        [pltpu.VMEM((2, 2, 8, 80, width // 2), bf), dma((32,))],
        flops=3 * 10**9,
        vmem=12, moved=6 * 10**6,
    )(normed, dq_b, dkv_b, sums)
    qb_came = [to_core(qb_other[k]) for k in range(2)]
    *qb_came, qa_x, p_came, d_z2 = fence(*qb_came, qa_x, p_came, d_z2)
    even = y == 0
    sum_own = p_own + jnp.where(even, f32(p_came[0]), 0.0)
    sum_4 = b16(f32(p_z[1]) + jnp.where(even, 0.0, f32(p_came[1])))
    sum_2 = f32(p_z[0]) + jnp.where(even, f32(p_came[1]), f32(p_came[0]))
    def qa_2(*index):
        return qa_1(0, *index) + f32(qa_x[index])

    def qb_1(side, *index):
        return f32(qb_mine[(side,) + index]) + f32(qb_came[side][index])

    qb_x, qa_y, hop, d_z1, d_z3 = fence(
        to_x(b16(qb_1(1))),
        to_y(b16(qa_2(1))),
        to_z(sum_4, 3),
        to_z(b16(d_part(1) + f32(d_z2)), 1),
        to_z(b16(d_part(3)), 3),
    )

    def qb_2(*index):
        return qb_1(0, *index) + f32(qb_x[index])

    f_tot = join(z_sum(u_part, *u_z), z_sum(d_part, d_z1, d_z3))
    fy_tot = join(f_tot, b16(y_keep[1] + f32(came_y[1])))
    qb_y, back_2, f_tot, fy_tot = fence(
        to_y(b16(qb_2(1))), to_z(b16(sum_2 + f32(hop)), 3), f_tot, fy_tot
    )

    def q_3(*index):
        first = qa_2(0, *index) + f32(qa_y[index])
        return jnp.concatenate([first, qb_2(0, *index) + f32(qb_y[index])], axis=-2)

    grad_tokens = call(
        tokens_kernel, [VM] * 5, VM, shape_of((tok, width), fl), vmem=4, moved=3 * 10**6
    )(sum_own, back_2, grad_first, own_tokens, vec)
    *q_z, over_x, f_tot = fence(*(to_z(b16(q_3(step)), step) for step in (1, 2, 3)), to_x(fy_tot), f_tot)
    f_x, back_y = over_x[:tok], over_x[tok:]
    q_sum = z_sum(q_3, *q_z)
    q_fx, q_fc = to_x(q_sum), to_core(q_sum)
    grad_up, grad_down = call(
        finish_f_kernel,
        [VM] * 4,
        [VM] * 2,
        [shape_of(up_weight.shape, fl), shape_of(down_weight.shape, fl)],
        [pltpu.VMEM((4, 96, width), bf)],
        vmem=8,
        moved=4 * 10**6,
    )(f_tot, f_x, to_core(f_tot), to_core(f_x))
    q_fx, q_fc, grad_up, grad_down = fence(q_fx, q_fc, grad_up, grad_down)
    q_fxc = to_core(q_fx)
    result = b16(residual + vec[7:8] + y_keep[0] + f32(came_y[0]) + f32(back_y))
    grad_qkv, grad_out, grad_gains, grad_shifts, grad_biases, grad_up_bias = call(
        finish_q_kernel,
        [VM] * 4,
        [VM] * 6,
        [
            shape_of(query_key_value_weight.shape, fl),
            shape_of(output_weight.shape, fl),
            shape_of(ln_gains.shape, fl),
            shape_of(ln_biases.shape, fl),
            shape_of(biases.shape, fl),
            shape_of(up_projection_bias.shape, fl),
        ],
        vmem=8,
        moved=3 * 10**6,
    )(q_sum, q_fx, q_fc, q_fxc)
    return (
        result[None],
        grad_tokens[None],
        grad_qkv,
        grad_out,
        grad_up,
        grad_down,
        grad_gains,
        grad_shifts,
        grad_biases,
        grad_up_bias,
    )


def solution(mesh):
    placed = (
        P("rep", "seq", None),
        P("rep", "seq"),
        P("seq", None),
        P("seq", None),
        P("seq", None),
        P("seq", None),
        P(None, "seq"),
        P(None, "seq"),
        P(None, "seq"),
        P("seq"),
        P("rep", "seq", None),
    )
    shape = dict(mesh.shape)
    small_slice = shape["rep"] == 4 and shape["seq"] == 8
    return jax.shard_map(
        on_device_fast if small_slice else on_device,
        mesh=mesh,
        in_specs=placed,
        out_specs=(
            P("rep", "seq", None),
            P("rep", "seq", None),
            P("seq", None),
            P("seq", None),
            P("seq", None),
            P("seq", None),
            P(None, "seq"),
            P(None, "seq"),
            P(None, "seq"),
            P("seq"),
        ),
        check_vma=False,
    )
```

```python
import math

import jax
import jax.numpy as jnp
from jax import lax
from jax.experimental import pallas as pl
from jax.experimental.pallas import tpu as pltpu
from jax.sharding import PartitionSpec as P

HEADS = 12
HD = 64


norm_eps = 1e-05
floor_score = -1e30


def layer_norm(values, gain, shift):
    center = values - jnp.mean(values, axis=-1, keepdims=True)
    spread = jnp.mean(center * center, axis=-1, keepdims=True)
    return center * lax.rsqrt(spread + norm_eps) * gain + shift


def head_split(matrix):
    return matrix.reshape(matrix.shape[0], HEADS, HD)


def masked_scores(queries, query_seg, query_pos, key_piece, seg_piece, offset):
    rows = key_piece.shape[0]
    scores = jnp.einsum(
        "qhd,khd->hqk", queries, head_split(key_piece), preferred_element_type=jnp.float32
    ) * HD ** (-0.5)
    key_pos = offset + jnp.arange(rows, dtype=jnp.int32)
    allowed = (query_seg[:, None] == seg_piece[None, :]) & (key_pos[None, :] <= query_pos[:, None])
    return (jnp.where(allowed[None], scores, floor_score), allowed)


def forward_block(running, pieces, offset, queries, query_seg, query_pos):
    top_run, total_run, accum = running
    key_piece, value_piece, seg_piece = pieces
    scores, allowed = masked_scores(queries, query_seg, query_pos, key_piece, seg_piece, offset)
    top_new = jnp.maximum(top_run, jnp.max(scores, axis=-1))
    probs = jnp.where(allowed[None], jnp.exp(scores - top_new[:, :, None]), 0.0)
    factor = jnp.exp(top_run - top_new)
    total_new = total_run * factor + jnp.sum(probs, axis=-1)
    update = jnp.einsum(
        "hqk,khd->qhd",
        probs.astype(jnp.bfloat16),
        head_split(value_piece),
        preferred_element_type=jnp.float32,
    )
    return (top_new, total_new, accum * factor.T[:, :, None] + update)


def in_blocks(block_fn, running, pieces):
    rows = pieces[0].shape[0]
    size = math.gcd(rows, 1024)
    stacked = tuple((member.reshape((rows // size, size) + member.shape[1:]) for member in pieces))
    offsets = jnp.arange(rows // size, dtype=jnp.int32) * size

    def scan_step(state_now, element):
        return (block_fn(state_now, element[0], element[1]), None)

    running, _unused = lax.scan(scan_step, running, (stacked, offsets))
    return running


def backward_block(
    number,
    state_now,
    whole,
    queries,
    query_seg,
    query_pos,
    grad_heads,
    log_total,
    delta,
    block_rows,
):
    grad_query, term = state_now
    offset = number * block_rows
    key_piece = lax.dynamic_slice_in_dim(whole[0], offset, block_rows, 0)
    value_piece = lax.dynamic_slice_in_dim(whole[1], offset, block_rows, 0)
    seg_piece = lax.dynamic_slice_in_dim(whole[2], offset, block_rows, 0)
    scores, allowed = masked_scores(queries, query_seg, query_pos, key_piece, seg_piece, offset)
    probs = jnp.where(allowed[None], jnp.exp(scores - log_total[:, :, None]), 0.0)
    grad_probs = jnp.einsum(
        "qhd,khd->hqk", grad_heads, head_split(value_piece), preferred_element_type=jnp.float32
    )
    grad_scores = (probs * (grad_probs - delta[:, :, None])).astype(jnp.bfloat16)
    grad_query = grad_query + jnp.einsum(
        "hqk,khd->qhd", grad_scores, head_split(key_piece), preferred_element_type=jnp.float32
    )
    grad_key = jnp.einsum(
        "hqk,qhd->khd", grad_scores, queries, preferred_element_type=jnp.float32
    ) * HD ** (-0.5)
    grad_value = jnp.einsum(
        "hqk,qhd->khd", probs.astype(jnp.bfloat16), grad_heads, preferred_element_type=jnp.float32
    )
    joined = jnp.concatenate(
        [grad_key.reshape(block_rows, -1), grad_value.reshape(block_rows, -1)], axis=1
    )
    term = lax.dynamic_update_slice_in_dim(term, joined, offset, 0)
    return (grad_query, term)


def on_device(
    tokens,
    segment_ids,
    query_key_value_weight,
    output_weight,
    up_weight,
    down_weight,
    ln_gains,
    ln_biases,
    biases,
    up_projection_bias,
    cotangent,
):
    gathered = (
        lax.all_gather(query_key_value_weight, "seq", axis=0, tiled=True),
        lax.all_gather(output_weight, "seq", axis=0, tiled=True),
        lax.all_gather(up_weight, "seq", axis=0, tiled=True),
        lax.all_gather(down_weight, "seq", axis=0, tiled=True),
        lax.all_gather(ln_gains, "seq", axis=1, tiled=True),
        lax.all_gather(ln_biases, "seq", axis=1, tiled=True),
        lax.all_gather(biases, "seq", axis=1, tiled=True),
        lax.all_gather(up_projection_bias, "seq", axis=0, tiled=True),
    )
    full_qkv, full_out, full_up, full_down, gains_all, shifts_all, biases_all, up_shift = gathered
    gains_f = gains_all.astype(jnp.float32)
    shifts_f = shifts_all.astype(jnp.float32)
    biases_f = biases_all.astype(jnp.float32)
    up_shift_f = up_shift.astype(jnp.float32)
    tokens_f = tokens[0].astype(jnp.float32)
    seg_local = segment_ids[0]
    tok_rows = tokens_f.shape[0]
    width = tokens_f.shape[1]
    seqlen = tok_rows * lax.axis_size("seq")
    query_pos = lax.axis_index("seq") * tok_rows + jnp.arange(tok_rows, dtype=jnp.int32)
    hidden_first = layer_norm(tokens_f, gains_f[0], shifts_f[0]).astype(jnp.bfloat16)
    query_key_value_bias = jnp.concatenate(
        [biases_f[0], jnp.zeros((width,), jnp.float32), biases_f[1]]
    )
    projected_rows = (
        jnp.dot(hidden_first, full_qkv, preferred_element_type=jnp.float32) + query_key_value_bias
    ).astype(jnp.bfloat16)
    queries = head_split(projected_rows[:, :width])
    key_rows = projected_rows[:, width : 2 * width]
    value_rows = projected_rows[:, 2 * width :]
    initial = (
        jnp.full((HEADS, tok_rows), floor_score, jnp.float32),
        jnp.zeros((HEADS, tok_rows), jnp.float32),
        jnp.zeros((tok_rows, HEADS, HD), jnp.float32),
    )

    def block_fn(running, pieces, offset):
        return forward_block(running, pieces, offset, queries, seg_local, query_pos)

    block_rows = math.gcd(seqlen, 1024)
    key_end = (lax.axis_index("seq") + 1) * tok_rows
    block_count = (key_end + block_rows - 1) // block_rows
    top_run, total_run, accum = in_blocks(
        block_fn,
        initial,
        (
            lax.all_gather(key_rows, "seq", axis=0, tiled=True),
            lax.all_gather(value_rows, "seq", axis=0, tiled=True),
            lax.all_gather(seg_local, "seq", axis=0, tiled=True),
        ),
    )
    log_total = top_run + jnp.log(total_run)
    attended_f = accum / total_run.T[:, :, None]
    attention_result = attended_f.reshape(tok_rows, width).astype(jnp.bfloat16)
    residual_first = (
        tokens_f
        + jnp.dot(attention_result, full_out, preferred_element_type=jnp.float32)
        + biases_f[2]
    )
    hidden_second = layer_norm(residual_first, gains_f[1], shifts_f[1]).astype(jnp.bfloat16)
    upward_rows = jnp.dot(hidden_second, full_up, preferred_element_type=jnp.float32) + up_shift_f
    activated_f, gelu_back = jax.vjp(jax.nn.gelu, upward_rows)
    activation_values = activated_f.astype(jnp.bfloat16)
    result = (
        residual_first
        + jnp.dot(activation_values, full_down, preferred_element_type=jnp.float32)
        + biases_f[3]
    )
    grad_y = cotangent[0]
    grad_y_f = grad_y.astype(jnp.float32)
    grad_down = jnp.einsum(
        "tf,td->fd", activation_values, grad_y, preferred_element_type=jnp.float32
    )
    grad_act = jnp.einsum("td,fd->tf", grad_y, full_down, preferred_element_type=jnp.float32)
    grad_up_pre = gelu_back(grad_act)[0].astype(jnp.bfloat16)
    grad_up = jnp.einsum(
        "td,tf->df", hidden_second, grad_up_pre, preferred_element_type=jnp.float32
    )
    grad_hidden_two = jnp.einsum(
        "tf,df->td", grad_up_pre, full_up, preferred_element_type=jnp.float32
    )
    _unused, norm_two_back = jax.vjp(layer_norm, residual_first, gains_f[1], shifts_f[1])
    grad_sum_part, grad_gain_two, grad_shift_two = norm_two_back(grad_hidden_two)
    grad_first = grad_y_f + grad_sum_part
    grad_first_bf = grad_first.astype(jnp.bfloat16)
    grad_out_w = jnp.einsum(
        "td,te->de", attention_result, grad_first_bf, preferred_element_type=jnp.float32
    )
    grad_attended = jnp.einsum(
        "te,de->td", grad_first_bf, full_out, preferred_element_type=jnp.float32
    ).astype(jnp.bfloat16)
    grad_heads = head_split(grad_attended)
    delta = jnp.einsum("qhd,qhd->hq", grad_heads.astype(jnp.float32), attended_f)
    whole = (
        lax.all_gather(key_rows, "seq", axis=0, tiled=True),
        lax.all_gather(value_rows, "seq", axis=0, tiled=True),
        lax.all_gather(seg_local, "seq", axis=0, tiled=True),
    )

    def backward_step(number, state_now):
        return backward_block(
            number,
            state_now,
            whole,
            queries,
            seg_local,
            query_pos,
            grad_heads,
            log_total,
            delta,
            block_rows,
        )

    start_state = (
        jnp.zeros((tok_rows, HEADS, HD), jnp.float32),
        jnp.zeros((seqlen, 2 * width), jnp.float32),
    )
    grad_query, term = lax.fori_loop(0, block_count, backward_step, start_state)
    grad_kv = lax.psum_scatter(term, "seq", scatter_dimension=0, tiled=True).astype(jnp.bfloat16)
    grad_q = (grad_query * HD ** (-0.5)).reshape(tok_rows, width).astype(jnp.bfloat16)
    grad_proj = jnp.concatenate([grad_q, grad_kv], axis=1)
    grad_qkv_w = jnp.einsum(
        "td,te->de", hidden_first, grad_proj, preferred_element_type=jnp.float32
    )
    grad_hidden_one = jnp.einsum(
        "te,de->td", grad_proj, full_qkv, preferred_element_type=jnp.float32
    )
    _unused_two, norm_one_back = jax.vjp(layer_norm, tokens_f, gains_f[0], shifts_f[0])
    grad_in_part, grad_gain_one, grad_shift_one = norm_one_back(grad_hidden_one)
    grad_tokens = grad_first + grad_in_part
    grad_proj_f = grad_proj.astype(jnp.float32)
    grad_bias_rows = jnp.stack(
        [
            jnp.sum(grad_proj_f[:, :width], axis=0),
            jnp.sum(grad_proj_f[:, 2 * width :], axis=0),
            jnp.sum(grad_first, axis=0),
            jnp.sum(grad_y_f, axis=0),
        ]
    )
    grad_up_shift = jnp.sum(grad_up_pre.astype(jnp.float32), axis=0)
    grad_gains = jnp.stack([grad_gain_one, grad_gain_two])
    grad_shifts = jnp.stack([grad_shift_one, grad_shift_two])
    shares = (
        lax.psum_scatter(grad_qkv_w, "seq", scatter_dimension=0, tiled=True),
        lax.psum_scatter(grad_out_w, "seq", scatter_dimension=0, tiled=True),
        lax.psum_scatter(grad_up, "seq", scatter_dimension=0, tiled=True),
        lax.psum_scatter(grad_down, "seq", scatter_dimension=0, tiled=True),
        lax.psum_scatter(grad_gains, "seq", scatter_dimension=1, tiled=True),
        lax.psum_scatter(grad_shifts, "seq", scatter_dimension=1, tiled=True),
        lax.psum_scatter(grad_bias_rows, "seq", scatter_dimension=1, tiled=True),
        lax.psum_scatter(grad_up_shift, "seq", scatter_dimension=0, tiled=True),
    )
    totals = (
        lax.psum(shares[0].astype(jnp.bfloat16), "rep").astype(jnp.float32),
        lax.psum(shares[1].astype(jnp.bfloat16), "rep").astype(jnp.float32),
        lax.psum(shares[2].astype(jnp.bfloat16), "rep").astype(jnp.float32),
        lax.psum(shares[3].astype(jnp.bfloat16), "rep").astype(jnp.float32),
        lax.psum(shares[4].astype(jnp.bfloat16), "rep").astype(jnp.float32),
        lax.psum(shares[5].astype(jnp.bfloat16), "rep").astype(jnp.float32),
        lax.psum(shares[6].astype(jnp.bfloat16), "rep").astype(jnp.float32),
        lax.psum(shares[7].astype(jnp.bfloat16), "rep").astype(jnp.float32),
    )
    return (
        result.astype(jnp.bfloat16)[None],
        grad_tokens[None],
        totals[0],
        totals[1],
        totals[2],
        totals[3],
        totals[4],
        totals[5],
        totals[6],
        totals[7],
    )


def f32(value):
    return value.astype(jnp.float32)


def b16(value):
    return value.astype(jnp.bfloat16)


def dot_nn(left, right):
    return jnp.dot(left, right, preferred_element_type=jnp.float32)


def dot_nt(left, right):
    return lax.dot_general(
        left, right, (((1,), (1,)), ((), ())), preferred_element_type=jnp.float32
    )


def dot_tn(left, right):
    return lax.dot_general(
        left, right, (((0,), (0,)), ((), ())), preferred_element_type=jnp.float32
    )


def norm_parts(values):
    center = values - jnp.mean(values, axis=-1, keepdims=True)
    rate = lax.rsqrt(jnp.mean(center * center, axis=-1, keepdims=True) + norm_eps)
    return center * rate, rate


def norm_back(grad, hat, rate, gain):
    scaled = grad * gain
    return rate * (
        scaled
        - jnp.mean(scaled, axis=-1, keepdims=True)
        - hat * jnp.mean(scaled * hat, axis=-1, keepdims=True)
    )


def place():
    rep, seq = lax.axis_index("rep"), lax.axis_index("seq")
    return lax.div(rep, 2), lax.rem(rep, 2), lax.rem(seq, 2), lax.div(seq, 2)


def piece_shard(number, y, z):
    if number < 3:
        return 2 * lax.rem(z + 3 - number, 4) + y
    return 2 * lax.rem(z + 7 - number, 4) + 1 - y


def pack96(parts):
    lane = lax.broadcasted_iota(jnp.int32, parts[0].shape, 1)
    one, two, three = (pltpu.roll(parts[k], 128 - 32 * k, 1) for k in (1, 2, 3))
    return jnp.concatenate(
        [
            jnp.where(lane < 96, parts[0], one),
            jnp.where(lane < 64, one, two),
            jnp.where(lane < 32, two, three),
        ],
        axis=1,
    )


def unpack96(block):
    tiles = [block[:, 128 * k : 128 * k + 128] for k in range(3)]
    lane = lax.broadcasted_iota(jnp.int32, tiles[0].shape, 1)
    return [
        tiles[0],
        jnp.where(lane < 32, pltpu.roll(tiles[0], 32, 1), pltpu.roll(tiles[1], 32, 1)),
        jnp.where(lane < 64, pltpu.roll(tiles[1], 64, 1), pltpu.roll(tiles[2], 64, 1)),
        pltpu.roll(tiles[2], 96, 1),
    ]


def choose(parts, index):
    out = parts[0]
    for number in range(1, len(parts)):
        out = jnp.where(index == number, parts[number], out)
    return out


class Copies:
    def __init__(self, sems, first=0):
        self.sems = sems
        self.first = first
        self.held = []

    def add(self, source, target):
        copy = pltpu.make_async_copy(source, target, self.sems.at[self.first + len(self.held)])
        copy.start()
        self.held.append(copy)

    def wait(self):
        for copy in self.held:
            copy.wait()
        self.held = []


def corners(x, c):
    return ((x, c), (1 - x, c), (x, 1 - c), (1 - x, 1 - c))


def fetch_qkv(copies, own, groups, full, full_out=None, own_out=None):
    x, c, y, z = place()
    rows = own.shape[0]
    half, width = rows // 2, own.shape[1] // 3
    row = pl.multiple_of((2 * z + y) * rows, 16)
    copies.add(own, full.at[pl.ds(row, rows), :])
    if full_out is not None:
        copies.add(own_out, full_out.at[pl.ds(row, rows), :])
    wide, side = 3 * width // 2, width // 2
    for number in range(7):
        for (xx, cc), group in zip(corners(x, c), groups, strict=True):
            piece = piece_of(group, number)
            at = pl.ds(pl.multiple_of(piece_shard(number, y, z) * rows + half * cc, 16), half)
            copies.add(
                piece.at[pl.ds(0, half), pl.ds(0, wide)],
                full.at[at, pl.ds(pl.multiple_of(wide * xx, 128), wide)],
            )
            if full_out is not None:
                copies.add(
                    piece.at[pl.ds(0, half), pl.ds(wide, side)],
                    full_out.at[at, pl.ds(pl.multiple_of(side * xx, 128), side)],
                )


def piece_of(group, number):
    behind, across, behind_across = group
    if number < 3:
        return behind.at[number]
    return across.at[0] if number == 3 else behind_across.at[number - 4]


def mask_bias(start, me, tok, target):
    keys, lanes = target.shape
    key_pos = (me - 4) * tok + lax.broadcasted_iota(jnp.int32, (keys, lanes), 0)
    lane = lax.broadcasted_iota(jnp.int32, (keys, lanes), 1)
    query_pos = me * tok + jnp.where(lane >= tok, lane - tok, lane)
    target[...] = jnp.where((key_pos >= start) & (key_pos <= query_pos), 0.0, floor_score)


def pair_stack(rows):
    lane = lax.broadcasted_iota(jnp.int32, rows.shape, 1)
    zero = jnp.zeros_like(rows)
    return jnp.concatenate([jnp.where(lane < HD, rows, zero), jnp.where(lane < HD, zero, rows)], axis=0)


def pair_join(transposed):
    both = transposed.T
    tok = both.shape[0] // 2
    lane = lax.broadcasted_iota(jnp.int32, (tok, 2 * HD), 1)
    return jnp.where(lane < HD, both[:tok], both[tok:])


def prep_kernel(
    tokens, segs, qkv, out, up, down, gains, shifts, biases, up_bias,
    t_out, q_out, f_out, fu_out, fd_out,
    scratch, wide, held_g, held_s, held_b, ids, line, sems,
):
    x, c, _y, _z = place()
    tok, width = tokens.shape[1:]
    rows = qkv.shape[0]
    half, side = rows // 2, width // 2
    p = 2 * x + c
    at = pl.ds(pl.multiple_of(half * c, 16), half)
    copies, others = Copies(sems), Copies(sems, 5)
    for source, target in ((gains, held_g), (shifts, held_s), (biases, held_b)):
        copies.add(source, target)
    copies.add(segs, ids)
    copies.add(up_bias, line)
    others.add(up, wide)
    wide_cols = 3 * side
    others.add(
        qkv.at[at, pl.ds(pl.multiple_of(wide_cols * x, 128), wide_cols)],
        q_out.at[pl.ds(0, half), pl.ds(0, wide_cols)],
    )
    others.add(
        out.at[at, pl.ds(pl.multiple_of(side * x, 128), side)],
        q_out.at[pl.ds(0, half), pl.ds(wide_cols, side)],
    )
    others.add(tokens.at[0], t_out.at[pl.ds(0, tok), :])
    own_rows = down.at[pl.ds(pl.multiple_of(rows * p, 16), rows), :]
    others.add(own_rows, f_out.at[pl.ds(rows, rows), :])
    others.add(own_rows, fd_out)
    copies.wait()
    scratch[...] = jnp.zeros_like(scratch)
    for first, held in ((0, held_g), (2, held_s), (4, held_b)):
        scratch[pl.ds(first, held.shape[0]), pl.ds(0, rows)] = f32(held[...])
    parts = unpack96(jnp.broadcast_to(f32(line[...]).reshape(1, line.shape[0]), (8, line.shape[0])))
    lane = lax.broadcasted_iota(jnp.int32, (8, 128), 1)
    row = lax.broadcasted_iota(jnp.int32, (8, 128), 0)
    ups = jnp.zeros((8, 128), jnp.float32)
    for number in range(4):
        ups = jnp.where((row == number) & (lane < rows), parts[number], ups)
    smalls = b16(jnp.concatenate([scratch[:, pl.ds(0, 128)], ups], axis=0))
    q_out[pl.ds(0, 16), pl.ds(2 * width, 128)] = smalls
    q_out[pl.ds(16, half - 16), pl.ds(2 * width, 128)] = jnp.zeros((half - 16, 128), jnp.bfloat16)
    scratch[...] = jnp.zeros_like(scratch)
    scratch[pl.ds(0, 1), pl.ds(0, tok)] = f32(ids[...])
    t_out[pl.ds(tok, 8), :] = b16(scratch[...])
    others.wait()
    for group in range(2):
        parts = []
        for shard in range(4 * group, 4 * group + 4):
            parts.append(choose(unpack96(f32(wide[:, pl.ds(384 * shard, 384)])), p))
        packed = b16(pack96(parts))
        f_out[pl.ds(0, rows), pl.ds(384 * group, 384)] = packed
        fu_out[:, pl.ds(384 * group, 384)] = packed


def front_kernel(
    seg, xo, x1, x2, x3, x4, first, own, own_o,
    g0, g1, g2, g3, g4, g5, g6, g7, g8, g9, g10, g11,
    q_out, kv_out, h_out, a_out, lse_out, start_out, vec_out, upb_out, wo_out, r_out, h2_out,
    full, small, bias, sems, vsems,
):
    x, c, y, z = place()
    me = 2 * z + y
    p = 2 * x + c
    tok, width = q_out.shape
    copies, vcopies = Copies(sems), Copies(vsems)
    vcopies.add(first.at[pl.ds(0, 16), pl.ds(2 * width, 128)], small.at[me])
    for number in range(7):
        source = piece_of((g0, g1, g2), number)
        vcopies.add(source.at[pl.ds(0, 16), pl.ds(2 * width, 128)], small.at[piece_shard(number, y, z)])
    groups = ((g0, g1, g2), (g3, g4, g5), (g6, g7, g8), (g9, g10, g11))
    fetch_qkv(copies, own, groups, full, wo_out, own_o)
    blocks = (xo, x1, x2, x3, x4)
    lane1 = lax.broadcasted_iota(jnp.int32, (1, tok), 1)
    start = jnp.full(seg.shape, 1 << 30, jnp.int32)
    for number in range(4):
        first_pos = jnp.full((1, 1), 1 << 30, jnp.int32)
        for back in range(5):
            ids = f32(blocks[back][pl.ds(tok, 8), pl.ds(0, tok)])[:1]
            pos = (me - back) * tok + lane1
            hit = (ids == float(number)) & (pos >= 0)
            first_pos = jnp.minimum(
                first_pos, jnp.min(jnp.where(hit, pos, 1 << 30), axis=1, keepdims=True)
            )
        start = jnp.where(seg[...] == number, first_pos, start)
    start_out[...] = start
    mask_bias(start, me, tok, bias)
    vcopies.wait()
    for group in range(2):
        held = [f32(small[4 * group + k]) for k in range(4)]
        vec_out[:, pl.ds(384 * group, 384)] = pack96([block[:8] for block in held])
        upb_out[:, pl.ds(384 * group, 384)] = pack96(
            [choose([jnp.broadcast_to(block[k : k + 1], (8, 128)) for k in range(8, 12)], p) for block in held]
        )
    vec = vec_out[...]
    for back in range(5):
        hat, _rate = norm_parts(f32(blocks[back][pl.ds(0, tok), :]))
        h_out[pl.ds((4 - back) * tok, tok), :] = b16(hat * vec[0:1] + vec[2:3])
    copies.wait()
    q_out[...] = b16(dot_nn(h_out[pl.ds(4 * tok, tok), :], full[:, pl.ds(0, width)]) + vec[4:5])

    def project(number, carry):
        col = pl.multiple_of(number * 256, 256)
        shift = jnp.where(number >= width // 256, 1.0, 0.0)
        bias_at = lax.rem(number, width // 256)
        piece = vec_out[pl.ds(5, 1), pl.ds(pl.multiple_of(bias_at * 256, 256), 256)]
        kv_out[:, pl.ds(col, 256)] = b16(
            dot_nn(h_out[...], full[:, pl.ds(pl.multiple_of(width + col, 256), 256)]) + piece * shift
        )
        return carry

    lax.fori_loop(0, 2 * width // 256, project, 0)

    def pair(number, carry):
        col = pl.multiple_of(number * 128, 128)
        queries = pair_stack(q_out[:, pl.ds(col, 128)] * jnp.bfloat16(0.125))
        scores = dot_nt(kv_out[:, pl.ds(col, 128)], queries) + bias[...]
        top = jnp.max(scores, axis=0, keepdims=True)
        probs = jnp.exp(scores - top)
        total = jnp.sum(probs, axis=0, keepdims=True)
        mixed = dot_tn(kv_out[:, pl.ds(pl.multiple_of(width + col, 128), 128)], b16(probs))
        a_out[:, pl.ds(col, 128)] = b16(pair_join(mixed / total))
        lse_out[number] = top + jnp.log(total)
        return carry

    lax.fori_loop(0, width // 128, pair, 0, unroll=3)
    residual = f32(xo[pl.ds(0, tok), :]) + dot_nn(a_out[...], wo_out[...]) + vec[6:7]
    r_out[...] = residual
    hat, _rate = norm_parts(residual)
    h2_out[...] = b16(hat * vec[1:2] + vec[3:4])


def feed_tokens(h2, dy, w_up, w_down, upb, act_out, du_out):
    root = math.sqrt(2.0 / math.pi)
    chunk = 256

    def feed(number, carry):
        col = pl.multiple_of(number * chunk, chunk)
        pre = dot_nn(h2[...], w_up[:, pl.ds(col, chunk)]) + upb[pl.ds(0, 1), pl.ds(col, chunk)]
        square = pre * pre
        bend = jnp.tanh(root * pre * (1.0 + 0.044715 * square))
        act = b16(0.5 * pre * (1.0 + bend))
        slope = 0.5 * (1.0 + bend) + 0.5 * pre * (1.0 - bend * bend) * (
            root * (1.0 + 3.0 * 0.044715 * square)
        )
        low = b16(dot_nt(dy[...], w_down[pl.ds(col, chunk), :]) * slope)
        act_out[:, pl.ds(col, chunk)] = act
        du_out[:, pl.ds(col, chunk)] = low
        return carry

    lax.fori_loop(0, w_up.shape[1] // chunk, feed, 0, unroll=True)
    return dot_nt(du_out[...], w_up[...])


def assemble_kernel(own, z1, z2, z3u, z3d, y0, y13, wu_out, wd_out, sems):
    _x, _c, y, z = place()
    rows = own.shape[0] // 2
    copies = Copies(sems)
    pieces = [(own, 2 * z + y)]
    for number, ref in ((0, z1), (1, z2), (3, y0)):
        pieces.append((ref, piece_shard(number, y, z)))
    for number, first in ((4, 0), (6, 2 * rows)):
        pieces.append((y13.at[pl.ds(first, 2 * rows), :], piece_shard(number, y, z)))
    for ref, shard in pieces:
        at = pl.ds(pl.multiple_of(shard * rows, 16), rows)
        copies.add(ref.at[pl.ds(0, rows), :], wu_out.at[at, :])
        copies.add(ref.at[pl.ds(rows, rows), :], wd_out.at[at, :])
    at = pl.ds(pl.multiple_of(piece_shard(2, y, z) * rows, 16), rows)
    copies.add(z3u, wu_out.at[at, :])
    copies.add(z3d, wd_out.at[at, :])
    copies.wait()


def near_kernel(
    h_own, h_c, dy_own, dy_c, upb, y2u, y2d, _wu, _wd,
    h2, dy, act_out, du_out, keep_out, send_out, wu_out, wd_out,
    sems,
):
    _x, _c, y, z = place()
    tok, width = h_own.shape
    rows = width // 8
    copies = Copies(sems)
    at = pl.ds(pl.multiple_of(piece_shard(5, y, z) * rows, 16), rows)
    copies.add(y2u, wu_out.at[at, :])
    copies.add(y2d, wd_out.at[at, :])
    h2[pl.ds(0, tok), :] = h_own[...]
    h2[pl.ds(tok, tok), :] = h_c[...]
    dy[pl.ds(0, tok), :] = dy_own[...]
    dy[pl.ds(tok, tok), :] = dy_c[...]
    copies.wait()
    grad = feed_tokens(h2, dy, wu_out, wd_out, upb, act_out, du_out)
    keep_out[...] = grad[:tok]
    send_out[...] = b16(grad[tok:])


def far_c_kernel(
    h_xc, dy_xc, upb, w_up, w_down, h_near, dy_near, act_near, du_near,
    hs, dys, acts, dus, send_out,
    sems,
):
    tok = dy_xc.shape[0]
    copies = Copies(sems)
    for source, target in ((h_near, hs), (dy_near, dys), (act_near, acts), (du_near, dus)):
        copies.add(source, target.at[pl.ds(0, 2 * tok), :])
    last = pl.ds(3 * tok, tok)
    hs[last, :] = h_xc[...]
    dys[last, :] = dy_xc[...]
    send_out[...] = b16(
        feed_tokens(h_xc, dy_xc, w_up, w_down, upb, acts.at[last, :], dus.at[last, :])
    )
    copies.wait()


def far_x_kernel(
    h_x, dy_x, upb, w_up, w_down, _hs, _dys, _acts, _dus,
    hs, dys, acts, dus, keep_out,
):
    tok = dy_x.shape[0]
    third = pl.ds(2 * tok, tok)
    hs[third, :] = h_x[...]
    dys[third, :] = dy_x[...]
    keep_out[...] = feed_tokens(h_x, dy_x, w_up, w_down, upb, acts.at[third, :], dus.at[third, :])


def weights_kernel(
    hs, dys, acts, dus, w_down,
    u_out, d_out, upb_out, keep_out, send_out,
    stage, sems,
):
    _x, _c, y, z = place()
    width = hs.shape[1]
    rows = width // 8
    upb_out[...] = jnp.sum(f32(dus[...]), axis=0, keepdims=True)

    def weight(number, carry):
        col = pl.multiple_of(number * 256, 256)
        stage[0, pl.ds(col, 256), :] = b16(dot_tn(hs[:, pl.ds(col, 256)], dus[...]))
        stage[1, pl.ds(col, 256), :] = b16(dot_tn(acts[:, pl.ds(col, 256)], dys[...]))
        return carry

    lax.fori_loop(0, width // 256, weight, 0)
    outs = Copies(sems)
    for shard in range(8):
        zz = lax.rem(shard // 2 + 4 - z, 4)
        yy = jnp.where(y == shard % 2, 0, 1)
        outs.add(stage.at[0, pl.ds(shard * rows, rows), :], u_out.at[yy, zz])
        outs.add(stage.at[1, pl.ds(shard * rows, rows), :], d_out.at[yy, zz])
    tok = hs.shape[0] // 4
    for number in range(4):
        part = dot_nn(acts[pl.ds(number * tok, tok), :], w_down[...])
        if number % 2:
            send_out[number // 2] = b16(part)
        else:
            keep_out[number // 2] = part
    outs.wait()


def scatter(stage, other, mine, sems):
    x, c, y, z = place()
    outs = Copies(sems)
    for shard in range(8):
        zz = lax.rem(shard // 2 + 4 - z, 4)
        yy = jnp.where(y == shard % 2, 0, 1)
        for xx in range(2):
            far = jnp.where(x == xx, 0, 1)
            outs.add(stage.at[1 - c, xx, shard], other.at[far, yy, zz])
            outs.add(stage.at[c, xx, shard], mine.at[far, yy, zz])
    outs.wait()


def post_kernel(
    residual, own, near, across, dy_in, vec_in, w_out, a_in,
    dr_out, da_out, dw_out, vec_out,
):
    vec = vec_in[...]
    grad_hidden = own[...] + f32(near[...]) + f32(across[...])
    hat, rate = norm_parts(residual[...])
    dy = f32(dy_in[...])
    grad_first = dy + norm_back(grad_hidden, hat, rate, vec[1:2])
    dr_out[...] = grad_first
    low = b16(grad_first)
    da_out[...] = b16(dot_nt(low, w_out[...]))
    dw_out[...] = dot_tn(a_in[...], low)
    zero = jnp.zeros((1, dy.shape[1]), jnp.float32)
    vec_out[...] = jnp.concatenate(
        [
            zero,
            jnp.sum(grad_hidden * hat, axis=0, keepdims=True),
            zero,
            jnp.sum(grad_hidden, axis=0, keepdims=True),
            zero,
            zero,
            jnp.sum(grad_first, axis=0, keepdims=True),
            jnp.sum(dy, axis=0, keepdims=True),
        ],
        axis=0,
    )


def back_pairs(first, q_in, kv_in, lse_in, da_in, bias, dq, dkv):
    width = q_in.shape[1]

    def pair(number, carry):
        col = pl.multiple_of((first + number) * 128, 128)
        vcol = pl.multiple_of(width + col, 128)
        to = pl.multiple_of(number * 128, 128)
        queries = pair_stack(q_in[:, pl.ds(col, 128)] * jnp.bfloat16(0.125))
        grads = pair_stack(da_in[:, pl.ds(col, 128)])
        keys = kv_in[:, pl.ds(col, 128)]
        probs = jnp.exp(dot_nt(keys, queries) + bias[...] - lse_in[first + number])
        dkv[:, pl.ds(pl.multiple_of(width // 2 + to, 128), 128)] = b16(dot_nn(b16(probs), grads))
        term = probs * dot_nt(kv_in[:, pl.ds(vcol, 128)], grads)
        low = b16(term - probs * jnp.sum(term, axis=0, keepdims=True))
        dkv[:, pl.ds(to, 128)] = b16(dot_nn(low, queries))
        dq[:, pl.ds(to, 128)] = b16(pair_join(dot_tn(keys, low)) * 0.125)
        return carry

    lax.fori_loop(0, 3, pair, 0, unroll=first == 0)


def qkv_weight(h_in, dq, dkv, stage, tail):
    tok, part = dq.shape
    keys = h_in.shape[0]

    def weight(number, carry):
        col = pl.multiple_of(number * 384, 384)
        key = dot_tn(h_in[:, pl.ds(col, 384)], dkv[...])
        query = dot_tn(h_in[pl.ds(keys - tok, tok), pl.ds(col, 384)], dq[...])
        for shard in range(4):
            for cc in range(2):
                for xx in range(2):
                    rows = slice(96 * shard + 48 * cc + 24 * xx, 96 * shard + 48 * cc + 24 * xx + 24)
                    blocks = [query[rows], key[rows, :part], key[rows, part:]] + tail(4 * number + shard, 48 * cc + 24 * xx)
                    stage[cc, xx, 4 * number + shard] = b16(jnp.concatenate(blocks, axis=0))
        return carry

    lax.fori_loop(0, 2, weight, 0)


def back_a_kernel(
    start_in, q_in, kv_in, h_in, lse_in, da_in, dw_in,
    other, mine, dq_out, dkv_out,
    bias, stage, sems,
):
    _x, _c, y, z = place()
    mask_bias(start_in[...], 2 * z + y, q_in.shape[0], bias)
    back_pairs(0, q_in, kv_in, lse_in, da_in, bias, dq_out, dkv_out)
    side = q_in.shape[1] // 2

    def out_rows(shard, row):
        rows = dw_in[pl.ds(pl.multiple_of(96 * shard + row, 8), 24), :]
        return [rows[:, :side], rows[:, side:]]

    qkv_weight(h_in, dq_out, dkv_out, stage, out_rows)
    scatter(stage, other, mine, sems)


def back_b_kernel(
    start_in, q_in, kv_in, lse_in, da_in, vec_in, upb_in, dq_a, dkv_a, xo, x1, x2, x3, x4,
    own, g0, g1, g2, g3, g4, g5, g6, g7, g8, g9, g10, g11,
    dq_out, dkv_out, p_own, p_y, p_z, sums_out,
    full, bias, sems,
):
    x, c, y, z = place()
    p = 2 * x + c
    tok, width = q_in.shape
    side = width // 2
    copies = Copies(sems)
    groups = ((g0, g1, g2), (g3, g4, g5), (g6, g7, g8), (g9, g10, g11))
    fetch_qkv(copies, own, groups, full)
    mask_bias(start_in[...], 2 * z + y, tok, bias)
    back_pairs(3, q_in, kv_in, lse_in, da_in, bias, dq_out, dkv_out)
    copies.wait()
    gain_sum = jnp.zeros((1, width), jnp.float32)
    shift_sum = jnp.zeros((1, width), jnp.float32)
    for back, block in enumerate((xo, x1, x2, x3, x4)):
        rows = pl.ds((4 - back) * tok, tok)
        grad = jnp.zeros((tok, width), jnp.float32)
        for number, (dq, dkv) in enumerate(((dq_a, dkv_a), (dq_out, dkv_out))):
            at = number * side
            grad = grad + dot_nt(dkv[rows, pl.ds(0, side)], full[:, pl.ds(width + at, side)])
            grad = grad + dot_nt(dkv[rows, pl.ds(side, side)], full[:, pl.ds(2 * width + at, side)])
            if back == 0:
                grad = grad + dot_nt(dq[...], full[:, pl.ds(at, side)])
        if back == 0:
            p_own[...] = grad
        elif back in (1, 3):
            p_y[back // 2] = b16(grad)
        else:
            p_z[back // 2 - 1] = b16(grad)
        hat, _rate = norm_parts(f32(block[pl.ds(0, tok), :]))
        gain_sum = gain_sum + jnp.sum(grad * hat, axis=0, keepdims=True)
        shift_sum = shift_sum + jnp.sum(grad, axis=0, keepdims=True)
    zero = jnp.zeros((1, width), jnp.float32)
    bias_q = jnp.concatenate([jnp.sum(f32(d[...]), axis=0, keepdims=True) for d in (dq_a, dq_out)], axis=1)
    bias_v = jnp.concatenate(
        [jnp.sum(f32(d[:, pl.ds(side, side)]), axis=0, keepdims=True) for d in (dkv_a, dkv_out)], axis=1
    )
    vec = vec_in[...] + jnp.concatenate(
        [gain_sum, zero, shift_sum, zero, bias_q, bias_v, zero, zero], axis=0
    )
    lane = lax.broadcasted_iota(jnp.int32, (8, 128), 1)
    line = lax.broadcasted_iota(jnp.int32, (8, 128), 0)
    for group in range(2):
        cols = pl.ds(384 * group, 384)
        vec_parts = unpack96(vec[:, 384 * group : 384 * group + 384])
        upb_parts = unpack96(jnp.broadcast_to(upb_in[:, cols], (8, 384)))
        for k in range(4):
            sums_out[4 * group + k] = jnp.concatenate(
                [
                    jnp.where(lane < 96, vec_parts[k], 0.0),
                    jnp.where((lane < 96) & (line == p), upb_parts[k], 0.0),
                ],
                axis=1,
            )


def back_c_kernel(h_in, dq, dkv, sums_in, other, mine, stage, sems):
    blank = jnp.zeros((8, 128), jnp.float32)
    qkv_weight(
        h_in, dq, dkv, stage, lambda shard, _row: [jnp.concatenate([sums_in[shard], blank], axis=1)]
    )
    scatter(stage, other, mine, sems)


def tokens_kernel(own, near, dr, xo, vec_in, grad_out):
    tok = own.shape[0]
    hat, rate = norm_parts(f32(xo[pl.ds(0, tok), :]))
    grad = own[...] + f32(near[...])
    grad_out[...] = dr[...] + norm_back(grad, hat, rate, vec_in[0:1, :])


def finish_f_kernel(f0, fx, fc, fcx, up, down, held):
    x, c, _y, _z = place()
    rows = f0.shape[0] // 2
    for (xx, cc), f in zip(corners(x, c), (f0, fx, fc, fcx), strict=True):
        p = 2 * xx + cc
        held[p] = f[pl.ds(0, rows), :]
        down[pl.ds(pl.multiple_of(rows * p, 16), rows), :] = f32(f[pl.ds(rows, rows), :])
    for group in range(2):
        parts = [unpack96(f32(held[k, :, pl.ds(384 * group, 384)])) for k in range(4)]
        for shard in range(4):
            up[:, pl.ds(384 * (4 * group + shard), 384)] = pack96([part[shard] for part in parts])


def finish_q_kernel(f0, fx, fc, fcx, qkv, out, gains, shifts, biases, up_bias):
    x, c, _y, _z = place()
    side = out.shape[1] // 2
    for (xx, cc), piece in zip(corners(x, c), (f0, fx, fc, fcx), strict=True):
        rows = pl.ds(pl.multiple_of(48 * cc + 24 * xx, 8), 24)
        blocks = f32(piece[...])
        for number in range(3):
            first, second = 24 * number, 24 * (number + 5)
            qkv[rows, pl.ds(2 * side * number, side)] = blocks[first : first + 24]
            qkv[rows, pl.ds(2 * side * number + side, side)] = blocks[second : second + 24]
        out[rows, pl.ds(0, side)] = blocks[72:96]
        out[rows, pl.ds(side, side)] = blocks[96:120]
    sums = f32(f0[...])[192:]
    part = gains.shape[1]
    gains[...] = sums[0:2, :part]
    shifts[...] = sums[2:4, :part]
    biases[...] = sums[4:8, :part]
    ups = sums[:, 128:256]
    packed = pack96([jnp.broadcast_to(ups[k : k + 1], (8, 128)) for k in range(4)])
    up_bias[...] = packed[0]


HB = pl.BlockSpec(memory_space=pltpu.HBM)
VM = pl.BlockSpec(memory_space=pltpu.VMEM)
AN = pl.BlockSpec(memory_space=pl.ANY)


def shape_of(shape, dtype):
    return jax.ShapeDtypeStruct(shape, dtype)


def call(kernel, ins, outs, out_shape, scratch=(), vmem=40, flops=0, moved=0, aliases=None):
    return pl.pallas_call(
        kernel,
        in_specs=ins,
        out_specs=outs,
        out_shape=out_shape,
        scratch_shapes=list(scratch),
        input_output_aliases=aliases or {},
        compiler_params=pltpu.CompilerParams(vmem_limit_bytes=vmem << 20),
        cost_estimate=pl.CostEstimate(flops=flops, bytes_accessed=moved, transcendentals=0),
    )


def fence(*values):
    return lax.optimization_barrier(values)


def swap_rep(value, bit):
    return lax.ppermute(value, "rep", [(k, k ^ bit) for k in range(4)])


def to_core(value):
    return swap_rep(value, 1)


def to_x(value):
    return swap_rep(value, 2)


def to_y(value):
    return lax.ppermute(value, "seq", [(k, k ^ 1) for k in range(8)])


def to_z(value, steps):
    return lax.ppermute(value, "seq", [(k, (k + 2 * steps) % 8) for k in range(8)])


def join(*parts):
    return jnp.concatenate(parts, axis=0)


def on_device_fast(
    tokens,
    segment_ids,
    query_key_value_weight,
    output_weight,
    up_weight,
    down_weight,
    ln_gains,
    ln_biases,
    biases,
    up_projection_bias,
    cotangent,
):
    seq = lax.axis_index("seq")
    y = seq % 2
    tok, width = tokens.shape[1:]
    hidden = up_weight.shape[1]
    keys = 5 * tok
    bf, fl = jnp.bfloat16, jnp.float32
    dma = pltpu.SemaphoreType.DMA
    grad_y = cotangent[0]
    own_tokens, piece_q, piece_f, piece_u, piece_d = call(
        prep_kernel,
        [HB] * 10,
        [VM] * 5,
        [
            shape_of((tok + 8, width), bf),
            shape_of((48, 2 * width + 128), bf),
            shape_of((192, width), bf),
            shape_of((96, width), bf),
            shape_of((96, width), bf),
        ],
        [
            pltpu.VMEM((8, width), fl),
            pltpu.VMEM((96, hidden), bf),
            pltpu.VMEM((2, 96), bf),
            pltpu.VMEM((2, 96), bf),
            pltpu.VMEM((4, 96), bf),
            pltpu.VMEM((1, tok), jnp.int32),
            pltpu.VMEM((384,), bf),
            dma((11,)),
        ],
        vmem=60, moved=4 * 10**6,
    )(
        tokens, segment_ids, query_key_value_weight, output_weight, up_weight, down_weight,
        ln_gains, ln_biases, biases, up_projection_bias,
    )

    q1, q3, q_y0, dy_x = fence(to_z(piece_q, 1), to_z(piece_q, 3), to_y(piece_q), to_x(grad_y))
    own_tokens, piece_f, q1, q_y0 = fence(own_tokens, piece_f, q1, q_y0, q3, dy_x)[:4]
    q2, x2, q_xy0, f_y0 = fence(to_z(q1, 1), to_z(own_tokens, 1), to_x(q_y0), to_y(piece_f))
    q_z = join(q1, q2, q3)
    q_z, x2, piece_d = fence(q_z, x2, piece_d, q_xy0, f_y0)[:3]
    q_y, q_xz, x4, f3d = fence(to_y(q_z), to_x(q_z), to_z(x2, 1), to_z(piece_d, 3))
    near = jnp.where(y == 0, own_tokens, x2)
    far = jnp.where(y == 0, x2, x4)
    near_far, q_y, piece_f, piece_u = fence(
        jnp.stack([near, far]), q_y, piece_f, piece_u, q_xz, f3d
    )[:4]
    crossed, q_xy, f1, f3u = fence(to_y(near_far), to_x(q_y), to_z(piece_f, 1), to_z(piece_u, 3))
    x1, x3 = crossed[0], crossed[1]
    q_z, q_y0, q_y, q_xz, q_xy0, q_xy = fence(q_z, q_y0, q_y, q_xz, q_xy0, q_xy, f1, f3u, crossed)[:6]
    q_cz, q_cy0, q_cy, q_cxz, q_cxy0, q_cxy = fence(
        *(to_core(v) for v in (q_z, q_y0, q_y, q_xz, q_xy0, q_xy))
    )
    f_13, f_1, q_cz = fence(join(f1, f3u, f3d), f1, q_cz, q_cy0, q_cy, q_cxz, q_cxy0, q_cxy)[:3]
    f_y13, f2 = to_y(f_13), to_z(f_1, 1)
    dy_c, dy_xc = to_core(grad_y), to_core(dy_x)

    def pieces(value):
        return value.reshape(value.shape[0] // 48, 48, value.shape[1])

    got_q = [
        pieces(v)
        for v in (q_z, q_y0, q_y, q_xz, q_xy0, q_xy, q_cz, q_cy0, q_cy, q_cxz, q_cxy0, q_cxy)
    ]
    seg = jnp.concatenate([segment_ids, segment_ids], axis=1)
    front = call(
        front_kernel,
        [VM] * 6 + [AN] * 15,
        [VM] * 11,
        [
            shape_of((tok, width), bf),
            shape_of((keys, 2 * width), bf),
            shape_of((keys, width), bf),
            shape_of((tok, width), bf),
            shape_of((width // 128, 1, 2 * tok), fl),
            shape_of((1, 2 * tok), jnp.int32),
            shape_of((8, width), fl),
            shape_of((8, width), fl),
            shape_of((width, width), bf),
            shape_of((tok, width), fl),
            shape_of((tok, width), bf),
        ],
        [
            pltpu.VMEM((width, 3 * width), bf),
            pltpu.VMEM((8, 16, 128), bf),
            pltpu.VMEM((keys, 2 * tok), fl),
            dma((2 + 56,)),
            dma((8,)),
        ],
        flops=7 * 10**9,
        vmem=16, moved=12 * 10**6,
    )(
        seg, own_tokens, x1, x2, x3, x4, piece_q, query_key_value_weight, output_weight, *got_q,
    )
    *front, f_y13, f2, dy_c, dy_xc = fence(*front, f_y13, f2, dy_c, dy_xc)
    queries, kv, normed, attended, lse, start, vec, upb, w_out, residual, hidden_2 = front
    w_half = call(
        assemble_kernel,
        [AN] * 7,
        [VM] * 2,
        [shape_of((width, width), bf)] * 2,
        [dma((14,))],
        vmem=4,
        moved=5 * 10**6,
    )(piece_f, f1, f2, f3u, f3d, f_y0, f_y13)
    h_x, h_c, f_y2u, f_y2d, *w_half = fence(
        to_x(hidden_2), to_core(hidden_2), to_y(f2[:96]), to_z(f_y13[96:192], 1), *w_half
    )
    act = shape_of((2 * tok, width), bf)
    acts = shape_of((4 * tok, width), bf)
    feed_shapes = [shape_of((tok, width), fl), shape_of((tok, width), bf)]
    *near_acts, keep_a, send_a, w_up, w_down = call(
        near_kernel,
        [VM] * 5 + [AN] * 2 + [VM] * 2,
        [VM] * 8,
        [act] * 4 + feed_shapes + [shape_of((width, width), bf)] * 2,
        [dma((2,))],
        flops=3 * 10**9,
        vmem=8,
        moved=6 * 10**6,
        aliases={7: 6, 8: 7},
    )(hidden_2, h_c, grad_y, dy_c, upb, f_y2u, f_y2d, *w_half)
    h_xc = to_core(h_x)
    keep_a, send_a, h_xc, w_up = fence(keep_a, send_a, h_xc, w_up)
    came_a = to_core(send_a)
    *all_acts, send_b = call(
        far_c_kernel,
        [VM] * 5 + [AN] * 4,
        [VM] * 5,
        [acts] * 4 + feed_shapes[1:],
        [dma((4,))],
        flops=15 * 10**8,
        vmem=8,
        moved=6 * 10**6,
    )(h_xc, dy_xc, upb, w_up, w_down, *near_acts)
    send_b, came_a, h_x = fence(send_b, came_a, h_x)
    came_b = to_core(send_b)
    *all_acts, keep_b = call(
        far_x_kernel,
        [VM] * 9,
        [VM] * 5,
        [acts] * 4 + feed_shapes[:1],
        flops=3 * 10**9,
        vmem=8,
        moved=6 * 10**6,
        aliases={5: 0, 6: 1, 7: 2, 8: 3},
    )(h_x, dy_x, upb, w_up, w_down, *all_acts)
    keep_b, came_b, *all_acts = fence(keep_b, came_b, *all_acts)
    back_x = to_x(b16(keep_b + f32(came_b)))
    u_terms, d_terms, upb_g, y_keep, y_send = call(
        weights_kernel,
        [VM] * 5,
        [AN, AN] + [VM] * 3,
        [
            shape_of((2, 4, 96, width), bf),
            shape_of((2, 4, 96, width), bf),
            shape_of((1, width), fl),
            shape_of((2, tok, width), fl),
            shape_of((2, tok, width), bf),
        ],
        [pltpu.VMEM((2, width, width), bf), dma((16,))],
        flops=3 * 10**9,
        vmem=12,
        moved=6 * 10**6,
    )(*all_acts, w_down)
    back_x, u_terms, d_terms, y_send = fence(back_x, u_terms, d_terms, y_send)
    u_came = to_y(u_terms[1])
    came_y = to_core(y_send)
    grad_first, grad_attended, dw_out, vec_g = call(
        post_kernel,
        [VM] * 8,
        [VM] * 4,
        [
            shape_of((tok, width), fl),
            shape_of((tok, width), bf),
            shape_of((width, width), fl),
            shape_of((8, width), fl),
        ],
        vmem=12,
        flops=10**9,
        moved=4 * 10**6,
    )(residual, keep_a, came_a, back_x, grad_y, vec, w_out, attended)
    back_scratch = [
        pltpu.VMEM((keys, 2 * tok), fl),
    ]
    qa_other, qa_mine, dq_a, dkv_a = call(
        back_a_kernel,
        [VM] * 7,
        [AN] * 2 + [VM] * 2,
        [
            shape_of((2, 2, 4, 120, width // 2), bf),
            shape_of((2, 2, 4, 120, width // 2), bf),
            shape_of((tok, width // 2), bf),
            shape_of((keys, width), bf),
        ],
        back_scratch + [pltpu.VMEM((2, 2, 8, 120, width // 2), bf), dma((32,))],
        flops=5 * 10**9,
        vmem=16, moved=10 * 10**6,
    )(start, queries, kv, normed, lse, grad_attended, dw_out)

    def both(mine, came):
        return lambda *index: f32(mine[index]) + f32(came[index])

    def z_sum(part, *came):
        return b16(part(0) + sum(f32(v) for v in came))

    dq_a, qa_other, u_came, came_y, d_send = fence(
        dq_a, qa_other, u_came, came_y, d_terms[1]
    )
    d_came, qa_came = to_y(d_send), to_core(qa_other)
    u_part = both(u_terms[0], u_came)
    u_z = [to_z(b16(u_part(step)), step) for step in (1, 2, 3)]
    dq_b, dkv_b, p_own, p_y, p_z, sums = call(
        back_b_kernel,
        [VM] * 14 + [AN] * 13,
        [VM] * 6,
        [
            shape_of((tok, width // 2), bf),
            shape_of((keys, width), bf),
            shape_of((tok, width), fl),
            shape_of((2, tok, width), bf),
            shape_of((2, tok, width), bf),
            shape_of((8, 8, 256), fl),
        ],
        [pltpu.VMEM((width, 3 * width), bf)] + back_scratch + [dma((1 + 28,))],
        flops=6 * 10**9,
        vmem=20, moved=10 * 10**6,
    )(
        start, queries, kv, lse, grad_attended, vec_g, upb_g, dq_a, dkv_a,
        own_tokens, x1, x2, x3, x4, query_key_value_weight, *got_q,
    )
    dq_b, qa_came, d_came, p_y, *u_z = fence(dq_b, qa_came, d_came, p_y, *u_z)
    p_came = to_y(p_y)
    qa_1 = both(qa_mine, qa_came)
    qa_x = to_x(b16(qa_1(1)))
    d_part = both(d_terms[0], d_came)
    d_z2 = to_z(b16(d_part(2)), 1)
    qb_other, qb_mine = call(
        back_c_kernel,
        [VM] * 4,
        [AN] * 2,
        [
            shape_of((2, 2, 4, 80, width // 2), bf),
            shape_of((2, 2, 4, 80, width // 2), bf),
        ],
        [pltpu.VMEM((2, 2, 8, 80, width // 2), bf), dma((32,))],
        flops=3 * 10**9,
        vmem=12, moved=6 * 10**6,
    )(normed, dq_b, dkv_b, sums)
    qb_came = [to_core(qb_other[k]) for k in range(2)]
    *qb_came, qa_x, p_came, d_z2 = fence(*qb_came, qa_x, p_came, d_z2)
    even = y == 0
    sum_own = p_own + jnp.where(even, f32(p_came[0]), 0.0)
    sum_4 = b16(f32(p_z[1]) + jnp.where(even, 0.0, f32(p_came[1])))
    sum_2 = f32(p_z[0]) + jnp.where(even, f32(p_came[1]), f32(p_came[0]))
    def qa_2(*index):
        return qa_1(0, *index) + f32(qa_x[index])

    def qb_1(side, *index):
        return f32(qb_mine[(side,) + index]) + f32(qb_came[side][index])

    qb_x, qa_y, hop, d_z1, d_z3 = fence(
        to_x(b16(qb_1(1))),
        to_y(b16(qa_2(1))),
        to_z(sum_4, 3),
        to_z(b16(d_part(1) + f32(d_z2)), 1),
        to_z(b16(d_part(3)), 3),
    )

    def qb_2(*index):
        return qb_1(0, *index) + f32(qb_x[index])

    f_tot = join(z_sum(u_part, *u_z), z_sum(d_part, d_z1, d_z3))
    fy_tot = join(f_tot, b16(y_keep[1] + f32(came_y[1])))
    qb_y, back_2, f_tot, fy_tot = fence(
        to_y(b16(qb_2(1))), to_z(b16(sum_2 + f32(hop)), 3), f_tot, fy_tot
    )

    def q_3(*index):
        first = qa_2(0, *index) + f32(qa_y[index])
        return jnp.concatenate([first, qb_2(0, *index) + f32(qb_y[index])], axis=-2)

    grad_tokens = call(
        tokens_kernel, [VM] * 5, VM, shape_of((tok, width), fl), vmem=4, moved=3 * 10**6
    )(sum_own, back_2, grad_first, own_tokens, vec)
    *q_z, over_x, f_tot = fence(*(to_z(b16(q_3(step)), step) for step in (1, 2, 3)), to_x(fy_tot), f_tot)
    f_x, back_y = over_x[:tok], over_x[tok:]
    q_sum = z_sum(q_3, *q_z)
    q_fx, q_fc = to_x(q_sum), to_core(q_sum)
    grad_up, grad_down = call(
        finish_f_kernel,
        [VM] * 4,
        [VM] * 2,
        [shape_of(up_weight.shape, fl), shape_of(down_weight.shape, fl)],
        [pltpu.VMEM((4, 96, width), bf)],
        vmem=8,
        moved=4 * 10**6,
    )(f_tot, f_x, to_core(f_tot), to_core(f_x))
    q_fx, q_fc, grad_up, grad_down = fence(q_fx, q_fc, grad_up, grad_down)
    q_fxc = to_core(q_fx)
    result = b16(residual + vec[7:8] + y_keep[0] + f32(came_y[0]) + f32(back_y))
    grad_qkv, grad_out, grad_gains, grad_shifts, grad_biases, grad_up_bias = call(
        finish_q_kernel,
        [VM] * 4,
        [VM] * 6,
        [
            shape_of(query_key_value_weight.shape, fl),
            shape_of(output_weight.shape, fl),
            shape_of(ln_gains.shape, fl),
            shape_of(ln_biases.shape, fl),
            shape_of(biases.shape, fl),
            shape_of(up_projection_bias.shape, fl),
        ],
        vmem=8,
        moved=3 * 10**6,
    )(q_sum, q_fx, q_fc, q_fxc)
    return (
        result[None],
        grad_tokens[None],
        grad_qkv,
        grad_out,
        grad_up,
        grad_down,
        grad_gains,
        grad_shifts,
        grad_biases,
        grad_up_bias,
    )


def solution(mesh):
    placed = (
        P("rep", "seq", None),
        P("rep", "seq"),
        P("seq", None),
        P("seq", None),
        P("seq", None),
        P("seq", None),
        P(None, "seq"),
        P(None, "seq"),
        P(None, "seq"),
        P("seq"),
        P("rep", "seq", None),
    )
    shape = dict(mesh.shape)
    small_slice = shape["rep"] == 4 and shape["seq"] == 8
    return jax.shard_map(
        on_device_fast if small_slice else on_device,
        mesh=mesh,
        in_specs=placed,
        out_specs=(
            P("rep", "seq", None),
            P("rep", "seq", None),
            P("seq", None),
            P("seq", None),
            P("seq", None),
            P("seq", None),
            P(None, "seq"),
            P(None, "seq"),
            P(None, "seq"),
            P("seq"),
        ),
        check_vma=False,
    )
```
